32 devices in a mesh: gx: 8 (over z, x), gy: 4 (over y, core).
Axes of the slice: x: 2, y: 2, z: 4, core: 2. Of those that a mesh axis runs over, the one named last changes fastest.
Arguments:
- residual: float32 [2, 256, 192, 256], P(None, 'gx', 'gy'), may hold values from -6 to 6
- accum_diag: float32 [2, 256, 192, 256], P(None, 'gx', 'gy'), may hold values from 2 to 4
- accum_cross: float32 [2, 256, 192, 256], P(None, 'gx', 'gy'), may hold values from -1 to 1
- mask: int32 [256, 192, 256], P('gx', 'gy'), may hold values from 0 to 1
- trans_x: float32 [256, 192, 256], P('gx', 'gy'), may hold values from 0.1 to 10
- trans_y: float32 [256, 192, 256], P('gx', 'gy'), may hold values from 0.1 to 10
- trans_z: float32 [256, 192, 256], P('gx', 'gy'), may hold values from 0.1 to 10
- frac_flow: float32 [256, 192, 256], P('gx', 'gy'), may hold values from 0 to 1
- split_layer: int32 [32, 24], P('gx', 'gy'), may hold values from 64 to 191
- coarse_inverse: float32 [8, 192, 192], P('gx'), may hold values from -0.0034179688 to 0.0034179688
Outputs:
- correction: float32 [2, 256, 192, 256], P(None, 'gx', 'gy')
The draws below stay inside these ranges and needn't reach their ends.
All inputs are finite; a program needn't handle non-finite values.
Results may differ from the reference program's by a relative error of at most 0.00027.
Values sent between devices are 32-bit elements; how exact they have to be, the bound alone decides.
No kernel may reach another device: no remote copies, remote signals or barrier semaphores. Data moves between devices by JAX's collectives and lax.ppermute only.
A program may use at most 192 MiB of HBM per device.

```python
import math
import jax
import jax.numpy as jnp
from jax import lax

CX = 32
CY = 48
NZ = 256
NX = 256
NY = 192
NC = 192
CELLS_AGG = 16384
N_GX = 8
N_GY = 4


def draw_mask(key, part):
    tile_rows = jnp.arange(NX, dtype=jnp.int32) // CX
    tile_cols = jnp.arange(NY, dtype=jnp.int32) // CY
    pattern = (tile_rows[:, None] * 5 + tile_cols[None, :] * 3) % 8
    percent = 35 + 60 * pattern // 7
    drawn = jax.random.randint(key, (NX, NY, NZ), 0, 100, dtype=jnp.int32)
    return (drawn < percent[:, :, None]).astype(jnp.int32)


def plant(values, stream_key, smallest, top_value):
    spot = [jax.random.randint(jax.random.fold_in(stream_key, axis), (), 0, length) for axis, length in enumerate(values.shape)]
    longest = values.shape.index(max(values.shape))
    next_to = spot[:longest] + [(spot[longest] + 1) % values.shape[longest]] + spot[longest + 1:]
    return values.at[tuple(spot)].set(smallest).at[tuple(next_to)].set(top_value)


def steps_of(own_key, dims, shards, smallest, top_value):
    level, own = 1.0, jax.random.fold_in(own_key, 6)
    for dim, parts in shards:
        heights = jnp.exp(jax.random.uniform(jax.random.fold_in(own, dim), (parts,), jnp.float32, smallest / len(shards), top_value / len(shards)))
        level = level * jnp.repeat(heights, dims[dim] // parts).reshape([-1 if axis == dim else 1 for axis in range(len(dims))])
    return level


def bell_draw(stream_key, extent, deviation, reach, cuts=(), held_as=jnp.bfloat16):
    entries = jax.random.normal(stream_key, extent, jnp.float32) * deviation
    if len(cuts) > 0:
        entries = steps_of(stream_key, extent, cuts, -0.22, 0.18) * entries
    return jnp.clip(entries, min=-reach, max=reach).astype(held_as)


def setup_inputs(seed: int = 0) -> dict:
    keys = jax.random.split(jax.random.key(seed), 11)
    residual = bell_draw(keys[0], (2, NX, NY, NZ), 1.0, 6.0, ((1, 8), (2, 4)), jnp.float32)
    accum_diag = jnp.clip(2.0 + 2.0 * jax.random.uniform(keys[1], (2, NX, NY, NZ), jnp.float32) ** steps_of(keys[1], (2, NX, NY, NZ), ((1, 8), (2, 4)), -0.2, 0.2), 2.0, 4.0)
    accum_cross = jnp.clip(jax.random.uniform(keys[2], (2, NX, NY, NZ), jnp.float32, -1.0, 1.0) * steps_of(keys[2], (2, NX, NY, NZ), ((1, 8), (2, 4)), -0.4, 0.0), -1.0, 1.0)
    mask = draw_mask(jax.random.fold_in(keys[10], 71), 0)
    trans_x = jnp.clip(jnp.exp(math.log(10.0) - 4.6051702 * jax.random.uniform(keys[4], (NX, NY, NZ), jnp.float32) ** steps_of(keys[4], (NX, NY, NZ), ((0, 8), (1, 4)), -0.2, 0.2)), 0.1, 10.0)
    trans_y = jnp.clip(jnp.exp(math.log(10.0) - 4.6051702 * jax.random.uniform(keys[5], (NX, NY, NZ), jnp.float32) ** steps_of(keys[5], (NX, NY, NZ), ((0, 8), (1, 4)), -0.2, 0.2)), 0.1, 10.0)
    trans_z = jnp.clip(jnp.exp(math.log(10.0) - 4.6051702 * jax.random.uniform(keys[6], (NX, NY, NZ), jnp.float32) ** steps_of(keys[6], (NX, NY, NZ), ((0, 8), (1, 4)), -0.2, 0.2)), 0.1, 10.0)
    frac_flow = jnp.clip(1.0 * jax.random.uniform(keys[7], (NX, NY, NZ), jnp.float32) ** steps_of(keys[7], (NX, NY, NZ), ((0, 8), (1, 4)), -0.2, 0.2), 0.0, 1.0)
    split_layer = plant(jax.random.randint(keys[8], (NX // 8, NY // 8), NZ // 4, 3 * NZ // 4), jax.random.fold_in(keys[8], 1), NZ // 4, (3 * NZ // 4) - 1).astype(jnp.int32)
    coarse_inverse = bell_draw(keys[9], (N_GX, NC, NC), (NC * CELLS_AGG) ** -0.5, 0.0034179688, ((0, 8),), jnp.float32)
    return {"residual": residual, "accum_diag": accum_diag, "accum_cross": accum_cross, "mask": mask, "trans_x": trans_x, "trans_y": trans_y, "trans_z": trans_z, "frac_flow": frac_flow, "split_layer": split_layer, "coarse_inverse": coarse_inverse}


relaxation = 2.0 / 3.0


def forward(field, along):
    size = field.shape[along]
    moved = lax.slice_in_dim(field, 1, size, axis=along)
    zero_shape = list(field.shape)
    zero_shape[along] = 1
    return jnp.concatenate([moved, jnp.zeros(zero_shape, field.dtype)], axis=along)


def backward(field, along):
    size = field.shape[along]
    moved = lax.slice_in_dim(field, 0, size - 1, axis=along)
    zero_shape = list(field.shape)
    zero_shape[along] = 1
    return jnp.concatenate([jnp.zeros(zero_shape, field.dtype), moved], axis=along)


def face_coefs(active, tran_x, tran_y, tran_z):
    face_x = tran_x * active * forward(active, 0)
    face_y = tran_y * active * forward(active, 1)
    face_z = tran_z * active * forward(active, 2)
    return face_x, face_y, face_z


def face_total(face_x, face_y, face_z):
    return face_x + backward(face_x, 0) + face_y + backward(face_y, 1) + face_z + backward(face_z, 2)


def net_flux(field, face_x, face_y, face_z):
    beside = face_x * forward(field, 0) + backward(face_x, 0) * backward(field, 0)
    beside = beside + face_y * forward(field, 1) + backward(face_y, 1) * backward(field, 1)
    beside = beside + face_z * forward(field, 2) + backward(face_z, 2) * backward(field, 2)
    return face_total(face_x, face_y, face_z) * field - beside


def weighted(face_x, face_y, face_z, fraction):
    return (face_x * (fraction + forward(fraction, 0)) * 0.5,
            face_y * (fraction + forward(fraction, 1)) * 0.5,
            face_z * (fraction + forward(fraction, 2)) * 0.5)


def below_split(split_layer, layers):
    levels = jnp.arange(layers, dtype=jnp.int32)
    return (levels[None, None, :] < split_layer[:, :, None]).astype(jnp.float32)


def restrict(field, split_layer):
    rows_b = field.shape[0] // 8
    cols_b = field.shape[1] // 8
    layers = field.shape[2]
    blocks = field.reshape(rows_b, 8, cols_b, 8, layers).sum(axis=(1, 3))
    lower_part = below_split(split_layer, layers)
    return jnp.stack([jnp.sum(blocks * lower_part, axis=-1), jnp.sum(blocks * (1.0 - lower_part), axis=-1)], axis=-1)


def prolong(values, split_layer, layers):
    rows_b = values.shape[0]
    cols_b = values.shape[1]
    lower_part = below_split(split_layer, layers)
    cellwise = values[:, :, 0:1] * lower_part + values[:, :, 1:2] * (1.0 - lower_part)
    spread = jnp.broadcast_to(cellwise[:, None, :, None, :], (rows_b, 8, cols_b, 8, layers))
    return spread.reshape(rows_b * 8, cols_b * 8, layers)


def reference(residual, accum_diag, accum_cross, mask, trans_x, trans_y, trans_z, frac_flow, split_layer, coarse_inverse):
    active = mask.astype(jnp.float32)
    pressure_res, saturation_res = residual[0], residual[1]
    diag_pp, diag_ss = accum_diag[0], accum_diag[1]
    cross_ps, cross_sp = accum_cross[0], accum_cross[1]
    weighting = cross_ps / diag_ss
    pressure_rhs = active * (pressure_res - weighting * saturation_res)
    schur_diag = active * (diag_pp - weighting * cross_sp) + (1.0 - active)
    face_x, face_y, face_z = face_coefs(active, trans_x, trans_y, trans_z)
    diagonal = schur_diag + face_total(face_x, face_y, face_z)
    sweep_one = relaxation * pressure_rhs / diagonal
    sweep_two = sweep_one + relaxation * (pressure_rhs - schur_diag * sweep_one - net_flux(sweep_one, face_x, face_y, face_z)) / diagonal
    remain = pressure_rhs - schur_diag * sweep_two - net_flux(sweep_two, face_x, face_y, face_z)
    coarse = restrict(remain, split_layer)
    grouped = coarse.reshape(N_GX, CX // 8, N_GY, CY // 8, 2).transpose(0, 2, 1, 3, 4).reshape(N_GX, NC)
    coarse_corr = jnp.einsum('tij,tj->ti', coarse_inverse, grouped, precision=lax.Precision.HIGHEST)
    back = coarse_corr.reshape(N_GX, N_GY, CX // 8, CY // 8, 2).transpose(0, 2, 1, 3, 4).reshape(NX // 8, NY // 8, 2)
    corrected = sweep_two + active * prolong(back, split_layer, NZ)
    jac_p = diag_pp * corrected + net_flux(corrected, face_x, face_y, face_z)
    wface_x, wface_y, wface_z = weighted(face_x, face_y, face_z, frac_flow)
    jac_s = cross_sp * corrected + net_flux(corrected, wface_x, wface_y, wface_z)
    update_p = pressure_res - jac_p
    update_s = saturation_res - jac_s
    determinant = diag_pp * diag_ss - cross_ps * cross_sp
    out_p = corrected + (diag_ss * update_p - cross_ps * update_s) / determinant
    out_s = (diag_pp * update_s - cross_sp * update_p) / determinant
    return jnp.stack([out_p, out_s])
```

```python
import functools

import jax
import jax.numpy as jnp
from jax import lax
from jax.experimental import pallas as pl
from jax.experimental.pallas import tpu as pltpu
from jax.sharding import PartitionSpec as P

relaxation = 2.0 / 3.0
F32 = jnp.float32
WHOLE = pl.BlockSpec(memory_space=pltpu.VMEM)
SCALARS = pl.BlockSpec(memory_space=pltpu.SMEM)
G = 8
EDGE_FIELDS = 4
PLANES = 3


def params(mib):
    return pltpu.CompilerParams(vmem_limit_bytes=mib << 20)


def cost(flops, size):
    return pl.CostEstimate(flops=flops, bytes_accessed=size, transcendentals=0)


def y_next(v):
    return pltpu.roll(v, v.shape[0] - 1, 0)


def y_prev(v):
    return pltpu.roll(v, 1, 0)


def z_next(v):
    return pltpu.roll(v, v.shape[1] - 1, 1)


def z_prev(v):
    return pltpu.roll(v, 1, 1)


def quasi_impes(active, rp, rs, dpp, dss, dps, dsp):
    weight = dps / dss
    return active * (rp - weight * rs), active * (dpp - weight * dsp) + (1.0 - active)


def swap_pairs(axis, size):
    near = [(i, i ^ 1) for i in range(size) if i ^ 1 < size]
    far = [(i, ((i + 1) ^ 1) - 1) for i in range(size) if 0 <= ((i + 1) ^ 1) - 1 < size]
    return near, far


def swap(message, axis, size):
    near, far = swap_pairs(axis, size)
    return lax.ppermute(message[0], axis, near), lax.ppermute(message[1], axis, far)


def y_message_kernel(split_ref, *refs):
    low, high = refs[:8], refs[8:16]
    near_ref, far_ref = refs[16:]
    even = lax.rem(lax.axis_index("gy"), 2) == 0
    step = pl.program_id(0)

    def fields(group):
        res, diag, crs, mask, tx, ty, tz, ff = group
        active = mask[...].astype(F32)
        b, c = quasi_impes(active, res[0], res[1], diag[0], diag[1], crs[0], crs[1])
        return active, b, c, tx[...], ty[...], tz[...], ff[...]

    shape = low[3].shape
    s = lax.broadcasted_iota(jnp.int32, shape, 1)
    lane = lax.broadcasted_iota(jnp.int32, shape, 2)

    def turn(v, k):
        return jnp.stack([pltpu.roll(v[i], k, 0) for i in range(v.shape[0])])

    a, b, c, tx, ty, tz, ff = fields(high)
    lower = (lane < split_ref[step, split_ref.shape[1] - 1]).astype(F32)
    up = (
        jnp.where(s >= 5, a, jnp.where(s >= 2, turn(ty, 5), turn(tx, 2))),
        jnp.where(
            s >= 6,
            b,
            jnp.where(
                s >= 4,
                turn(c, 6),
                jnp.where(s >= 2, turn(tz, 4), jnp.where(s == 1, turn(ff, 2), lower)),
            ),
        ),
    )
    a, b, c, tx, ty, tz, ff = fields(low)
    lower = (lane < split_ref[step, 0]).astype(F32)
    down = (
        jnp.where(s < 3, a, jnp.where(s < 6, turn(ty, 3), turn(tx, 6))),
        jnp.where(
            s < 2,
            b,
            jnp.where(
                s < 4,
                turn(c, 2),
                jnp.where(s < 6, turn(tz, 4), jnp.where(s == 6, turn(ff, 6), lower)),
            ),
        ),
    )
    for k in range(2):
        near_ref[:, 8 * k : 8 * k + 8, :] = jnp.where(even, up[k], down[k])
        far_ref[:, 8 * k : 8 * k + 8, :] = jnp.where(even, down[k], up[k])


class Ghosts:
    def __init__(self, near_ref, far_ref):
        self.refs = near_ref, far_ref
        self.even = lax.rem(lax.axis_index("gy"), 2) == 0

    def tiles(self, x, k):
        near, far = (ref[x, 8 * k : 8 * k + 8, :] for ref in self.refs)
        return jnp.where(self.even, near, far), jnp.where(self.even, far, near)

    def pick(self, tiles, high_turn, low_turn, rings):
        high, low = tiles
        s = lax.broadcasted_iota(jnp.int32, high.shape, 0)
        high = pltpu.roll(high, high_turn, 0) if high_turn else high
        low = pltpu.roll(low, low_turn, 0) if low_turn else low
        return jnp.where(s < rings, high, jnp.where(s >= G - rings, low, 0.0))

    def first(self, x):
        t = self.tiles(x, 0)
        return self.pick(t, 0, 0, 3), self.pick(t, 2, 6, 2), self.pick(t, 5, 3, 3)

    def second(self, x):
        t = self.tiles(x, 1)
        c = jnp.maximum(self.pick(t, 6, 2, 2), 1.0)
        return self.pick(t, 0, 0, 2), c, self.pick(t, 4, 4, 2)

    def active(self, x):
        return self.pick(self.tiles(x, 0), 0, 0, 3)

    def frac_and_lower(self, x):
        t = self.tiles(x, 1)
        return self.pick(t, 2, 6, 1), self.pick(t, 1, 7, 1)


def join(own, ghost):
    return jnp.concatenate([own, ghost], axis=0)


class Rows:
    def __init__(self, res, diag, crs, mask, tx, ty, tz, ghosts):
        self.res, self.diag, self.crs, self.mask = res, diag, crs, mask
        self.tx, self.ty, self.tz, self.ghosts = tx, ty, tz, ghosts

    def active(self, x):
        return join(self.mask[x].astype(F32), self.ghosts.active(x))

    def trans_x(self, x):
        return join(self.tx[x], self.ghosts.first(x)[1])

    def all(self, x):
        ga, gtx, gty = self.ghosts.first(x)
        gb, gc, gtz = self.ghosts.second(x)
        own = self.mask[x].astype(F32)
        b, c = quasi_impes(
            own, self.res[0, x], self.res[1, x], self.diag[0, x], self.diag[1, x],
            self.crs[0, x], self.crs[1, x],
        )
        a = join(own, ga)
        lane = lax.broadcasted_iota(jnp.int32, a.shape, 1)
        ey = join(self.ty[x], gty) * a * y_next(a)
        ez = jnp.where(lane < a.shape[1] - 1, join(self.tz[x], gtz) * a * z_next(a), 0.0)
        return a, join(b, gb), join(c, gc), join(self.tx[x], gtx) * a, ey, ez


def in_plane_total(ey, ez):
    return ey + y_prev(ey) + ez + z_prev(ez)


def in_plane_sum(ey, ez, p):
    return ey * y_next(p) + y_prev(ey * p) + ez * z_next(p) + z_prev(ez * p)


def x_message_kernel(split_ref, res, diag, crs, mask, tx, ty, tz, ff, ynear, yfar, inv, near_ref, far_ref):
    even = lax.rem(lax.axis_index("gx"), 2) == 0
    j = lax.axis_index("gy")
    rows = Rows(res, diag, crs, mask, tx, ty, tz, Ghosts(ynear, yfar))
    last = mask.shape[0] - 1
    own = mask.shape[1]
    ext = own + G
    per_tile = 2 * split_ref.shape[0] * split_ref.shape[1]
    a1, b1, c1, t1, ey1, ez1 = rows.all(last - 1)
    a0, b0, c0, t0, ey0, ez0 = rows.all(last)
    inner = t1 * a0
    beyond = rows.active(last - 2) * rows.trans_x(last - 2) * a1
    first = relaxation * b1 / (c1 + inner + beyond + in_plane_total(ey1, ez1))
    up = (b0, c0 + inner + in_plane_total(ey0, ez0), t0, ey0, ez0, inner * first, ff[last])
    a0, b0, c0, t0, ey0, ez0 = rows.all(0)
    a1, b1, c1, t1, ey1, ez1 = rows.all(1)
    inner = t0 * a1
    beyond = t1 * rows.active(2)
    first = relaxation * b1 / (c1 + inner + beyond + in_plane_total(ey1, ez1))
    down = (b0, c0 + inner + in_plane_total(ey0, ez0), a0, ey0, ez0, inner * first, ff[0])
    at = 0
    for k in range(EDGE_FIELDS + PLANES):
        n = ext if k < EDGE_FIELDS else own
        near_ref[at : at + n, :] = jnp.where(even, up[k][:n], down[k][:n])
        far_ref[at : at + n, :] = jnp.where(even, down[k][:n], up[k][:n])
        at += n
    wide = near_ref.shape[1]
    unknowns = inv.shape[2]
    top = inv[0, pl.ds(pl.multiple_of(j * per_tile + per_tile - 16, 8), 16), :]
    bottom = inv[0, pl.ds(pl.multiple_of(j * per_tile, 8), 16), :]
    for k in range(0, unknowns, wide):
        n = min(wide, unknowns - k)
        if n < wide:
            near_ref[at : at + 16, :] = jnp.zeros((16, wide), F32)
            far_ref[at : at + 16, :] = jnp.zeros((16, wide), F32)
        near_ref[at : at + 16, :n] = jnp.where(even, top[:, k : k + n], bottom[:, k : k + n])
        far_ref[at : at + 16, :n] = jnp.where(even, bottom[:, k : k + n], top[:, k : k + n])
        at += 16
    lane = lax.broadcasted_iota(jnp.int32, (1, wide), 1)
    zero = jnp.zeros((8, wide), F32)
    near_ref[at : at + 8, :] = zero
    far_ref[at : at + 8, :] = zero
    for q in range(split_ref.shape[1]):
        top = (lane < split_ref[split_ref.shape[0] - 1, q]).astype(F32)
        bottom = (lane < split_ref[0, q]).astype(F32)
        near_ref[at + q : at + q + 1, :] = jnp.where(even, top, bottom)
        far_ref[at + q : at + q + 1, :] = jnp.where(even, bottom, top)


def x_message_rows(own, unknowns, wide):
    return EDGE_FIELDS * (own + G) + PLANES * own + 16 * pl.cdiv(unknowns, wide) + 8


class Planes:
    def __init__(self, near_ref, far_ref, own):
        self.refs, self.own = (near_ref, far_ref), own
        self.even = lax.rem(lax.axis_index("gx"), 2) == 0

    def rows(self, at, n, side):
        near, far = (ref[at : at + n, :] for ref in self.refs)
        return jnp.where(self.even, near, far) if side else jnp.where(self.even, far, near)

    def field(self, k, side):
        ext = self.own + G
        if k < EDGE_FIELDS:
            return self.rows(k * ext, ext, side)
        at = EDGE_FIELDS * ext + (k - EDGE_FIELDS) * self.own
        return self.rows(at, self.own, side)

    def extra(self, at, n, side):
        return self.rows(EDGE_FIELDS * (self.own + G) + PLANES * self.own + at, n, side)


def interior_kernel(res, diag, crs, mask, tx, ty, tz, ynear, yfar,
                    act, rhs, tot, gain, fx, fy, fz, one, two, acc):
    rows = Rows(res, diag, crs, mask, tx, ty, tz, Ghosts(ynear, yfar))
    n = mask.shape[0]
    own = mask.shape[1]

    act[0] = rows.active(0)

    def faces(x, before):
        a, b, c, t, ey, ez = rows.all(x)

        @pl.when(x < n - 1)
        def _():
            act[x + 1] = rows.active(x + 1)

        here = t * act[jnp.minimum(x + 1, n - 1)]
        ex = jnp.where(x < n - 1, here, 0.0)
        total = c + ex + before + in_plane_total(ey, ez)
        g = relaxation / total
        rhs[x] = b
        tot[x] = total
        gain[x] = g
        fx[x] = jnp.where(x < n - 1, here, t)
        fy[x] = ey
        fz[x] = ez
        one[x] = g * b
        return ex

    lax.fori_loop(0, n, faces, jnp.zeros(act.shape[1:], F32))

    def second(x, carry):
        p = one[x]
        s = fx[x] * one[x + 1] + fx[x - 1] * one[x - 1] + in_plane_sum(fy[x], fz[x], p)
        two[x] = gain[x] * ((2.0 - relaxation) * rhs[x] + s)
        return carry

    lax.fori_loop(2, n - 2, second, 0)

    def rest(x):
        p = two[x]
        s = fx[x] * two[x + 1] + fx[x - 1] * two[x - 1] + in_plane_sum(fy[x], fz[x], p)
        return (rhs[x] - tot[x] * p + s)[:own]

    for q in range(n // 8):
        acc[q] = lax.fori_loop(
            max(8 * q, 3), min(8 * q + 8, n - 3), lambda x, v: v + rest(x), jnp.zeros((own, mask.shape[2]), F32)
        )


def edge_kernel(split_ref, xnear, xfar, act, rhs, tot, fx, fy, fz, one, two, acc, sent, edge_two, edge_fx):
    n, ext = act.shape[0], act.shape[1]
    own = ext - G
    wide = act.shape[2]
    planes = Planes(xnear, xfar, own)
    none = jnp.zeros((G, wide), F32)

    class Far:
        def __init__(self, side):
            self.b = planes.field(0, side)
            self.total = jnp.maximum(planes.field(1, side), 1.0)
            self.key = planes.field(2, side)
            self.ey = planes.field(3, side)
            self.ez = join(planes.field(4, side), none)
            self.beyond = join(planes.field(5, side), none)

    low, high = Far(0), Far(1)
    ex = {-1: low.key * act[0], n - 1: fx[n - 1] * high.key}
    edge_fx[0] = ex[-1]
    edge_fx[1] = ex[n - 1]
    total = {
        -1: low.total + ex[-1],
        0: tot[0] + ex[-1],
        n - 1: tot[n - 1] + ex[n - 1],
        n: high.total + ex[n - 1],
    }
    b_of = lambda x: low.b if x == -1 else high.b if x == n else rhs[x]
    ey_of = lambda x: low.ey if x == -1 else high.ey if x == n else fy[x]
    ez_of = lambda x: low.ez if x == -1 else high.ez if x == n else fz[x]
    ex_of = lambda x: ex[x] if x in ex else fx[x]
    total_of = lambda x: total[x] if x in total else tot[x]
    gain = {x: relaxation / total[x] for x in total}
    first = {x: gain[x] * b_of(x) for x in total}
    first_of = lambda x: first[x] if x in first else one[x]

    def beside(x, field_of):
        s = in_plane_sum(ey_of(x), ez_of(x), field_of(x))
        s = s + (low.beyond if x == -1 else ex_of(x - 1) * field_of(x - 1))
        return s + (high.beyond if x == n else ex_of(x) * field_of(x + 1))

    second = {}
    for slot, x in enumerate((-1, 0, 1, n - 2, n - 1, n)):
        g = gain[x] if x in gain else relaxation / tot[x]
        second[x] = g * ((2.0 - relaxation) * b_of(x) + beside(x, first_of))
        edge_two[slot] = second[x]
    second_of = lambda x: second[x] if x in second else two[x]

    def rest(x):
        return (b_of(x) - total_of(x) * second_of(x) + beside(x, second_of))[:own]

    rows_b, cols_b = split_ref.shape
    lane = lax.broadcasted_iota(jnp.int32, (1, wide), 1)
    lower, upper = [], []
    for q in range(rows_b):
        field = acc[q]
        for x in (0, 1, 2, n - 3, n - 2, n - 1):
            if x // 8 == q:
                field = field + rest(x)
        for r in range(cols_b):
            column = jnp.sum(field[8 * r : 8 * r + 8], axis=0, keepdims=True)
            below = lane < split_ref[q, r]
            lower.append(jnp.where(below, column, 0.0))
            upper.append(jnp.where(below, 0.0, column))
    count = rows_b * cols_b
    low_sum = jnp.sum(jnp.concatenate(lower, axis=0), axis=1, keepdims=True)
    high_sum = jnp.sum(jnp.concatenate(upper, axis=0), axis=1, keepdims=True)
    span = sent.shape[1]
    place = lax.broadcasted_iota(jnp.int32, (count, span), 1) - 2 * count * lax.axis_index("gy")
    which = 2 * lax.broadcasted_iota(jnp.int32, (count, span), 0)
    laid = jnp.where(place == which, low_sum, jnp.where(place == which + 1, high_sum, 0.0))
    sent[...] = jnp.broadcast_to(jnp.sum(laid, axis=0, keepdims=True), sent.shape)


def final_kernel(tiles_y, split_ref, res, diag, crs, frac, inv, ynear, yfar, xnear, xfar,
                 act, fx, fy, fz, two, edge_two, edge_fx, got, out, coarse, three, held, sems):
    i, j = lax.axis_index("gx"), lax.axis_index("gy")
    n, ext = act.shape[0], act.shape[1]
    own = ext - G
    wide = act.shape[2]
    unknowns = inv.shape[2]
    rows_b, cols_b = split_ref.shape
    per_tile = 2 * rows_b * cols_b
    ghosts = Ghosts(ynear, yfar)
    planes = Planes(xnear, xfar, own)

    all_got = got[...]
    owner = lax.broadcasted_iota(jnp.int32, all_got.shape, 0)

    def row_of(tile_row):
        mine = (owner >= tile_row * tiles_y) & (owner < (tile_row + 1) * tiles_y)
        return jnp.sum(jnp.where(mine, all_got, 0.0), axis=0, keepdims=True)

    coarse_res = row_of(i)

    def solve(tile):
        start = pl.multiple_of(jnp.clip(tile, 0, tiles_y - 1) * per_tile, 8)
        block = inv[0, pl.ds(start, per_tile), :]
        e = jnp.sum(block * coarse_res[:, :unknowns], axis=1, keepdims=True)
        return jnp.broadcast_to(e, (per_tile, wide))

    lane = lax.broadcasted_iota(jnp.int32, (1, wide), 1)
    s = lax.broadcasted_iota(jnp.int32, (G, wide), 0)
    mine, before, after = solve(j), solve(j - 1), solve(j + 1)

    def one_of(e, k):
        return jnp.broadcast_to(e[k : k + 1], (8, wide))

    for q in range(rows_b):
        for r in range(cols_b):
            k = 2 * (q * cols_b + r)
            coarse[q + 1, 8 * r : 8 * r + 8, :] = jnp.where(
                lane < split_ref[q, r], one_of(mine, k), one_of(mine, k + 1)
            )
        below = ghosts.frac_and_lower(8 * q)[1] > 0.5
        k_high, k_low = 2 * q * cols_b, 2 * (q * cols_b + cols_b - 1)
        coarse[q + 1, own:ext, :] = jnp.where(
            s == 0,
            jnp.where(below, one_of(after, k_high), one_of(after, k_high + 1)),
            jnp.where(below, one_of(before, k_low), one_of(before, k_low + 1)),
        )
    blocks = pl.cdiv(unknowns, wide)
    for side, tile_row in ((0, i - 1), (1, i + 1)):
        other = row_of(tile_row)
        e = jnp.zeros((16, 1), F32)
        for k in range(blocks):
            w = min(wide, unknowns - k * wide)
            part = planes.extra(16 * k, 16, side)[:, :w] * other[:, k * wide : k * wide + w]
            e = e + jnp.sum(part, axis=1, keepdims=True)
        e = jnp.broadcast_to(e, (16, wide))
        below = planes.extra(16 * blocks, 8, side)
        skip = 16 - 2 * cols_b if side == 0 else 0
        at = 0 if side == 0 else rows_b + 1
        for r in range(cols_b):
            k = skip + 2 * r
            coarse[at, 8 * r : 8 * r + 8, :] = jnp.where(
                one_of(below, r) > 0.5, one_of(e, k), one_of(e, k + 1)
            )
        coarse[at, own:ext, :] = jnp.zeros((G, wide), F32)

    three[0] = edge_two[0] + coarse[0]
    three[1] = edge_two[1] + act[0] * coarse[1]
    three[2] = edge_two[2] + act[1] * coarse[1]
    three[n - 1] = edge_two[3] + act[n - 2] * coarse[rows_b]
    three[n] = edge_two[4] + act[n - 1] * coarse[rows_b]
    three[n + 1] = edge_two[5] + coarse[rows_b + 1]

    def correct(x, carry):
        three[x + 1] = two[x] + act[x] * coarse[x // 8 + 1]
        return carry

    lax.fori_loop(2, n - 2, correct, 0)

    def row(x, ex, ff_after, qx_before, sx_before):
        p = three[x + 1]
        f = frac[x]
        fe = join(f, ghosts.frac_and_lower(x)[0])
        ey, ez = fy[x], fz[x][:own]
        po = p[:own]
        qx = ex[:own] * (three[x + 2][:own] - po)
        qy = ey * (y_next(p) - p)
        qz = ez * (z_next(po) - po)
        sx = qx * (0.5 * (f + ff_after))
        sy = qy * (0.5 * (fe + y_next(fe)))
        sz = qz * (0.5 * (f + z_next(f)))
        flux_p = (qx_before - qx) + (y_prev(qy) - qy)[:own] + (z_prev(qz) - qz)
        flux_s = (sx_before - sx) + (y_prev(sy) - sy)[:own] + (z_prev(sz) - sz)
        dpp, dss, dps, dsp = diag[0, x], diag[1, x], crs[0, x], crs[1, x]
        up = res[0, x] - (dpp * po + flux_p)
        us = res[1, x] - (dsp * po + flux_s)
        inverse = 1.0 / (dpp * dss - dps * dsp)
        held[0, x] = po + (dss * up - dps * us) * inverse
        held[1, x] = (dpp * us - dsp * up) * inverse
        return qx, sx

    def copies(q):
        return [
            pltpu.make_async_copy(
                held.at[k, pl.ds(8 * q, 8)], out.at[k, pl.ds(8 * q, 8)], sems.at[k, q]
            )
            for k in range(2)
        ]

    qx = edge_fx[0][:own] * (three[1][:own] - three[0][:own])
    sx = qx * (0.5 * (planes.field(6, 0) + frac[0]))
    carry = qx, sx
    for q in range(n // 8):
        stop = min(8 * q + 8, n - 1)
        carry = lax.fori_loop(8 * q, stop, lambda x, v: row(x, fx[x], frac[x + 1], *v), carry)
        if stop == n - 1:
            row(n - 1, edge_fx[1], planes.field(6, 1), *carry)
        for copy in copies(q):
            copy.start()
    for q in range(n // 8):
        for copy in copies(q):
            copy.wait()


def shards(tiles_x, tiles_y, residual, accum_diag, accum_cross, mask, trans_x, trans_y, trans_z,
           frac_flow, split_layer, coarse_inverse):
    n, own, wide = mask.shape
    ext = own + G
    unknowns = coarse_inverse.shape[2]
    raw = (residual, accum_diag, accum_cross, mask, trans_x, trans_y, trans_z)
    columns = (*raw, frac_flow)
    groups = own // 8

    def group_spec(array, group):
        lead = array.shape[:-3]
        zero = (0,) * len(lead)
        return pl.BlockSpec((*lead, 8, 8, wide), lambda x: (*zero, x, group, 0))

    message = jax.ShapeDtypeStruct((n, 16, wide), F32)
    message_spec = pl.BlockSpec((8, 16, wide), lambda x: (x, 0, 0))
    y_messages = pl.pallas_call(
        y_message_kernel,
        grid=(n // 8,),
        in_specs=[SCALARS]
        + [group_spec(v, 0) for v in columns]
        + [group_spec(v, groups - 1) for v in columns],
        out_specs=[message_spec] * 2,
        out_shape=[message] * 2,
        compiler_params=params(16),
        name="y_messages",
    )(split_layer, *columns, *columns)
    ynear, yfar = swap(y_messages, "gy", tiles_y)

    x_message = jax.ShapeDtypeStruct((x_message_rows(own, unknowns, wide), wide), F32)
    x_messages = pl.pallas_call(
        x_message_kernel,
        in_specs=[SCALARS] + [WHOLE] * 11,
        out_specs=[WHOLE] * 2,
        out_shape=[x_message] * 2,
        compiler_params=params(16),
        name="x_messages",
    )(split_layer, *columns, ynear, yfar, coarse_inverse)
    xnear, xfar = swap(x_messages, "gx", tiles_x)

    field = jax.ShapeDtypeStruct((n, ext, wide), F32)
    act, rhs, tot, gain, fx, fy, fz, one, two, acc = pl.pallas_call(
        interior_kernel,
        in_specs=[WHOLE] * 9,
        out_specs=[WHOLE] * 10,
        out_shape=[field] * 9 + [jax.ShapeDtypeStruct((n // 8, own, wide), F32)],
        compiler_params=params(16),
        cost_estimate=cost(60_000_000, 30_000_000),
        name="interior",
    )(*raw, ynear, yfar)

    devices = tiles_x * tiles_y
    span = pl.cdiv(unknowns, 128) * 128
    sent, edge_two, edge_fx = pl.pallas_call(
        edge_kernel,
        in_specs=[SCALARS] + [WHOLE] * 11,
        out_specs=[WHOLE] * 3,
        out_shape=[
            jax.ShapeDtypeStruct((devices, span), F32),
            jax.ShapeDtypeStruct((6, ext, wide), F32),
            jax.ShapeDtypeStruct((2, ext, wide), F32),
        ],
        compiler_params=params(16),
        name="edges",
    )(split_layer, xnear, xfar, act, rhs, tot, fx, fy, fz, one, two, acc)
    got = lax.all_to_all(sent, ("gx", "gy"), 0, 0, tiled=True)

    return pl.pallas_call(
        functools.partial(final_kernel, tiles_y),
        in_specs=[SCALARS] + [WHOLE] * 17,
        out_specs=pl.BlockSpec(memory_space=pl.ANY),
        out_shape=jax.ShapeDtypeStruct((2, n, own, wide), F32),
        scratch_shapes=[
            pltpu.VMEM((n // 8 + 2, ext, wide), F32),
            pltpu.VMEM((n + 2, ext, wide), F32),
            pltpu.VMEM((2, n, own, wide), F32),
            pltpu.SemaphoreType.DMA((2, n // 8)),
        ],
        compiler_params=params(16),
        name="final",
    )(split_layer, residual, accum_diag, accum_cross, frac_flow, coarse_inverse, ynear, yfar, xnear, xfar,
      act, fx, fy, fz, two, edge_two, edge_fx, got)


def solution(mesh):
    placed = (
        P(None, "gx", "gy", None),
        P(None, "gx", "gy", None),
        P(None, "gx", "gy", None),
        P("gx", "gy", None),
        P("gx", "gy", None),
        P("gx", "gy", None),
        P("gx", "gy", None),
        P("gx", "gy", None),
        P("gx", "gy"),
        P("gx", None, None),
    )
    return jax.shard_map(
        functools.partial(shards, mesh.shape["gx"], mesh.shape["gy"]),
        mesh=mesh,
        in_specs=placed,
        out_specs=P(None, "gx", "gy", None),
        check_vma=False,
    )
```

```python
import functools

import jax
import jax.numpy as jnp
from jax import lax
from jax.experimental import pallas as pl
from jax.experimental.pallas import tpu as pltpu
from jax.sharding import PartitionSpec as P

relaxation = 2.0 / 3.0
F32 = jnp.float32
WHOLE = pl.BlockSpec(memory_space=pltpu.VMEM)
SCALARS = pl.BlockSpec(memory_space=pltpu.SMEM)
G = 8
EDGE_FIELDS = 4
PLANES = 3


def params(mib):
    return pltpu.CompilerParams(vmem_limit_bytes=mib << 20)


def cost(flops, size):
    return pl.CostEstimate(flops=flops, bytes_accessed=size, transcendentals=0)


def y_next(v):
    return pltpu.roll(v, v.shape[0] - 1, 0)


def y_prev(v):
    return pltpu.roll(v, 1, 0)


def z_next(v):
    return pltpu.roll(v, v.shape[1] - 1, 1)


def z_prev(v):
    return pltpu.roll(v, 1, 1)


def quasi_impes(active, rp, rs, dpp, dss, dps, dsp):
    weight = dps / dss
    return active * (rp - weight * rs), active * (dpp - weight * dsp) + (1.0 - active)


def swap_pairs(axis, size):
    near = [(i, i ^ 1) for i in range(size) if i ^ 1 < size]
    far = [(i, ((i + 1) ^ 1) - 1) for i in range(size) if 0 <= ((i + 1) ^ 1) - 1 < size]
    return near, far


def swap(message, axis, size):
    near, far = swap_pairs(axis, size)
    return lax.ppermute(message[0], axis, near), lax.ppermute(message[1], axis, far)


def y_message_kernel(split_ref, *refs):
    low, high = refs[:8], refs[8:16]
    near_ref, far_ref = refs[16:]
    even = lax.rem(lax.axis_index("gy"), 2) == 0
    step = pl.program_id(0)

    def fields(group):
        res, diag, crs, mask, tx, ty, tz, ff = group
        active = mask[...].astype(F32)
        b, c = quasi_impes(active, res[0], res[1], diag[0], diag[1], crs[0], crs[1])
        return active, b, c, tx[...], ty[...], tz[...], ff[...]

    shape = low[3].shape
    s = lax.broadcasted_iota(jnp.int32, shape, 1)
    lane = lax.broadcasted_iota(jnp.int32, shape, 2)

    def turn(v, k):
        return jnp.stack([pltpu.roll(v[i], k, 0) for i in range(v.shape[0])])

    a, b, c, tx, ty, tz, ff = fields(high)
    lower = (lane < split_ref[step, split_ref.shape[1] - 1]).astype(F32)
    up = (
        jnp.where(s >= 5, a, jnp.where(s >= 2, turn(ty, 5), turn(tx, 2))),
        jnp.where(
            s >= 6,
            b,
            jnp.where(
                s >= 4,
                turn(c, 6),
                jnp.where(s >= 2, turn(tz, 4), jnp.where(s == 1, turn(ff, 2), lower)),
            ),
        ),
    )
    a, b, c, tx, ty, tz, ff = fields(low)
    lower = (lane < split_ref[step, 0]).astype(F32)
    down = (
        jnp.where(s < 3, a, jnp.where(s < 6, turn(ty, 3), turn(tx, 6))),
        jnp.where(
            s < 2,
            b,
            jnp.where(
                s < 4,
                turn(c, 2),
                jnp.where(s < 6, turn(tz, 4), jnp.where(s == 6, turn(ff, 6), lower)),
            ),
        ),
    )
    for k in range(2):
        near_ref[:, 8 * k : 8 * k + 8, :] = jnp.where(even, up[k], down[k])
        far_ref[:, 8 * k : 8 * k + 8, :] = jnp.where(even, down[k], up[k])


class Ghosts:
    def __init__(self, near_ref, far_ref):
        self.refs = near_ref, far_ref
        self.even = lax.rem(lax.axis_index("gy"), 2) == 0

    def tiles(self, x, k):
        near, far = (ref[x, 8 * k : 8 * k + 8, :] for ref in self.refs)
        return jnp.where(self.even, near, far), jnp.where(self.even, far, near)

    def pick(self, tiles, high_turn, low_turn, rings):
        high, low = tiles
        s = lax.broadcasted_iota(jnp.int32, high.shape, 0)
        high = pltpu.roll(high, high_turn, 0) if high_turn else high
        low = pltpu.roll(low, low_turn, 0) if low_turn else low
        return jnp.where(s < rings, high, jnp.where(s >= G - rings, low, 0.0))

    def first(self, x):
        t = self.tiles(x, 0)
        return self.pick(t, 0, 0, 3), self.pick(t, 2, 6, 2), self.pick(t, 5, 3, 3)

    def second(self, x):
        t = self.tiles(x, 1)
        c = jnp.maximum(self.pick(t, 6, 2, 2), 1.0)
        return self.pick(t, 0, 0, 2), c, self.pick(t, 4, 4, 2)

    def active(self, x):
        return self.pick(self.tiles(x, 0), 0, 0, 3)

    def frac_and_lower(self, x):
        t = self.tiles(x, 1)
        return self.pick(t, 2, 6, 1), self.pick(t, 1, 7, 1)


def join(own, ghost):
    return jnp.concatenate([own, ghost], axis=0)


class Rows:
    def __init__(self, res, diag, crs, mask, tx, ty, tz, ghosts):
        self.res, self.diag, self.crs, self.mask = res, diag, crs, mask
        self.tx, self.ty, self.tz, self.ghosts = tx, ty, tz, ghosts

    def active(self, x):
        return join(self.mask[x].astype(F32), self.ghosts.active(x))

    def trans_x(self, x):
        return join(self.tx[x], self.ghosts.first(x)[1])

    def all(self, x):
        ga, gtx, gty = self.ghosts.first(x)
        gb, gc, gtz = self.ghosts.second(x)
        own = self.mask[x].astype(F32)
        b, c = quasi_impes(
            own, self.res[0, x], self.res[1, x], self.diag[0, x], self.diag[1, x],
            self.crs[0, x], self.crs[1, x],
        )
        a = join(own, ga)
        lane = lax.broadcasted_iota(jnp.int32, a.shape, 1)
        ey = join(self.ty[x], gty) * a * y_next(a)
        ez = jnp.where(lane < a.shape[1] - 1, join(self.tz[x], gtz) * a * z_next(a), 0.0)
        return a, join(b, gb), join(c, gc), join(self.tx[x], gtx) * a, ey, ez


def in_plane_total(ey, ez):
    return ey + y_prev(ey) + ez + z_prev(ez)


def in_plane_sum(ey, ez, p):
    return ey * y_next(p) + y_prev(ey * p) + ez * z_next(p) + z_prev(ez * p)


def x_message_kernel(split_ref, res, diag, crs, mask, tx, ty, tz, ff, ynear, yfar, inv, near_ref, far_ref):
    even = lax.rem(lax.axis_index("gx"), 2) == 0
    j = lax.axis_index("gy")
    rows = Rows(res, diag, crs, mask, tx, ty, tz, Ghosts(ynear, yfar))
    last = mask.shape[0] - 1
    own = mask.shape[1]
    ext = own + G
    per_tile = 2 * split_ref.shape[0] * split_ref.shape[1]
    a1, b1, c1, t1, ey1, ez1 = rows.all(last - 1)
    a0, b0, c0, t0, ey0, ez0 = rows.all(last)
    inner = t1 * a0
    beyond = rows.active(last - 2) * rows.trans_x(last - 2) * a1
    first = relaxation * b1 / (c1 + inner + beyond + in_plane_total(ey1, ez1))
    up = (b0, c0 + inner + in_plane_total(ey0, ez0), t0, ey0, ez0, inner * first, ff[last])
    a0, b0, c0, t0, ey0, ez0 = rows.all(0)
    a1, b1, c1, t1, ey1, ez1 = rows.all(1)
    inner = t0 * a1
    beyond = t1 * rows.active(2)
    first = relaxation * b1 / (c1 + inner + beyond + in_plane_total(ey1, ez1))
    down = (b0, c0 + inner + in_plane_total(ey0, ez0), a0, ey0, ez0, inner * first, ff[0])
    at = 0
    for k in range(EDGE_FIELDS + PLANES):
        n = ext if k < EDGE_FIELDS else own
        near_ref[at : at + n, :] = jnp.where(even, up[k][:n], down[k][:n])
        far_ref[at : at + n, :] = jnp.where(even, down[k][:n], up[k][:n])
        at += n
    wide = near_ref.shape[1]
    unknowns = inv.shape[2]
    top = inv[0, pl.ds(pl.multiple_of(j * per_tile + per_tile - 16, 8), 16), :]
    bottom = inv[0, pl.ds(pl.multiple_of(j * per_tile, 8), 16), :]
    for k in range(0, unknowns, wide):
        n = min(wide, unknowns - k)
        if n < wide:
            near_ref[at : at + 16, :] = jnp.zeros((16, wide), F32)
            far_ref[at : at + 16, :] = jnp.zeros((16, wide), F32)
        near_ref[at : at + 16, :n] = jnp.where(even, top[:, k : k + n], bottom[:, k : k + n])
        far_ref[at : at + 16, :n] = jnp.where(even, bottom[:, k : k + n], top[:, k : k + n])
        at += 16
    lane = lax.broadcasted_iota(jnp.int32, (1, wide), 1)
    zero = jnp.zeros((8, wide), F32)
    near_ref[at : at + 8, :] = zero
    far_ref[at : at + 8, :] = zero
    for q in range(split_ref.shape[1]):
        top = (lane < split_ref[split_ref.shape[0] - 1, q]).astype(F32)
        bottom = (lane < split_ref[0, q]).astype(F32)
        near_ref[at + q : at + q + 1, :] = jnp.where(even, top, bottom)
        far_ref[at + q : at + q + 1, :] = jnp.where(even, bottom, top)


def x_message_rows(own, unknowns, wide):
    return EDGE_FIELDS * (own + G) + PLANES * own + 16 * pl.cdiv(unknowns, wide) + 8


class Planes:
    def __init__(self, near_ref, far_ref, own):
        self.refs, self.own = (near_ref, far_ref), own
        self.even = lax.rem(lax.axis_index("gx"), 2) == 0

    def rows(self, at, n, side):
        near, far = (ref[at : at + n, :] for ref in self.refs)
        return jnp.where(self.even, near, far) if side else jnp.where(self.even, far, near)

    def field(self, k, side):
        ext = self.own + G
        if k < EDGE_FIELDS:
            return self.rows(k * ext, ext, side)
        at = EDGE_FIELDS * ext + (k - EDGE_FIELDS) * self.own
        return self.rows(at, self.own, side)

    def extra(self, at, n, side):
        return self.rows(EDGE_FIELDS * (self.own + G) + PLANES * self.own + at, n, side)


def interior_kernel(res, diag, crs, mask, tx, ty, tz, ynear, yfar,
                    act, rhs, tot, gain, fx, fy, fz, one, two, acc):
    rows = Rows(res, diag, crs, mask, tx, ty, tz, Ghosts(ynear, yfar))
    n = mask.shape[0]
    own = mask.shape[1]

    act[0] = rows.active(0)

    def faces(x, before):
        a, b, c, t, ey, ez = rows.all(x)

        @pl.when(x < n - 1)
        def _():
            act[x + 1] = rows.active(x + 1)

        here = t * act[jnp.minimum(x + 1, n - 1)]
        ex = jnp.where(x < n - 1, here, 0.0)
        total = c + ex + before + in_plane_total(ey, ez)
        g = relaxation / total
        rhs[x] = b
        tot[x] = total
        gain[x] = g
        fx[x] = jnp.where(x < n - 1, here, t)
        fy[x] = ey
        fz[x] = ez
        one[x] = g * b
        return ex

    lax.fori_loop(0, n, faces, jnp.zeros(act.shape[1:], F32))

    def second(x, carry):
        p = one[x]
        s = fx[x] * one[x + 1] + fx[x - 1] * one[x - 1] + in_plane_sum(fy[x], fz[x], p)
        two[x] = gain[x] * ((2.0 - relaxation) * rhs[x] + s)
        return carry

    lax.fori_loop(2, n - 2, second, 0)

    def rest(x):
        p = two[x]
        s = fx[x] * two[x + 1] + fx[x - 1] * two[x - 1] + in_plane_sum(fy[x], fz[x], p)
        return (rhs[x] - tot[x] * p + s)[:own]

    for q in range(n // 8):
        acc[q] = lax.fori_loop(
            max(8 * q, 3), min(8 * q + 8, n - 3), lambda x, v: v + rest(x), jnp.zeros((own, mask.shape[2]), F32)
        )


def edge_kernel(split_ref, xnear, xfar, act, rhs, tot, fx, fy, fz, one, two, acc, sent, edge_two, edge_fx):
    n, ext = act.shape[0], act.shape[1]
    own = ext - G
    wide = act.shape[2]
    planes = Planes(xnear, xfar, own)
    none = jnp.zeros((G, wide), F32)

    class Far:
        def __init__(self, side):
            self.b = planes.field(0, side)
            self.total = jnp.maximum(planes.field(1, side), 1.0)
            self.key = planes.field(2, side)
            self.ey = planes.field(3, side)
            self.ez = join(planes.field(4, side), none)
            self.beyond = join(planes.field(5, side), none)

    low, high = Far(0), Far(1)
    ex = {-1: low.key * act[0], n - 1: fx[n - 1] * high.key}
    edge_fx[0] = ex[-1]
    edge_fx[1] = ex[n - 1]
    total = {
        -1: low.total + ex[-1],
        0: tot[0] + ex[-1],
        n - 1: tot[n - 1] + ex[n - 1],
        n: high.total + ex[n - 1],
    }
    b_of = lambda x: low.b if x == -1 else high.b if x == n else rhs[x]
    ey_of = lambda x: low.ey if x == -1 else high.ey if x == n else fy[x]
    ez_of = lambda x: low.ez if x == -1 else high.ez if x == n else fz[x]
    ex_of = lambda x: ex[x] if x in ex else fx[x]
    total_of = lambda x: total[x] if x in total else tot[x]
    gain = {x: relaxation / total[x] for x in total}
    first = {x: gain[x] * b_of(x) for x in total}
    first_of = lambda x: first[x] if x in first else one[x]

    def beside(x, field_of):
        s = in_plane_sum(ey_of(x), ez_of(x), field_of(x))
        s = s + (low.beyond if x == -1 else ex_of(x - 1) * field_of(x - 1))
        return s + (high.beyond if x == n else ex_of(x) * field_of(x + 1))

    second = {}
    for slot, x in enumerate((-1, 0, 1, n - 2, n - 1, n)):
        g = gain[x] if x in gain else relaxation / tot[x]
        second[x] = g * ((2.0 - relaxation) * b_of(x) + beside(x, first_of))
        edge_two[slot] = second[x]
    second_of = lambda x: second[x] if x in second else two[x]

    def rest(x):
        return (b_of(x) - total_of(x) * second_of(x) + beside(x, second_of))[:own]

    rows_b, cols_b = split_ref.shape
    lane = lax.broadcasted_iota(jnp.int32, (1, wide), 1)
    lower, upper = [], []
    for q in range(rows_b):
        field = acc[q]
        for x in (0, 1, 2, n - 3, n - 2, n - 1):
            if x // 8 == q:
                field = field + rest(x)
        for r in range(cols_b):
            column = jnp.sum(field[8 * r : 8 * r + 8], axis=0, keepdims=True)
            below = lane < split_ref[q, r]
            lower.append(jnp.where(below, column, 0.0))
            upper.append(jnp.where(below, 0.0, column))
    count = rows_b * cols_b
    low_sum = jnp.sum(jnp.concatenate(lower, axis=0), axis=1, keepdims=True)
    high_sum = jnp.sum(jnp.concatenate(upper, axis=0), axis=1, keepdims=True)
    span = sent.shape[1]
    place = lax.broadcasted_iota(jnp.int32, (count, span), 1) - 2 * count * lax.axis_index("gy")
    which = 2 * lax.broadcasted_iota(jnp.int32, (count, span), 0)
    laid = jnp.where(place == which, low_sum, jnp.where(place == which + 1, high_sum, 0.0))
    sent[...] = jnp.broadcast_to(jnp.sum(laid, axis=0, keepdims=True), sent.shape)


def final_kernel(tiles_y, split_ref, res, diag, crs, frac, inv, ynear, yfar, xnear, xfar,
                 act, fx, fy, fz, two, edge_two, edge_fx, got, out, coarse, three, held, sems):
    i, j = lax.axis_index("gx"), lax.axis_index("gy")
    n, ext = act.shape[0], act.shape[1]
    own = ext - G
    wide = act.shape[2]
    unknowns = inv.shape[2]
    rows_b, cols_b = split_ref.shape
    per_tile = 2 * rows_b * cols_b
    ghosts = Ghosts(ynear, yfar)
    planes = Planes(xnear, xfar, own)

    all_got = got[...]
    owner = lax.broadcasted_iota(jnp.int32, all_got.shape, 0)

    def row_of(tile_row):
        mine = (owner >= tile_row * tiles_y) & (owner < (tile_row + 1) * tiles_y)
        return jnp.sum(jnp.where(mine, all_got, 0.0), axis=0, keepdims=True)

    coarse_res = row_of(i)

    def solve(tile):
        start = pl.multiple_of(jnp.clip(tile, 0, tiles_y - 1) * per_tile, 8)
        block = inv[0, pl.ds(start, per_tile), :]
        e = jnp.sum(block * coarse_res[:, :unknowns], axis=1, keepdims=True)
        return jnp.broadcast_to(e, (per_tile, wide))

    lane = lax.broadcasted_iota(jnp.int32, (1, wide), 1)
    s = lax.broadcasted_iota(jnp.int32, (G, wide), 0)
    mine, before, after = solve(j), solve(j - 1), solve(j + 1)

    def one_of(e, k):
        return jnp.broadcast_to(e[k : k + 1], (8, wide))

    for q in range(rows_b):
        for r in range(cols_b):
            k = 2 * (q * cols_b + r)
            coarse[q + 1, 8 * r : 8 * r + 8, :] = jnp.where(
                lane < split_ref[q, r], one_of(mine, k), one_of(mine, k + 1)
            )
        below = ghosts.frac_and_lower(8 * q)[1] > 0.5
        k_high, k_low = 2 * q * cols_b, 2 * (q * cols_b + cols_b - 1)
        coarse[q + 1, own:ext, :] = jnp.where(
            s == 0,
            jnp.where(below, one_of(after, k_high), one_of(after, k_high + 1)),
            jnp.where(below, one_of(before, k_low), one_of(before, k_low + 1)),
        )
    blocks = pl.cdiv(unknowns, wide)
    for side, tile_row in ((0, i - 1), (1, i + 1)):
        other = row_of(tile_row)
        e = jnp.zeros((16, 1), F32)
        for k in range(blocks):
            w = min(wide, unknowns - k * wide)
            part = planes.extra(16 * k, 16, side)[:, :w] * other[:, k * wide : k * wide + w]
            e = e + jnp.sum(part, axis=1, keepdims=True)
        e = jnp.broadcast_to(e, (16, wide))
        below = planes.extra(16 * blocks, 8, side)
        skip = 16 - 2 * cols_b if side == 0 else 0
        at = 0 if side == 0 else rows_b + 1
        for r in range(cols_b):
            k = skip + 2 * r
            coarse[at, 8 * r : 8 * r + 8, :] = jnp.where(
                one_of(below, r) > 0.5, one_of(e, k), one_of(e, k + 1)
            )
        coarse[at, own:ext, :] = jnp.zeros((G, wide), F32)

    three[0] = edge_two[0] + coarse[0]
    three[1] = edge_two[1] + act[0] * coarse[1]
    three[2] = edge_two[2] + act[1] * coarse[1]
    three[n - 1] = edge_two[3] + act[n - 2] * coarse[rows_b]
    three[n] = edge_two[4] + act[n - 1] * coarse[rows_b]
    three[n + 1] = edge_two[5] + coarse[rows_b + 1]

    def correct(x, carry):
        three[x + 1] = two[x] + act[x] * coarse[x // 8 + 1]
        return carry

    lax.fori_loop(2, n - 2, correct, 0)

    def row(x, ex, ff_after, qx_before, sx_before):
        p = three[x + 1]
        f = frac[x]
        fe = join(f, ghosts.frac_and_lower(x)[0])
        ey, ez = fy[x], fz[x][:own]
        po = p[:own]
        qx = ex[:own] * (three[x + 2][:own] - po)
        qy = ey * (y_next(p) - p)
        qz = ez * (z_next(po) - po)
        sx = qx * (0.5 * (f + ff_after))
        sy = qy * (0.5 * (fe + y_next(fe)))
        sz = qz * (0.5 * (f + z_next(f)))
        flux_p = (qx_before - qx) + (y_prev(qy) - qy)[:own] + (z_prev(qz) - qz)
        flux_s = (sx_before - sx) + (y_prev(sy) - sy)[:own] + (z_prev(sz) - sz)
        dpp, dss, dps, dsp = diag[0, x], diag[1, x], crs[0, x], crs[1, x]
        up = res[0, x] - (dpp * po + flux_p)
        us = res[1, x] - (dsp * po + flux_s)
        inverse = 1.0 / (dpp * dss - dps * dsp)
        held[0, x] = po + (dss * up - dps * us) * inverse
        held[1, x] = (dpp * us - dsp * up) * inverse
        return qx, sx

    def copies(q):
        return [
            pltpu.make_async_copy(
                held.at[k, pl.ds(8 * q, 8)], out.at[k, pl.ds(8 * q, 8)], sems.at[k, q]
            )
            for k in range(2)
        ]

    qx = edge_fx[0][:own] * (three[1][:own] - three[0][:own])
    sx = qx * (0.5 * (planes.field(6, 0) + frac[0]))
    carry = qx, sx
    for q in range(n // 8):
        stop = min(8 * q + 8, n - 1)
        carry = lax.fori_loop(8 * q, stop, lambda x, v: row(x, fx[x], frac[x + 1], *v), carry)
        if stop == n - 1:
            row(n - 1, edge_fx[1], planes.field(6, 1), *carry)
        for copy in copies(q):
            copy.start()
    for q in range(n // 8):
        for copy in copies(q):
            copy.wait()


def shards(tiles_x, tiles_y, residual, accum_diag, accum_cross, mask, trans_x, trans_y, trans_z,
           frac_flow, split_layer, coarse_inverse):
    n, own, wide = mask.shape
    ext = own + G
    unknowns = coarse_inverse.shape[2]
    raw = (residual, accum_diag, accum_cross, mask, trans_x, trans_y, trans_z)
    columns = (*raw, frac_flow)
    groups = own // 8

    def group_spec(array, group):
        lead = array.shape[:-3]
        zero = (0,) * len(lead)
        return pl.BlockSpec((*lead, 8, 8, wide), lambda x: (*zero, x, group, 0))

    far_columns = [pltpu.with_memory_space_constraint(v, pltpu.HBM) for v in columns]
    message = jax.ShapeDtypeStruct((n, 16, wide), F32)
    message_spec = pl.BlockSpec((8, 16, wide), lambda x: (x, 0, 0))
    y_messages = pl.pallas_call(
        y_message_kernel,
        grid=(n // 8,),
        in_specs=[SCALARS]
        + [group_spec(v, 0) for v in columns]
        + [group_spec(v, groups - 1) for v in columns],
        out_specs=[message_spec] * 2,
        out_shape=[message] * 2,
        compiler_params=params(16),
        name="y_messages",
    )(split_layer, *far_columns, *far_columns)
    ynear, yfar = swap(y_messages, "gy", tiles_y)

    x_message = jax.ShapeDtypeStruct((x_message_rows(own, unknowns, wide), wide), F32)
    x_messages = pl.pallas_call(
        x_message_kernel,
        in_specs=[SCALARS] + [WHOLE] * 11,
        out_specs=[WHOLE] * 2,
        out_shape=[x_message] * 2,
        compiler_params=params(16),
        name="x_messages",
    )(split_layer, *columns, ynear, yfar, coarse_inverse)
    xnear, xfar = swap(x_messages, "gx", tiles_x)

    field = jax.ShapeDtypeStruct((n, ext, wide), F32)
    act, rhs, tot, gain, fx, fy, fz, one, two, acc = pl.pallas_call(
        interior_kernel,
        in_specs=[WHOLE] * 9,
        out_specs=[WHOLE] * 10,
        out_shape=[field] * 9 + [jax.ShapeDtypeStruct((n // 8, own, wide), F32)],
        compiler_params=params(16),
        cost_estimate=cost(60_000_000, 30_000_000),
        name="interior",
    )(*raw, ynear, yfar)

    devices = tiles_x * tiles_y
    span = pl.cdiv(unknowns, 128) * 128
    sent, edge_two, edge_fx = pl.pallas_call(
        edge_kernel,
        in_specs=[SCALARS] + [WHOLE] * 11,
        out_specs=[WHOLE] * 3,
        out_shape=[
            jax.ShapeDtypeStruct((devices, span), F32),
            jax.ShapeDtypeStruct((6, ext, wide), F32),
            jax.ShapeDtypeStruct((2, ext, wide), F32),
        ],
        compiler_params=params(16),
        name="edges",
    )(split_layer, xnear, xfar, act, rhs, tot, fx, fy, fz, one, two, acc)
    got = lax.all_to_all(sent, ("gx", "gy"), 0, 0, tiled=True)

    return pl.pallas_call(
        functools.partial(final_kernel, tiles_y),
        in_specs=[SCALARS] + [WHOLE] * 17,
        out_specs=pl.BlockSpec(memory_space=pl.ANY),
        out_shape=jax.ShapeDtypeStruct((2, n, own, wide), F32),
        scratch_shapes=[
            pltpu.VMEM((n // 8 + 2, ext, wide), F32),
            pltpu.VMEM((n + 2, ext, wide), F32),
            pltpu.VMEM((2, n, own, wide), F32),
            pltpu.SemaphoreType.DMA((2, n // 8)),
        ],
        compiler_params=params(16),
        name="final",
    )(split_layer, residual, accum_diag, accum_cross, frac_flow, coarse_inverse, ynear, yfar, xnear, xfar,
      act, fx, fy, fz, two, edge_two, edge_fx, got)


def solution(mesh):
    placed = (
        P(None, "gx", "gy", None),
        P(None, "gx", "gy", None),
        P(None, "gx", "gy", None),
        P("gx", "gy", None),
        P("gx", "gy", None),
        P("gx", "gy", None),
        P("gx", "gy", None),
        P("gx", "gy", None),
        P("gx", "gy"),
        P("gx", None, None),
    )
    return jax.shard_map(
        functools.partial(shards, mesh.shape["gx"], mesh.shape["gy"]),
        mesh=mesh,
        in_specs=placed,
        out_specs=P(None, "gx", "gy", None),
        check_vma=False,
    )
```

```python
import functools

import jax
import jax.numpy as jnp
from jax import lax
from jax.experimental import pallas as pl
from jax.experimental.pallas import tpu as pltpu
from jax.sharding import PartitionSpec as P

relaxation = 2.0 / 3.0
F32 = jnp.float32
WHOLE = pl.BlockSpec(memory_space=pltpu.VMEM)
SCALARS = pl.BlockSpec(memory_space=pltpu.SMEM)
G = 8
EDGE_FIELDS = 4
PLANES = 3


def params(mib):
    return pltpu.CompilerParams(vmem_limit_bytes=mib << 20)


def cost(flops, size):
    return pl.CostEstimate(flops=flops, bytes_accessed=size, transcendentals=0)


def z_next(v):
    return pltpu.roll(v, v.shape[1] - 1, 1)


def z_prev(v):
    return pltpu.roll(v, 1, 1)


def quasi_impes(active, rp, rs, dpp, dss, dps, dsp):
    weight = dps / dss
    return active * (rp - weight * rs), active * (dpp - weight * dsp) + (1.0 - active)


def swap_pairs(axis, size):
    near = [(i, i ^ 1) for i in range(size) if i ^ 1 < size]
    far = [(i, ((i + 1) ^ 1) - 1) for i in range(size) if 0 <= ((i + 1) ^ 1) - 1 < size]
    return near, far


def swap(message, axis, size):
    near, far = swap_pairs(axis, size)
    return lax.ppermute(message[0], axis, near), lax.ppermute(message[1], axis, far)


def y_message_kernel(split_ref, *refs):
    low, high = refs[:8], refs[8:16]
    near_ref, far_ref = refs[16:]
    even = lax.rem(lax.axis_index("gy"), 2) == 0
    step = pl.program_id(0)

    def fields(group):
        res, diag, crs, mask, tx, ty, tz, ff = group
        active = mask[...].astype(F32)
        b, c = quasi_impes(active, res[0], res[1], diag[0], diag[1], crs[0], crs[1])
        return active, b, c, tx[...], ty[...], tz[...], ff[...]

    shape = low[3].shape
    s = lax.broadcasted_iota(jnp.int32, shape, 1)
    lane = lax.broadcasted_iota(jnp.int32, shape, 2)

    def turn(v, k):
        return jnp.stack([pltpu.roll(v[i], k, 0) for i in range(v.shape[0])])

    a, b, c, tx, ty, tz, ff = fields(high)
    lower = (lane < split_ref[step, split_ref.shape[1] - 1]).astype(F32)
    up = (
        jnp.where(s >= 5, a, jnp.where(s >= 2, turn(ty, 5), turn(tx, 2))),
        jnp.where(
            s >= 6,
            b,
            jnp.where(
                s >= 4,
                turn(c, 6),
                jnp.where(s >= 2, turn(tz, 4), jnp.where(s == 1, turn(ff, 2), lower)),
            ),
        ),
    )
    a, b, c, tx, ty, tz, ff = fields(low)
    lower = (lane < split_ref[step, 0]).astype(F32)
    down = (
        jnp.where(s < 3, a, jnp.where(s < 6, turn(ty, 3), turn(tx, 6))),
        jnp.where(
            s < 2,
            b,
            jnp.where(
                s < 4,
                turn(c, 2),
                jnp.where(s < 6, turn(tz, 4), jnp.where(s == 6, turn(ff, 6), lower)),
            ),
        ),
    )
    for k in range(2):
        near_ref[:, 8 * k : 8 * k + 8, :] = jnp.where(even, up[k], down[k])
        far_ref[:, 8 * k : 8 * k + 8, :] = jnp.where(even, down[k], up[k])


class Ghosts:
    def __init__(self, near_ref, far_ref):
        self.refs = near_ref, far_ref
        self.even = lax.rem(lax.axis_index("gy"), 2) == 0

    def tiles(self, x, k):
        near, far = (ref[x, 8 * k : 8 * k + 8, :] for ref in self.refs)
        return jnp.where(self.even, near, far), jnp.where(self.even, far, near)

    def pick(self, tiles, high_turn, low_turn, rings):
        high, low = tiles
        s = lax.broadcasted_iota(jnp.int32, high.shape, 0)
        high = pltpu.roll(high, high_turn, 0) if high_turn else high
        low = pltpu.roll(low, low_turn, 0) if low_turn else low
        return jnp.where(s < rings, high, jnp.where(s >= G - rings, low, 0.0))

    def first(self, x):
        t = self.tiles(x, 0)
        return self.pick(t, 0, 0, 3), self.pick(t, 2, 6, 2), self.pick(t, 5, 3, 3)

    def second(self, x):
        t = self.tiles(x, 1)
        c = jnp.maximum(self.pick(t, 6, 2, 2), 1.0)
        return self.pick(t, 0, 0, 2), c, self.pick(t, 4, 4, 2)

    def active(self, x):
        return self.pick(self.tiles(x, 0), 0, 0, 3)

    def frac_and_lower(self, x):
        t = self.tiles(x, 1)
        return self.pick(t, 2, 6, 1), self.pick(t, 1, 7, 1)


def group(k):
    return slice(8 * k, 8 * k + 8)


def turned_next(mine, after, s):
    return jnp.where(s == G - 1, after, mine)


def turned_prev(mine, before, s):
    return jnp.where(s == 0, before, mine)


def turn_next(v):
    return pltpu.roll(v, G - 1, 0)


def turn_prev(v):
    return pltpu.roll(v, 1, 0)


def places(wide):
    shape = (G, wide)
    return lax.broadcasted_iota(jnp.int32, shape, 0), lax.broadcasted_iota(jnp.int32, shape, 1)


def along_z(tz, a, lane):
    return jnp.where(lane < a.shape[1] - 1, tz * a * z_next(a), 0.0)


def prep_kernel(res_hbm, diag_hbm, crs_hbm, mask_hbm, tx_hbm, ty_hbm, tz_hbm,
                rhs, own_diag, tot, gain, one, fx, fy, fz, al0, al1, be0, be1,
                res, diag, crs, mask, tx, ty, tz, sems):
    n, own, wide = mask.shape
    groups = own // 8
    chunk = 4
    s, lane = places(wide)

    def copies(q):
        at = pl.ds(chunk * q, chunk)
        pairs = (
            (res_hbm.at[:, at], res.at[:, at]),
            (diag_hbm.at[:, at], diag.at[:, at]),
            (crs_hbm.at[:, at], crs.at[:, at]),
            (tx_hbm.at[at], tx.at[at]),
            (ty_hbm.at[at], ty.at[at]),
            (tz_hbm.at[at], tz.at[at]),
        )
        return [pltpu.make_async_copy(a, b, sems.at[k + 1, q]) for k, (a, b) in enumerate(pairs)]

    def masks(q):
        at = pl.ds(chunk * q, chunk)
        return pltpu.make_async_copy(mask_hbm.at[at], mask.at[at], sems.at[0, q])

    for q in range(n // chunk):
        for copy in (masks(q), *copies(q)):
            copy.start()
    masks(0).wait()

    def row(x, carry):
        first, last = x == 0, x == n - 1
        after = jnp.minimum(x + 1, n - 1)
        before = jnp.maximum(x - 1, 0)
        a_after = mask[x, group(0), :].astype(F32)
        turned_after = turn_next(a_after)
        ey_before = jnp.zeros((G, wide), F32)
        for k in range(groups):
            here = group(k)
            a, turned = a_after, turned_after
            rp, rs = res[0, x, here, :], res[1, x, here, :]
            dpp, dss = diag[0, x, here, :], diag[1, x, here, :]
            dps, dsp = crs[0, x, here, :], crs[1, x, here, :]
            det = dpp * dss - dps * dsp
            both = 1.0 / (dss * det)
            inverse = both * dss
            weight = dps * (both * det)
            b = a * (rp - weight * rs)
            c = a * (dpp - weight * dsp) + (1.0 - a)
            rhs[x, here, :] = b
            own_diag[x, here, :] = c
            al0[x, here, :] = dss * inverse
            al1[x, here, :] = dps * inverse
            be0[x, here, :] = dpp * inverse
            be1[x, here, :] = dsp * inverse
            t = tx[x, here, :] * a
            ex = t * mask[after, here, :].astype(F32)
            fx[x, here, :] = jnp.where(last, t, ex)
            total = c + jnp.where(last, 0.0, ex)
            total = total + jnp.where(first, 0.0, fx[before, here, :])
            ez = along_z(tz[x, here, :], a, lane)
            fz[x, here, :] = ez
            total = total + ez + z_prev(ez)
            ey = ty[x, here, :] * a
            if k < groups - 1:
                a_after = mask[x, group(k + 1), :].astype(F32)
                turned_after = turn_next(a_after)
                ey = ey * turned_next(turned, turned_after, s)
                inside = ey
            else:
                ey = jnp.where(s == G - 1, ey, ey * turned)
                inside = jnp.where(s == G - 1, 0.0, ey)
            fy[x, here, :] = ey
            ey_turned = turn_prev(inside)
            total = total + inside + turned_prev(ey_turned, ey_before, s)
            ey_before = ey_turned
            tot[x, here, :] = total
            if 0 < k < groups - 1:
                g = relaxation / total
                gain[x, here, :] = g
                one[x, here, :] = g * b
        return carry

    def part(q, carry):
        @pl.when(q < n // chunk - 1)
        def _():
            masks(q + 1).wait()

        for copy in copies(q):
            copy.wait()
        return lax.fori_loop(chunk * q, chunk * q + chunk, row, carry)

    lax.fori_loop(0, n // chunk, part, 0)


class Finished:
    def __init__(self, x, n, ghosts, mask, rhs, tot, fx, fy, s, lane):
        groups = mask.shape[1] // 8
        first, last = x == 0, x == n - 1
        ga, gtx, gty = ghosts.first(x)
        gb, gc, gtz = ghosts.second(x)
        before, after = jnp.maximum(x - 1, 0), jnp.minimum(x + 1, n - 1)
        a_before, tx_before, _ = ghosts.first(before)
        a_after = ghosts.active(after)
        turned = turn_next(ga)
        end = fy[x, group(groups - 1), :]
        end = jnp.where(s == G - 1, end * turned, end)
        a_first = mask[x, group(0), :].astype(F32)
        ey = gty * ga * turned_next(turned, turn_next(a_first), s)
        ey_turned = turn_prev(ey)
        ez = along_z(gtz, ga, lane)
        t = gtx * ga
        ex = t * a_after
        total = gc + ez + z_prev(ez) + ey + turned_prev(ey_turned, turn_prev(end), s)
        total = total + jnp.where(last, 0.0, ex) + jnp.where(first, 0.0, tx_before * a_before * ga)
        self.end = end
        self.fx, self.fy, self.fz = jnp.where(last, t, ex), ey, ez
        self.rhs = gb
        self.total = (
            tot[x, group(0), :] + jnp.where(s == 0, ey_turned, 0.0),
            tot[x, group(groups - 1), :] + jnp.where(s == G - 1, end, 0.0),
            total,
        )
        self.all_rhs = (rhs[x, group(0), :], rhs[x, group(groups - 1), :], gb)


def slot_of(k, groups):
    return {0: 0, groups - 1: 1, groups: 2}[k]


def x_message_kernel(split_ref, mask, ff, rhs, tot, gain, one, fx, fy, fz, ynear, yfar, inv, near_ref, far_ref):
    even = lax.rem(lax.axis_index("gx"), 2) == 0
    j = lax.axis_index("gy")
    n, own, wide = mask.shape
    groups = own // 8
    s, lane = places(wide)
    ghosts = Ghosts(ynear, yfar)
    per_tile = 2 * split_ref.shape[0] * split_ref.shape[1]
    finished = {x: Finished(x, n, ghosts, mask, rhs, tot, fx, fy, s, lane) for x in (0, 1, n - 2, n - 1)}
    at = 0
    for k in range(groups + 1):
        here = group(k)
        touched = k in (0, groups - 1, groups)

        def first_of(x):
            done = finished[x]
            if not touched:
                return one[x, here, :]
            slot = slot_of(k, groups)
            return relaxation * done.all_rhs[slot] / done.total[slot]

        def of(x, key):
            done = finished[x]
            total = done.total[slot_of(k, groups)] if touched else tot[x, here, :]
            if k == groups:
                return done.rhs, total, key, done.fy
            return rhs[x, here, :], total, key, done.end if k == groups - 1 else fy[x, here, :]

        if k == groups:
            up = of(n - 1, finished[n - 1].fx)
            down = of(0, ghosts.active(0))
        else:
            up = of(n - 1, fx[n - 1, here, :])
            down = of(0, mask[0, here, :].astype(F32))
            up += (fz[n - 1, here, :], fx[n - 2, here, :] * first_of(n - 2), ff[n - 1, here, :])
            down += (fz[0, here, :], fx[0, here, :] * first_of(1), ff[0, here, :])
        for f in range(len(up)):
            ext = own + G
            start = f * ext if f < EDGE_FIELDS else EDGE_FIELDS * ext + (f - EDGE_FIELDS) * own
            start += 8 * k
            near_ref[start : start + 8, :] = jnp.where(even, up[f], down[f])
            far_ref[start : start + 8, :] = jnp.where(even, down[f], up[f])
    at = EDGE_FIELDS * (own + G) + PLANES * own
    unknowns = inv.shape[2]
    top = inv[0, pl.ds(pl.multiple_of(j * per_tile + per_tile - 16, 8), 16), :]
    bottom = inv[0, pl.ds(pl.multiple_of(j * per_tile, 8), 16), :]
    for k in range(0, unknowns, wide):
        w = min(wide, unknowns - k)
        if w < wide:
            near_ref[at : at + 16, :] = jnp.zeros((16, wide), F32)
            far_ref[at : at + 16, :] = jnp.zeros((16, wide), F32)
        near_ref[at : at + 16, :w] = jnp.where(even, top[:, k : k + w], bottom[:, k : k + w])
        far_ref[at : at + 16, :w] = jnp.where(even, bottom[:, k : k + w], top[:, k : k + w])
        at += 16
    lane = lax.broadcasted_iota(jnp.int32, (1, wide), 1)
    zero = jnp.zeros((8, wide), F32)
    near_ref[at : at + 8, :] = zero
    far_ref[at : at + 8, :] = zero
    for q in range(split_ref.shape[1]):
        top = (lane < split_ref[split_ref.shape[0] - 1, q]).astype(F32)
        bottom = (lane < split_ref[0, q]).astype(F32)
        near_ref[at + q : at + q + 1, :] = jnp.where(even, top, bottom)
        far_ref[at + q : at + q + 1, :] = jnp.where(even, bottom, top)


def x_message_rows(own, unknowns, wide):
    return EDGE_FIELDS * (own + G) + PLANES * own + 16 * pl.cdiv(unknowns, wide) + 8


class Planes:
    def __init__(self, near_ref, far_ref, own):
        self.refs, self.own = (near_ref, far_ref), own
        self.even = lax.rem(lax.axis_index("gx"), 2) == 0

    def rows(self, at, n, side):
        near, far = (ref[at : at + n, :] for ref in self.refs)
        return jnp.where(self.even, near, far) if side else jnp.where(self.even, far, near)

    def field(self, f, k, side):
        ext = self.own + G
        if f < EDGE_FIELDS:
            return self.rows(f * ext + 8 * k, 8, side)
        at = EDGE_FIELDS * ext + (f - EDGE_FIELDS) * self.own
        if 8 * k == self.own:
            return jnp.zeros((8, self.refs[0].shape[1]), F32)
        return self.rows(at + 8 * k, 8, side)

    def extra(self, at, n, side):
        return self.rows(EDGE_FIELDS * (self.own + G) + PLANES * self.own + at, n, side)


class Inside:
    def __init__(self, groups, ff, rhs, gain, one, fx, fy, fz, gain3, one3, six, end):
        self.groups, self.own_ff, self.own_rhs = groups, ff, rhs
        self.own_gain, self.own_one, self.own_fx, self.own_fy, self.own_fz = gain, one, fx, fy, fz
        self.gain3, self.one3, self.six, self.end = gain3, one3, six, end

    def pick(self, own, which, x, k):
        return self.six[which, x] if k == self.groups else own[x, group(k), :]

    def three(self, own, other, x, k):
        if 0 < k < self.groups - 1:
            return own[x, group(k), :]
        return other[x, group(slot_of(k, self.groups)), :]

    def rhs(self, x, k):
        return self.pick(self.own_rhs, 0, x, k)

    def fx(self, x, k):
        return self.pick(self.own_fx, 1, x, k)

    def fy(self, x, k):
        if k == self.groups - 1:
            return self.end[x]
        return self.pick(self.own_fy, 2, x, k)

    def fz(self, x, k):
        return self.pick(self.own_fz, 3, x, k)

    def ff(self, x, k):
        return self.pick(self.own_ff, 4, x, k)

    def gain(self, x, k):
        return self.three(self.own_gain, self.gain3, x, k)

    def one(self, x, k):
        return self.three(self.own_one, self.one3, x, k)

    def before(self, x, k):
        return self.fx(x - 1, k) * self.one(x - 1, k)

    def after(self, x, k):
        return self.fx(x, k) * self.one(x + 1, k)


def second_row(o, x, s, put):
    total = o.groups + 1
    p = o.one(x, 0)
    p_turned = turn_next(p)
    w_turned = turn_prev(o.fy(x, total - 1) * o.one(x, total - 1))
    for k in range(total):
        p_after = o.one(x, (k + 1) % total)
        after_turned = turn_next(p_after)
        ey, ez = o.fy(x, k), o.fz(x, k)
        mine = turn_prev(ey * p)
        beside = ey * turned_next(p_turned, after_turned, s) + turned_prev(mine, w_turned, s)
        beside = beside + ez * z_next(p) + z_prev(ez * p)
        beside = beside + o.after(x, k) + o.before(x, k)
        put(k, o.gain(x, k) * ((2.0 - relaxation) * o.rhs(x, k) + beside))
        p, p_turned, w_turned = p_after, after_turned, mine


def x_flux(o, x, k, two):
    step = two(x + 1, k) - two(x, k)
    ex = o.fx(x, k)
    return ex * step, ex * (o.ff(x, k) + o.ff(x + 1, k)) * step


def flux_row(o, x, s, lane, two, res, own_diag, split, carried, put):
    groups = o.groups

    def faces_y(k, p, p_turned, p_after, f, f_turned, f_after):
        ey = o.fy(x, k)
        weighted = ey * (f + turned_next(f_turned, f_after, s))
        return ey, weighted, turned_next(p_turned, p_after, s) - p

    p0, f0 = two(x, 0), o.ff(x, 0)
    p0_turned, f0_turned = turn_next(p0), turn_next(f0)
    p, f = two(x, groups), o.ff(x, groups)
    ghost = faces_y(groups, p, turn_next(p), p0_turned, f, turn_next(f), f0_turned)
    turned = [turn_prev(v) for v in ghost]
    p, f, p_turned, f_turned = p0, f0, p0_turned, f0_turned
    for k in range(groups):
        here = group(k)
        p_after, f_after = two(x, k + 1), o.ff(x, k + 1)
        p_after_turned, f_after_turned = turn_next(p_after), turn_next(f_after)
        mine = faces_y(k, p, p_turned, p_after_turned, f, f_turned, f_after_turned)
        mine_turned = [turn_prev(v) for v in mine]
        ey, wy, dy = mine
        ey_before, wy_before, dy_before = (
            turned_prev(a, b, s) for a, b in zip(mine_turned, turned, strict=True)
        )
        ez = o.fz(x, k)
        wz = ez * (f + z_next(f))
        dz = z_next(p) - p
        ez_before, wz_before, dz_before = z_prev(ez), z_prev(wz), z_prev(dz)
        qx, sx = x_flux(o, x, k, two)
        gained = (qx - carried[0, here, :]) + (ey * dy - ey_before * dy_before)
        gained = gained + (ez * dz - ez_before * dz_before)
        weighed = (sx - carried[1, here, :]) + (wy * dy - wy_before * dy_before)
        weighed = weighed + (wz * dz - wz_before * dz_before)
        carried[0, here, :] = qx
        carried[1, here, :] = sx
        rest = o.rhs(x, k) - own_diag[x, here, :] * p + gained
        below = lane < split(k)
        put(
            k,
            rest,
            res[0, x, here, :] + gained,
            res[1, x, here, :] + 0.5 * weighed,
            jnp.where(s == 0, ey_before, ey),
            jnp.where(s == 0, wy_before, wy),
            jnp.where(below, ez, ez_before),
            jnp.where(below, wz, wz_before),
        )
        turned = mine_turned
        p, f, p_turned, f_turned = p_after, f_after, p_after_turned, f_after_turned


FLUXES = 6


def interior_kernel(split_ref, res, mask, ff, rhs, own_diag, tot, gain, one, fx, fy, fz, ynear, yfar,
                    tot3, gain3, one3, six, end, two, acc, *flux_and_carried):
    flux, carried = flux_and_carried[:FLUXES], flux_and_carried[FLUXES]
    n, own, wide = mask.shape
    groups = own // 8
    s, lane = places(wide)
    ghosts = Ghosts(ynear, yfar)

    def finish(x, carry):
        done = Finished(x, n, ghosts, mask, rhs, tot, fx, fy, s, lane)
        for slot in range(3):
            g = relaxation / done.total[slot]
            tot3[x, group(slot), :] = done.total[slot]
            gain3[x, group(slot), :] = g
            one3[x, group(slot), :] = g * done.all_rhs[slot]
        end[x] = done.end
        for k, v in enumerate((done.rhs, done.fx, done.fy, done.fz, ghosts.frac_and_lower(x)[0])):
            six[k, x] = v
        return carry

    lax.fori_loop(0, n, finish, 0)
    o = Inside(groups, ff, rhs, gain, one, fx, fy, fz, gain3, one3, six, end)

    def second(x, carry):
        def put(k, v):
            two[x, group(k), :] = v

        second_row(o, x, s, put)
        return carry

    lax.fori_loop(2, n - 2, second, 0)

    def two_of(x, k):
        return two[x, group(k), :]

    for k in range(groups):
        carried[0, group(k), :], carried[1, group(k), :] = x_flux(o, 2, k, two_of)
    acc[...] = jnp.zeros_like(acc)

    def row(x, carry):
        def put(k, rest, *values):
            acc[x // 8, group(k), :] += rest
            for f, v in enumerate(values):
                flux[f][x, group(k), :] = v

        flux_row(o, x, s, lane, two_of, res, own_diag, lambda k: split_ref[x // 8, k], carried, put)
        return carry

    lax.fori_loop(3, n - 3, row, 0)


class Edges(Inside):
    def beyond(self, n, planes, act, tot, tot3, one_edge, gain_edge, edge_fx):
        self.n, self.planes = n, planes
        self.slots = {-1: 0, 0: 1, n - 1: 2, n: 3}
        self.one_edge, self.gain_edge, self.edge_fx = one_edge, gain_edge, edge_fx
        self.far = {-1: 0, n: 1}
        for k in range(self.groups + 1):
            here = group(k)
            low = planes.field(2, k, 0) * act(k)
            high = super().fx(n - 1, k) * planes.field(2, k, 1)
            edge_fx[0, here, :] = low
            edge_fx[1, here, :] = high
            for x, slot in self.slots.items():
                face = low if x <= 0 else high
                if x in self.far:
                    total = jnp.maximum(planes.field(1, k, self.far[x]), 1.0) + face
                else:
                    total = self.three(tot, tot3, x, k) + face
                g = relaxation / total
                gain_edge[slot, here, :] = g
                one_edge[slot, here, :] = g * self.rhs(x, k)

    def rhs(self, x, k):
        return self.planes.field(0, k, self.far[x]) if x in self.far else super().rhs(x, k)

    def fx(self, x, k):
        if x in (-1, self.n - 1):
            return self.edge_fx[0 if x == -1 else 1, group(k), :]
        return super().fx(x, k)

    def fy(self, x, k):
        return self.planes.field(3, k, self.far[x]) if x in self.far else super().fy(x, k)

    def fz(self, x, k):
        return self.planes.field(4, k, self.far[x]) if x in self.far else super().fz(x, k)

    def ff(self, x, k):
        return self.planes.field(6, k, self.far[x]) if x in self.far else super().ff(x, k)

    def gain(self, x, k):
        return self.gain_edge[self.slots[x], group(k), :] if x in self.slots else super().gain(x, k)

    def one(self, x, k):
        return self.one_edge[self.slots[x], group(k), :] if x in self.slots else super().one(x, k)

    def before(self, x, k):
        return self.planes.field(5, k, 0) if x == -1 else super().before(x, k)

    def after(self, x, k):
        return self.planes.field(5, k, 1) if x == self.n else super().after(x, k)


def edge_kernel(split_ref, res, mask, ff, rhs, own_diag, tot, gain, one, fx, fy, fz, ynear, yfar, xnear, xfar,
                tot3, gain3, one3, six, end, two, acc,
                sent, edge_flux, edge_fx, one_edge, gain_edge, two_edge, carried, total_acc):
    n, own, wide = mask.shape
    groups = own // 8
    s, lane = places(wide)
    planes = Planes(xnear, xfar, own)
    ghosts = Ghosts(ynear, yfar)
    o = Edges(groups, ff, rhs, gain, one, fx, fy, fz, gain3, one3, six, end)

    def act(k):
        return ghosts.active(0) if k == groups else mask[0, group(k), :].astype(F32)

    o.beyond(n, planes, act, tot, tot3, one_edge, gain_edge, edge_fx)
    slots = {x: slot for slot, x in enumerate((-1, 0, 1, n - 2, n - 1, n))}
    for x, slot in slots.items():

        def put_two(k, v, slot=slot):
            two_edge[slot, group(k), :] = v

        second_row(o, x, s, put_two)

    def two_of(x, k):
        return two_edge[slots[x], group(k), :] if x in slots else two[x, group(k), :]

    total_acc[...] = acc[...]
    for slot, x in enumerate((0, 1, 2, n - 3, n - 2, n - 1)):
        if slot % 3 == 0:
            for k in range(groups):
                carried[0, group(k), :], carried[1, group(k), :] = x_flux(o, x - 1, k, two_of)

        def put(k, rest, *values, x=x, slot=slot):
            total_acc[x // 8, group(k), :] += rest
            for f, v in enumerate(values):
                edge_flux[f, slot, group(k), :] = v

        flux_row(o, x, s, lane, two_of, res, own_diag, lambda k, x=x: split_ref[x // 8, k], carried, put)

    rows_b, cols_b = split_ref.shape
    lane = lax.broadcasted_iota(jnp.int32, (1, wide), 1)
    lower, upper = [], []
    for q in range(rows_b):
        for r in range(cols_b):
            column = jnp.sum(total_acc[q, group(r), :], axis=0, keepdims=True)
            below = lane < split_ref[q, r]
            lower.append(jnp.where(below, column, 0.0))
            upper.append(jnp.where(below, 0.0, column))
    count = rows_b * cols_b
    low_sum = jnp.sum(jnp.concatenate(lower, axis=0), axis=1, keepdims=True)
    high_sum = jnp.sum(jnp.concatenate(upper, axis=0), axis=1, keepdims=True)
    span = sent.shape[1]
    place = lax.broadcasted_iota(jnp.int32, (count, span), 1) - 2 * count * lax.axis_index("gy")
    which = 2 * lax.broadcasted_iota(jnp.int32, (count, span), 0)
    laid = jnp.where(place == which, low_sum, jnp.where(place == which + 1, high_sum, 0.0))
    sent[...] = jnp.broadcast_to(jnp.sum(laid, axis=0, keepdims=True), sent.shape)


def final_kernel(tiles_y, split_ref, frac, inv, ynear, yfar, xnear, xfar, fx, edge_flux, edge_fx,
                 al0, al1, be0, be1, got, *rest):
    flux = rest[:FLUXES]
    out, coarse, step_y, step_z, held, sems = rest[FLUXES:]
    i, j = lax.axis_index("gx"), lax.axis_index("gy")
    n, own, wide = frac.shape
    ext = own + G
    unknowns = inv.shape[2]
    rows_b, cols_b = split_ref.shape
    per_tile = 2 * rows_b * cols_b
    ghosts = Ghosts(ynear, yfar)
    planes = Planes(xnear, xfar, own)
    s8, lane8 = places(wide)

    all_got = got[...]
    owner = lax.broadcasted_iota(jnp.int32, all_got.shape, 0)

    def row_of(tile_row):
        mine = (owner >= tile_row * tiles_y) & (owner < (tile_row + 1) * tiles_y)
        return jnp.sum(jnp.where(mine, all_got, 0.0), axis=0, keepdims=True)

    coarse_res = row_of(i)

    def solve(tile):
        start = pl.multiple_of(jnp.clip(tile, 0, tiles_y - 1) * per_tile, 8)
        block = inv[0, pl.ds(start, per_tile), :]
        e = jnp.sum(block * coarse_res[:, :unknowns], axis=1, keepdims=True)
        return jnp.broadcast_to(e, (per_tile, wide))

    mine, before, after = solve(j), solve(j - 1), solve(j + 1)

    def one_of(e, k):
        return jnp.broadcast_to(e[k : k + 1], (8, wide))

    for q in range(rows_b):
        for r in range(cols_b):
            k = 2 * (q * cols_b + r)
            low, high = one_of(mine, k), one_of(mine, k + 1)
            split = split_ref[q, r]
            coarse[q + 1, group(r), :] = jnp.where(lane8 < split, low, high)
            jump = high - low
            step_z[q, group(r), :] = jnp.where(
                lane8 == split - 1, jump, jnp.where(lane8 == split, -jump, 0.0)
            )
        below = ghosts.frac_and_lower(8 * q)[1] > 0.5
        k_high, k_low = 2 * q * cols_b, 2 * (q * cols_b + cols_b - 1)
        coarse[q + 1, own:ext, :] = jnp.where(
            s8 == 0,
            jnp.where(below, one_of(after, k_high), one_of(after, k_high + 1)),
            jnp.where(below, one_of(before, k_low), one_of(before, k_low + 1)),
        )
        for r in range(cols_b):
            here = coarse[q + 1, group(r), :]
            ahead = turn_next(coarse[q + 1, group(r + 1), :])
            behind = turn_prev(coarse[q + 1, group(r - 1 if r else cols_b), :])
            step_y[q, group(r), :] = jnp.where(
                s8 == G - 1, ahead - here, jnp.where(s8 == 0, behind - here, 0.0)
            )
    blocks = pl.cdiv(unknowns, wide)
    for side, tile_row in ((0, i - 1), (1, i + 1)):
        other = row_of(tile_row)
        e = jnp.zeros((16, 1), F32)
        for k in range(blocks):
            w = min(wide, unknowns - k * wide)
            part = planes.extra(16 * k, 16, side)[:, :w] * other[:, k * wide : k * wide + w]
            e = e + jnp.sum(part, axis=1, keepdims=True)
        e = jnp.broadcast_to(e, (16, wide))
        below = planes.extra(16 * blocks, 8, side)
        skip = 16 - 2 * cols_b if side == 0 else 0
        at = 0 if side == 0 else rows_b + 1
        for r in range(cols_b):
            k = skip + 2 * r
            coarse[at, group(r), :] = jnp.where(one_of(below, r) > 0.5, one_of(e, k), one_of(e, k + 1))

    def solved(x, q, values, beside):
        for r in range(cols_b):
            here = group(r)
            u, v, wy, sy, wz, sz = (value(r) for value in values)
            along_y, along_z = step_y[q, here, :], step_z[q, here, :]
            u = u + (wy * along_y + wz * along_z)
            weighed = sy * along_y + sz * along_z
            if beside is not None:
                ex, sx, step = beside(r)
                u = u + ex * step
                weighed = weighed + sx * step
            v = v + 0.5 * weighed
            held[0, x, here, :] = al0[x, here, :] * u - al1[x, here, :] * v
            held[1, x, here, :] = be0[x, here, :] * v - be1[x, here, :] * u

    def copies(q):
        return [
            pltpu.make_async_copy(
                held.at[k, pl.ds(8 * q, 8)], out.at[k, pl.ds(8 * q, 8)], sems.at[k, q]
            )
            for k in range(2)
        ]

    def frac_of(x, r):
        if x in (-1, n):
            return planes.field(6, r, 0 if x == -1 else 1)
        return frac[x, group(r), :]

    def face(x, r):
        if x in (-1, n - 1):
            ex = edge_fx[0 if x == -1 else 1, group(r), :]
        else:
            ex = fx[x, group(r), :]
        return ex, ex * (frac_of(x, r) + frac_of(x + 1, r))

    outer = {x: slot for slot, x in enumerate((0, 1, 2, n - 3, n - 2, n - 1))}

    def values_of(x):
        if isinstance(x, int) and x in outer:
            return [lambda r, f=f: edge_flux[f, outer[x], group(r), :] for f in range(FLUXES)]
        return [lambda r, f=f: flux[f][x, group(r), :] for f in range(FLUXES)]

    for q in range(rows_b):
        first, last = 8 * q, 8 * q + 7

        def ahead(r, q=q, last=last):
            return *face(last, r), coarse[q + 2, group(r), :] - coarse[q + 1, group(r), :]

        def behind(r, q=q, first=first):
            return *face(first - 1, r), coarse[q, group(r), :] - coarse[q + 1, group(r), :]

        solved(first, q, values_of(first), behind)
        start, stop = first + 1, last
        while start in outer:
            solved(start, q, values_of(start), None)
            start += 1
        while stop - 1 in outer:
            stop -= 1
            solved(stop, q, values_of(stop), None)

        def row(x, carry, q=q):
            solved(x, q, values_of(x), None)
            return carry

        lax.fori_loop(start, stop, row, 0)
        solved(last, q, values_of(last), ahead)
        for copy in copies(q):
            copy.start()
    for q in range(rows_b):
        for copy in copies(q):
            copy.wait()


def shards(tiles_x, tiles_y, residual, accum_diag, accum_cross, mask, trans_x, trans_y, trans_z,
           frac_flow, split_layer, coarse_inverse):
    n, own, wide = mask.shape
    ext = own + G
    unknowns = coarse_inverse.shape[2]
    columns = (residual, accum_diag, accum_cross, mask, trans_x, trans_y, trans_z, frac_flow)
    far_columns = [pltpu.with_memory_space_constraint(v, pltpu.HBM) for v in columns]
    groups = own // 8

    def group_spec(array, k):
        lead = array.shape[:-3]
        zero = (0,) * len(lead)
        return pl.BlockSpec((*lead, 8, 8, wide), lambda x: (*zero, x, k, 0))

    def array(*shape):
        return jax.ShapeDtypeStruct(shape, F32)

    y_messages = pl.pallas_call(
        y_message_kernel,
        grid=(n // 8,),
        in_specs=[SCALARS]
        + [group_spec(v, 0) for v in columns]
        + [group_spec(v, groups - 1) for v in columns],
        out_specs=[pl.BlockSpec((8, 16, wide), lambda x: (x, 0, 0))] * 2,
        out_shape=[array(n, 16, wide)] * 2,
        compiler_params=params(16),
        name="y_messages",
    )(split_layer, *far_columns, *far_columns)
    ynear, yfar = swap(y_messages, "gy", tiles_y)

    rhs, own_diag, tot, gain, one, fx, fy, fz, al0, al1, be0, be1 = pl.pallas_call(
        prep_kernel,
        in_specs=[pl.BlockSpec(memory_space=pltpu.HBM)] * 7,
        out_specs=[WHOLE] * 12,
        out_shape=[array(n, own, wide)] * 12,
        scratch_shapes=[pltpu.VMEM(v.shape, v.dtype) for v in columns[:7]]
        + [pltpu.SemaphoreType.DMA((7, n // 4))],
        compiler_params=params(18),
        cost_estimate=cost(60_000_000, 30_000_000),
        name="prep",
    )(*far_columns[:7])
    shared = (rhs, tot, gain, one, fx, fy, fz)

    x_messages = pl.pallas_call(
        x_message_kernel,
        in_specs=[SCALARS] + [WHOLE] * 12,
        out_specs=[WHOLE] * 2,
        out_shape=[array(x_message_rows(own, unknowns, wide), wide)] * 2,
        compiler_params=params(8),
        name="x_messages",
    )(split_layer, mask, frac_flow, *shared, ynear, yfar, coarse_inverse)
    xnear, xfar = swap(x_messages, "gx", tiles_x)

    shared = (residual, mask, frac_flow, rhs, own_diag, tot, gain, one, fx, fy, fz, ynear, yfar)
    tot3, gain3, one3, six, end, two, acc, *flux = pl.pallas_call(
        interior_kernel,
        in_specs=[SCALARS] + [WHOLE] * 13,
        out_specs=[WHOLE] * (7 + FLUXES),
        out_shape=[array(n, 3 * G, wide)] * 3
        + [
            array(5, n, G, wide),
            array(n, G, wide),
            array(n, ext, wide),
            array(n // 8, own, wide),
        ]
        + [array(n, own, wide)] * FLUXES,
        scratch_shapes=[pltpu.VMEM((2, own, wide), F32)],
        compiler_params=params(8),
        cost_estimate=cost(60_000_000, 30_000_000),
        name="interior",
    )(split_layer, *shared)

    devices = tiles_x * tiles_y
    span = pl.cdiv(unknowns, 128) * 128
    sent, edge_flux, edge_fx = pl.pallas_call(
        edge_kernel,
        in_specs=[SCALARS] + [WHOLE] * 22,
        out_specs=[WHOLE] * 3,
        out_shape=[array(devices, span), array(FLUXES, 6, own, wide), array(2, ext, wide)],
        scratch_shapes=[
            pltpu.VMEM((4, ext, wide), F32),
            pltpu.VMEM((4, ext, wide), F32),
            pltpu.VMEM((6, ext, wide), F32),
            pltpu.VMEM((2, own, wide), F32),
            pltpu.VMEM((n // 8, own, wide), F32),
        ],
        compiler_params=params(8),
        name="edges",
    )(split_layer, *shared, xnear, xfar, tot3, gain3, one3, six, end, two, acc)
    got = lax.all_to_all(sent, ("gx", "gy"), 0, 0, tiled=True)

    return pl.pallas_call(
        functools.partial(final_kernel, tiles_y),
        in_specs=[SCALARS] + [WHOLE] * (14 + FLUXES),
        out_specs=pl.BlockSpec(memory_space=pl.ANY),
        out_shape=array(2, n, own, wide),
        scratch_shapes=[
            pltpu.VMEM((n // 8 + 2, ext, wide), F32),
            pltpu.VMEM((n // 8, own, wide), F32),
            pltpu.VMEM((n // 8, own, wide), F32),
            pltpu.VMEM((2, n, own, wide), F32),
            pltpu.SemaphoreType.DMA((2, n // 8)),
        ],
        compiler_params=params(12),
        name="final",
    )(split_layer, frac_flow, coarse_inverse, ynear, yfar, xnear, xfar, fx, edge_flux, edge_fx,
      al0, al1, be0, be1, got, *flux)


def solution(mesh):
    placed = (
        P(None, "gx", "gy", None),
        P(None, "gx", "gy", None),
        P(None, "gx", "gy", None),
        P("gx", "gy", None),
        P("gx", "gy", None),
        P("gx", "gy", None),
        P("gx", "gy", None),
        P("gx", "gy", None),
        P("gx", "gy"),
        P("gx", None, None),
    )
    return jax.shard_map(
        functools.partial(shards, mesh.shape["gx"], mesh.shape["gy"]),
        mesh=mesh,
        in_specs=placed,
        out_specs=P(None, "gx", "gy", None),
        check_vma=False,
    )
```

```python
import functools

import jax
import jax.numpy as jnp
from jax import lax
from jax.experimental import pallas as pl
from jax.experimental.pallas import tpu as pltpu
from jax.sharding import PartitionSpec as P

relaxation = 2.0 / 3.0
F32 = jnp.float32
WHOLE = pl.BlockSpec(memory_space=pltpu.VMEM)
SCALARS = pl.BlockSpec(memory_space=pltpu.SMEM)
G = 8
PLANES = 6


def params(mib):
    return pltpu.CompilerParams(vmem_limit_bytes=mib << 20)


def cost(flops, size):
    return pl.CostEstimate(flops=flops, bytes_accessed=size, transcendentals=0)


def z_next(v):
    return pltpu.roll(v, v.shape[1] - 1, 1)


def z_prev(v):
    return pltpu.roll(v, 1, 1)


def quasi_impes(active, rp, rs, dpp, dss, dps, dsp):
    weight = dps / dss
    return active * (rp - weight * rs), active * (dpp - weight * dsp) + (1.0 - active)


def swap_pairs(axis, size):
    near = [(i, i ^ 1) for i in range(size) if i ^ 1 < size]
    far = [(i, ((i + 1) ^ 1) - 1) for i in range(size) if 0 <= ((i + 1) ^ 1) - 1 < size]
    return near, far


def swap(message, axis, size):
    near, far = swap_pairs(axis, size)
    return lax.ppermute(message[0], axis, near), lax.ppermute(message[1], axis, far)


def y_message_kernel(split_ref, *refs):
    low, high = refs[:8], refs[8:16]
    near_ref, far_ref = refs[16:]
    even = lax.rem(lax.axis_index("gy"), 2) == 0
    step = pl.program_id(0)

    def fields(group):
        res, diag, crs, mask, tx, ty, tz, ff = group
        active = mask[...].astype(F32)
        b, c = quasi_impes(active, res[0], res[1], diag[0], diag[1], crs[0], crs[1])
        return active, b, c, tx[...], ty[...], tz[...], ff[...]

    shape = low[3].shape
    s = lax.broadcasted_iota(jnp.int32, shape, 1)
    lane = lax.broadcasted_iota(jnp.int32, shape, 2)

    def turn(v, k):
        return jnp.stack([pltpu.roll(v[i], k, 0) for i in range(v.shape[0])])

    a, b, c, tx, ty, tz, ff = fields(high)
    splits = split_ref[pl.ds(step, 1), :]
    lower = (lane < splits[:, -1:].reshape(1, 1, 1)).astype(F32)
    up = (
        jnp.where(s >= 5, a, jnp.where(s >= 2, turn(ty, 5), turn(tx, 2))),
        jnp.where(
            s >= 6,
            b,
            jnp.where(
                s >= 4,
                turn(c, 6),
                jnp.where(s >= 2, turn(tz, 4), jnp.where(s == 1, turn(ff, 2), lower)),
            ),
        ),
    )
    a, b, c, tx, ty, tz, ff = fields(low)
    lower = (lane < splits[:, :1].reshape(1, 1, 1)).astype(F32)
    down = (
        jnp.where(s < 3, a, jnp.where(s < 6, turn(ty, 3), turn(tx, 6))),
        jnp.where(
            s < 2,
            b,
            jnp.where(
                s < 4,
                turn(c, 2),
                jnp.where(s < 6, turn(tz, 4), jnp.where(s == 6, turn(ff, 6), lower)),
            ),
        ),
    )
    for k in range(2):
        near_ref[:, 8 * k : 8 * k + 8, :] = jnp.where(even, up[k], down[k])
        far_ref[:, 8 * k : 8 * k + 8, :] = jnp.where(even, down[k], up[k])


class Ghosts:
    def __init__(self, near_ref, far_ref):
        self.refs = near_ref, far_ref
        self.even = lax.rem(lax.axis_index("gy"), 2) == 0

    def tiles(self, x, k):
        near, far = (ref[x, 8 * k : 8 * k + 8, :] for ref in self.refs)
        return jnp.where(self.even, near, far), jnp.where(self.even, far, near)

    def pick(self, tiles, high_turn, low_turn, rings):
        high, low = tiles
        s = lax.broadcasted_iota(jnp.int32, high.shape, 0)
        high = pltpu.roll(high, high_turn, 0) if high_turn else high
        low = pltpu.roll(low, low_turn, 0) if low_turn else low
        return jnp.where(s < rings, high, jnp.where(s >= G - rings, low, 0.0))

    def first(self, x):
        t = self.tiles(x, 0)
        return self.pick(t, 0, 0, 3), self.pick(t, 2, 6, 2), self.pick(t, 5, 3, 3)

    def second(self, x):
        t = self.tiles(x, 1)
        c = jnp.maximum(self.pick(t, 6, 2, 2), 1.0)
        return self.pick(t, 0, 0, 2), c, self.pick(t, 4, 4, 2)

    def active(self, x):
        return self.pick(self.tiles(x, 0), 0, 0, 3)

    def frac_and_lower(self, x):
        t = self.tiles(x, 1)
        return self.pick(t, 2, 6, 1), self.pick(t, 1, 7, 1)


def group(k):
    return slice(8 * k, 8 * k + 8)


def turned_next(mine, after, s):
    return jnp.where(s == G - 1, after, mine)


def turned_prev(mine, before, s):
    return jnp.where(s == 0, before, mine)


def turn_next(v):
    return pltpu.roll(v, G - 1, 0)


def turn_prev(v):
    return pltpu.roll(v, 1, 0)


def places(wide):
    shape = (G, wide)
    return lax.broadcasted_iota(jnp.int32, shape, 0), lax.broadcasted_iota(jnp.int32, shape, 1)


def along_z(tz, a, lane):
    return jnp.where(lane < a.shape[1] - 1, tz * a * z_next(a), 0.0)


def prep_kernel(res_hbm, diag_hbm, crs_hbm, mask_hbm, tx_hbm, ty_hbm, tz_hbm,
                rhs, own_diag, tot, gain, one, fx, fy, fz, al0, al1, be0, be1,
                res, diag, crs, mask, tx, ty, tz, sems):
    n, own, wide = mask.shape
    groups = own // 8
    chunk = 4
    s, lane = places(wide)

    def copies(q):
        at = pl.ds(chunk * q, chunk)
        pairs = (
            (res_hbm.at[:, at], res.at[:, at]),
            (diag_hbm.at[:, at], diag.at[:, at]),
            (crs_hbm.at[:, at], crs.at[:, at]),
            (tx_hbm.at[at], tx.at[at]),
            (ty_hbm.at[at], ty.at[at]),
            (tz_hbm.at[at], tz.at[at]),
        )
        return [pltpu.make_async_copy(a, b, sems.at[k + 1, q]) for k, (a, b) in enumerate(pairs)]

    def masks(q):
        at = pl.ds(chunk * q, chunk)
        return pltpu.make_async_copy(mask_hbm.at[at], mask.at[at], sems.at[0, q])

    for q in range(n // chunk):
        for copy in (masks(q), *copies(q)):
            copy.start()
    masks(0).wait()

    def row(x, carry):
        first, last = x == 0, x == n - 1
        after = jnp.minimum(x + 1, n - 1)
        before = jnp.maximum(x - 1, 0)
        a_after = mask[x, group(0), :].astype(F32)
        turned_after = turn_next(a_after)
        ey_before = jnp.zeros((G, wide), F32)
        for k in range(groups):
            here = group(k)
            a, turned = a_after, turned_after
            rp, rs = res[0, x, here, :], res[1, x, here, :]
            dpp, dss = diag[0, x, here, :], diag[1, x, here, :]
            dps, dsp = crs[0, x, here, :], crs[1, x, here, :]
            det = dpp * dss - dps * dsp
            both = 1.0 / (dss * det)
            inverse = both * dss
            weight = dps * (both * det)
            b = a * (rp - weight * rs)
            c = a * (dpp - weight * dsp) + (1.0 - a)
            rhs[x, here, :] = b
            own_diag[x, here, :] = c
            al0[x, here, :] = dss * inverse
            al1[x, here, :] = dps * inverse
            be0[x, here, :] = dpp * inverse
            be1[x, here, :] = dsp * inverse
            t = tx[x, here, :] * a
            ex = t * mask[after, here, :].astype(F32)
            fx[x, here, :] = jnp.where(last, t, ex)
            total = c + jnp.where(last, 0.0, ex)
            total = total + jnp.where(first, 0.0, fx[before, here, :])
            ez = along_z(tz[x, here, :], a, lane)
            fz[x, here, :] = ez
            total = total + ez + z_prev(ez)
            ey = ty[x, here, :] * a
            if k < groups - 1:
                a_after = mask[x, group(k + 1), :].astype(F32)
                turned_after = turn_next(a_after)
                ey = ey * turned_next(turned, turned_after, s)
                inside = ey
            else:
                ey = jnp.where(s == G - 1, ey, ey * turned)
                inside = jnp.where(s == G - 1, 0.0, ey)
            fy[x, here, :] = ey
            ey_turned = turn_prev(inside)
            total = total + inside + turned_prev(ey_turned, ey_before, s)
            ey_before = ey_turned
            tot[x, here, :] = total
            if 0 < k < groups - 1:
                g = relaxation / total
                gain[x, here, :] = g
                one[x, here, :] = g * b
        return carry

    def part(q, carry):
        @pl.when(q < n // chunk - 1)
        def _():
            masks(q + 1).wait()

        for copy in copies(q):
            copy.wait()
        return lax.fori_loop(0, chunk, lambda k, v: row(chunk * q + k, v), carry, unroll=2)

    lax.fori_loop(0, n // chunk, part, 0)


class Finished:
    def __init__(self, x, n, ghosts, mask, rhs, tot, fx, fy, s, lane):
        groups = mask.shape[1] // 8
        first, last = x == 0, x == n - 1
        ga, gtx, gty = ghosts.first(x)
        gb, gc, gtz = ghosts.second(x)
        before, after = jnp.maximum(x - 1, 0), jnp.minimum(x + 1, n - 1)
        a_before, tx_before, _ = ghosts.first(before)
        a_after = ghosts.active(after)
        turned = turn_next(ga)
        end = fy[x, group(groups - 1), :]
        end = jnp.where(s == G - 1, end * turned, end)
        a_first = mask[x, group(0), :].astype(F32)
        ey = gty * ga * turned_next(turned, turn_next(a_first), s)
        ey_turned = turn_prev(ey)
        ez = along_z(gtz, ga, lane)
        t = gtx * ga
        ex = t * a_after
        total = gc + ez + z_prev(ez) + ey + turned_prev(ey_turned, turn_prev(end), s)
        total = total + jnp.where(last, 0.0, ex) + jnp.where(first, 0.0, tx_before * a_before * ga)
        self.end = end
        self.fx, self.fy, self.fz = jnp.where(last, t, ex), ey, ez
        self.rhs = gb
        self.total = (
            tot[x, group(0), :] + jnp.where(s == 0, ey_turned, 0.0),
            tot[x, group(groups - 1), :] + jnp.where(s == G - 1, end, 0.0),
            total,
        )
        self.all_rhs = (rhs[x, group(0), :], rhs[x, group(groups - 1), :], gb)


def slot_of(k, groups):
    return {0: 0, groups - 1: 1, groups: 2}[k]


def x_message_kernel(mask, rhs, tot, gain, one, fx, fy, fz, ynear, yfar, near_ref, far_ref):
    even = lax.rem(lax.axis_index("gx"), 2) == 0
    n, own, wide = mask.shape
    groups = own // 8
    s, lane = places(wide)
    ghosts = Ghosts(ynear, yfar)
    finished = {x: Finished(x, n, ghosts, mask, rhs, tot, fx, fy, s, lane) for x in (0, 1, n - 2, n - 1)}
    for k in range(groups + 1):
        here = group(k)
        touched = k in (0, groups - 1, groups)

        def first_of(x):
            done = finished[x]
            if not touched:
                return one[x, here, :]
            slot = slot_of(k, groups)
            return relaxation * done.all_rhs[slot] / done.total[slot]

        def of(x, key):
            done = finished[x]
            total = done.total[slot_of(k, groups)] if touched else tot[x, here, :]
            if k == groups:
                return done.rhs, total, key, done.fy
            return rhs[x, here, :], total, key, done.end if k == groups - 1 else fy[x, here, :]

        if k == groups:
            up = of(n - 1, finished[n - 1].fx)
            down = of(0, ghosts.active(0))
        else:
            up = of(n - 1, fx[n - 1, here, :])
            down = of(0, mask[0, here, :].astype(F32))
            up += (fz[n - 1, here, :], fx[n - 2, here, :] * first_of(n - 2))
            down += (fz[0, here, :], fx[0, here, :] * first_of(1))
        if k == groups:
            b, total, key, ey = (jnp.where(even, p, q) for p, q in zip(up, down, strict=True))
            ob, ototal, okey, oey = (jnp.where(even, q, p) for p, q in zip(up, down, strict=True))
            for ref, (b, total, key, ey) in (
                (near_ref, (b, total, key, ey)),
                (far_ref, (ob, ototal, okey, oey)),
            ):
                at = PLANES * own
                ref[at : at + G, :] = jnp.where((s == 0) | (s == G - 1), b, pltpu.roll(total, 4, 0))
                ref[at + G : at + 2 * G, :] = jnp.where((s < 2) | (s >= G - 2), key, pltpu.roll(ey, 4, 0))
        else:
            for f in range(PLANES):
                start = f * own + 8 * k
                near_ref[start : start + 8, :] = jnp.where(even, up[f], down[f])
                far_ref[start : start + 8, :] = jnp.where(even, down[f], up[f])


def late_messages(split_ref, ff, inv, near_ref, far_ref):
    even = lax.rem(lax.axis_index("gx"), 2) == 0
    j = lax.axis_index("gy")
    n, own, wide = ff.shape
    per_tile = 2 * split_ref.shape[0] * split_ref.shape[1]
    near_ref[0:own, :] = jnp.where(even, ff[n - 1], ff[0])
    far_ref[0:own, :] = jnp.where(even, ff[0], ff[n - 1])
    at = own
    unknowns = inv.shape[2]
    top = inv[0, pl.ds(pl.multiple_of(j * per_tile + per_tile - 16, 8), 16), :]
    bottom = inv[0, pl.ds(pl.multiple_of(j * per_tile, 8), 16), :]
    for k in range(0, unknowns, wide):
        w = min(wide, unknowns - k)
        if w < wide:
            near_ref[at : at + 16, :] = jnp.zeros((16, wide), F32)
            far_ref[at : at + 16, :] = jnp.zeros((16, wide), F32)
        near_ref[at : at + 16, :w] = jnp.where(even, top[:, k : k + w], bottom[:, k : k + w])
        far_ref[at : at + 16, :w] = jnp.where(even, bottom[:, k : k + w], top[:, k : k + w])
        at += 16
    lane = lax.broadcasted_iota(jnp.int32, (1, wide), 1)
    zero = jnp.zeros((8, wide), F32)
    near_ref[at : at + 8, :] = zero
    far_ref[at : at + 8, :] = zero
    for q in range(split_ref.shape[1]):
        top = (lane < split_ref[split_ref.shape[0] - 1, q]).astype(F32)
        bottom = (lane < split_ref[0, q]).astype(F32)
        near_ref[at + q : at + q + 1, :] = jnp.where(even, top, bottom)
        far_ref[at + q : at + q + 1, :] = jnp.where(even, bottom, top)


def late_rows(own, unknowns, wide):
    return own + 16 * pl.cdiv(unknowns, wide) + 8


class Planes:
    def __init__(self, near_ref, far_ref, own):
        self.refs, self.own = (near_ref, far_ref), own
        self.even = lax.rem(lax.axis_index("gx"), 2) == 0

    def rows(self, at, n, side):
        near, far = (ref[at : at + n, :] for ref in self.refs)
        return jnp.where(self.even, near, far) if side else jnp.where(self.even, far, near)

    def field(self, f, k, side):
        if 8 * k < self.own:
            return self.rows(f * self.own + 8 * k, 8, side)
        s, _ = places(self.refs[0].shape[1])
        ends = (s == 0) | (s == G - 1)
        if f < 2:
            tile = self.rows(PLANES * self.own, G, side)
            return jnp.where(ends, pltpu.roll(tile, 4, 0) if f else tile, 0.0)
        if f < 4:
            tile = self.rows(PLANES * self.own + G, G, side)
            if f == 2:
                return jnp.where((s < 2) | (s >= G - 2), tile, 0.0)
            return jnp.where(s == G - 1, pltpu.roll(tile, 4, 0), 0.0)
        return jnp.zeros_like(s, F32)


class Inside:
    def __init__(self, groups, ff, rhs, gain, one, fx, fy, fz, gain3, one3, six, end):
        self.groups, self.own_ff, self.own_rhs = groups, ff, rhs
        self.own_gain, self.own_one, self.own_fx, self.own_fy, self.own_fz = gain, one, fx, fy, fz
        self.gain3, self.one3, self.six, self.end = gain3, one3, six, end

    def pick(self, own, which, x, k):
        return self.six[which, x] if k == self.groups else own[x, group(k), :]

    def three(self, own, other, x, k):
        if 0 < k < self.groups - 1:
            return own[x, group(k), :]
        return other[x, group(slot_of(k, self.groups)), :]

    def rhs(self, x, k):
        return self.pick(self.own_rhs, 0, x, k)

    def fx(self, x, k):
        return self.pick(self.own_fx, 1, x, k)

    def fy(self, x, k):
        if k == self.groups - 1:
            return self.end[x]
        return self.pick(self.own_fy, 2, x, k)

    def fz(self, x, k):
        return self.pick(self.own_fz, 3, x, k)

    def ff(self, x, k):
        return self.pick(self.own_ff, 4, x, k)

    def gain(self, x, k):
        return self.three(self.own_gain, self.gain3, x, k)

    def one(self, x, k):
        return self.three(self.own_one, self.one3, x, k)

    def before(self, x, k):
        return self.fx(x - 1, k) * self.one(x - 1, k)

    def after(self, x, k):
        return self.fx(x, k) * self.one(x + 1, k)

    def outermost(self, x):
        return False


def second_row(o, x, s, put):
    total = o.groups + 1
    p = o.one(x, 0)
    p_turned = turn_next(p)
    w_turned = turn_prev(o.fy(x, total - 1) * o.one(x, total - 1))
    for k in range(total):
        p_after = o.one(x, (k + 1) % total)
        after_turned = turn_next(p_after)
        ey, ez = o.fy(x, k), o.fz(x, k)
        mine = turn_prev(ey * p)
        beside = ey * turned_next(p_turned, after_turned, s) + turned_prev(mine, w_turned, s)
        beside = beside + ez * z_next(p) + z_prev(ez * p)
        beside = beside + o.after(x, k) + o.before(x, k)
        put(k, o.gain(x, k) * ((2.0 - relaxation) * o.rhs(x, k) + beside))
        p, p_turned, w_turned = p_after, after_turned, mine


def x_flux(o, x, k, two):
    step = two(x + 1, k) - two(x, k)
    ex = o.fx(x, k)
    if o.outermost(x):
        return ex * step, jnp.zeros_like(step)
    return ex * step, ex * (o.ff(x, k) + o.ff(x + 1, k)) * step


def flux_row(o, x, s, lane, two, res, own_diag, split, carried, put):
    groups = o.groups

    def faces_y(k, p, p_turned, p_after, f, f_turned, f_after):
        ey = o.fy(x, k)
        weighted = ey * (f + turned_next(f_turned, f_after, s))
        return ey, weighted, turned_next(p_turned, p_after, s) - p

    p0, f0 = two(x, 0), o.ff(x, 0)
    p0_turned, f0_turned = turn_next(p0), turn_next(f0)
    p, f = two(x, groups), o.ff(x, groups)
    ghost = faces_y(groups, p, turn_next(p), p0_turned, f, turn_next(f), f0_turned)
    turned = [turn_prev(v) for v in ghost]
    p, f, p_turned, f_turned = p0, f0, p0_turned, f0_turned
    for k in range(groups):
        here = group(k)
        p_after, f_after = two(x, k + 1), o.ff(x, k + 1)
        p_after_turned, f_after_turned = turn_next(p_after), turn_next(f_after)
        mine = faces_y(k, p, p_turned, p_after_turned, f, f_turned, f_after_turned)
        mine_turned = [turn_prev(v) for v in mine]
        ey, wy, dy = mine
        ey_before, wy_before, dy_before = (
            turned_prev(a, b, s) for a, b in zip(mine_turned, turned, strict=True)
        )
        ez = o.fz(x, k)
        wz = ez * (f + z_next(f))
        dz = z_next(p) - p
        ez_before, wz_before, dz_before = z_prev(ez), z_prev(wz), z_prev(dz)
        qx, sx = x_flux(o, x, k, two)
        gained = (qx - carried[0, here, :]) + (ey * dy - ey_before * dy_before)
        gained = gained + (ez * dz - ez_before * dz_before)
        weighed = (sx - carried[1, here, :]) + (wy * dy - wy_before * dy_before)
        weighed = weighed + (wz * dz - wz_before * dz_before)
        carried[0, here, :] = qx
        carried[1, here, :] = sx
        rest = o.rhs(x, k) - own_diag[x, here, :] * p + gained
        below = lane < split(k)
        put(
            k,
            rest,
            res[0, x, here, :] + gained,
            res[1, x, here, :] + 0.5 * weighed,
            jnp.where(s == 0, ey_before, ey),
            jnp.where(s == 0, wy_before, wy),
            jnp.where(below, ez, ez_before),
            jnp.where(below, wz, wz_before),
        )
        turned = mine_turned
        p, f, p_turned, f_turned = p_after, f_after, p_after_turned, f_after_turned


FLUXES = 6


def interior_kernel(split_ref, inv, res, mask, ff, rhs, own_diag, tot, gain, one, fx, fy, fz, ynear, yfar,
                    late_near, late_far, tot3, gain3, one3, six, end, two, acc, *flux_and_carried):
    flux, carried = flux_and_carried[:FLUXES], flux_and_carried[FLUXES]
    late_messages(split_ref, ff, inv, late_near, late_far)
    n, own, wide = mask.shape
    groups = own // 8
    s, lane = places(wide)
    ghosts = Ghosts(ynear, yfar)

    def finish(x, carry):
        done = Finished(x, n, ghosts, mask, rhs, tot, fx, fy, s, lane)
        for slot in range(3):
            g = relaxation / done.total[slot]
            tot3[x, group(slot), :] = done.total[slot]
            gain3[x, group(slot), :] = g
            one3[x, group(slot), :] = g * done.all_rhs[slot]
        end[x] = done.end
        for k, v in enumerate((done.rhs, done.fx, done.fy, done.fz, ghosts.frac_and_lower(x)[0])):
            six[k, x] = v
        return carry

    lax.fori_loop(0, n, finish, 0, unroll=8)
    o = Inside(groups, ff, rhs, gain, one, fx, fy, fz, gain3, one3, six, end)

    def second(x, carry):
        def put(k, v):
            two[x, group(k), :] = v

        second_row(o, x, s, put)
        return carry

    lax.fori_loop(2, n - 2, second, 0, unroll=4)

    def two_of(x, k):
        return two[x, group(k), :]

    for k in range(groups):
        carried[0, group(k), :], carried[1, group(k), :] = x_flux(o, 2, k, two_of)
    acc[...] = jnp.zeros_like(acc)

    def row(x, carry):
        def put(k, rest, *values):
            acc[x // 8, group(k), :] += rest
            for f, v in enumerate(values):
                flux[f][x, group(k), :] = v

        flux_row(o, x, s, lane, two_of, res, own_diag, lambda k: split_ref[x // 8, k], carried, put)
        return carry

    lax.fori_loop(3, n - 3, row, 0, unroll=2)


class Edges(Inside):
    def beyond(self, n, planes, act, tot, tot3, one_edge, gain_edge, edge_fx):
        self.n, self.planes = n, planes
        self.slots = {-1: 0, 0: 1, n - 1: 2, n: 3}
        self.one_edge, self.gain_edge, self.edge_fx = one_edge, gain_edge, edge_fx
        self.far = {-1: 0, n: 1}
        for k in range(self.groups + 1):
            here = group(k)
            low = planes.field(2, k, 0) * act(k)
            high = super().fx(n - 1, k) * planes.field(2, k, 1)
            edge_fx[0, here, :] = low
            edge_fx[1, here, :] = high
            for x, slot in self.slots.items():
                face = low if x <= 0 else high
                if x in self.far:
                    total = jnp.maximum(planes.field(1, k, self.far[x]), 1.0) + face
                else:
                    total = self.three(tot, tot3, x, k) + face
                g = relaxation / total
                gain_edge[slot, here, :] = g
                one_edge[slot, here, :] = g * self.rhs(x, k)

    def rhs(self, x, k):
        return self.planes.field(0, k, self.far[x]) if x in self.far else super().rhs(x, k)

    def fx(self, x, k):
        if x in (-1, self.n - 1):
            return self.edge_fx[0 if x == -1 else 1, group(k), :]
        return super().fx(x, k)

    def fy(self, x, k):
        return self.planes.field(3, k, self.far[x]) if x in self.far else super().fy(x, k)

    def fz(self, x, k):
        return self.planes.field(4, k, self.far[x]) if x in self.far else super().fz(x, k)

    def outermost(self, x):
        return x in (-1, self.n - 1)

    def gain(self, x, k):
        return self.gain_edge[self.slots[x], group(k), :] if x in self.slots else super().gain(x, k)

    def one(self, x, k):
        return self.one_edge[self.slots[x], group(k), :] if x in self.slots else super().one(x, k)

    def before(self, x, k):
        return self.planes.field(5, k, 0) if x == -1 else super().before(x, k)

    def after(self, x, k):
        return self.planes.field(5, k, 1) if x == self.n else super().after(x, k)


def edge_kernel(split_ref, res, mask, ff, rhs, own_diag, tot, gain, one, fx, fy, fz, ynear, yfar, xnear, xfar,
                tot3, gain3, one3, six, end, two, acc,
                sent, edge_flux, edge_fx, edge_step, one_edge, gain_edge, two_edge, carried, total_acc):
    n, own, wide = mask.shape
    groups = own // 8
    s, lane = places(wide)
    planes = Planes(xnear, xfar, own)
    ghosts = Ghosts(ynear, yfar)
    o = Edges(groups, ff, rhs, gain, one, fx, fy, fz, gain3, one3, six, end)

    def act(k):
        return ghosts.active(0) if k == groups else mask[0, group(k), :].astype(F32)

    o.beyond(n, planes, act, tot, tot3, one_edge, gain_edge, edge_fx)
    slots = {x: slot for slot, x in enumerate((-1, 0, 1, n - 2, n - 1, n))}
    for x, slot in slots.items():

        def put_two(k, v, slot=slot):
            two_edge[slot, group(k), :] = v

        second_row(o, x, s, put_two)

    def two_of(x, k):
        return two_edge[slots[x], group(k), :] if x in slots else two[x, group(k), :]

    for k in range(groups):
        edge_step[0, group(k), :] = two_of(0, k) - two_of(-1, k)
        edge_step[1, group(k), :] = two_of(n, k) - two_of(n - 1, k)
    total_acc[...] = acc[...]
    for slot, x in enumerate((0, 1, 2, n - 3, n - 2, n - 1)):
        if slot % 3 == 0:
            for k in range(groups):
                carried[0, group(k), :], carried[1, group(k), :] = x_flux(o, x - 1, k, two_of)

        def put(k, rest, *values, x=x, slot=slot):
            total_acc[x // 8, group(k), :] += rest
            for f, v in enumerate(values):
                edge_flux[f, slot, group(k), :] = v

        flux_row(o, x, s, lane, two_of, res, own_diag, lambda k, x=x: split_ref[x // 8, k], carried, put)

    rows_b, cols_b = split_ref.shape
    lane = lax.broadcasted_iota(jnp.int32, (1, wide), 1)
    lower, upper = [], []
    for q in range(rows_b):
        for r in range(cols_b):
            column = jnp.sum(total_acc[q, group(r), :], axis=0, keepdims=True)
            below = lane < split_ref[q, r]
            lower.append(jnp.where(below, column, 0.0))
            upper.append(jnp.where(below, 0.0, column))
    count = rows_b * cols_b
    low_sum = jnp.sum(jnp.concatenate(lower, axis=0), axis=1, keepdims=True)
    high_sum = jnp.sum(jnp.concatenate(upper, axis=0), axis=1, keepdims=True)
    span = sent.shape[1]
    place = lax.broadcasted_iota(jnp.int32, (count, span), 1) - 2 * count * lax.axis_index("gy")
    which = 2 * lax.broadcasted_iota(jnp.int32, (count, span), 0)
    laid = jnp.where(place == which, low_sum, jnp.where(place == which + 1, high_sum, 0.0))
    sent[...] = jnp.broadcast_to(jnp.sum(laid, axis=0, keepdims=True), sent.shape)


def final_kernel(tiles_y, split_ref, frac, inv, ynear, yfar, xnear, xfar, fx, edge_flux, edge_fx, edge_step,
                 al0, al1, be0, be1, got, *rest):
    flux = rest[:FLUXES]
    out, coarse, step_y, step_z, held, sems = rest[FLUXES:]
    i, j = lax.axis_index("gx"), lax.axis_index("gy")
    n, own, wide = frac.shape
    ext = own + G
    unknowns = inv.shape[2]
    rows_b, cols_b = split_ref.shape
    per_tile = 2 * rows_b * cols_b
    ghosts = Ghosts(ynear, yfar)
    planes = Planes(xnear, xfar, own)
    s8, lane8 = places(wide)

    all_got = got[...]
    owner = lax.broadcasted_iota(jnp.int32, all_got.shape, 0)

    def row_of(tile_row):
        mine = (owner >= tile_row * tiles_y) & (owner < (tile_row + 1) * tiles_y)
        return jnp.sum(jnp.where(mine, all_got, 0.0), axis=0, keepdims=True)

    coarse_res = row_of(i)

    def solve(tile):
        start = pl.multiple_of(jnp.clip(tile, 0, tiles_y - 1) * per_tile, 8)
        block = inv[0, pl.ds(start, per_tile), :]
        e = jnp.sum(block * coarse_res[:, :unknowns], axis=1, keepdims=True)
        return jnp.broadcast_to(e, (per_tile, wide))

    mine, before, after = solve(j), solve(j - 1), solve(j + 1)

    def one_of(e, k):
        return jnp.broadcast_to(e[k : k + 1], (8, wide))

    for q in range(rows_b):
        for r in range(cols_b):
            k = 2 * (q * cols_b + r)
            low, high = one_of(mine, k), one_of(mine, k + 1)
            split = split_ref[q, r]
            coarse[q + 1, group(r), :] = jnp.where(lane8 < split, low, high)
            jump = high - low
            step_z[q, group(r), :] = jnp.where(
                lane8 == split - 1, jump, jnp.where(lane8 == split, -jump, 0.0)
            )
        below = ghosts.frac_and_lower(8 * q)[1] > 0.5
        k_high, k_low = 2 * q * cols_b, 2 * (q * cols_b + cols_b - 1)
        coarse[q + 1, own:ext, :] = jnp.where(
            s8 == 0,
            jnp.where(below, one_of(after, k_high), one_of(after, k_high + 1)),
            jnp.where(below, one_of(before, k_low), one_of(before, k_low + 1)),
        )
        for r in range(cols_b):
            here = coarse[q + 1, group(r), :]
            ahead = turn_next(coarse[q + 1, group(r + 1), :])
            behind = turn_prev(coarse[q + 1, group(r - 1 if r else cols_b), :])
            step_y[q, group(r), :] = jnp.where(
                s8 == G - 1, ahead - here, jnp.where(s8 == 0, behind - here, 0.0)
            )
    blocks = pl.cdiv(unknowns, wide)
    for side, tile_row in ((0, i - 1), (1, i + 1)):
        other = row_of(tile_row)
        e = jnp.zeros((16, 1), F32)
        for k in range(blocks):
            w = min(wide, unknowns - k * wide)
            part = planes.rows(own + 16 * k, 16, side)[:, :w] * other[:, k * wide : k * wide + w]
            e = e + jnp.sum(part, axis=1, keepdims=True)
        e = jnp.broadcast_to(e, (16, wide))
        below = planes.rows(own + 16 * blocks, 8, side)
        skip = 16 - 2 * cols_b if side == 0 else 0
        at = 0 if side == 0 else rows_b + 1
        for r in range(cols_b):
            k = skip + 2 * r
            coarse[at, group(r), :] = jnp.where(one_of(below, r) > 0.5, one_of(e, k), one_of(e, k + 1))

    def solved(x, q, values, beside):
        for r in range(cols_b):
            here = group(r)
            u, v, wy, sy, wz, sz = (value(r) for value in values)
            along_y, along_z = step_y[q, here, :], step_z[q, here, :]
            u = u + (wy * along_y + wz * along_z)
            weighed = sy * along_y + sz * along_z
            if beside is not None:
                ex, sx, step, sweep_step = beside(r)
                u = u + ex * step
                weighed = weighed + sx * (step + sweep_step)
            v = v + 0.5 * weighed
            held[0, x, here, :] = al0[x, here, :] * u - al1[x, here, :] * v
            held[1, x, here, :] = be0[x, here, :] * v - be1[x, here, :] * u

    def copies(q):
        return [
            pltpu.make_async_copy(
                held.at[k, pl.ds(8 * q, 8)], out.at[k, pl.ds(8 * q, 8)], sems.at[k, q]
            )
            for k in range(2)
        ]

    def frac_of(x, r):
        if x in (-1, n):
            return planes.rows(8 * r, 8, 0 if x == -1 else 1)
        return frac[x, group(r), :]

    def face(x, r):
        if x in (-1, n - 1):
            ex = edge_fx[0 if x == -1 else 1, group(r), :]
        else:
            ex = fx[x, group(r), :]
        return ex, ex * (frac_of(x, r) + frac_of(x + 1, r))

    outer = {x: slot for slot, x in enumerate((0, 1, 2, n - 3, n - 2, n - 1))}

    def values_of(x):
        if isinstance(x, int) and x in outer:
            return [lambda r, f=f: edge_flux[f, outer[x], group(r), :] for f in range(FLUXES)]
        return [lambda r, f=f: flux[f][x, group(r), :] for f in range(FLUXES)]

    for q in range(rows_b):
        first, last = 8 * q, 8 * q + 7

        def ahead(r, q=q, last=last):
            more = edge_step[1, group(r), :] if last == n - 1 else 0.0
            return *face(last, r), coarse[q + 2, group(r), :] - coarse[q + 1, group(r), :], more

        def behind(r, q=q, first=first):
            more = -edge_step[0, group(r), :] if first == 0 else 0.0
            return *face(first - 1, r), coarse[q, group(r), :] - coarse[q + 1, group(r), :], more

        solved(first, q, values_of(first), behind)
        start, stop = first + 1, last
        while start in outer:
            solved(start, q, values_of(start), None)
            start += 1
        while stop - 1 in outer:
            stop -= 1
            solved(stop, q, values_of(stop), None)

        def row(x, carry, q=q):
            solved(x, q, values_of(x), None)
            return carry

        lax.fori_loop(start, stop, row, 0, unroll=3 if (stop - start) % 3 == 0 else 1)
        solved(last, q, values_of(last), ahead)
        for copy in copies(q):
            copy.start()
    for q in range(rows_b):
        for copy in copies(q):
            copy.wait()


def shards(tiles_x, tiles_y, residual, accum_diag, accum_cross, mask, trans_x, trans_y, trans_z,
           frac_flow, split_layer, coarse_inverse):
    n, own, wide = mask.shape
    ext = own + G
    unknowns = coarse_inverse.shape[2]
    columns = (residual, accum_diag, accum_cross, mask, trans_x, trans_y, trans_z, frac_flow)
    far_columns = [pltpu.with_memory_space_constraint(v, pltpu.HBM) for v in columns]
    groups = own // 8

    def group_spec(array, k):
        lead = array.shape[:-3]
        zero = (0,) * len(lead)
        return pl.BlockSpec((*lead, 8, 8, wide), lambda x: (*zero, x, k, 0))

    def array(*shape):
        return jax.ShapeDtypeStruct(shape, F32)

    y_messages = pl.pallas_call(
        y_message_kernel,
        grid=(n // 8,),
        in_specs=[pl.BlockSpec(split_layer.shape, lambda x: (0, 0))]
        + [group_spec(v, 0) for v in columns]
        + [group_spec(v, groups - 1) for v in columns],
        out_specs=[pl.BlockSpec((8, 16, wide), lambda x: (x, 0, 0))] * 2,
        out_shape=[array(n, 16, wide)] * 2,
        compiler_params=params(16),
        name="y_messages",
    )(pltpu.with_memory_space_constraint(split_layer, pltpu.HBM), *far_columns, *far_columns)
    ynear, yfar = swap(y_messages, "gy", tiles_y)

    rhs, own_diag, tot, gain, one, fx, fy, fz, al0, al1, be0, be1 = pl.pallas_call(
        prep_kernel,
        in_specs=[pl.BlockSpec(memory_space=pltpu.HBM)] * 7,
        out_specs=[WHOLE] * 12,
        out_shape=[array(n, own, wide)] * 12,
        scratch_shapes=[pltpu.VMEM(v.shape, v.dtype) for v in columns[:7]]
        + [pltpu.SemaphoreType.DMA((7, n // 4))],
        compiler_params=params(18),
        cost_estimate=cost(60_000_000, 30_000_000),
        name="prep",
    )(*far_columns[:7])
    shared = (rhs, tot, gain, one, fx, fy, fz)

    x_messages = pl.pallas_call(
        x_message_kernel,
        in_specs=[WHOLE] * 10,
        out_specs=[WHOLE] * 2,
        out_shape=[array(PLANES * own + 2 * G, wide)] * 2,
        compiler_params=params(8),
        name="x_messages",
    )(mask, *shared, ynear, yfar)
    xnear, xfar = swap(x_messages, "gx", tiles_x)

    shared = (residual, mask, frac_flow, rhs, own_diag, tot, gain, one, fx, fy, fz, ynear, yfar)
    late_near, late_far, tot3, gain3, one3, six, end, two, acc, *flux = pl.pallas_call(
        interior_kernel,
        in_specs=[SCALARS] + [WHOLE] * 14,
        out_specs=[WHOLE] * (9 + FLUXES),
        out_shape=[array(late_rows(own, unknowns, wide), wide)] * 2
        + [array(n, 3 * G, wide)] * 3
        + [
            array(5, n, G, wide),
            array(n, G, wide),
            array(n, ext, wide),
            array(n // 8, own, wide),
        ]
        + [array(n, own, wide)] * FLUXES,
        scratch_shapes=[pltpu.VMEM((2, own, wide), F32)],
        compiler_params=params(8),
        cost_estimate=cost(60_000_000, 30_000_000),
        name="interior",
    )(split_layer, coarse_inverse, *shared)
    late_near, late_far = swap((late_near, late_far), "gx", tiles_x)

    devices = tiles_x * tiles_y
    span = pl.cdiv(unknowns, 128) * 128
    sent, edge_flux, edge_fx, edge_step = pl.pallas_call(
        edge_kernel,
        in_specs=[SCALARS] + [WHOLE] * 22,
        out_specs=[WHOLE] * 4,
        out_shape=[
            array(devices, span),
            array(FLUXES, 6, own, wide),
            array(2, ext, wide),
            array(2, own, wide),
        ],
        scratch_shapes=[
            pltpu.VMEM((4, ext, wide), F32),
            pltpu.VMEM((4, ext, wide), F32),
            pltpu.VMEM((6, ext, wide), F32),
            pltpu.VMEM((2, own, wide), F32),
            pltpu.VMEM((n // 8, own, wide), F32),
        ],
        compiler_params=params(8),
        name="edges",
    )(split_layer, *shared, xnear, xfar, tot3, gain3, one3, six, end, two, acc)
    got = lax.all_to_all(sent, ("gx", "gy"), 0, 0, tiled=True)

    return pl.pallas_call(
        functools.partial(final_kernel, tiles_y),
        in_specs=[SCALARS] + [WHOLE] * (15 + FLUXES),
        out_specs=pl.BlockSpec(memory_space=pl.ANY),
        out_shape=array(2, n, own, wide),
        scratch_shapes=[
            pltpu.VMEM((n // 8 + 2, ext, wide), F32),
            pltpu.VMEM((n // 8, own, wide), F32),
            pltpu.VMEM((n // 8, own, wide), F32),
            pltpu.VMEM((2, n, own, wide), F32),
            pltpu.SemaphoreType.DMA((2, n // 8)),
        ],
        compiler_params=params(12),
        name="final",
    )(split_layer, frac_flow, coarse_inverse, ynear, yfar, late_near, late_far, fx, edge_flux, edge_fx,
      edge_step, al0, al1, be0, be1, got, *flux)


def solution(mesh):
    placed = (
        P(None, "gx", "gy", None),
        P(None, "gx", "gy", None),
        P(None, "gx", "gy", None),
        P("gx", "gy", None),
        P("gx", "gy", None),
        P("gx", "gy", None),
        P("gx", "gy", None),
        P("gx", "gy", None),
        P("gx", "gy"),
        P("gx", None, None),
    )
    return jax.shard_map(
        functools.partial(shards, mesh.shape["gx"], mesh.shape["gy"]),
        mesh=mesh,
        in_specs=placed,
        out_specs=P(None, "gx", "gy", None),
        check_vma=False,
    )
```

```python
import functools

import jax
import jax.numpy as jnp
from jax import lax
from jax.experimental import pallas as pl
from jax.experimental.pallas import tpu as pltpu
from jax.sharding import PartitionSpec as P

relaxation = 2.0 / 3.0
F32 = jnp.float32
WHOLE = pl.BlockSpec(memory_space=pltpu.VMEM)
SCALARS = pl.BlockSpec(memory_space=pltpu.SMEM)
G = 8
PLANES = 6


def params(mib):
    return pltpu.CompilerParams(vmem_limit_bytes=mib << 20)


def cost(flops, size):
    return pl.CostEstimate(flops=flops, bytes_accessed=size, transcendentals=0)


def z_next(v):
    return pltpu.roll(v, v.shape[1] - 1, 1)


def z_prev(v):
    return pltpu.roll(v, 1, 1)


def quasi_impes(active, rp, rs, dpp, dss, dps, dsp):
    weight = dps / dss
    return active * (rp - weight * rs), active * (dpp - weight * dsp) + (1.0 - active)


def swap_pairs(axis, size):
    near = [(i, i ^ 1) for i in range(size) if i ^ 1 < size]
    far = [(i, ((i + 1) ^ 1) - 1) for i in range(size) if 0 <= ((i + 1) ^ 1) - 1 < size]
    return near, far


def swap(message, axis, size):
    near, far = swap_pairs(axis, size)
    return lax.ppermute(message[0], axis, near), lax.ppermute(message[1], axis, far)


def y_message_kernel(split_ref, *refs):
    low, high = refs[:8], refs[8:16]
    near_ref, far_ref = refs[16:]
    even = lax.rem(lax.axis_index("gy"), 2) == 0
    step = pl.program_id(0)

    def fields(group):
        res, diag, crs, mask, tx, ty, tz, ff = group
        active = mask[...].astype(F32)
        b, c = quasi_impes(active, res[0], res[1], diag[0], diag[1], crs[0], crs[1])
        return active, b, c, tx[...], ty[...], tz[...], ff[...]

    shape = low[3].shape
    s = lax.broadcasted_iota(jnp.int32, shape, 1)
    lane = lax.broadcasted_iota(jnp.int32, shape, 2)

    def turn(v, k):
        return jnp.stack([pltpu.roll(v[i], k, 0) for i in range(v.shape[0])])

    a, b, c, tx, ty, tz, ff = fields(high)
    splits = split_ref[pl.ds(step, 1), :]
    lower = (lane < splits[:, -1:].reshape(1, 1, 1)).astype(F32)
    up = (
        jnp.where(s >= 5, a, jnp.where(s >= 2, turn(ty, 5), turn(tx, 2))),
        jnp.where(
            s >= 6,
            b,
            jnp.where(
                s >= 4,
                turn(c, 6),
                jnp.where(s >= 2, turn(tz, 4), jnp.where(s == 1, turn(ff, 2), lower)),
            ),
        ),
    )
    a, b, c, tx, ty, tz, ff = fields(low)
    lower = (lane < splits[:, :1].reshape(1, 1, 1)).astype(F32)
    down = (
        jnp.where(s < 3, a, jnp.where(s < 6, turn(ty, 3), turn(tx, 6))),
        jnp.where(
            s < 2,
            b,
            jnp.where(
                s < 4,
                turn(c, 2),
                jnp.where(s < 6, turn(tz, 4), jnp.where(s == 6, turn(ff, 6), lower)),
            ),
        ),
    )
    for k in range(2):
        near_ref[:, 8 * k : 8 * k + 8, :] = jnp.where(even, up[k], down[k])
        far_ref[:, 8 * k : 8 * k + 8, :] = jnp.where(even, down[k], up[k])


class Ghosts:
    def __init__(self, near_ref, far_ref):
        self.refs = near_ref, far_ref
        self.even = lax.rem(lax.axis_index("gy"), 2) == 0

    def tiles(self, x, k):
        near, far = (ref[x, 8 * k : 8 * k + 8, :] for ref in self.refs)
        return jnp.where(self.even, near, far), jnp.where(self.even, far, near)

    def pick(self, tiles, high_turn, low_turn, rings):
        high, low = tiles
        s = lax.broadcasted_iota(jnp.int32, high.shape, 0)
        high = pltpu.roll(high, high_turn, 0) if high_turn else high
        low = pltpu.roll(low, low_turn, 0) if low_turn else low
        return jnp.where(s < rings, high, jnp.where(s >= G - rings, low, 0.0))

    def first(self, x):
        t = self.tiles(x, 0)
        return self.pick(t, 0, 0, 3), self.pick(t, 2, 6, 2), self.pick(t, 5, 3, 3)

    def second(self, x):
        t = self.tiles(x, 1)
        c = jnp.maximum(self.pick(t, 6, 2, 2), 1.0)
        return self.pick(t, 0, 0, 2), c, self.pick(t, 4, 4, 2)

    def active(self, x):
        return self.pick(self.tiles(x, 0), 0, 0, 3)

    def frac_and_lower(self, x):
        t = self.tiles(x, 1)
        return self.pick(t, 2, 6, 1), self.pick(t, 1, 7, 1)


def group(k):
    return slice(8 * k, 8 * k + 8)


def turned_next(mine, after, s):
    return jnp.where(s == G - 1, after, mine)


def turned_prev(mine, before, s):
    return jnp.where(s == 0, before, mine)


def turn_next(v):
    return pltpu.roll(v, G - 1, 0)


def turn_prev(v):
    return pltpu.roll(v, 1, 0)


def places(wide):
    shape = (G, wide)
    return lax.broadcasted_iota(jnp.int32, shape, 0), lax.broadcasted_iota(jnp.int32, shape, 1)


def along_z(tz, a, lane):
    return jnp.where(lane < a.shape[1] - 1, tz * a * z_next(a), 0.0)


def prep_kernel(res_hbm, diag_hbm, crs_hbm, mask_hbm, tx_hbm, ty_hbm, tz_hbm,
                rhs, own_diag, tot, gain, one, fx, fy, fz, al0, al1, be0, be1,
                res, diag, crs, mask, tx, ty, tz, sems):
    n, own, wide = mask.shape
    groups = own // 8
    chunk = 4
    s, lane = places(wide)

    def copies(q):
        at = pl.ds(chunk * q, chunk)
        pairs = (
            (res_hbm.at[:, at], res.at[:, at]),
            (diag_hbm.at[:, at], diag.at[:, at]),
            (crs_hbm.at[:, at], crs.at[:, at]),
            (tx_hbm.at[at], tx.at[at]),
            (ty_hbm.at[at], ty.at[at]),
            (tz_hbm.at[at], tz.at[at]),
        )
        return [pltpu.make_async_copy(a, b, sems.at[k + 1, q]) for k, (a, b) in enumerate(pairs)]

    def masks(q):
        at = pl.ds(chunk * q, chunk)
        return pltpu.make_async_copy(mask_hbm.at[at], mask.at[at], sems.at[0, q])

    for q in range(n // chunk):
        for copy in (masks(q), *copies(q)):
            copy.start()
    masks(0).wait()

    def row(x, carry):
        first, last = x == 0, x == n - 1
        after = jnp.minimum(x + 1, n - 1)
        before = jnp.maximum(x - 1, 0)
        a_after = mask[x, group(0), :].astype(F32)
        turned_after = turn_next(a_after)
        ey_before = jnp.zeros((G, wide), F32)
        for k in range(groups):
            here = group(k)
            a, turned = a_after, turned_after
            rp, rs = res[0, x, here, :], res[1, x, here, :]
            dpp, dss = diag[0, x, here, :], diag[1, x, here, :]
            dps, dsp = crs[0, x, here, :], crs[1, x, here, :]
            det = dpp * dss - dps * dsp
            both = 1.0 / (dss * det)
            inverse = both * dss
            weight = dps * (both * det)
            b = a * (rp - weight * rs)
            c = a * (dpp - weight * dsp) + (1.0 - a)
            rhs[x, here, :] = b
            own_diag[x, here, :] = c
            al0[x, here, :] = dss * inverse
            al1[x, here, :] = dps * inverse
            be0[x, here, :] = dpp * inverse
            be1[x, here, :] = dsp * inverse
            t = tx[x, here, :] * a
            ex = t * mask[after, here, :].astype(F32)
            fx[x, here, :] = jnp.where(last, t, ex)
            total = c + jnp.where(last, 0.0, ex)
            total = total + jnp.where(first, 0.0, fx[before, here, :])
            ez = along_z(tz[x, here, :], a, lane)
            fz[x, here, :] = ez
            total = total + ez + z_prev(ez)
            ey = ty[x, here, :] * a
            if k < groups - 1:
                a_after = mask[x, group(k + 1), :].astype(F32)
                turned_after = turn_next(a_after)
                ey = ey * turned_next(turned, turned_after, s)
                inside = ey
            else:
                ey = jnp.where(s == G - 1, ey, ey * turned)
                inside = jnp.where(s == G - 1, 0.0, ey)
            fy[x, here, :] = ey
            ey_turned = turn_prev(inside)
            total = total + inside + turned_prev(ey_turned, ey_before, s)
            ey_before = ey_turned
            tot[x, here, :] = total
            if 0 < k < groups - 1:
                g = relaxation / total
                gain[x, here, :] = g
                one[x, here, :] = g * b
        return carry

    def part(q, carry):
        @pl.when(q < n // chunk - 1)
        def _():
            masks(q + 1).wait()

        for copy in copies(q):
            copy.wait()
        return lax.fori_loop(0, chunk, lambda k, v: row(chunk * q + k, v), carry, unroll=2)

    lax.fori_loop(0, n // chunk, part, 0)


class Finished:
    def __init__(self, x, n, ghosts, mask, rhs, tot, fx, fy, s, lane):
        groups = mask.shape[1] // 8
        first, last = x == 0, x == n - 1
        ga, gtx, gty = ghosts.first(x)
        gb, gc, gtz = ghosts.second(x)
        before, after = jnp.maximum(x - 1, 0), jnp.minimum(x + 1, n - 1)
        a_before, tx_before, _ = ghosts.first(before)
        a_after = ghosts.active(after)
        turned = turn_next(ga)
        end = fy[x, group(groups - 1), :]
        end = jnp.where(s == G - 1, end * turned, end)
        a_first = mask[x, group(0), :].astype(F32)
        ey = gty * ga * turned_next(turned, turn_next(a_first), s)
        ey_turned = turn_prev(ey)
        ez = along_z(gtz, ga, lane)
        t = gtx * ga
        ex = t * a_after
        total = gc + ez + z_prev(ez) + ey + turned_prev(ey_turned, turn_prev(end), s)
        total = total + jnp.where(last, 0.0, ex) + jnp.where(first, 0.0, tx_before * a_before * ga)
        self.end = end
        self.fx, self.fy, self.fz = jnp.where(last, t, ex), ey, ez
        self.rhs = gb
        self.total = (
            tot[x, group(0), :] + jnp.where(s == 0, ey_turned, 0.0),
            tot[x, group(groups - 1), :] + jnp.where(s == G - 1, end, 0.0),
            total,
        )
        self.all_rhs = (rhs[x, group(0), :], rhs[x, group(groups - 1), :], gb)


def slot_of(k, groups):
    return {0: 0, groups - 1: 1, groups: 2}[k]


def x_message_kernel(mask, rhs, tot, gain, one, fx, fy, fz, ynear, yfar, near_ref, far_ref):
    even = lax.rem(lax.axis_index("gx"), 2) == 0
    n, own, wide = mask.shape
    groups = own // 8
    s, lane = places(wide)
    ghosts = Ghosts(ynear, yfar)
    finished = {x: Finished(x, n, ghosts, mask, rhs, tot, fx, fy, s, lane) for x in (0, 1, n - 2, n - 1)}
    for k in range(groups + 1):
        here = group(k)
        touched = k in (0, groups - 1, groups)

        def first_of(x):
            done = finished[x]
            if not touched:
                return one[x, here, :]
            slot = slot_of(k, groups)
            return relaxation * done.all_rhs[slot] / done.total[slot]

        def of(x, key):
            done = finished[x]
            total = done.total[slot_of(k, groups)] if touched else tot[x, here, :]
            if k == groups:
                return done.rhs, total, key, done.fy
            return rhs[x, here, :], total, key, done.end if k == groups - 1 else fy[x, here, :]

        if k == groups:
            up = of(n - 1, finished[n - 1].fx)
            down = of(0, ghosts.active(0))
        else:
            up = of(n - 1, fx[n - 1, here, :])
            down = of(0, mask[0, here, :].astype(F32))
            up += (fz[n - 1, here, :], fx[n - 2, here, :] * first_of(n - 2))
            down += (fz[0, here, :], fx[0, here, :] * first_of(1))
        if k == groups:
            b, total, key, ey = (jnp.where(even, p, q) for p, q in zip(up, down, strict=True))
            ob, ototal, okey, oey = (jnp.where(even, q, p) for p, q in zip(up, down, strict=True))
            for ref, (b, total, key, ey) in (
                (near_ref, (b, total, key, ey)),
                (far_ref, (ob, ototal, okey, oey)),
            ):
                at = PLANES * own
                ref[at : at + G, :] = jnp.where((s == 0) | (s == G - 1), b, pltpu.roll(total, 4, 0))
                ref[at + G : at + 2 * G, :] = jnp.where((s < 2) | (s >= G - 2), key, pltpu.roll(ey, 4, 0))
        else:
            for f in range(PLANES):
                start = f * own + 8 * k
                near_ref[start : start + 8, :] = jnp.where(even, up[f], down[f])
                far_ref[start : start + 8, :] = jnp.where(even, down[f], up[f])


def late_messages(split_ref, ff, inv, near_ref, far_ref):
    even = lax.rem(lax.axis_index("gx"), 2) == 0
    j = lax.axis_index("gy")
    n, own, wide = ff.shape
    per_tile = 2 * split_ref.shape[0] * split_ref.shape[1]
    near_ref[0:own, :] = jnp.where(even, ff[n - 1], ff[0])
    far_ref[0:own, :] = jnp.where(even, ff[0], ff[n - 1])
    at = own
    unknowns = inv.shape[2]
    top = inv[0, pl.ds(pl.multiple_of(j * per_tile + per_tile - 16, 8), 16), :]
    bottom = inv[0, pl.ds(pl.multiple_of(j * per_tile, 8), 16), :]
    for k in range(0, unknowns, wide):
        w = min(wide, unknowns - k)
        if w < wide:
            near_ref[at : at + 16, :] = jnp.zeros((16, wide), F32)
            far_ref[at : at + 16, :] = jnp.zeros((16, wide), F32)
        near_ref[at : at + 16, :w] = jnp.where(even, top[:, k : k + w], bottom[:, k : k + w])
        far_ref[at : at + 16, :w] = jnp.where(even, bottom[:, k : k + w], top[:, k : k + w])
        at += 16
    lane = lax.broadcasted_iota(jnp.int32, (1, wide), 1)
    zero = jnp.zeros((8, wide), F32)
    near_ref[at : at + 8, :] = zero
    far_ref[at : at + 8, :] = zero
    for q in range(split_ref.shape[1]):
        top = (lane < split_ref[split_ref.shape[0] - 1, q]).astype(F32)
        bottom = (lane < split_ref[0, q]).astype(F32)
        near_ref[at + q : at + q + 1, :] = jnp.where(even, top, bottom)
        far_ref[at + q : at + q + 1, :] = jnp.where(even, bottom, top)


def late_rows(own, unknowns, wide):
    return own + 16 * pl.cdiv(unknowns, wide) + 8


class Planes:
    def __init__(self, near_ref, far_ref, own):
        self.refs, self.own = (near_ref, far_ref), own
        self.even = lax.rem(lax.axis_index("gx"), 2) == 0

    def rows(self, at, n, side):
        near, far = (ref[at : at + n, :] for ref in self.refs)
        return jnp.where(self.even, near, far) if side else jnp.where(self.even, far, near)

    def field(self, f, k, side):
        if 8 * k < self.own:
            return self.rows(f * self.own + 8 * k, 8, side)
        s, _ = places(self.refs[0].shape[1])
        ends = (s == 0) | (s == G - 1)
        if f < 2:
            tile = self.rows(PLANES * self.own, G, side)
            return jnp.where(ends, pltpu.roll(tile, 4, 0) if f else tile, 0.0)
        if f < 4:
            tile = self.rows(PLANES * self.own + G, G, side)
            if f == 2:
                return jnp.where((s < 2) | (s >= G - 2), tile, 0.0)
            return jnp.where(s == G - 1, pltpu.roll(tile, 4, 0), 0.0)
        return jnp.zeros_like(s, F32)


class Inside:
    def __init__(self, groups, ff, rhs, gain, one, fx, fy, fz, gain3, one3, six, end):
        self.groups, self.own_ff, self.own_rhs = groups, ff, rhs
        self.own_gain, self.own_one, self.own_fx, self.own_fy, self.own_fz = gain, one, fx, fy, fz
        self.gain3, self.one3, self.six, self.end = gain3, one3, six, end

    def pick(self, own, which, x, k):
        return self.six[which, x] if k == self.groups else own[x, group(k), :]

    def three(self, own, other, x, k):
        if 0 < k < self.groups - 1:
            return own[x, group(k), :]
        return other[x, group(slot_of(k, self.groups)), :]

    def rhs(self, x, k):
        return self.pick(self.own_rhs, 0, x, k)

    def fx(self, x, k):
        return self.pick(self.own_fx, 1, x, k)

    def fy(self, x, k):
        if k == self.groups - 1:
            return self.end[x]
        return self.pick(self.own_fy, 2, x, k)

    def fz(self, x, k):
        return self.pick(self.own_fz, 3, x, k)

    def ff(self, x, k):
        return self.pick(self.own_ff, 4, x, k)

    def gain(self, x, k):
        return self.three(self.own_gain, self.gain3, x, k)

    def one(self, x, k):
        return self.three(self.own_one, self.one3, x, k)

    def before(self, x, k):
        return self.fx(x - 1, k) * self.one(x - 1, k)

    def after(self, x, k):
        return self.fx(x, k) * self.one(x + 1, k)

    def faces_x(self, x, k):
        ex = self.fx(x, k)
        return ex, ex * (self.ff(x, k) + self.ff(x + 1, k))


def second_row(o, x, s, put):
    total = o.groups + 1
    p = o.one(x, 0)
    p_turned = turn_next(p)
    w_turned = turn_prev(o.fy(x, total - 1) * o.one(x, total - 1))
    for k in range(total):
        p_after = o.one(x, (k + 1) % total)
        after_turned = turn_next(p_after)
        ey, ez = o.fy(x, k), o.fz(x, k)
        mine = turn_prev(ey * p)
        beside = ey * turned_next(p_turned, after_turned, s) + turned_prev(mine, w_turned, s)
        beside = beside + ez * z_next(p) + z_prev(ez * p)
        beside = beside + o.after(x, k) + o.before(x, k)
        put(k, o.gain(x, k) * ((2.0 - relaxation) * o.rhs(x, k) + beside))
        p, p_turned, w_turned = p_after, after_turned, mine


def x_flux(o, x, k, two):
    step = two(x + 1, k) - two(x, k)
    ex, wx = o.faces_x(x, k)
    return ex * step, wx * step


def flux_row(o, x, s, lane, two, res, own_diag, split, carried, put):
    groups = o.groups

    def faces_y(k, p, p_turned, p_after, f, f_turned, f_after):
        ey = o.fy(x, k)
        weighted = ey * (f + turned_next(f_turned, f_after, s))
        return ey, weighted, turned_next(p_turned, p_after, s) - p

    p0, f0 = two(x, 0), o.ff(x, 0)
    p0_turned, f0_turned = turn_next(p0), turn_next(f0)
    p, f = two(x, groups), o.ff(x, groups)
    ghost = faces_y(groups, p, turn_next(p), p0_turned, f, turn_next(f), f0_turned)
    turned = [turn_prev(v) for v in ghost]
    p, f, p_turned, f_turned = p0, f0, p0_turned, f0_turned
    for k in range(groups):
        here = group(k)
        p_after, f_after = two(x, k + 1), o.ff(x, k + 1)
        p_after_turned, f_after_turned = turn_next(p_after), turn_next(f_after)
        mine = faces_y(k, p, p_turned, p_after_turned, f, f_turned, f_after_turned)
        mine_turned = [turn_prev(v) for v in mine]
        ey, wy, dy = mine
        ey_before, wy_before, dy_before = (
            turned_prev(a, b, s) for a, b in zip(mine_turned, turned, strict=True)
        )
        ez = o.fz(x, k)
        wz = ez * (f + z_next(f))
        dz = z_next(p) - p
        ez_before, wz_before, dz_before = z_prev(ez), z_prev(wz), z_prev(dz)
        qx, sx = x_flux(o, x, k, two)
        if carried is None:
            qx_before, sx_before = x_flux(o, x - 1, k, two)
        else:
            qx_before, sx_before = carried[0, here, :], carried[1, here, :]
            carried[0, here, :] = qx
            carried[1, here, :] = sx
        gained = (qx - qx_before) + (ey * dy - ey_before * dy_before)
        gained = gained + (ez * dz - ez_before * dz_before)
        weighed = (sx - sx_before) + (wy * dy - wy_before * dy_before)
        weighed = weighed + (wz * dz - wz_before * dz_before)
        rest = o.rhs(x, k) - own_diag[x, here, :] * p + gained
        below = lane < split(k)
        put(
            k,
            rest,
            res[0, x, here, :] + gained,
            res[1, x, here, :] + 0.5 * weighed,
            jnp.where(s == 0, ey_before, ey),
            jnp.where(s == 0, wy_before, wy),
            jnp.where(below, ez, ez_before),
            jnp.where(below, wz, wz_before),
        )
        turned = mine_turned
        p, f, p_turned, f_turned = p_after, f_after, p_after_turned, f_after_turned


FLUXES = 6


def interior_kernel(split_ref, inv, res, mask, ff, rhs, own_diag, tot, gain, one, fx, fy, fz, ynear, yfar,
                    late_near, late_far, tot3, gain3, one3, six, end, two, acc, *flux_and_carried):
    flux, carried = flux_and_carried[:FLUXES], flux_and_carried[FLUXES]
    late_messages(split_ref, ff, inv, late_near, late_far)
    n, own, wide = mask.shape
    groups = own // 8
    s, lane = places(wide)
    ghosts = Ghosts(ynear, yfar)

    def finish(x, carry):
        done = Finished(x, n, ghosts, mask, rhs, tot, fx, fy, s, lane)
        for slot in range(3):
            g = relaxation / done.total[slot]
            tot3[x, group(slot), :] = done.total[slot]
            gain3[x, group(slot), :] = g
            one3[x, group(slot), :] = g * done.all_rhs[slot]
        end[x] = done.end
        for k, v in enumerate((done.rhs, done.fx, done.fy, done.fz, ghosts.frac_and_lower(x)[0])):
            six[k, x] = v
        return carry

    lax.fori_loop(0, n, finish, 0, unroll=8)
    o = Inside(groups, ff, rhs, gain, one, fx, fy, fz, gain3, one3, six, end)

    def second(x, carry):
        def put(k, v):
            two[x, group(k), :] = v

        second_row(o, x, s, put)
        return carry

    lax.fori_loop(2, n - 2, second, 0, unroll=4)

    def two_of(x, k):
        return two[x, group(k), :]

    for k in range(groups):
        carried[0, group(k), :], carried[1, group(k), :] = x_flux(o, 2, k, two_of)
    acc[...] = jnp.zeros_like(acc)

    def row(x, carry):
        def put(k, rest, *values):
            acc[x // 8, group(k), :] += rest
            for f, v in enumerate(values):
                flux[f][x, group(k), :] = v

        flux_row(o, x, s, lane, two_of, res, own_diag, lambda k: split_ref[x // 8, k], carried, put)
        return carry

    lax.fori_loop(3, n - 3, row, 0, unroll=2)


class Edges(Inside):
    def beyond(self, n, planes, act, tot, tot3, one_edge, gain_edge, edge_fx):
        self.n, self.planes = n, planes
        self.slots = {-1: 0, 0: 1, n - 1: 2, n: 3}
        self.one_edge, self.gain_edge, self.edge_fx = one_edge, gain_edge, edge_fx
        self.far = {-1: 0, n: 1}
        for k in range(self.groups + 1):
            here = group(k)
            low = planes.field(2, k, 0) * act(k)
            high = super().fx(n - 1, k) * planes.field(2, k, 1)
            edge_fx[0, here, :] = low
            edge_fx[1, here, :] = high
            for x, slot in self.slots.items():
                face = low if x <= 0 else high
                if x in self.far:
                    total = jnp.maximum(planes.field(1, k, self.far[x]), 1.0) + face
                else:
                    total = self.three(tot, tot3, x, k) + face
                g = relaxation / total
                gain_edge[slot, here, :] = g
                one_edge[slot, here, :] = g * self.rhs(x, k)

    def rhs(self, x, k):
        return self.planes.field(0, k, self.far[x]) if x in self.far else super().rhs(x, k)

    def fx(self, x, k):
        if x in (-1, self.n - 1):
            return self.edge_fx[0 if x == -1 else 1, group(k), :]
        return super().fx(x, k)

    def fy(self, x, k):
        return self.planes.field(3, k, self.far[x]) if x in self.far else super().fy(x, k)

    def fz(self, x, k):
        return self.planes.field(4, k, self.far[x]) if x in self.far else super().fz(x, k)

    def gain(self, x, k):
        return self.gain_edge[self.slots[x], group(k), :] if x in self.slots else super().gain(x, k)

    def one(self, x, k):
        return self.one_edge[self.slots[x], group(k), :] if x in self.slots else super().one(x, k)

    def before(self, x, k):
        return self.planes.field(5, k, 0) if x == -1 else super().before(x, k)

    def after(self, x, k):
        return self.planes.field(5, k, 1) if x == self.n else super().after(x, k)


def edge_kernel(split_ref, res, mask, ff, rhs, own_diag, tot, gain, one, fx, fy, fz, ynear, yfar, xnear, xfar,
                tot3, gain3, one3, six, end, two, acc, *others):
    flux = others[FLUXES : 2 * FLUXES]
    sent, edge_fx, edge_step, one_edge, gain_edge, two_edge, near_fx, total_acc = others[2 * FLUXES :]
    n, own, wide = mask.shape
    groups = own // 8
    s, lane = places(wide)
    planes = Planes(xnear, xfar, own)
    ghosts = Ghosts(ynear, yfar)
    o = Edges(groups, ff, rhs, gain, one, fx, fy, fz, gain3, one3, six, end)

    def act(k):
        return ghosts.active(0) if k == groups else mask[0, group(k), :].astype(F32)

    o.beyond(n, planes, act, tot, tot3, one_edge, gain_edge, edge_fx)
    depth = 5
    bases = (-1, n - depth + 1)
    for side, base in enumerate(bases):
        for r in range(depth):
            x, slot = base + r, depth * side + r
            if x in (-1, 0, 1, n - 2, n - 1, n):

                def put_two(k, v, slot=slot):
                    two_edge[slot, group(k), :] = v

                second_row(o, x, s, put_two)
            else:
                two_edge[slot] = two[x]
            if x == n:
                continue
            for k in range(groups):
                ex = o.fx(x, k)
                near_fx[0, slot, group(k), :] = ex
                if x in (-1, n - 1):
                    near_fx[1, slot, group(k), :] = jnp.zeros_like(ex)
                else:
                    near_fx[1, slot, group(k), :] = ex * (o.ff(x, k) + o.ff(x + 1, k))
    for k in range(groups):
        edge_step[0, group(k), :] = two_edge[1, group(k), :] - two_edge[0, group(k), :]
        edge_step[1, group(k), :] = two_edge[2 * depth - 1, group(k), :] - two_edge[2 * depth - 2, group(k), :]
    total_acc[...] = acc[...]
    plain = Inside(groups, ff, rhs, gain, one, fx, fy, fz, gain3, one3, six, end)

    def row(r, carry):
        high = r >= depth - 2
        x = jnp.where(high, n - 2 * (depth - 2) + r, r)
        shift = jnp.where(high, depth - bases[1], -bases[0])

        def two_of(x, k):
            return two_edge[x + shift, group(k), :]

        def faces_x(x, k):
            return near_fx[0, x + shift, group(k), :], near_fx[1, x + shift, group(k), :]

        plain.faces_x = faces_x

        def put(k, rest, *values):
            total_acc[x // 8, group(k), :] += rest
            for f, v in enumerate(values):
                flux[f][x, group(k), :] = v

        flux_row(plain, x, s, lane, two_of, res, own_diag, lambda k: split_ref[x // 8, k], None, put)
        return carry

    lax.fori_loop(0, 2 * (depth - 2), row, 0, unroll=2)

    rows_b, cols_b = split_ref.shape
    lane = lax.broadcasted_iota(jnp.int32, (1, wide), 1)
    lower, upper = [], []
    for q in range(rows_b):
        for r in range(cols_b):
            column = jnp.sum(total_acc[q, group(r), :], axis=0, keepdims=True)
            below = lane < split_ref[q, r]
            lower.append(jnp.where(below, column, 0.0))
            upper.append(jnp.where(below, 0.0, column))
    count = rows_b * cols_b
    low_sum = jnp.sum(jnp.concatenate(lower, axis=0), axis=1, keepdims=True)
    high_sum = jnp.sum(jnp.concatenate(upper, axis=0), axis=1, keepdims=True)
    span = sent.shape[1]
    place = lax.broadcasted_iota(jnp.int32, (count, span), 1) - 2 * count * lax.axis_index("gy")
    which = 2 * lax.broadcasted_iota(jnp.int32, (count, span), 0)
    laid = jnp.where(place == which, low_sum, jnp.where(place == which + 1, high_sum, 0.0))
    sent[...] = jnp.broadcast_to(jnp.sum(laid, axis=0, keepdims=True), sent.shape)


def final_kernel(tiles_y, split_ref, frac, inv, ynear, yfar, xnear, xfar, fx, edge_fx, edge_step,
                 al0, al1, be0, be1, got, *rest):
    flux = rest[:FLUXES]
    out, coarse, step_y, step_z, across, held, sems = rest[FLUXES:]
    i, j = lax.axis_index("gx"), lax.axis_index("gy")
    n, own, wide = frac.shape
    ext = own + G
    unknowns = inv.shape[2]
    rows_b, cols_b = split_ref.shape
    per_tile = 2 * rows_b * cols_b
    ghosts = Ghosts(ynear, yfar)
    planes = Planes(xnear, xfar, own)
    s8, lane8 = places(wide)

    all_got = got[...]
    owner = lax.broadcasted_iota(jnp.int32, all_got.shape, 0)

    def row_of(tile_row):
        mine = (owner >= tile_row * tiles_y) & (owner < (tile_row + 1) * tiles_y)
        return jnp.sum(jnp.where(mine, all_got, 0.0), axis=0, keepdims=True)

    coarse_res = row_of(i)

    def solve(tile):
        start = pl.multiple_of(jnp.clip(tile, 0, tiles_y - 1) * per_tile, 8)
        block = inv[0, pl.ds(start, per_tile), :]
        e = jnp.sum(block * coarse_res[:, :unknowns], axis=1, keepdims=True)
        return jnp.broadcast_to(e, (per_tile, wide))

    mine, before, after = solve(j), solve(j - 1), solve(j + 1)

    def one_of(e, k):
        return jnp.broadcast_to(e[k : k + 1], (8, wide))

    for q in range(rows_b):
        for r in range(cols_b):
            k = 2 * (q * cols_b + r)
            low, high = one_of(mine, k), one_of(mine, k + 1)
            split = split_ref[q, r]
            coarse[q + 1, group(r), :] = jnp.where(lane8 < split, low, high)
            jump = high - low
            step_z[q, group(r), :] = jnp.where(
                lane8 == split - 1, jump, jnp.where(lane8 == split, -jump, 0.0)
            )
        below = ghosts.frac_and_lower(8 * q)[1] > 0.5
        k_high, k_low = 2 * q * cols_b, 2 * (q * cols_b + cols_b - 1)
        coarse[q + 1, own:ext, :] = jnp.where(
            s8 == 0,
            jnp.where(below, one_of(after, k_high), one_of(after, k_high + 1)),
            jnp.where(below, one_of(before, k_low), one_of(before, k_low + 1)),
        )
        for r in range(cols_b):
            here = coarse[q + 1, group(r), :]
            ahead = turn_next(coarse[q + 1, group(r + 1), :])
            behind = turn_prev(coarse[q + 1, group(r - 1 if r else cols_b), :])
            step_y[q, group(r), :] = jnp.where(
                s8 == G - 1, ahead - here, jnp.where(s8 == 0, behind - here, 0.0)
            )
    blocks = pl.cdiv(unknowns, wide)
    for side, tile_row in ((0, i - 1), (1, i + 1)):
        other = row_of(tile_row)
        e = jnp.zeros((16, 1), F32)
        for k in range(blocks):
            w = min(wide, unknowns - k * wide)
            part = planes.rows(own + 16 * k, 16, side)[:, :w] * other[:, k * wide : k * wide + w]
            e = e + jnp.sum(part, axis=1, keepdims=True)
        e = jnp.broadcast_to(e, (16, wide))
        below = planes.rows(own + 16 * blocks, 8, side)
        skip = 16 - 2 * cols_b if side == 0 else 0
        at = 0 if side == 0 else rows_b + 1
        for r in range(cols_b):
            k = skip + 2 * r
            coarse[at, group(r), :] = jnp.where(one_of(below, r) > 0.5, one_of(e, k), one_of(e, k + 1))

    for q in range(rows_b + 1):
        x = 8 * q - 1
        for r in range(cols_b):
            here = group(r)
            ex = edge_fx[0, here, :] if q == 0 else edge_fx[1, here, :] if q == rows_b else fx[x, here, :]
            f_before = planes.rows(8 * r, 8, 0) if q == 0 else frac[x, here, :]
            f_after = planes.rows(8 * r, 8, 1) if q == rows_b else frac[x + 1, here, :]
            step = coarse[q + 1, here, :] - coarse[q, here, :]
            across[0, q, here, :] = ex * step
            if q in (0, rows_b):
                step = step + edge_step[0 if q == 0 else 1, here, :]
            across[1, q, here, :] = ex * (0.5 * (f_before + f_after)) * step

    def solved(x, q, beside=None, sign=None):
        for r in range(cols_b):
            here = group(r)
            u, v, wy, sy, wz, sz = (ref[x, here, :] for ref in flux)
            along_y, along_z = step_y[q, here, :], step_z[q, here, :]
            u = u + (wy * along_y + wz * along_z)
            v = v + 0.5 * (sy * along_y + sz * along_z)
            if beside is not None:
                u = sign(u, across[0, beside, here, :])
                v = sign(v, across[1, beside, here, :])
            held[0, x, here, :] = al0[x, here, :] * u - al1[x, here, :] * v
            held[1, x, here, :] = be0[x, here, :] * v - be1[x, here, :] * u

    def copies(q):
        return [
            pltpu.make_async_copy(
                held.at[k, pl.ds(4 * q, 4)], out.at[k, pl.ds(4 * q, 4)], sems.at[k, q]
            )
            for k in range(2)
        ]

    def block(q, carry):
        x = 8 * q
        solved(x, q, q, jnp.subtract)
        for k in range(1, 4):
            solved(x + k, q)
        for copy in copies(2 * q):
            copy.start()
        for k in range(4, 7):
            solved(x + k, q)
        solved(x + 7, q, q + 1, jnp.add)
        for copy in copies(2 * q + 1):
            copy.start()
        return carry

    lax.fori_loop(0, rows_b, block, 0)
    for q in range(2 * rows_b):
        for copy in copies(q):
            copy.wait()


def shards(tiles_x, tiles_y, residual, accum_diag, accum_cross, mask, trans_x, trans_y, trans_z,
           frac_flow, split_layer, coarse_inverse):
    n, own, wide = mask.shape
    ext = own + G
    unknowns = coarse_inverse.shape[2]
    columns = (residual, accum_diag, accum_cross, mask, trans_x, trans_y, trans_z, frac_flow)
    far_columns = [pltpu.with_memory_space_constraint(v, pltpu.HBM) for v in columns]
    groups = own // 8

    def group_spec(array, k):
        lead = array.shape[:-3]
        zero = (0,) * len(lead)
        return pl.BlockSpec((*lead, 8, 8, wide), lambda x: (*zero, x, k, 0))

    def array(*shape):
        return jax.ShapeDtypeStruct(shape, F32)

    y_messages = pl.pallas_call(
        y_message_kernel,
        grid=(n // 8,),
        in_specs=[pl.BlockSpec(split_layer.shape, lambda x: (0, 0))]
        + [group_spec(v, 0) for v in columns]
        + [group_spec(v, groups - 1) for v in columns],
        out_specs=[pl.BlockSpec((8, 16, wide), lambda x: (x, 0, 0))] * 2,
        out_shape=[array(n, 16, wide)] * 2,
        compiler_params=params(16),
        name="y_messages",
    )(pltpu.with_memory_space_constraint(split_layer, pltpu.HBM), *far_columns, *far_columns)
    ynear, yfar = swap(y_messages, "gy", tiles_y)

    rhs, own_diag, tot, gain, one, fx, fy, fz, al0, al1, be0, be1 = pl.pallas_call(
        prep_kernel,
        in_specs=[pl.BlockSpec(memory_space=pltpu.HBM)] * 7,
        out_specs=[WHOLE] * 12,
        out_shape=[array(n, own, wide)] * 12,
        scratch_shapes=[pltpu.VMEM(v.shape, v.dtype) for v in columns[:7]]
        + [pltpu.SemaphoreType.DMA((7, n // 4))],
        compiler_params=params(18),
        cost_estimate=cost(60_000_000, 30_000_000),
        name="prep",
    )(*far_columns[:7])
    shared = (rhs, tot, gain, one, fx, fy, fz)

    x_messages = pl.pallas_call(
        x_message_kernel,
        in_specs=[WHOLE] * 10,
        out_specs=[WHOLE] * 2,
        out_shape=[array(PLANES * own + 2 * G, wide)] * 2,
        compiler_params=params(8),
        name="x_messages",
    )(mask, *shared, ynear, yfar)
    xnear, xfar = swap(x_messages, "gx", tiles_x)

    shared = (residual, mask, frac_flow, rhs, own_diag, tot, gain, one, fx, fy, fz, ynear, yfar)
    late_near, late_far, tot3, gain3, one3, six, end, two, acc, *flux = pl.pallas_call(
        interior_kernel,
        in_specs=[SCALARS] + [WHOLE] * 14,
        out_specs=[WHOLE] * (9 + FLUXES),
        out_shape=[array(late_rows(own, unknowns, wide), wide)] * 2
        + [array(n, 3 * G, wide)] * 3
        + [
            array(5, n, G, wide),
            array(n, G, wide),
            array(n, ext, wide),
            array(n // 8, own, wide),
        ]
        + [array(n, own, wide)] * FLUXES,
        scratch_shapes=[pltpu.VMEM((2, own, wide), F32)],
        compiler_params=params(8),
        cost_estimate=cost(60_000_000, 30_000_000),
        name="interior",
    )(split_layer, coarse_inverse, *shared)
    late_near, late_far = swap((late_near, late_far), "gx", tiles_x)

    devices = tiles_x * tiles_y
    span = pl.cdiv(unknowns, 128) * 128
    *flux, sent, edge_fx, edge_step = pl.pallas_call(
        edge_kernel,
        in_specs=[SCALARS] + [WHOLE] * (22 + FLUXES),
        out_specs=[WHOLE] * (3 + FLUXES),
        out_shape=[array(n, own, wide)] * FLUXES
        + [
            array(devices, span),
            array(2, ext, wide),
            array(2, own, wide),
        ],
        scratch_shapes=[
            pltpu.VMEM((4, ext, wide), F32),
            pltpu.VMEM((4, ext, wide), F32),
            pltpu.VMEM((10, ext, wide), F32),
            pltpu.VMEM((2, 10, own, wide), F32),
            pltpu.VMEM((n // 8, own, wide), F32),
        ],
        input_output_aliases={23 + f: f for f in range(FLUXES)},
        compiler_params=params(8),
        name="edges",
    )(split_layer, *shared, xnear, xfar, tot3, gain3, one3, six, end, two, acc, *flux)
    got = lax.all_to_all(sent, ("gx", "gy"), 0, 0, tiled=True)

    return pl.pallas_call(
        functools.partial(final_kernel, tiles_y),
        in_specs=[SCALARS] + [WHOLE] * (14 + FLUXES),
        out_specs=pl.BlockSpec(memory_space=pl.ANY),
        out_shape=array(2, n, own, wide),
        scratch_shapes=[
            pltpu.VMEM((n // 8 + 2, ext, wide), F32),
            pltpu.VMEM((n // 8, own, wide), F32),
            pltpu.VMEM((n // 8, own, wide), F32),
            pltpu.VMEM((2, n // 8 + 1, own, wide), F32),
            pltpu.VMEM((2, n, own, wide), F32),
            pltpu.SemaphoreType.DMA((2, n // 4)),
        ],
        compiler_params=params(12),
        name="final",
    )(split_layer, frac_flow, coarse_inverse, ynear, yfar, late_near, late_far, fx, edge_fx,
      edge_step, al0, al1, be0, be1, got, *flux)


def solution(mesh):
    placed = (
        P(None, "gx", "gy", None),
        P(None, "gx", "gy", None),
        P(None, "gx", "gy", None),
        P("gx", "gy", None),
        P("gx", "gy", None),
        P("gx", "gy", None),
        P("gx", "gy", None),
        P("gx", "gy", None),
        P("gx", "gy"),
        P("gx", None, None),
    )
    return jax.shard_map(
        functools.partial(shards, mesh.shape["gx"], mesh.shape["gy"]),
        mesh=mesh,
        in_specs=placed,
        out_specs=P(None, "gx", "gy", None),
        check_vma=False,
    )
```

```python
import functools

import jax
import jax.numpy as jnp
from jax import lax
from jax.experimental import pallas as pl
from jax.experimental.pallas import tpu as pltpu
from jax.sharding import PartitionSpec as P

relaxation = 2.0 / 3.0
F32 = jnp.float32
WHOLE = pl.BlockSpec(memory_space=pltpu.VMEM)
SCALARS = pl.BlockSpec(memory_space=pltpu.SMEM)
G = 8
PLANES = 6


def params(mib):
    return pltpu.CompilerParams(vmem_limit_bytes=mib << 20)


def cost(flops, size):
    return pl.CostEstimate(flops=flops, bytes_accessed=size, transcendentals=0)


def z_next(v):
    return pltpu.roll(v, v.shape[1] - 1, 1)


def z_prev(v):
    return pltpu.roll(v, 1, 1)


def quasi_impes(active, rp, rs, dpp, dss, dps, dsp):
    weight = dps / dss
    return active * (rp - weight * rs), active * (dpp - weight * dsp) + (1.0 - active)


def swap_pairs(axis, size):
    near = [(i, i ^ 1) for i in range(size) if i ^ 1 < size]
    far = [(i, ((i + 1) ^ 1) - 1) for i in range(size) if 0 <= ((i + 1) ^ 1) - 1 < size]
    return near, far


def swap(message, axis, size):
    near, far = swap_pairs(axis, size)
    return lax.ppermute(message[0], axis, near), lax.ppermute(message[1], axis, far)


def group(k):
    return slice(8 * k, 8 * k + 8)


def turned_next(mine, after, s):
    return jnp.where(s == G - 1, after, mine)


def turned_prev(mine, before, s):
    return jnp.where(s == 0, before, mine)


def turn_next(v):
    return pltpu.roll(v, G - 1, 0)


def turn_prev(v):
    return pltpu.roll(v, 1, 0)


def places(wide):
    shape = (G, wide)
    return lax.broadcasted_iota(jnp.int32, shape, 0), lax.broadcasted_iota(jnp.int32, shape, 1)


def along_z(tz, a, lane):
    return jnp.where(lane < a.shape[1] - 1, tz * a * z_next(a), 0.0)


Y_TURNS = {
    "c": (6, 2),
    "a": (4, 4),
    "tx": (3, 5),
    "e": (3, 6),
    "tz": (1, 7),
}
Y_PLACES = {
    "c": ((4, 5), (2, 3)),
    "a": ((3,), (4,)),
    "tx": ((2,), (5,)),
    "e": ((1,), (6,)),
    "tz": ((0,), (7,)),
}


def y_message_kernel(split_ref, *refs):
    far, (near_ref, far_ref) = refs[:8], refs[8:10]
    low, high, sems = refs[10:18], refs[18:26], refs[26]
    n, _, wide = low[3].shape
    own = far[3].shape[1]
    even = lax.rem(lax.axis_index("gy"), 2) == 0
    s, lane = places(wide)
    chunk = 8

    def copy(f, side, q):
        rows, columns = pl.ds(chunk * q, chunk), pl.ds(own - 8 if side else 0, 8)
        held = (high if side else low)[f]
        if len(held.shape) == 4:
            source, target = far[f].at[:, rows, columns], held.at[:, rows]
        else:
            source, target = far[f].at[rows, columns], held.at[rows]
        return pltpu.make_async_copy(source, target, sems.at[q, f, side])

    ahead = [(f, side) for f in (3,) for side in (0, 1)]
    behind = [(f, side) for f in (0, 1, 2, 4, 5, 6, 7) for side in (0, 1)]
    for q in range(n // chunk):
        for f, side in ahead + behind:
            copy(f, side, q).start()
    for f, side in ahead:
        copy(f, side, 0).wait()

    def fields(group, x, side):
        res, diag, crs, mask, tx, ty, tz, ff = group
        first, last = x == 0, x == n - 1
        before, after = jnp.maximum(x - 1, 0), jnp.minimum(x + 1, n - 1)
        a = mask[x].astype(F32)
        b, c = quasi_impes(a, res[0, x], res[1, x], diag[0, x], diag[1, x], crs[0, x], crs[1, x])
        ty_a = ty[x] * a
        ey = ty_a * turn_next(a)
        ez = along_z(tz[x], a, lane)
        more = ez + z_prev(ez) + jnp.where(last, 0.0, tx[x] * a * mask[after].astype(F32))
        more = more + jnp.where(first, 0.0, tx[before] * mask[before].astype(F32) * a)
        more = more + (ey if side else turn_prev(ey))
        c = jnp.where(s == (1 if side else 6), c + more, c)
        tile = b
        for name, v in (("c", c), ("a", a), ("tx", tx[x]), ("e", ey), ("tz", tz[x])):
            moved = pltpu.roll(v, Y_TURNS[name][side], 0)
            for place in Y_PLACES[name][side]:
                tile = jnp.where(s == place, moved, tile)
        outer = slice(0, 1) if side else slice(7, 8)
        return tile, ty_a[outer], ff[x][outer]

    def put(rows, up, down):
        near_ref[rows, :] = jnp.where(even, up, down)
        far_ref[rows, :] = jnp.where(even, down, up)

    def row(x):
        up, down = fields(high, x, 0), fields(low, x, 1)
        put(pl.ds(pl.multiple_of(8 * x, 8), 8), up[0], down[0])
        put(pl.ds(8 * n + x, 1), up[1], down[1])
        put(pl.ds(9 * n + x, 1), up[2], down[2])

    def part(q, carry):
        @pl.when(q < n // chunk - 1)
        def _():
            for f, side in ahead:
                copy(f, side, q + 1).wait()

        for f, side in behind:
            copy(f, side, q).wait()

        def some(k, v):
            row(chunk * q + k)
            return v

        return lax.fori_loop(0, chunk, some, carry, unroll=4)

    put(slice(10 * n, y_message_rows(n)), *[jnp.zeros((y_message_rows(n) - 10 * n, wide), F32)] * 2)
    for q in range(n // 8):
        splits = split_ref[q : q + 1, :]
        up = (lane[:1] < splits[:, -1:]).astype(F32)
        down = (lane[:1] < splits[:, :1]).astype(F32)
        put(slice(10 * n + 2 + q, 10 * n + 3 + q), up, down)
    lax.fori_loop(0, n // chunk, part, 0)
    corners = [
        (tx[n - 1, at, :] * mask[n - 1, at, :].astype(F32), mask[0, at, :].astype(F32))
        for mask, tx, at in ((high[3], high[4], slice(6, 7)), (low[3], low[4], slice(1, 2)))
    ]
    for k in range(2):
        put(slice(10 * n + k, 10 * n + k + 1), corners[0][k], corners[1][k])


def y_message_rows(n):
    return 10 * n + pl.cdiv(2 + n // 8, 8) * 8


class Ghosts:
    def __init__(self, near_ref, far_ref, n):
        self.refs, self.n = (near_ref, far_ref), n
        self.even = lax.rem(lax.axis_index("gy"), 2) == 0
        self.s, _ = places(near_ref.shape[1])

    def both(self, rows):
        near, far = (ref[rows, :] for ref in self.refs)
        return jnp.where(self.even, far, near), jnp.where(self.even, near, far)

    def tiles(self, x):
        return self.both(pl.ds(pl.multiple_of(8 * x, 8), 8))

    def pick(self, tiles, name, low_at=(G - 1,), high_at=(0,)):
        low, high = tiles
        if name != "b":
            up, down = Y_TURNS[name]
            low, high = pltpu.roll(low, 8 - up, 0), pltpu.roll(high, 8 - down, 0)
        picked = jnp.zeros_like(low)
        for place in low_at:
            picked = jnp.where(self.s == place, low, picked)
        for place in high_at:
            picked = jnp.where(self.s == place, high, picked)
        return picked

    def row(self, at, low_at=G - 1, high_at=0):
        low, high = self.both(pl.ds(at, 1))
        return jnp.where(self.s == low_at, low, jnp.where(self.s == high_at, high, 0.0))

    def active(self, x):
        return self.pick(self.tiles(x), "a")

    def first_active(self):
        return self.active(0) + self.row(10 * self.n + 1, G - 2, 1)

    def last_trans(self):
        return self.row(10 * self.n, G - 2, 1)

    def frac(self, x):
        return self.row(9 * self.n + x)

    def lower(self, q):
        return self.row(10 * self.n + 2 + q)


def prep_kernel(res_hbm, diag_hbm, crs, mask_hbm, tx_hbm, ty_hbm, tz_hbm,
                rhs, own_diag, tot, gain, one, fx, fy, fz, al0, al1, be0, be1,
                res, diag, mask, tx, ty, tz, sems):
    n, own, wide = mask.shape
    groups = own // 8
    chunk = 4
    s, lane = places(wide)

    def copies(q):
        at = pl.ds(chunk * q, chunk)
        pairs = (
            (res_hbm.at[:, at], res.at[:, at]),
            (diag_hbm.at[:, at], diag.at[:, at]),
            (tx_hbm.at[at], tx.at[at]),
            (ty_hbm.at[at], ty.at[at]),
            (tz_hbm.at[at], tz.at[at]),
        )
        return [pltpu.make_async_copy(a, b, sems.at[k + 1, q]) for k, (a, b) in enumerate(pairs)]

    def masks(q):
        at = pl.ds(chunk * q, chunk)
        return pltpu.make_async_copy(mask_hbm.at[at], mask.at[at], sems.at[0, q])

    for q in range(n // chunk):
        for copy in (masks(q), *copies(q)):
            copy.start()
    masks(0).wait()

    def row(x, carry):
        first, last = x == 0, x == n - 1
        after = jnp.minimum(x + 1, n - 1)
        before = jnp.maximum(x - 1, 0)
        a_after = mask[x, group(0), :].astype(F32)
        turned_after = turn_next(a_after)
        ey_before = jnp.zeros((G, wide), F32)
        for k in range(groups):
            here = group(k)
            a, turned = a_after, turned_after
            rp, rs = res[0, x, here, :], res[1, x, here, :]
            dpp, dss = diag[0, x, here, :], diag[1, x, here, :]
            dps, dsp = crs[0, x, here, :], crs[1, x, here, :]
            det = dpp * dss - dps * dsp
            both = 1.0 / (dss * det)
            inverse = both * dss
            weight = dps * (both * det)
            b = a * (rp - weight * rs)
            c = a * (dpp - weight * dsp) + (1.0 - a)
            rhs[x, here, :] = b
            own_diag[x, here, :] = c
            al0[x, here, :] = dss * inverse
            al1[x, here, :] = dps * inverse
            be0[x, here, :] = dpp * inverse
            be1[x, here, :] = dsp * inverse
            t = tx[x, here, :] * a
            ex = t * mask[after, here, :].astype(F32)
            fx[x, here, :] = jnp.where(last, t, ex)
            total = c + jnp.where(last, 0.0, ex)
            total = total + jnp.where(first, 0.0, fx[before, here, :])
            ez = along_z(tz[x, here, :], a, lane)
            fz[x, here, :] = ez
            total = total + ez + z_prev(ez)
            ey = ty[x, here, :] * a
            if k < groups - 1:
                a_after = mask[x, group(k + 1), :].astype(F32)
                turned_after = turn_next(a_after)
                ey = ey * turned_next(turned, turned_after, s)
                inside = ey
            else:
                ey = jnp.where(s == G - 1, ey, ey * turned)
                inside = jnp.where(s == G - 1, 0.0, ey)
            fy[x, here, :] = ey
            ey_turned = turn_prev(inside)
            total = total + inside + turned_prev(ey_turned, ey_before, s)
            ey_before = ey_turned
            tot[x, here, :] = total
            if 0 < k < groups - 1:
                g = relaxation / total
                gain[x, here, :] = g
                one[x, here, :] = g * b
        return carry

    def part(q, carry):
        @pl.when(q < n // chunk - 1)
        def _():
            masks(q + 1).wait()

        for copy in copies(q):
            copy.wait()
        return lax.fori_loop(0, chunk, lambda k, v: row(chunk * q + k, v), carry, unroll=2)

    lax.fori_loop(0, n // chunk, part, 0)


class Finished:
    def __init__(self, x, n, ghosts, mask, rhs, tot, fx, fy, s, lane):
        groups = mask.shape[1] // 8
        first, last = x == 0, x == n - 1
        tiles = ghosts.tiles(x)
        ga, gtx, gtz = (ghosts.pick(tiles, name) for name in ("a", "tx", "tz"))
        gb = ghosts.pick(tiles, "b", (G - 1, G - 2), (0, 1))
        gc = jnp.maximum(ghosts.pick(tiles, "c", (G - 1, G - 2), (0, 1)), 1.0)
        before, after = jnp.maximum(x - 1, 0), jnp.minimum(x + 1, n - 1)
        tiles_before = ghosts.tiles(before)
        a_before, tx_before = ghosts.pick(tiles_before, "a"), ghosts.pick(tiles_before, "tx")
        a_after = ghosts.active(after)
        end = fy[x, group(groups - 1), :]
        end = jnp.where(s == G - 1, end * turn_next(ga), end)
        a_first = turn_next(mask[x, group(0), :].astype(F32))
        ey = ghosts.pick(tiles, "e", (G - 2,), (0,))
        ey = jnp.where(s == G - 1, ghosts.row(8 * n + x) * a_first, ey)
        ey_turned = turn_prev(ey)
        ez = along_z(gtz, ga, lane)
        t = gtx * ga
        ex = t * a_after
        total = gc + ez + z_prev(ez) + ey + turned_prev(ey_turned, turn_prev(end), s)
        total = total + jnp.where(last, 0.0, ex) + jnp.where(first, 0.0, tx_before * a_before * ga)
        self.end = end
        self.fx, self.fy, self.fz = jnp.where(last, t + ghosts.last_trans(), ex), ey, ez
        self.rhs = gb
        self.total = (
            tot[x, group(0), :] + jnp.where(s == 0, ey_turned, 0.0),
            tot[x, group(groups - 1), :] + jnp.where(s == G - 1, end, 0.0),
            total,
        )
        self.all_rhs = (rhs[x, group(0), :], rhs[x, group(groups - 1), :], gb)


def slot_of(k, groups):
    return {0: 0, groups - 1: 1, groups: 2}[k]


def x_message_kernel(mask, rhs, tot, gain, one, fx, fy, fz, ynear, yfar, near_ref, far_ref):
    even = lax.rem(lax.axis_index("gx"), 2) == 0
    n, own, wide = mask.shape
    groups = own // 8
    s, lane = places(wide)
    ghosts = Ghosts(ynear, yfar, n)
    finished = {x: Finished(x, n, ghosts, mask, rhs, tot, fx, fy, s, lane) for x in (0, 1, n - 2, n - 1)}
    for k in range(groups + 1):
        here = group(k)
        touched = k in (0, groups - 1, groups)

        def first_of(x):
            done = finished[x]
            if not touched:
                return one[x, here, :]
            slot = slot_of(k, groups)
            return relaxation * done.all_rhs[slot] / done.total[slot]

        def of(x, key):
            done = finished[x]
            total = done.total[slot_of(k, groups)] if touched else tot[x, here, :]
            if k == groups:
                return done.rhs, total, key, done.fy
            return rhs[x, here, :], total, key, done.end if k == groups - 1 else fy[x, here, :]

        if k == groups:
            up = of(n - 1, finished[n - 1].fx)
            down = of(0, ghosts.first_active())
        else:
            up = of(n - 1, fx[n - 1, here, :])
            down = of(0, mask[0, here, :].astype(F32))
            up += (fz[n - 1, here, :], fx[n - 2, here, :] * first_of(n - 2))
            down += (fz[0, here, :], fx[0, here, :] * first_of(1))
        if k == groups:
            b, total, key, ey = (jnp.where(even, p, q) for p, q in zip(up, down, strict=True))
            ob, ototal, okey, oey = (jnp.where(even, q, p) for p, q in zip(up, down, strict=True))
            for ref, (b, total, key, ey) in (
                (near_ref, (b, total, key, ey)),
                (far_ref, (ob, ototal, okey, oey)),
            ):
                at = PLANES * own
                ref[at : at + G, :] = jnp.where((s == 0) | (s == G - 1), b, pltpu.roll(total, 4, 0))
                ref[at + G : at + 2 * G, :] = jnp.where((s < 2) | (s >= G - 2), key, pltpu.roll(ey, 4, 0))
        else:
            for f in range(PLANES):
                start = f * own + 8 * k
                near_ref[start : start + 8, :] = jnp.where(even, up[f], down[f])
                far_ref[start : start + 8, :] = jnp.where(even, down[f], up[f])


def late_messages(split_ref, ff, inv, near_ref, far_ref):
    even = lax.rem(lax.axis_index("gx"), 2) == 0
    j = lax.axis_index("gy")
    n, own, wide = ff.shape
    per_tile = 2 * split_ref.shape[0] * split_ref.shape[1]
    near_ref[0:own, :] = jnp.where(even, ff[n - 1], ff[0])
    far_ref[0:own, :] = jnp.where(even, ff[0], ff[n - 1])
    at = own
    unknowns = inv.shape[2]
    top = inv[0, pl.ds(pl.multiple_of(j * per_tile + per_tile - 16, 8), 16), :]
    bottom = inv[0, pl.ds(pl.multiple_of(j * per_tile, 8), 16), :]
    for k in range(0, unknowns, wide):
        w = min(wide, unknowns - k)
        if w < wide:
            near_ref[at : at + 16, :] = jnp.zeros((16, wide), F32)
            far_ref[at : at + 16, :] = jnp.zeros((16, wide), F32)
        near_ref[at : at + 16, :w] = jnp.where(even, top[:, k : k + w], bottom[:, k : k + w])
        far_ref[at : at + 16, :w] = jnp.where(even, bottom[:, k : k + w], top[:, k : k + w])
        at += 16
    lane = lax.broadcasted_iota(jnp.int32, (1, wide), 1)
    zero = jnp.zeros((8, wide), F32)
    near_ref[at : at + 8, :] = zero
    far_ref[at : at + 8, :] = zero
    for q in range(split_ref.shape[1]):
        top = (lane < split_ref[split_ref.shape[0] - 1, q]).astype(F32)
        bottom = (lane < split_ref[0, q]).astype(F32)
        near_ref[at + q : at + q + 1, :] = jnp.where(even, top, bottom)
        far_ref[at + q : at + q + 1, :] = jnp.where(even, bottom, top)


def late_rows(own, unknowns, wide):
    return own + 16 * pl.cdiv(unknowns, wide) + 8


class Planes:
    def __init__(self, near_ref, far_ref, own):
        self.refs, self.own = (near_ref, far_ref), own
        self.even = lax.rem(lax.axis_index("gx"), 2) == 0

    def rows(self, at, n, side):
        near, far = (ref[at : at + n, :] for ref in self.refs)
        return jnp.where(self.even, near, far) if side else jnp.where(self.even, far, near)

    def field(self, f, k, side):
        if 8 * k < self.own:
            return self.rows(f * self.own + 8 * k, 8, side)
        s, _ = places(self.refs[0].shape[1])
        ends = (s == 0) | (s == G - 1)
        if f < 2:
            tile = self.rows(PLANES * self.own, G, side)
            return jnp.where(ends, pltpu.roll(tile, 4, 0) if f else tile, 0.0)
        if f < 4:
            tile = self.rows(PLANES * self.own + G, G, side)
            if f == 2:
                return jnp.where((s < 2) | (s >= G - 2), tile, 0.0)
            return jnp.where(s == G - 1, pltpu.roll(tile, 4, 0), 0.0)
        return jnp.zeros_like(s, F32)


class Inside:
    def __init__(self, groups, ff, rhs, gain, one, fx, fy, fz, gain3, one3, six, end):
        self.groups, self.own_ff, self.own_rhs = groups, ff, rhs
        self.own_gain, self.own_one, self.own_fx, self.own_fy, self.own_fz = gain, one, fx, fy, fz
        self.gain3, self.one3, self.six, self.end = gain3, one3, six, end

    def pick(self, own, which, x, k):
        return self.six[which, x] if k == self.groups else own[x, group(k), :]

    def three(self, own, other, x, k):
        if 0 < k < self.groups - 1:
            return own[x, group(k), :]
        return other[x, group(slot_of(k, self.groups)), :]

    def rhs(self, x, k):
        return self.pick(self.own_rhs, 0, x, k)

    def fx(self, x, k):
        return self.pick(self.own_fx, 1, x, k)

    def fy(self, x, k):
        if k == self.groups - 1:
            return self.end[x]
        return self.pick(self.own_fy, 2, x, k)

    def fz(self, x, k):
        return self.pick(self.own_fz, 3, x, k)

    def ff(self, x, k):
        return self.pick(self.own_ff, 4, x, k)

    def gain(self, x, k):
        return self.three(self.own_gain, self.gain3, x, k)

    def one(self, x, k):
        return self.three(self.own_one, self.one3, x, k)

    def before(self, x, k):
        return self.fx(x - 1, k) * self.one(x - 1, k)

    def after(self, x, k):
        return self.fx(x, k) * self.one(x + 1, k)

    def faces_x(self, x, k):
        ex = self.fx(x, k)
        return ex, ex * (self.ff(x, k) + self.ff(x + 1, k))


def second_row(o, x, s, put):
    total = o.groups + 1
    p = o.one(x, 0)
    p_turned = turn_next(p)
    w_turned = turn_prev(o.fy(x, total - 1) * o.one(x, total - 1))
    for k in range(total):
        p_after = o.one(x, (k + 1) % total)
        after_turned = turn_next(p_after)
        ey, ez = o.fy(x, k), o.fz(x, k)
        mine = turn_prev(ey * p)
        beside = ey * turned_next(p_turned, after_turned, s) + turned_prev(mine, w_turned, s)
        beside = beside + ez * z_next(p) + z_prev(ez * p)
        beside = beside + o.after(x, k) + o.before(x, k)
        put(k, o.gain(x, k) * ((2.0 - relaxation) * o.rhs(x, k) + beside))
        p, p_turned, w_turned = p_after, after_turned, mine


def x_flux(o, x, k, two):
    step = two(x + 1, k) - two(x, k)
    ex, wx = o.faces_x(x, k)
    return ex * step, wx * step


def flux_row(o, x, s, lane, two, res, own_diag, split, carried, put):
    groups = o.groups

    def faces_y(k, p, p_turned, p_after, f, f_turned, f_after):
        ey = o.fy(x, k)
        weighted = ey * (f + turned_next(f_turned, f_after, s))
        return ey, weighted, turned_next(p_turned, p_after, s) - p

    p0, f0 = two(x, 0), o.ff(x, 0)
    p0_turned, f0_turned = turn_next(p0), turn_next(f0)
    p, f = two(x, groups), o.ff(x, groups)
    ghost = faces_y(groups, p, turn_next(p), p0_turned, f, turn_next(f), f0_turned)
    turned = [turn_prev(v) for v in ghost]
    p, f, p_turned, f_turned = p0, f0, p0_turned, f0_turned
    for k in range(groups):
        here = group(k)
        p_after, f_after = two(x, k + 1), o.ff(x, k + 1)
        p_after_turned, f_after_turned = turn_next(p_after), turn_next(f_after)
        mine = faces_y(k, p, p_turned, p_after_turned, f, f_turned, f_after_turned)
        mine_turned = [turn_prev(v) for v in mine]
        ey, wy, dy = mine
        ey_before, wy_before, dy_before = (
            turned_prev(a, b, s) for a, b in zip(mine_turned, turned, strict=True)
        )
        ez = o.fz(x, k)
        wz = ez * (f + z_next(f))
        dz = z_next(p) - p
        ez_before, wz_before, dz_before = z_prev(ez), z_prev(wz), z_prev(dz)
        qx, sx = x_flux(o, x, k, two)
        if carried is None:
            qx_before, sx_before = x_flux(o, x - 1, k, two)
        else:
            qx_before, sx_before = carried[0, here, :], carried[1, here, :]
            carried[0, here, :] = qx
            carried[1, here, :] = sx
        gained = (qx - qx_before) + (ey * dy - ey_before * dy_before)
        gained = gained + (ez * dz - ez_before * dz_before)
        weighed = (sx - sx_before) + (wy * dy - wy_before * dy_before)
        weighed = weighed + (wz * dz - wz_before * dz_before)
        rest = o.rhs(x, k) - own_diag[x, here, :] * p + gained
        below = lane < split(k)
        put(
            k,
            rest,
            res[0, x, here, :] + gained,
            res[1, x, here, :] + 0.5 * weighed,
            jnp.where(s == 0, ey_before, ey),
            jnp.where(s == 0, wy_before, wy),
            jnp.where(below, ez, ez_before),
            jnp.where(below, wz, wz_before),
        )
        turned = mine_turned
        p, f, p_turned, f_turned = p_after, f_after, p_after_turned, f_after_turned


FLUXES = 6


def interior_kernel(split_ref, inv, res, mask, ff, rhs, own_diag, tot, gain, one, fx, fy, fz, ynear, yfar,
                    late_near, late_far, tot3, gain3, one3, six, end, two, acc, *flux_and_carried):
    flux, carried = flux_and_carried[:FLUXES], flux_and_carried[FLUXES]
    late_messages(split_ref, ff, inv, late_near, late_far)
    n, own, wide = mask.shape
    groups = own // 8
    s, lane = places(wide)
    ghosts = Ghosts(ynear, yfar, n)

    def finish(x, carry):
        done = Finished(x, n, ghosts, mask, rhs, tot, fx, fy, s, lane)
        for slot in range(3):
            g = relaxation / done.total[slot]
            tot3[x, group(slot), :] = done.total[slot]
            gain3[x, group(slot), :] = g
            one3[x, group(slot), :] = g * done.all_rhs[slot]
        end[x] = done.end
        for k, v in enumerate((done.rhs, done.fx, done.fy, done.fz, ghosts.frac(x))):
            six[k, x] = v
        return carry

    lax.fori_loop(0, n, finish, 0, unroll=8)
    o = Inside(groups, ff, rhs, gain, one, fx, fy, fz, gain3, one3, six, end)

    def second(x, carry):
        def put(k, v):
            two[x, group(k), :] = v

        second_row(o, x, s, put)
        return carry

    lax.fori_loop(2, n - 2, second, 0, unroll=4)

    def two_of(x, k):
        return two[x, group(k), :]

    for k in range(groups):
        carried[0, group(k), :], carried[1, group(k), :] = x_flux(o, 2, k, two_of)
    acc[...] = jnp.zeros_like(acc)

    def row(x, carry):
        def put(k, rest, *values):
            acc[x // 8, group(k), :] += rest
            for f, v in enumerate(values):
                flux[f][x, group(k), :] = v

        flux_row(o, x, s, lane, two_of, res, own_diag, lambda k: split_ref[x // 8, k], carried, put)
        return carry

    lax.fori_loop(3, n - 3, row, 0, unroll=2)


class Edges(Inside):
    def beyond(self, n, planes, act, tot, tot3, one_edge, gain_edge, edge_fx):
        self.n, self.planes = n, planes
        self.slots = {-1: 0, 0: 1, n - 1: 2, n: 3}
        self.one_edge, self.gain_edge, self.edge_fx = one_edge, gain_edge, edge_fx
        self.far = {-1: 0, n: 1}
        for k in range(self.groups + 1):
            here = group(k)
            low = planes.field(2, k, 0) * act(k)
            high = super().fx(n - 1, k) * planes.field(2, k, 1)
            edge_fx[0, here, :] = low
            edge_fx[1, here, :] = high
            for x, slot in self.slots.items():
                face = low if x <= 0 else high
                if x in self.far:
                    total = jnp.maximum(planes.field(1, k, self.far[x]), 1.0) + face
                else:
                    total = self.three(tot, tot3, x, k) + face
                g = relaxation / total
                gain_edge[slot, here, :] = g
                one_edge[slot, here, :] = g * self.rhs(x, k)

    def rhs(self, x, k):
        return self.planes.field(0, k, self.far[x]) if x in self.far else super().rhs(x, k)

    def fx(self, x, k):
        if x in (-1, self.n - 1):
            return self.edge_fx[0 if x == -1 else 1, group(k), :]
        return super().fx(x, k)

    def fy(self, x, k):
        return self.planes.field(3, k, self.far[x]) if x in self.far else super().fy(x, k)

    def fz(self, x, k):
        return self.planes.field(4, k, self.far[x]) if x in self.far else super().fz(x, k)

    def gain(self, x, k):
        return self.gain_edge[self.slots[x], group(k), :] if x in self.slots else super().gain(x, k)

    def one(self, x, k):
        return self.one_edge[self.slots[x], group(k), :] if x in self.slots else super().one(x, k)

    def before(self, x, k):
        return self.planes.field(5, k, 0) if x == -1 else super().before(x, k)

    def after(self, x, k):
        return self.planes.field(5, k, 1) if x == self.n else super().after(x, k)


def edge_kernel(split_ref, res, mask, ff, rhs, own_diag, tot, gain, one, fx, fy, fz, ynear, yfar, xnear, xfar,
                tot3, gain3, one3, six, end, two, acc, *others):
    flux = others[FLUXES : 2 * FLUXES]
    sent, edge_fx, edge_step, one_edge, gain_edge, two_edge, near_fx, total_acc = others[2 * FLUXES :]
    n, own, wide = mask.shape
    groups = own // 8
    s, lane = places(wide)
    planes = Planes(xnear, xfar, own)
    ghosts = Ghosts(ynear, yfar, n)
    o = Edges(groups, ff, rhs, gain, one, fx, fy, fz, gain3, one3, six, end)

    def act(k):
        return ghosts.first_active() if k == groups else mask[0, group(k), :].astype(F32)

    o.beyond(n, planes, act, tot, tot3, one_edge, gain_edge, edge_fx)
    depth = 5
    bases = (-1, n - depth + 1)
    for side, base in enumerate(bases):
        for r in range(depth):
            x, slot = base + r, depth * side + r
            if x in (-1, 0, 1, n - 2, n - 1, n):

                def put_two(k, v, slot=slot):
                    two_edge[slot, group(k), :] = v

                second_row(o, x, s, put_two)
            else:
                two_edge[slot] = two[x]
            if x == n:
                continue
            for k in range(groups):
                ex = o.fx(x, k)
                near_fx[0, slot, group(k), :] = ex
                if x in (-1, n - 1):
                    near_fx[1, slot, group(k), :] = jnp.zeros_like(ex)
                else:
                    near_fx[1, slot, group(k), :] = ex * (o.ff(x, k) + o.ff(x + 1, k))
    for k in range(groups):
        edge_step[0, group(k), :] = two_edge[1, group(k), :] - two_edge[0, group(k), :]
        edge_step[1, group(k), :] = two_edge[2 * depth - 1, group(k), :] - two_edge[2 * depth - 2, group(k), :]
    total_acc[...] = acc[...]
    plain = Inside(groups, ff, rhs, gain, one, fx, fy, fz, gain3, one3, six, end)

    def row(r, carry):
        high = r >= depth - 2
        x = jnp.where(high, n - 2 * (depth - 2) + r, r)
        shift = jnp.where(high, depth - bases[1], -bases[0])

        def two_of(x, k):
            return two_edge[x + shift, group(k), :]

        def faces_x(x, k):
            return near_fx[0, x + shift, group(k), :], near_fx[1, x + shift, group(k), :]

        plain.faces_x = faces_x

        def put(k, rest, *values):
            total_acc[x // 8, group(k), :] += rest
            for f, v in enumerate(values):
                flux[f][x, group(k), :] = v

        flux_row(plain, x, s, lane, two_of, res, own_diag, lambda k: split_ref[x // 8, k], None, put)
        return carry

    lax.fori_loop(0, 2 * (depth - 2), row, 0, unroll=2)

    rows_b, cols_b = split_ref.shape
    lane = lax.broadcasted_iota(jnp.int32, (1, wide), 1)
    lower, upper = [], []
    for q in range(rows_b):
        for r in range(cols_b):
            column = jnp.sum(total_acc[q, group(r), :], axis=0, keepdims=True)
            below = lane < split_ref[q, r]
            lower.append(jnp.where(below, column, 0.0))
            upper.append(jnp.where(below, 0.0, column))
    count = rows_b * cols_b
    low_sum = jnp.sum(jnp.concatenate(lower, axis=0), axis=1, keepdims=True)
    high_sum = jnp.sum(jnp.concatenate(upper, axis=0), axis=1, keepdims=True)
    span = sent.shape[1]
    place = lax.broadcasted_iota(jnp.int32, (count, span), 1) - 2 * count * lax.axis_index("gy")
    which = 2 * lax.broadcasted_iota(jnp.int32, (count, span), 0)
    laid = jnp.where(place == which, low_sum, jnp.where(place == which + 1, high_sum, 0.0))
    sent[...] = jnp.broadcast_to(jnp.sum(laid, axis=0, keepdims=True), sent.shape)


def final_kernel(tiles_y, split_ref, frac, inv, ynear, yfar, xnear, xfar, fx, edge_fx, edge_step,
                 al0, al1, be0, be1, got, *rest):
    flux = rest[:FLUXES]
    out, coarse, step_y, step_z, across, held, sems = rest[FLUXES:]
    i, j = lax.axis_index("gx"), lax.axis_index("gy")
    n, own, wide = frac.shape
    ext = own + G
    unknowns = inv.shape[2]
    rows_b, cols_b = split_ref.shape
    per_tile = 2 * rows_b * cols_b
    ghosts = Ghosts(ynear, yfar, n)
    planes = Planes(xnear, xfar, own)
    s8, lane8 = places(wide)

    all_got = got[...]
    owner = lax.broadcasted_iota(jnp.int32, all_got.shape, 0)

    def row_of(tile_row):
        mine = (owner >= tile_row * tiles_y) & (owner < (tile_row + 1) * tiles_y)
        return jnp.sum(jnp.where(mine, all_got, 0.0), axis=0, keepdims=True)

    coarse_res = row_of(i)

    def solve(tile):
        start = pl.multiple_of(jnp.clip(tile, 0, tiles_y - 1) * per_tile, 8)
        block = inv[0, pl.ds(start, per_tile), :]
        e = jnp.sum(block * coarse_res[:, :unknowns], axis=1, keepdims=True)
        return jnp.broadcast_to(e, (per_tile, wide))

    mine, before, after = solve(j), solve(j - 1), solve(j + 1)

    def one_of(e, k):
        return jnp.broadcast_to(e[k : k + 1], (8, wide))

    for q in range(rows_b):
        for r in range(cols_b):
            k = 2 * (q * cols_b + r)
            low, high = one_of(mine, k), one_of(mine, k + 1)
            split = split_ref[q, r]
            coarse[q + 1, group(r), :] = jnp.where(lane8 < split, low, high)
            jump = high - low
            step_z[q, group(r), :] = jnp.where(
                lane8 == split - 1, jump, jnp.where(lane8 == split, -jump, 0.0)
            )
        below = ghosts.lower(q) > 0.5
        k_high, k_low = 2 * q * cols_b, 2 * (q * cols_b + cols_b - 1)
        coarse[q + 1, own:ext, :] = jnp.where(
            s8 == 0,
            jnp.where(below, one_of(after, k_high), one_of(after, k_high + 1)),
            jnp.where(below, one_of(before, k_low), one_of(before, k_low + 1)),
        )
        for r in range(cols_b):
            here = coarse[q + 1, group(r), :]
            ahead = turn_next(coarse[q + 1, group(r + 1), :])
            behind = turn_prev(coarse[q + 1, group(r - 1 if r else cols_b), :])
            step_y[q, group(r), :] = jnp.where(
                s8 == G - 1, ahead - here, jnp.where(s8 == 0, behind - here, 0.0)
            )
    blocks = pl.cdiv(unknowns, wide)
    for side, tile_row in ((0, i - 1), (1, i + 1)):
        other = row_of(tile_row)
        e = jnp.zeros((16, 1), F32)
        for k in range(blocks):
            w = min(wide, unknowns - k * wide)
            part = planes.rows(own + 16 * k, 16, side)[:, :w] * other[:, k * wide : k * wide + w]
            e = e + jnp.sum(part, axis=1, keepdims=True)
        e = jnp.broadcast_to(e, (16, wide))
        below = planes.rows(own + 16 * blocks, 8, side)
        skip = 16 - 2 * cols_b if side == 0 else 0
        at = 0 if side == 0 else rows_b + 1
        for r in range(cols_b):
            k = skip + 2 * r
            coarse[at, group(r), :] = jnp.where(one_of(below, r) > 0.5, one_of(e, k), one_of(e, k + 1))

    for q in range(rows_b + 1):
        x = 8 * q - 1
        for r in range(cols_b):
            here = group(r)
            ex = edge_fx[0, here, :] if q == 0 else edge_fx[1, here, :] if q == rows_b else fx[x, here, :]
            f_before = planes.rows(8 * r, 8, 0) if q == 0 else frac[x, here, :]
            f_after = planes.rows(8 * r, 8, 1) if q == rows_b else frac[x + 1, here, :]
            step = coarse[q + 1, here, :] - coarse[q, here, :]
            across[0, q, here, :] = ex * step
            if q in (0, rows_b):
                step = step + edge_step[0 if q == 0 else 1, here, :]
            across[1, q, here, :] = ex * (0.5 * (f_before + f_after)) * step

    def solved(x, q, beside=None, sign=None):
        for r in range(cols_b):
            here = group(r)
            u, v, wy, sy, wz, sz = (ref[x, here, :] for ref in flux)
            along_y, along_z = step_y[q, here, :], step_z[q, here, :]
            u = u + (wy * along_y + wz * along_z)
            v = v + 0.5 * (sy * along_y + sz * along_z)
            if beside is not None:
                u = sign(u, across[0, beside, here, :])
                v = sign(v, across[1, beside, here, :])
            held[0, x, here, :] = al0[x, here, :] * u - al1[x, here, :] * v
            held[1, x, here, :] = be0[x, here, :] * v - be1[x, here, :] * u

    def copies(q):
        return [
            pltpu.make_async_copy(
                held.at[k, pl.ds(4 * q, 4)], out.at[k, pl.ds(4 * q, 4)], sems.at[k, q]
            )
            for k in range(2)
        ]

    def block(q, carry):
        x = 8 * q
        solved(x, q, q, jnp.subtract)
        for k in range(1, 4):
            solved(x + k, q)
        for copy in copies(2 * q):
            copy.start()
        for k in range(4, 7):
            solved(x + k, q)
        solved(x + 7, q, q + 1, jnp.add)
        for copy in copies(2 * q + 1):
            copy.start()
        return carry

    lax.fori_loop(0, rows_b, block, 0)
    for q in range(2 * rows_b):
        for copy in copies(q):
            copy.wait()


def shards(tiles_x, tiles_y, residual, accum_diag, accum_cross, mask, trans_x, trans_y, trans_z,
           frac_flow, split_layer, coarse_inverse):
    n, own, wide = mask.shape
    ext = own + G
    unknowns = coarse_inverse.shape[2]
    columns = (residual, accum_diag, accum_cross, mask, trans_x, trans_y, trans_z, frac_flow)
    hbm = pl.BlockSpec(memory_space=pltpu.HBM)
    far_columns = [pltpu.with_memory_space_constraint(v, pltpu.HBM) for v in columns]

    def array(*shape):
        return jax.ShapeDtypeStruct(shape, F32)

    y_messages = pl.pallas_call(
        y_message_kernel,
        in_specs=[WHOLE] + [hbm] * 8,
        out_specs=[WHOLE] * 2,
        out_shape=[array(y_message_rows(n), wide)] * 2,
        scratch_shapes=[pltpu.VMEM((*v.shape[:-2], 8, wide), v.dtype) for v in columns] * 2
        + [pltpu.SemaphoreType.DMA((n // 8, 8, 2))],
        compiler_params=params(16),
        name="y_messages",
    )(pltpu.with_memory_space_constraint(split_layer, pltpu.HBM), *far_columns)
    ynear, yfar = swap(y_messages, "gy", tiles_y)

    rhs, own_diag, tot, gain, one, fx, fy, fz, al0, al1, be0, be1 = pl.pallas_call(
        prep_kernel,
        in_specs=[hbm] * 2 + [WHOLE] + [hbm] * 4,
        out_specs=[WHOLE] * 12,
        out_shape=[array(n, own, wide)] * 12,
        scratch_shapes=[pltpu.VMEM(v.shape, v.dtype) for v in columns[:2] + columns[3:7]]
        + [pltpu.SemaphoreType.DMA((6, n // 4))],
        compiler_params=params(16),
        cost_estimate=cost(60_000_000, 30_000_000),
        name="prep",
    )(*far_columns[:2], accum_cross, *far_columns[3:7])
    shared = (rhs, tot, gain, one, fx, fy, fz)

    x_messages = pl.pallas_call(
        x_message_kernel,
        in_specs=[WHOLE] * 10,
        out_specs=[WHOLE] * 2,
        out_shape=[array(PLANES * own + 2 * G, wide)] * 2,
        compiler_params=params(8),
        name="x_messages",
    )(mask, *shared, ynear, yfar)
    xnear, xfar = swap(x_messages, "gx", tiles_x)

    shared = (residual, mask, frac_flow, rhs, own_diag, tot, gain, one, fx, fy, fz, ynear, yfar)
    late_near, late_far, tot3, gain3, one3, six, end, two, acc, *flux = pl.pallas_call(
        interior_kernel,
        in_specs=[SCALARS] + [WHOLE] * 14,
        out_specs=[WHOLE] * (9 + FLUXES),
        out_shape=[array(late_rows(own, unknowns, wide), wide)] * 2
        + [array(n, 3 * G, wide)] * 3
        + [
            array(5, n, G, wide),
            array(n, G, wide),
            array(n, ext, wide),
            array(n // 8, own, wide),
        ]
        + [array(n, own, wide)] * FLUXES,
        scratch_shapes=[pltpu.VMEM((2, own, wide), F32)],
        compiler_params=params(8),
        cost_estimate=cost(60_000_000, 30_000_000),
        name="interior",
    )(split_layer, coarse_inverse, *shared)
    late_near, late_far = swap((late_near, late_far), "gx", tiles_x)

    devices = tiles_x * tiles_y
    span = pl.cdiv(unknowns, 128) * 128
    *flux, sent, edge_fx, edge_step = pl.pallas_call(
        edge_kernel,
        in_specs=[SCALARS] + [WHOLE] * (22 + FLUXES),
        out_specs=[WHOLE] * (3 + FLUXES),
        out_shape=[array(n, own, wide)] * FLUXES
        + [
            array(devices, span),
            array(2, ext, wide),
            array(2, own, wide),
        ],
        scratch_shapes=[
            pltpu.VMEM((4, ext, wide), F32),
            pltpu.VMEM((4, ext, wide), F32),
            pltpu.VMEM((10, ext, wide), F32),
            pltpu.VMEM((2, 10, own, wide), F32),
            pltpu.VMEM((n // 8, own, wide), F32),
        ],
        input_output_aliases={23 + f: f for f in range(FLUXES)},
        compiler_params=params(8),
        name="edges",
    )(split_layer, *shared, xnear, xfar, tot3, gain3, one3, six, end, two, acc, *flux)
    got = lax.all_to_all(sent, ("gx", "gy"), 0, 0, tiled=True)

    return pl.pallas_call(
        functools.partial(final_kernel, tiles_y),
        in_specs=[SCALARS] + [WHOLE] * (14 + FLUXES),
        out_specs=pl.BlockSpec(memory_space=pl.ANY),
        out_shape=array(2, n, own, wide),
        scratch_shapes=[
            pltpu.VMEM((n // 8 + 2, ext, wide), F32),
            pltpu.VMEM((n // 8, own, wide), F32),
            pltpu.VMEM((n // 8, own, wide), F32),
            pltpu.VMEM((2, n // 8 + 1, own, wide), F32),
            pltpu.VMEM((2, n, own, wide), F32),
            pltpu.SemaphoreType.DMA((2, n // 4)),
        ],
        compiler_params=params(12),
        name="final",
    )(split_layer, frac_flow, coarse_inverse, ynear, yfar, late_near, late_far, fx, edge_fx,
      edge_step, al0, al1, be0, be1, got, *flux)


def solution(mesh):
    placed = (
        P(None, "gx", "gy", None),
        P(None, "gx", "gy", None),
        P(None, "gx", "gy", None),
        P("gx", "gy", None),
        P("gx", "gy", None),
        P("gx", "gy", None),
        P("gx", "gy", None),
        P("gx", "gy", None),
        P("gx", "gy"),
        P("gx", None, None),
    )
    return jax.shard_map(
        functools.partial(shards, mesh.shape["gx"], mesh.shape["gy"]),
        mesh=mesh,
        in_specs=placed,
        out_specs=P(None, "gx", "gy", None),
        check_vma=False,
    )
```

```python
import functools

import jax
import jax.numpy as jnp
from jax import lax
from jax.experimental import pallas as pl
from jax.experimental.pallas import tpu as pltpu
from jax.sharding import PartitionSpec as P

relaxation = 2.0 / 3.0
F32 = jnp.float32
WHOLE = pl.BlockSpec(memory_space=pltpu.VMEM)
SCALARS = pl.BlockSpec(memory_space=pltpu.SMEM)
G = 8
PLANES = 6


def params(mib):
    return pltpu.CompilerParams(vmem_limit_bytes=mib << 20)


def cost(flops, size):
    return pl.CostEstimate(flops=flops, bytes_accessed=size, transcendentals=0)


def z_next(v):
    return pltpu.roll(v, v.shape[1] - 1, 1)


def z_prev(v):
    return pltpu.roll(v, 1, 1)


def quasi_impes(active, rp, rs, dpp, dss, dps, dsp):
    weight = dps / dss
    return active * (rp - weight * rs), active * (dpp - weight * dsp) + (1.0 - active)


def swap_pairs(axis, size):
    near = [(i, i ^ 1) for i in range(size) if i ^ 1 < size]
    far = [(i, ((i + 1) ^ 1) - 1) for i in range(size) if 0 <= ((i + 1) ^ 1) - 1 < size]
    return near, far


def swap(message, axis, size):
    near, far = swap_pairs(axis, size)
    return lax.ppermute(message[0], axis, near), lax.ppermute(message[1], axis, far)


def group(k):
    return slice(8 * k, 8 * k + 8)


def turned_next(mine, after, s):
    return jnp.where(s == G - 1, after, mine)


def turned_prev(mine, before, s):
    return jnp.where(s == 0, before, mine)


def turn_next(v):
    return pltpu.roll(v, G - 1, 0)


def turn_prev(v):
    return pltpu.roll(v, 1, 0)


def places(wide):
    shape = (G, wide)
    return lax.broadcasted_iota(jnp.int32, shape, 0), lax.broadcasted_iota(jnp.int32, shape, 1)


def along_z(tz, a, lane):
    return jnp.where(lane < a.shape[1] - 1, tz * a * z_next(a), 0.0)


Y_TURNS = {
    "c": (6, 2),
    "a": (4, 4),
    "tx": (3, 5),
    "e": (3, 6),
    "tz": (1, 7),
}
Y_PLACES = {
    "c": ((4, 5), (2, 3)),
    "a": ((3,), (4,)),
    "tx": ((2,), (5,)),
    "e": ((1,), (6,)),
    "tz": ((0,), (7,)),
}


def y_message_kernel(split_ref, *refs):
    low, high, (near_ref, far_ref) = refs[:8], refs[8:16], refs[16:]
    n, _, wide = low[3].shape
    even = lax.rem(lax.axis_index("gy"), 2) == 0
    step = pl.program_id(0)
    x0 = pl.multiple_of(8 * step, 8)
    shape = (8, G, wide)
    row, s, lane = (lax.broadcasted_iota(jnp.int32, shape, k) for k in range(3))

    def turn(v, k):
        return jnp.stack([pltpu.roll(v[i], k, 0) for i in range(v.shape[0])])

    def fields(group, side):
        res, diag, crs, mask, tx, ty, tz, ff = group
        before, after = jnp.maximum(x0 - 1, 0), jnp.minimum(x0 + 8, n - 1)
        a, trans = mask[pl.ds(x0, 8)].astype(F32), tx[pl.ds(x0, 8)]
        t = trans * a
        a_after = jnp.concatenate([a[1:], mask[pl.ds(after, 1)].astype(F32)], axis=0)
        t_before = jnp.concatenate([tx[pl.ds(before, 1)] * mask[pl.ds(before, 1)].astype(F32), t[:7]], axis=0)
        b, c = quasi_impes(a, res[0], res[1], diag[0], diag[1], crs[0], crs[1])
        ty_a = ty[...] * a
        ey = ty_a * turn(a, G - 1)
        a_above = jnp.stack([z_next(a[i]) for i in range(8)])
        ez = jnp.where(lane < wide - 1, tz[...] * a * a_above, 0.0)
        more = ez + jnp.stack([z_prev(ez[i]) for i in range(8)])
        more = more + jnp.where(row + x0 == n - 1, 0.0, t * a_after)
        more = more + jnp.where(row + x0 == 0, 0.0, t_before * a)
        more = more + (ey if side else turn(ey, 1))
        c = jnp.where(s == (1 if side else 6), c + more, c)
        tile = b
        for name, v in (("c", c), ("a", a), ("tx", trans), ("e", ey), ("tz", tz[...])):
            moved = turn(v, Y_TURNS[name][side])
            for place in Y_PLACES[name][side]:
                tile = jnp.where(s == place, moved, tile)
        outer = slice(0, 1) if side else slice(7, 8)
        return tile, ty_a[:, outer], ff[:, outer, :]

    def put(rows, up, down):
        near_ref[rows, :] = jnp.where(even, up, down)
        far_ref[rows, :] = jnp.where(even, down, up)

    up, down = fields(high, 0), fields(low, 1)
    for k in range(8):
        put(pl.ds(pl.multiple_of(8 * (x0 + k), 8), 8), up[0][k], down[0][k])
        put(pl.ds(8 * n + x0 + k, 1), up[1][k], down[1][k])
        put(pl.ds(9 * n + x0 + k, 1), up[2][k], down[2][k])

    @pl.when(step == 0)
    def _():
        put(slice(10 * n, y_message_rows(n)), *[jnp.zeros((y_message_rows(n) - 10 * n, wide), F32)] * 2)
        first_lane = lax.broadcasted_iota(jnp.int32, (1, wide), 1)
        for q in range(n // 8):
            splits = split_ref[q : q + 1, :]
            above = (first_lane < splits[:, -1:]).astype(F32)
            below = (first_lane < splits[:, :1]).astype(F32)
            put(slice(10 * n + 2 + q, 10 * n + 3 + q), above, below)
        corners = [
            (tx[n - 1, at, :] * mask[n - 1, at, :].astype(F32), mask[0, at, :].astype(F32))
            for mask, tx, at in ((high[3], high[4], slice(6, 7)), (low[3], low[4], slice(1, 2)))
        ]
        for k in range(2):
            put(slice(10 * n + k, 10 * n + k + 1), corners[0][k], corners[1][k])


def y_message_rows(n):
    return 10 * n + pl.cdiv(2 + n // 8, 8) * 8


class Ghosts:
    def __init__(self, near_ref, far_ref, n):
        self.refs, self.n = (near_ref, far_ref), n
        self.even = lax.rem(lax.axis_index("gy"), 2) == 0
        self.s, _ = places(near_ref.shape[1])

    def both(self, rows):
        near, far = (ref[rows, :] for ref in self.refs)
        return jnp.where(self.even, far, near), jnp.where(self.even, near, far)

    def tiles(self, x):
        return self.both(pl.ds(pl.multiple_of(8 * x, 8), 8))

    def pick(self, tiles, name, low_at=(G - 1,), high_at=(0,)):
        low, high = tiles
        if name != "b":
            up, down = Y_TURNS[name]
            low, high = pltpu.roll(low, 8 - up, 0), pltpu.roll(high, 8 - down, 0)
        picked = jnp.zeros_like(low)
        for place in low_at:
            picked = jnp.where(self.s == place, low, picked)
        for place in high_at:
            picked = jnp.where(self.s == place, high, picked)
        return picked

    def row(self, at, low_at=G - 1, high_at=0):
        low, high = self.both(pl.ds(at, 1))
        return jnp.where(self.s == low_at, low, jnp.where(self.s == high_at, high, 0.0))

    def active(self, x):
        return self.pick(self.tiles(x), "a")

    def first_active(self):
        return self.active(0) + self.row(10 * self.n + 1, G - 2, 1)

    def last_trans(self):
        return self.row(10 * self.n, G - 2, 1)

    def frac(self, x):
        return self.row(9 * self.n + x)

    def lower(self, q):
        return self.row(10 * self.n + 2 + q)


def prep_kernel(res_hbm, diag_hbm, crs, mask_hbm, tx_hbm, ty_hbm, tz_hbm,
                rhs, own_diag, tot, gain, one, fx, fy, fz, al0, al1, be0, be1,
                res, diag, mask, tx, ty, tz, sems):
    n, own, wide = mask.shape
    groups = own // 8
    chunk = 4
    s, lane = places(wide)

    def copies(q):
        at = pl.ds(chunk * q, chunk)
        pairs = (
            (res_hbm.at[:, at], res.at[:, at]),
            (diag_hbm.at[:, at], diag.at[:, at]),
            (tx_hbm.at[at], tx.at[at]),
            (ty_hbm.at[at], ty.at[at]),
            (tz_hbm.at[at], tz.at[at]),
        )
        return [pltpu.make_async_copy(a, b, sems.at[k + 1, q]) for k, (a, b) in enumerate(pairs)]

    def masks(q):
        at = pl.ds(chunk * q, chunk)
        return pltpu.make_async_copy(mask_hbm.at[at], mask.at[at], sems.at[0, q])

    for q in range(n // chunk):
        for copy in (masks(q), *copies(q)):
            copy.start()
    masks(0).wait()

    def row(x, carry):
        first, last = x == 0, x == n - 1
        after = jnp.minimum(x + 1, n - 1)
        before = jnp.maximum(x - 1, 0)
        a_after = mask[x, group(0), :].astype(F32)
        turned_after = turn_next(a_after)
        ey_before = jnp.zeros((G, wide), F32)
        for k in range(groups):
            here = group(k)
            a, turned = a_after, turned_after
            rp, rs = res[0, x, here, :], res[1, x, here, :]
            dpp, dss = diag[0, x, here, :], diag[1, x, here, :]
            dps, dsp = crs[0, x, here, :], crs[1, x, here, :]
            det = dpp * dss - dps * dsp
            both = 1.0 / (dss * det)
            inverse = both * dss
            weight = dps * (both * det)
            b = a * (rp - weight * rs)
            c = a * (dpp - weight * dsp) + (1.0 - a)
            rhs[x, here, :] = b
            own_diag[x, here, :] = c
            al0[x, here, :] = dss * inverse
            al1[x, here, :] = dps * inverse
            be0[x, here, :] = dpp * inverse
            be1[x, here, :] = dsp * inverse
            t = tx[x, here, :] * a
            ex = t * mask[after, here, :].astype(F32)
            fx[x, here, :] = jnp.where(last, t, ex)
            total = c + jnp.where(last, 0.0, ex)
            total = total + jnp.where(first, 0.0, fx[before, here, :])
            ez = along_z(tz[x, here, :], a, lane)
            fz[x, here, :] = ez
            total = total + ez + z_prev(ez)
            ey = ty[x, here, :] * a
            if k < groups - 1:
                a_after = mask[x, group(k + 1), :].astype(F32)
                turned_after = turn_next(a_after)
                ey = ey * turned_next(turned, turned_after, s)
                inside = ey
            else:
                ey = jnp.where(s == G - 1, ey, ey * turned)
                inside = jnp.where(s == G - 1, 0.0, ey)
            fy[x, here, :] = ey
            ey_turned = turn_prev(inside)
            total = total + inside + turned_prev(ey_turned, ey_before, s)
            ey_before = ey_turned
            tot[x, here, :] = total
            if 0 < k < groups - 1:
                g = relaxation / total
                gain[x, here, :] = g
                one[x, here, :] = g * b
        return carry

    def part(q, carry):
        @pl.when(q < n // chunk - 1)
        def _():
            masks(q + 1).wait()

        for copy in copies(q):
            copy.wait()
        return lax.fori_loop(0, chunk, lambda k, v: row(chunk * q + k, v), carry, unroll=2)

    lax.fori_loop(0, n // chunk, part, 0)


class Finished:
    def __init__(self, x, n, ghosts, mask, rhs, tot, fx, fy, s, lane):
        groups = mask.shape[1] // 8
        first, last = x == 0, x == n - 1
        tiles = ghosts.tiles(x)
        ga, gtx, gtz = (ghosts.pick(tiles, name) for name in ("a", "tx", "tz"))
        gb = ghosts.pick(tiles, "b", (G - 1, G - 2), (0, 1))
        gc = jnp.maximum(ghosts.pick(tiles, "c", (G - 1, G - 2), (0, 1)), 1.0)
        before, after = jnp.maximum(x - 1, 0), jnp.minimum(x + 1, n - 1)
        tiles_before = ghosts.tiles(before)
        a_before, tx_before = ghosts.pick(tiles_before, "a"), ghosts.pick(tiles_before, "tx")
        a_after = ghosts.active(after)
        end = fy[x, group(groups - 1), :]
        end = jnp.where(s == G - 1, end * turn_next(ga), end)
        a_first = turn_next(mask[x, group(0), :].astype(F32))
        ey = ghosts.pick(tiles, "e", (G - 2,), (0,))
        ey = jnp.where(s == G - 1, ghosts.row(8 * n + x) * a_first, ey)
        ey_turned = turn_prev(ey)
        ez = along_z(gtz, ga, lane)
        t = gtx * ga
        ex = t * a_after
        total = gc + ez + z_prev(ez) + ey + turned_prev(ey_turned, turn_prev(end), s)
        total = total + jnp.where(last, 0.0, ex) + jnp.where(first, 0.0, tx_before * a_before * ga)
        self.end = end
        self.fx, self.fy, self.fz = jnp.where(last, t + ghosts.last_trans(), ex), ey, ez
        self.rhs = gb
        self.total = (
            tot[x, group(0), :] + jnp.where(s == 0, ey_turned, 0.0),
            tot[x, group(groups - 1), :] + jnp.where(s == G - 1, end, 0.0),
            total,
        )
        self.all_rhs = (rhs[x, group(0), :], rhs[x, group(groups - 1), :], gb)


def slot_of(k, groups):
    return {0: 0, groups - 1: 1, groups: 2}[k]


def x_message_kernel(mask, rhs, tot, gain, one, fx, fy, fz, ynear, yfar, near_ref, far_ref):
    even = lax.rem(lax.axis_index("gx"), 2) == 0
    n, own, wide = mask.shape
    groups = own // 8
    s, lane = places(wide)
    ghosts = Ghosts(ynear, yfar, n)
    finished = {x: Finished(x, n, ghosts, mask, rhs, tot, fx, fy, s, lane) for x in (0, 1, n - 2, n - 1)}
    for k in range(groups + 1):
        here = group(k)
        touched = k in (0, groups - 1, groups)

        def first_of(x):
            done = finished[x]
            if not touched:
                return one[x, here, :]
            slot = slot_of(k, groups)
            return relaxation * done.all_rhs[slot] / done.total[slot]

        def of(x, key):
            done = finished[x]
            total = done.total[slot_of(k, groups)] if touched else tot[x, here, :]
            if k == groups:
                return done.rhs, total, key, done.fy
            return rhs[x, here, :], total, key, done.end if k == groups - 1 else fy[x, here, :]

        if k == groups:
            up = of(n - 1, finished[n - 1].fx)
            down = of(0, ghosts.first_active())
        else:
            up = of(n - 1, fx[n - 1, here, :])
            down = of(0, mask[0, here, :].astype(F32))
            up += (fz[n - 1, here, :], fx[n - 2, here, :] * first_of(n - 2))
            down += (fz[0, here, :], fx[0, here, :] * first_of(1))
        if k == groups:
            b, total, key, ey = (jnp.where(even, p, q) for p, q in zip(up, down, strict=True))
            ob, ototal, okey, oey = (jnp.where(even, q, p) for p, q in zip(up, down, strict=True))
            for ref, (b, total, key, ey) in (
                (near_ref, (b, total, key, ey)),
                (far_ref, (ob, ototal, okey, oey)),
            ):
                at = PLANES * own
                ref[at : at + G, :] = jnp.where((s == 0) | (s == G - 1), b, pltpu.roll(total, 4, 0))
                ref[at + G : at + 2 * G, :] = jnp.where((s < 2) | (s >= G - 2), key, pltpu.roll(ey, 4, 0))
        else:
            for f in range(PLANES):
                start = f * own + 8 * k
                near_ref[start : start + 8, :] = jnp.where(even, up[f], down[f])
                far_ref[start : start + 8, :] = jnp.where(even, down[f], up[f])


def late_messages(split_ref, ff, inv, near_ref, far_ref):
    even = lax.rem(lax.axis_index("gx"), 2) == 0
    j = lax.axis_index("gy")
    n, own, wide = ff.shape
    per_tile = 2 * split_ref.shape[0] * split_ref.shape[1]
    near_ref[0:own, :] = jnp.where(even, ff[n - 1], ff[0])
    far_ref[0:own, :] = jnp.where(even, ff[0], ff[n - 1])
    at = own
    unknowns = inv.shape[2]
    top = inv[0, pl.ds(pl.multiple_of(j * per_tile + per_tile - 16, 8), 16), :]
    bottom = inv[0, pl.ds(pl.multiple_of(j * per_tile, 8), 16), :]
    for k in range(0, unknowns, wide):
        w = min(wide, unknowns - k)
        if w < wide:
            near_ref[at : at + 16, :] = jnp.zeros((16, wide), F32)
            far_ref[at : at + 16, :] = jnp.zeros((16, wide), F32)
        near_ref[at : at + 16, :w] = jnp.where(even, top[:, k : k + w], bottom[:, k : k + w])
        far_ref[at : at + 16, :w] = jnp.where(even, bottom[:, k : k + w], top[:, k : k + w])
        at += 16
    lane = lax.broadcasted_iota(jnp.int32, (1, wide), 1)
    zero = jnp.zeros((8, wide), F32)
    near_ref[at : at + 8, :] = zero
    far_ref[at : at + 8, :] = zero
    for q in range(split_ref.shape[1]):
        top = (lane < split_ref[split_ref.shape[0] - 1, q]).astype(F32)
        bottom = (lane < split_ref[0, q]).astype(F32)
        near_ref[at + q : at + q + 1, :] = jnp.where(even, top, bottom)
        far_ref[at + q : at + q + 1, :] = jnp.where(even, bottom, top)


def late_rows(own, unknowns, wide):
    return own + 16 * pl.cdiv(unknowns, wide) + 8


class Planes:
    def __init__(self, near_ref, far_ref, own):
        self.refs, self.own = (near_ref, far_ref), own
        self.even = lax.rem(lax.axis_index("gx"), 2) == 0

    def rows(self, at, n, side):
        near, far = (ref[at : at + n, :] for ref in self.refs)
        return jnp.where(self.even, near, far) if side else jnp.where(self.even, far, near)

    def field(self, f, k, side):
        if 8 * k < self.own:
            return self.rows(f * self.own + 8 * k, 8, side)
        s, _ = places(self.refs[0].shape[1])
        ends = (s == 0) | (s == G - 1)
        if f < 2:
            tile = self.rows(PLANES * self.own, G, side)
            return jnp.where(ends, pltpu.roll(tile, 4, 0) if f else tile, 0.0)
        if f < 4:
            tile = self.rows(PLANES * self.own + G, G, side)
            if f == 2:
                return jnp.where((s < 2) | (s >= G - 2), tile, 0.0)
            return jnp.where(s == G - 1, pltpu.roll(tile, 4, 0), 0.0)
        return jnp.zeros_like(s, F32)


class Inside:
    def __init__(self, groups, ff, rhs, gain, one, fx, fy, fz, gain3, one3, six, end):
        self.groups, self.own_ff, self.own_rhs = groups, ff, rhs
        self.own_gain, self.own_one, self.own_fx, self.own_fy, self.own_fz = gain, one, fx, fy, fz
        self.gain3, self.one3, self.six, self.end = gain3, one3, six, end

    def pick(self, own, which, x, k):
        return self.six[which, x] if k == self.groups else own[x, group(k), :]

    def three(self, own, other, x, k):
        if 0 < k < self.groups - 1:
            return own[x, group(k), :]
        return other[x, group(slot_of(k, self.groups)), :]

    def rhs(self, x, k):
        return self.pick(self.own_rhs, 0, x, k)

    def fx(self, x, k):
        return self.pick(self.own_fx, 1, x, k)

    def fy(self, x, k):
        if k == self.groups - 1:
            return self.end[x]
        return self.pick(self.own_fy, 2, x, k)

    def fz(self, x, k):
        return self.pick(self.own_fz, 3, x, k)

    def ff(self, x, k):
        return self.pick(self.own_ff, 4, x, k)

    def gain(self, x, k):
        return self.three(self.own_gain, self.gain3, x, k)

    def one(self, x, k):
        return self.three(self.own_one, self.one3, x, k)

    def before(self, x, k):
        return self.fx(x - 1, k) * self.one(x - 1, k)

    def after(self, x, k):
        return self.fx(x, k) * self.one(x + 1, k)

    def faces_x(self, x, k):
        ex = self.fx(x, k)
        return ex, ex * (self.ff(x, k) + self.ff(x + 1, k))


def second_row(o, x, s, put):
    total = o.groups + 1
    p = o.one(x, 0)
    p_turned = turn_next(p)
    w_turned = turn_prev(o.fy(x, total - 1) * o.one(x, total - 1))
    for k in range(total):
        p_after = o.one(x, (k + 1) % total)
        after_turned = turn_next(p_after)
        ey, ez = o.fy(x, k), o.fz(x, k)
        mine = turn_prev(ey * p)
        beside = ey * turned_next(p_turned, after_turned, s) + turned_prev(mine, w_turned, s)
        beside = beside + ez * z_next(p) + z_prev(ez * p)
        beside = beside + o.after(x, k) + o.before(x, k)
        put(k, o.gain(x, k) * ((2.0 - relaxation) * o.rhs(x, k) + beside))
        p, p_turned, w_turned = p_after, after_turned, mine


def x_flux(o, x, k, two):
    step = two(x + 1, k) - two(x, k)
    ex, wx = o.faces_x(x, k)
    return ex * step, wx * step


def flux_row(o, x, s, lane, two, res, own_diag, split, carried, put):
    groups = o.groups

    def faces_y(k, p, p_turned, p_after, f, f_turned, f_after):
        ey = o.fy(x, k)
        weighted = ey * (f + turned_next(f_turned, f_after, s))
        return ey, weighted, turned_next(p_turned, p_after, s) - p

    p0, f0 = two(x, 0), o.ff(x, 0)
    p0_turned, f0_turned = turn_next(p0), turn_next(f0)
    p, f = two(x, groups), o.ff(x, groups)
    ghost = faces_y(groups, p, turn_next(p), p0_turned, f, turn_next(f), f0_turned)
    turned = [turn_prev(v) for v in ghost]
    p, f, p_turned, f_turned = p0, f0, p0_turned, f0_turned
    for k in range(groups):
        here = group(k)
        p_after, f_after = two(x, k + 1), o.ff(x, k + 1)
        p_after_turned, f_after_turned = turn_next(p_after), turn_next(f_after)
        mine = faces_y(k, p, p_turned, p_after_turned, f, f_turned, f_after_turned)
        mine_turned = [turn_prev(v) for v in mine]
        ey, wy, dy = mine
        ey_before, wy_before, dy_before = (
            turned_prev(a, b, s) for a, b in zip(mine_turned, turned, strict=True)
        )
        ez = o.fz(x, k)
        wz = ez * (f + z_next(f))
        dz = z_next(p) - p
        ez_before, wz_before, dz_before = z_prev(ez), z_prev(wz), z_prev(dz)
        qx, sx = x_flux(o, x, k, two)
        if carried is None:
            qx_before, sx_before = x_flux(o, x - 1, k, two)
        else:
            qx_before, sx_before = carried[0, here, :], carried[1, here, :]
            carried[0, here, :] = qx
            carried[1, here, :] = sx
        gained = (qx - qx_before) + (ey * dy - ey_before * dy_before)
        gained = gained + (ez * dz - ez_before * dz_before)
        weighed = (sx - sx_before) + (wy * dy - wy_before * dy_before)
        weighed = weighed + (wz * dz - wz_before * dz_before)
        rest = o.rhs(x, k) - own_diag[x, here, :] * p + gained
        below = lane < split(k)
        put(
            k,
            rest,
            res[0, x, here, :] + gained,
            res[1, x, here, :] + 0.5 * weighed,
            jnp.where(s == 0, ey_before, ey),
            jnp.where(s == 0, wy_before, wy),
            jnp.where(below, ez, ez_before),
            jnp.where(below, wz, wz_before),
        )
        turned = mine_turned
        p, f, p_turned, f_turned = p_after, f_after, p_after_turned, f_after_turned


FLUXES = 6


def interior_kernel(split_ref, inv, res, mask, ff, rhs, own_diag, tot, gain, one, fx, fy, fz, ynear, yfar,
                    late_near, late_far, tot3, gain3, one3, six, end, two, acc, *flux_and_carried):
    flux, carried = flux_and_carried[:FLUXES], flux_and_carried[FLUXES]
    late_messages(split_ref, ff, inv, late_near, late_far)
    n, own, wide = mask.shape
    groups = own // 8
    s, lane = places(wide)
    ghosts = Ghosts(ynear, yfar, n)

    def finish(x, carry):
        done = Finished(x, n, ghosts, mask, rhs, tot, fx, fy, s, lane)
        for slot in range(3):
            g = relaxation / done.total[slot]
            tot3[x, group(slot), :] = done.total[slot]
            gain3[x, group(slot), :] = g
            one3[x, group(slot), :] = g * done.all_rhs[slot]
        end[x] = done.end
        for k, v in enumerate((done.rhs, done.fx, done.fy, done.fz, ghosts.frac(x))):
            six[k, x] = v
        return carry

    lax.fori_loop(0, n, finish, 0, unroll=8)
    o = Inside(groups, ff, rhs, gain, one, fx, fy, fz, gain3, one3, six, end)

    def second(x, carry):
        def put(k, v):
            two[x, group(k), :] = v

        second_row(o, x, s, put)
        return carry

    lax.fori_loop(2, n - 2, second, 0, unroll=4)

    def two_of(x, k):
        return two[x, group(k), :]

    for k in range(groups):
        carried[0, group(k), :], carried[1, group(k), :] = x_flux(o, 2, k, two_of)
    acc[...] = jnp.zeros_like(acc)

    def row(x, carry):
        def put(k, rest, *values):
            acc[x // 8, group(k), :] += rest
            for f, v in enumerate(values):
                flux[f][x, group(k), :] = v

        flux_row(o, x, s, lane, two_of, res, own_diag, lambda k: split_ref[x // 8, k], carried, put)
        return carry

    lax.fori_loop(3, n - 3, row, 0, unroll=2)


class Edges(Inside):
    def beyond(self, n, planes, act, tot, tot3, one_edge, gain_edge, edge_fx):
        self.n, self.planes = n, planes
        self.slots = {-1: 0, 0: 1, n - 1: 2, n: 3}
        self.one_edge, self.gain_edge, self.edge_fx = one_edge, gain_edge, edge_fx
        self.far = {-1: 0, n: 1}
        for k in range(self.groups + 1):
            here = group(k)
            low = planes.field(2, k, 0) * act(k)
            high = super().fx(n - 1, k) * planes.field(2, k, 1)
            edge_fx[0, here, :] = low
            edge_fx[1, here, :] = high
            for x, slot in self.slots.items():
                face = low if x <= 0 else high
                if x in self.far:
                    total = jnp.maximum(planes.field(1, k, self.far[x]), 1.0) + face
                else:
                    total = self.three(tot, tot3, x, k) + face
                g = relaxation / total
                gain_edge[slot, here, :] = g
                one_edge[slot, here, :] = g * self.rhs(x, k)

    def rhs(self, x, k):
        return self.planes.field(0, k, self.far[x]) if x in self.far else super().rhs(x, k)

    def fx(self, x, k):
        if x in (-1, self.n - 1):
            return self.edge_fx[0 if x == -1 else 1, group(k), :]
        return super().fx(x, k)

    def fy(self, x, k):
        return self.planes.field(3, k, self.far[x]) if x in self.far else super().fy(x, k)

    def fz(self, x, k):
        return self.planes.field(4, k, self.far[x]) if x in self.far else super().fz(x, k)

    def gain(self, x, k):
        return self.gain_edge[self.slots[x], group(k), :] if x in self.slots else super().gain(x, k)

    def one(self, x, k):
        return self.one_edge[self.slots[x], group(k), :] if x in self.slots else super().one(x, k)

    def before(self, x, k):
        return self.planes.field(5, k, 0) if x == -1 else super().before(x, k)

    def after(self, x, k):
        return self.planes.field(5, k, 1) if x == self.n else super().after(x, k)


def edge_kernel(split_ref, res, mask, ff, rhs, own_diag, tot, gain, one, fx, fy, fz, ynear, yfar, xnear, xfar,
                tot3, gain3, one3, six, end, two, acc, *others):
    flux = others[FLUXES : 2 * FLUXES]
    sent, edge_fx, edge_step, one_edge, gain_edge, two_edge, near_fx, total_acc = others[2 * FLUXES :]
    n, own, wide = mask.shape
    groups = own // 8
    s, lane = places(wide)
    planes = Planes(xnear, xfar, own)
    ghosts = Ghosts(ynear, yfar, n)
    o = Edges(groups, ff, rhs, gain, one, fx, fy, fz, gain3, one3, six, end)

    def act(k):
        return ghosts.first_active() if k == groups else mask[0, group(k), :].astype(F32)

    o.beyond(n, planes, act, tot, tot3, one_edge, gain_edge, edge_fx)
    depth = 5
    bases = (-1, n - depth + 1)
    for side, base in enumerate(bases):
        for r in range(depth):
            x, slot = base + r, depth * side + r
            if x in (-1, 0, 1, n - 2, n - 1, n):

                def put_two(k, v, slot=slot):
                    two_edge[slot, group(k), :] = v

                second_row(o, x, s, put_two)
            else:
                two_edge[slot] = two[x]
            if x == n:
                continue
            for k in range(groups):
                ex = o.fx(x, k)
                near_fx[0, slot, group(k), :] = ex
                if x in (-1, n - 1):
                    near_fx[1, slot, group(k), :] = jnp.zeros_like(ex)
                else:
                    near_fx[1, slot, group(k), :] = ex * (o.ff(x, k) + o.ff(x + 1, k))
    for k in range(groups):
        edge_step[0, group(k), :] = two_edge[1, group(k), :] - two_edge[0, group(k), :]
        edge_step[1, group(k), :] = two_edge[2 * depth - 1, group(k), :] - two_edge[2 * depth - 2, group(k), :]
    total_acc[...] = acc[...]
    plain = Inside(groups, ff, rhs, gain, one, fx, fy, fz, gain3, one3, six, end)

    def row(r, carry):
        high = r >= depth - 2
        x = jnp.where(high, n - 2 * (depth - 2) + r, r)
        shift = jnp.where(high, depth - bases[1], -bases[0])

        def two_of(x, k):
            return two_edge[x + shift, group(k), :]

        def faces_x(x, k):
            return near_fx[0, x + shift, group(k), :], near_fx[1, x + shift, group(k), :]

        plain.faces_x = faces_x

        def put(k, rest, *values):
            total_acc[x // 8, group(k), :] += rest
            for f, v in enumerate(values):
                flux[f][x, group(k), :] = v

        flux_row(plain, x, s, lane, two_of, res, own_diag, lambda k: split_ref[x // 8, k], None, put)
        return carry

    lax.fori_loop(0, 2 * (depth - 2), row, 0, unroll=2)

    rows_b, cols_b = split_ref.shape
    lane = lax.broadcasted_iota(jnp.int32, (1, wide), 1)
    lower, upper = [], []
    for q in range(rows_b):
        for r in range(cols_b):
            column = jnp.sum(total_acc[q, group(r), :], axis=0, keepdims=True)
            below = lane < split_ref[q, r]
            lower.append(jnp.where(below, column, 0.0))
            upper.append(jnp.where(below, 0.0, column))
    count = rows_b * cols_b
    low_sum = jnp.sum(jnp.concatenate(lower, axis=0), axis=1, keepdims=True)
    high_sum = jnp.sum(jnp.concatenate(upper, axis=0), axis=1, keepdims=True)
    span = sent.shape[1]
    place = lax.broadcasted_iota(jnp.int32, (count, span), 1) - 2 * count * lax.axis_index("gy")
    which = 2 * lax.broadcasted_iota(jnp.int32, (count, span), 0)
    laid = jnp.where(place == which, low_sum, jnp.where(place == which + 1, high_sum, 0.0))
    sent[...] = jnp.broadcast_to(jnp.sum(laid, axis=0, keepdims=True), sent.shape)


def final_kernel(tiles_y, split_ref, frac, inv, ynear, yfar, xnear, xfar, fx, edge_fx, edge_step,
                 al0, al1, be0, be1, got, *rest):
    flux = rest[:FLUXES]
    out, coarse, step_y, step_z, across, held, sems = rest[FLUXES:]
    i, j = lax.axis_index("gx"), lax.axis_index("gy")
    n, own, wide = frac.shape
    ext = own + G
    unknowns = inv.shape[2]
    rows_b, cols_b = split_ref.shape
    per_tile = 2 * rows_b * cols_b
    ghosts = Ghosts(ynear, yfar, n)
    planes = Planes(xnear, xfar, own)
    s8, lane8 = places(wide)

    all_got = got[...]
    owner = lax.broadcasted_iota(jnp.int32, all_got.shape, 0)

    def row_of(tile_row):
        mine = (owner >= tile_row * tiles_y) & (owner < (tile_row + 1) * tiles_y)
        return jnp.sum(jnp.where(mine, all_got, 0.0), axis=0, keepdims=True)

    coarse_res = row_of(i)

    def solve(tile):
        start = pl.multiple_of(jnp.clip(tile, 0, tiles_y - 1) * per_tile, 8)
        block = inv[0, pl.ds(start, per_tile), :]
        e = jnp.sum(block * coarse_res[:, :unknowns], axis=1, keepdims=True)
        return jnp.broadcast_to(e, (per_tile, wide))

    mine, before, after = solve(j), solve(j - 1), solve(j + 1)

    def one_of(e, k):
        return jnp.broadcast_to(e[k : k + 1], (8, wide))

    for q in range(rows_b):
        for r in range(cols_b):
            k = 2 * (q * cols_b + r)
            low, high = one_of(mine, k), one_of(mine, k + 1)
            split = split_ref[q, r]
            coarse[q + 1, group(r), :] = jnp.where(lane8 < split, low, high)
            jump = high - low
            step_z[q, group(r), :] = jnp.where(
                lane8 == split - 1, jump, jnp.where(lane8 == split, -jump, 0.0)
            )
        below = ghosts.lower(q) > 0.5
        k_high, k_low = 2 * q * cols_b, 2 * (q * cols_b + cols_b - 1)
        coarse[q + 1, own:ext, :] = jnp.where(
            s8 == 0,
            jnp.where(below, one_of(after, k_high), one_of(after, k_high + 1)),
            jnp.where(below, one_of(before, k_low), one_of(before, k_low + 1)),
        )
        for r in range(cols_b):
            here = coarse[q + 1, group(r), :]
            ahead = turn_next(coarse[q + 1, group(r + 1), :])
            behind = turn_prev(coarse[q + 1, group(r - 1 if r else cols_b), :])
            step_y[q, group(r), :] = jnp.where(
                s8 == G - 1, ahead - here, jnp.where(s8 == 0, behind - here, 0.0)
            )
    blocks = pl.cdiv(unknowns, wide)
    for side, tile_row in ((0, i - 1), (1, i + 1)):
        other = row_of(tile_row)
        e = jnp.zeros((16, 1), F32)
        for k in range(blocks):
            w = min(wide, unknowns - k * wide)
            part = planes.rows(own + 16 * k, 16, side)[:, :w] * other[:, k * wide : k * wide + w]
            e = e + jnp.sum(part, axis=1, keepdims=True)
        e = jnp.broadcast_to(e, (16, wide))
        below = planes.rows(own + 16 * blocks, 8, side)
        skip = 16 - 2 * cols_b if side == 0 else 0
        at = 0 if side == 0 else rows_b + 1
        for r in range(cols_b):
            k = skip + 2 * r
            coarse[at, group(r), :] = jnp.where(one_of(below, r) > 0.5, one_of(e, k), one_of(e, k + 1))

    for q in range(rows_b + 1):
        x = 8 * q - 1
        for r in range(cols_b):
            here = group(r)
            ex = edge_fx[0, here, :] if q == 0 else edge_fx[1, here, :] if q == rows_b else fx[x, here, :]
            f_before = planes.rows(8 * r, 8, 0) if q == 0 else frac[x, here, :]
            f_after = planes.rows(8 * r, 8, 1) if q == rows_b else frac[x + 1, here, :]
            step = coarse[q + 1, here, :] - coarse[q, here, :]
            across[0, q, here, :] = ex * step
            if q in (0, rows_b):
                step = step + edge_step[0 if q == 0 else 1, here, :]
            across[1, q, here, :] = ex * (0.5 * (f_before + f_after)) * step

    def solved(x, q, beside=None, sign=None):
        for r in range(cols_b):
            here = group(r)
            u, v, wy, sy, wz, sz = (ref[x, here, :] for ref in flux)
            along_y, along_z = step_y[q, here, :], step_z[q, here, :]
            u = u + (wy * along_y + wz * along_z)
            v = v + 0.5 * (sy * along_y + sz * along_z)
            if beside is not None:
                u = sign(u, across[0, beside, here, :])
                v = sign(v, across[1, beside, here, :])
            held[0, x, here, :] = al0[x, here, :] * u - al1[x, here, :] * v
            held[1, x, here, :] = be0[x, here, :] * v - be1[x, here, :] * u

    def copies(q):
        return [
            pltpu.make_async_copy(
                held.at[k, pl.ds(4 * q, 4)], out.at[k, pl.ds(4 * q, 4)], sems.at[k, q]
            )
            for k in range(2)
        ]

    def block(q, carry):
        x = 8 * q
        solved(x, q, q, jnp.subtract)
        for k in range(1, 4):
            solved(x + k, q)
        for copy in copies(2 * q):
            copy.start()
        for k in range(4, 7):
            solved(x + k, q)
        solved(x + 7, q, q + 1, jnp.add)
        for copy in copies(2 * q + 1):
            copy.start()
        return carry

    lax.fori_loop(0, rows_b, block, 0)
    for q in range(2 * rows_b):
        for copy in copies(q):
            copy.wait()


def shards(tiles_x, tiles_y, residual, accum_diag, accum_cross, mask, trans_x, trans_y, trans_z,
           frac_flow, split_layer, coarse_inverse):
    n, own, wide = mask.shape
    ext = own + G
    unknowns = coarse_inverse.shape[2]
    columns = (residual, accum_diag, accum_cross, mask, trans_x, trans_y, trans_z, frac_flow)
    hbm = pl.BlockSpec(memory_space=pltpu.HBM)
    far_columns = [pltpu.with_memory_space_constraint(v, pltpu.HBM) for v in columns]

    def array(*shape):
        return jax.ShapeDtypeStruct(shape, F32)

    def group_spec(k, f):
        if f in (3, 4):
            return pl.BlockSpec((n, G, wide), lambda x: (0, k, 0))
        lead = columns[f].shape[:-3]
        return pl.BlockSpec((*lead, 8, G, wide), lambda x: (*(0,) * len(lead), x, k, 0))

    y_messages = pl.pallas_call(
        y_message_kernel,
        grid=(n // 8,),
        in_specs=[pl.BlockSpec(split_layer.shape, lambda x: (0, 0))]
        + [group_spec(0, f) for f in range(8)]
        + [group_spec(own // 8 - 1, f) for f in range(8)],
        out_specs=[WHOLE] * 2,
        out_shape=[array(y_message_rows(n), wide)] * 2,
        compiler_params=params(16),
        name="y_messages",
    )(pltpu.with_memory_space_constraint(split_layer, pltpu.HBM), *far_columns, *far_columns)
    ynear, yfar = swap(y_messages, "gy", tiles_y)

    rhs, own_diag, tot, gain, one, fx, fy, fz, al0, al1, be0, be1 = pl.pallas_call(
        prep_kernel,
        in_specs=[hbm] * 2 + [WHOLE] + [hbm] * 4,
        out_specs=[WHOLE] * 12,
        out_shape=[array(n, own, wide)] * 12,
        scratch_shapes=[pltpu.VMEM(v.shape, v.dtype) for v in columns[:2] + columns[3:7]]
        + [pltpu.SemaphoreType.DMA((6, n // 4))],
        compiler_params=params(16),
        cost_estimate=cost(60_000_000, 30_000_000),
        name="prep",
    )(*far_columns[:2], accum_cross, *far_columns[3:7])
    shared = (rhs, tot, gain, one, fx, fy, fz)

    x_messages = pl.pallas_call(
        x_message_kernel,
        in_specs=[WHOLE] * 10,
        out_specs=[WHOLE] * 2,
        out_shape=[array(PLANES * own + 2 * G, wide)] * 2,
        compiler_params=params(8),
        name="x_messages",
    )(mask, *shared, ynear, yfar)
    xnear, xfar = swap(x_messages, "gx", tiles_x)

    shared = (residual, mask, frac_flow, rhs, own_diag, tot, gain, one, fx, fy, fz, ynear, yfar)
    late_near, late_far, tot3, gain3, one3, six, end, two, acc, *flux = pl.pallas_call(
        interior_kernel,
        in_specs=[SCALARS] + [WHOLE] * 14,
        out_specs=[WHOLE] * (9 + FLUXES),
        out_shape=[array(late_rows(own, unknowns, wide), wide)] * 2
        + [array(n, 3 * G, wide)] * 3
        + [
            array(5, n, G, wide),
            array(n, G, wide),
            array(n, ext, wide),
            array(n // 8, own, wide),
        ]
        + [array(n, own, wide)] * FLUXES,
        scratch_shapes=[pltpu.VMEM((2, own, wide), F32)],
        compiler_params=params(8),
        cost_estimate=cost(60_000_000, 30_000_000),
        name="interior",
    )(split_layer, coarse_inverse, *shared)
    late_near, late_far = swap((late_near, late_far), "gx", tiles_x)

    devices = tiles_x * tiles_y
    span = pl.cdiv(unknowns, 128) * 128
    *flux, sent, edge_fx, edge_step = pl.pallas_call(
        edge_kernel,
        in_specs=[SCALARS] + [WHOLE] * (22 + FLUXES),
        out_specs=[WHOLE] * (3 + FLUXES),
        out_shape=[array(n, own, wide)] * FLUXES
        + [
            array(devices, span),
            array(2, ext, wide),
            array(2, own, wide),
        ],
        scratch_shapes=[
            pltpu.VMEM((4, ext, wide), F32),
            pltpu.VMEM((4, ext, wide), F32),
            pltpu.VMEM((10, ext, wide), F32),
            pltpu.VMEM((2, 10, own, wide), F32),
            pltpu.VMEM((n // 8, own, wide), F32),
        ],
        input_output_aliases={23 + f: f for f in range(FLUXES)},
        compiler_params=params(8),
        name="edges",
    )(split_layer, *shared, xnear, xfar, tot3, gain3, one3, six, end, two, acc, *flux)
    got = lax.all_to_all(sent, ("gx", "gy"), 0, 0, tiled=True)

    return pl.pallas_call(
        functools.partial(final_kernel, tiles_y),
        in_specs=[SCALARS] + [WHOLE] * (14 + FLUXES),
        out_specs=pl.BlockSpec(memory_space=pl.ANY),
        out_shape=array(2, n, own, wide),
        scratch_shapes=[
            pltpu.VMEM((n // 8 + 2, ext, wide), F32),
            pltpu.VMEM((n // 8, own, wide), F32),
            pltpu.VMEM((n // 8, own, wide), F32),
            pltpu.VMEM((2, n // 8 + 1, own, wide), F32),
            pltpu.VMEM((2, n, own, wide), F32),
            pltpu.SemaphoreType.DMA((2, n // 4)),
        ],
        compiler_params=params(12),
        name="final",
    )(split_layer, frac_flow, coarse_inverse, ynear, yfar, late_near, late_far, fx, edge_fx,
      edge_step, al0, al1, be0, be1, got, *flux)


def solution(mesh):
    placed = (
        P(None, "gx", "gy", None),
        P(None, "gx", "gy", None),
        P(None, "gx", "gy", None),
        P("gx", "gy", None),
        P("gx", "gy", None),
        P("gx", "gy", None),
        P("gx", "gy", None),
        P("gx", "gy", None),
        P("gx", "gy"),
        P("gx", None, None),
    )
    return jax.shard_map(
        functools.partial(shards, mesh.shape["gx"], mesh.shape["gy"]),
        mesh=mesh,
        in_specs=placed,
        out_specs=P(None, "gx", "gy", None),
        check_vma=False,
    )
```

```python
import functools

import jax
import jax.numpy as jnp
from jax import lax
from jax.experimental import pallas as pl
from jax.experimental.pallas import tpu as pltpu
from jax.sharding import PartitionSpec as P

relaxation = 2.0 / 3.0
F32 = jnp.float32
WHOLE = pl.BlockSpec(memory_space=pltpu.VMEM)
SCALARS = pl.BlockSpec(memory_space=pltpu.SMEM)
G = 8
STEP = 16
PLANES = 6


def params(mib):
    return pltpu.CompilerParams(vmem_limit_bytes=mib << 20)


def cost(flops, size):
    return pl.CostEstimate(flops=flops, bytes_accessed=size, transcendentals=0)


def z_next(v):
    return pltpu.roll(v, v.shape[1] - 1, 1)


def z_prev(v):
    return pltpu.roll(v, 1, 1)


def quasi_impes(active, rp, rs, dpp, dss, dps, dsp):
    weight = dps / dss
    return active * (rp - weight * rs), active * (dpp - weight * dsp) + (1.0 - active)


def swap_pairs(axis, size):
    near = [(i, i ^ 1) for i in range(size) if i ^ 1 < size]
    far = [(i, ((i + 1) ^ 1) - 1) for i in range(size) if 0 <= ((i + 1) ^ 1) - 1 < size]
    return near, far


def swap(message, axis, size):
    near, far = swap_pairs(axis, size)
    return lax.ppermute(message[0], axis, near), lax.ppermute(message[1], axis, far)


def group(k):
    return slice(8 * k, 8 * k + 8)


def turned_next(mine, after, s):
    return jnp.where(s == G - 1, after, mine)


def turned_prev(mine, before, s):
    return jnp.where(s == 0, before, mine)


def turn_next(v):
    return pltpu.roll(v, G - 1, 0)


def turn_prev(v):
    return pltpu.roll(v, 1, 0)


def places(wide):
    shape = (G, wide)
    return lax.broadcasted_iota(jnp.int32, shape, 0), lax.broadcasted_iota(jnp.int32, shape, 1)


def along_z(tz, a, lane):
    return jnp.where(lane < a.shape[1] - 1, tz * a * z_next(a), 0.0)


Y_TURNS = {
    "c": (6, 2),
    "a": (4, 4),
    "tx": (3, 5),
    "e": (3, 6),
    "tz": (1, 7),
}
Y_PLACES = {
    "c": ((4, 5), (2, 3)),
    "a": ((3,), (4,)),
    "tx": ((2,), (5,)),
    "e": ((1,), (6,)),
    "tz": ((0,), (7,)),
}


def y_message_kernel(split_ref, *refs):
    low, high, (near_ref, far_ref) = refs[:8], refs[8:16], refs[16:]
    n, _, wide = low[3].shape
    even = lax.rem(lax.axis_index("gy"), 2) == 0
    step = pl.program_id(0)
    x0 = pl.multiple_of(STEP * step, 8)
    shape = (STEP, G, wide)
    row, s, lane = (lax.broadcasted_iota(jnp.int32, shape, k) for k in range(3))

    def turn(v, k):
        return jnp.stack([pltpu.roll(v[i], k, 0) for i in range(v.shape[0])])

    def fields(group, side):
        res, diag, crs, mask, tx, ty, tz, ff = group
        before, after = jnp.maximum(x0 - 1, 0), jnp.minimum(x0 + STEP, n - 1)
        a, trans = mask[pl.ds(x0, STEP)].astype(F32), tx[pl.ds(x0, STEP)]
        t = trans * a
        a_after = jnp.concatenate([a[1:], mask[pl.ds(after, 1)].astype(F32)], axis=0)
        t_before = jnp.concatenate([tx[pl.ds(before, 1)] * mask[pl.ds(before, 1)].astype(F32), t[:-1]], axis=0)
        b, c = quasi_impes(a, res[0], res[1], diag[0], diag[1], crs[0], crs[1])
        ty_a = ty[...] * a
        ey = ty_a * turn(a, G - 1)
        a_above = jnp.stack([z_next(a[i]) for i in range(STEP)])
        ez = jnp.where(lane < wide - 1, tz[...] * a * a_above, 0.0)
        more = ez + jnp.stack([z_prev(ez[i]) for i in range(STEP)])
        more = more + jnp.where(row + x0 == n - 1, 0.0, t * a_after)
        more = more + jnp.where(row + x0 == 0, 0.0, t_before * a)
        more = more + (ey if side else turn(ey, 1))
        c = jnp.where(s == (1 if side else 6), c + more, c)
        tile = b
        for name, v in (("c", c), ("a", a), ("tx", trans), ("e", ey), ("tz", tz[...])):
            moved = turn(v, Y_TURNS[name][side])
            for place in Y_PLACES[name][side]:
                tile = jnp.where(s == place, moved, tile)
        outer = slice(0, 1) if side else slice(7, 8)
        return tile, ty_a[:, outer], ff[:, outer, :]

    def put(rows, up, down):
        near_ref[rows, :] = jnp.where(even, up, down)
        far_ref[rows, :] = jnp.where(even, down, up)

    up, down = fields(high, 0), fields(low, 1)
    for k in range(STEP):
        put(pl.ds(pl.multiple_of(8 * (x0 + k), 8), 8), up[0][k], down[0][k])
        put(pl.ds(8 * n + x0 + k, 1), up[1][k], down[1][k])
        put(pl.ds(9 * n + x0 + k, 1), up[2][k], down[2][k])

    @pl.when(step == 0)
    def _():
        put(slice(10 * n, y_message_rows(n)), *[jnp.zeros((y_message_rows(n) - 10 * n, wide), F32)] * 2)
        first_lane = lax.broadcasted_iota(jnp.int32, (1, wide), 1)
        for q in range(n // 8):
            splits = split_ref[q : q + 1, :]
            above = (first_lane < splits[:, -1:]).astype(F32)
            below = (first_lane < splits[:, :1]).astype(F32)
            put(slice(10 * n + 2 + q, 10 * n + 3 + q), above, below)
        corners = [
            (tx[n - 1, at, :] * mask[n - 1, at, :].astype(F32), mask[0, at, :].astype(F32))
            for mask, tx, at in ((high[3], high[4], slice(6, 7)), (low[3], low[4], slice(1, 2)))
        ]
        for k in range(2):
            put(slice(10 * n + k, 10 * n + k + 1), corners[0][k], corners[1][k])


def y_message_rows(n):
    return 10 * n + pl.cdiv(2 + n // 8, 8) * 8


class Ghosts:
    def __init__(self, near_ref, far_ref, n):
        self.refs, self.n = (near_ref, far_ref), n
        self.even = lax.rem(lax.axis_index("gy"), 2) == 0
        self.s, _ = places(near_ref.shape[1])

    def both(self, rows):
        near, far = (ref[rows, :] for ref in self.refs)
        return jnp.where(self.even, far, near), jnp.where(self.even, near, far)

    def tiles(self, x):
        return self.both(pl.ds(pl.multiple_of(8 * x, 8), 8))

    def pick(self, tiles, name, low_at=(G - 1,), high_at=(0,)):
        low, high = tiles
        if name != "b":
            up, down = Y_TURNS[name]
            low, high = pltpu.roll(low, 8 - up, 0), pltpu.roll(high, 8 - down, 0)
        picked = jnp.zeros_like(low)
        for place in low_at:
            picked = jnp.where(self.s == place, low, picked)
        for place in high_at:
            picked = jnp.where(self.s == place, high, picked)
        return picked

    def row(self, at, low_at=G - 1, high_at=0):
        low, high = self.both(pl.ds(at, 1))
        return jnp.where(self.s == low_at, low, jnp.where(self.s == high_at, high, 0.0))

    def active(self, x):
        return self.pick(self.tiles(x), "a")

    def first_active(self):
        return self.active(0) + self.row(10 * self.n + 1, G - 2, 1)

    def last_trans(self):
        return self.row(10 * self.n, G - 2, 1)

    def frac(self, x):
        return self.row(9 * self.n + x)

    def lower(self, q):
        return self.row(10 * self.n + 2 + q)


def prep_kernel(res_hbm, diag_hbm, crs, mask_hbm, tx_hbm, ty_hbm, tz_hbm,
                rhs, own_diag, tot, gain, one, fx, fy, fz, al0, al1, be0, be1,
                res, diag, mask, tx, ty, tz, sems):
    n, own, wide = mask.shape
    groups = own // 8
    chunk = 4
    s, lane = places(wide)

    def copies(q):
        at = pl.ds(chunk * q, chunk)
        pairs = (
            (res_hbm.at[:, at], res.at[:, at]),
            (diag_hbm.at[:, at], diag.at[:, at]),
            (tx_hbm.at[at], tx.at[at]),
            (ty_hbm.at[at], ty.at[at]),
            (tz_hbm.at[at], tz.at[at]),
        )
        return [pltpu.make_async_copy(a, b, sems.at[k + 1, q]) for k, (a, b) in enumerate(pairs)]

    def masks(q):
        at = pl.ds(chunk * q, chunk)
        return pltpu.make_async_copy(mask_hbm.at[at], mask.at[at], sems.at[0, q])

    for q in range(n // chunk):
        for copy in (masks(q), *copies(q)):
            copy.start()
    masks(0).wait()

    def row(x, carry):
        first, last = x == 0, x == n - 1
        after = jnp.minimum(x + 1, n - 1)
        before = jnp.maximum(x - 1, 0)
        a_after = mask[x, group(0), :].astype(F32)
        turned_after = turn_next(a_after)
        ey_before = jnp.zeros((G, wide), F32)
        for k in range(groups):
            here = group(k)
            a, turned = a_after, turned_after
            rp, rs = res[0, x, here, :], res[1, x, here, :]
            dpp, dss = diag[0, x, here, :], diag[1, x, here, :]
            dps, dsp = crs[0, x, here, :], crs[1, x, here, :]
            det = dpp * dss - dps * dsp
            both = 1.0 / (dss * det)
            inverse = both * dss
            weight = dps * (both * det)
            b = a * (rp - weight * rs)
            c = a * (dpp - weight * dsp) + (1.0 - a)
            rhs[x, here, :] = b
            own_diag[x, here, :] = c
            al0[x, here, :] = dss * inverse
            al1[x, here, :] = dps * inverse
            be0[x, here, :] = dpp * inverse
            be1[x, here, :] = dsp * inverse
            t = tx[x, here, :] * a
            ex = t * mask[after, here, :].astype(F32)
            fx[x, here, :] = jnp.where(last, t, ex)
            total = c + jnp.where(last, 0.0, ex)
            total = total + jnp.where(first, 0.0, fx[before, here, :])
            ez = along_z(tz[x, here, :], a, lane)
            fz[x, here, :] = ez
            total = total + ez + z_prev(ez)
            ey = ty[x, here, :] * a
            if k < groups - 1:
                a_after = mask[x, group(k + 1), :].astype(F32)
                turned_after = turn_next(a_after)
                ey = ey * turned_next(turned, turned_after, s)
                inside = ey
            else:
                ey = jnp.where(s == G - 1, ey, ey * turned)
                inside = jnp.where(s == G - 1, 0.0, ey)
            fy[x, here, :] = ey
            ey_turned = turn_prev(inside)
            total = total + inside + turned_prev(ey_turned, ey_before, s)
            ey_before = ey_turned
            tot[x, here, :] = total
            if 0 < k < groups - 1:
                g = relaxation / total
                gain[x, here, :] = g
                one[x, here, :] = g * b
        return carry

    def part(q, carry):
        @pl.when(q < n // chunk - 1)
        def _():
            masks(q + 1).wait()

        for copy in copies(q):
            copy.wait()
        return lax.fori_loop(0, chunk, lambda k, v: row(chunk * q + k, v), carry, unroll=2)

    lax.fori_loop(0, n // chunk, part, 0)


class Finished:
    def __init__(self, x, n, ghosts, mask, rhs, tot, fx, fy, s, lane, ex_before=None):
        groups = mask.shape[1] // 8
        first, last = x == 0, x == n - 1
        tiles = ghosts.tiles(x)
        ga, gtx, gtz = (ghosts.pick(tiles, name) for name in ("a", "tx", "tz"))
        gb = ghosts.pick(tiles, "b", (G - 1, G - 2), (0, 1))
        gc = jnp.maximum(ghosts.pick(tiles, "c", (G - 1, G - 2), (0, 1)), 1.0)
        before, after = jnp.maximum(x - 1, 0), jnp.minimum(x + 1, n - 1)
        if ex_before is None:
            tiles_before = ghosts.tiles(before)
            ex_before = ghosts.pick(tiles_before, "a") * ghosts.pick(tiles_before, "tx") * ga
            ex_before = jnp.where(first, 0.0, ex_before)
        a_after = ghosts.active(after)
        end = fy[x, group(groups - 1), :]
        end = jnp.where(s == G - 1, end * turn_next(ga), end)
        a_first = turn_next(mask[x, group(0), :].astype(F32))
        ey = ghosts.pick(tiles, "e", (G - 2,), (0,))
        ey = jnp.where(s == G - 1, ghosts.row(8 * n + x) * a_first, ey)
        ey_turned = turn_prev(ey)
        ez = along_z(gtz, ga, lane)
        t = gtx * ga
        ex = t * a_after
        total = gc + ez + z_prev(ez) + ey + turned_prev(ey_turned, turn_prev(end), s)
        total = total + jnp.where(last, 0.0, ex) + ex_before
        self.ex = ex
        self.end = end
        self.fx, self.fy, self.fz = jnp.where(last, t + ghosts.last_trans(), ex), ey, ez
        self.rhs = gb
        self.total = (
            tot[x, group(0), :] + jnp.where(s == 0, ey_turned, 0.0),
            tot[x, group(groups - 1), :] + jnp.where(s == G - 1, end, 0.0),
            total,
        )
        self.all_rhs = (rhs[x, group(0), :], rhs[x, group(groups - 1), :], gb)


def slot_of(k, groups):
    return {0: 0, groups - 1: 1, groups: 2}[k]


def x_message_kernel(mask, rhs, tot, gain, one, fx, fy, fz, ynear, yfar, near_ref, far_ref):
    even = lax.rem(lax.axis_index("gx"), 2) == 0
    n, own, wide = mask.shape
    groups = own // 8
    s, lane = places(wide)
    ghosts = Ghosts(ynear, yfar, n)
    finished = {x: Finished(x, n, ghosts, mask, rhs, tot, fx, fy, s, lane) for x in (0, 1, n - 2, n - 1)}
    for k in range(groups + 1):
        here = group(k)
        touched = k in (0, groups - 1, groups)

        def first_of(x):
            done = finished[x]
            if not touched:
                return one[x, here, :]
            slot = slot_of(k, groups)
            return relaxation * done.all_rhs[slot] / done.total[slot]

        def of(x, key):
            done = finished[x]
            total = done.total[slot_of(k, groups)] if touched else tot[x, here, :]
            if k == groups:
                return done.rhs, total, key, done.fy
            return rhs[x, here, :], total, key, done.end if k == groups - 1 else fy[x, here, :]

        if k == groups:
            up = of(n - 1, finished[n - 1].fx)
            down = of(0, ghosts.first_active())
        else:
            up = of(n - 1, fx[n - 1, here, :])
            down = of(0, mask[0, here, :].astype(F32))
            up += (fz[n - 1, here, :], fx[n - 2, here, :] * first_of(n - 2))
            down += (fz[0, here, :], fx[0, here, :] * first_of(1))
        if k == groups:
            b, total, key, ey = (jnp.where(even, p, q) for p, q in zip(up, down, strict=True))
            ob, ototal, okey, oey = (jnp.where(even, q, p) for p, q in zip(up, down, strict=True))
            for ref, (b, total, key, ey) in (
                (near_ref, (b, total, key, ey)),
                (far_ref, (ob, ototal, okey, oey)),
            ):
                at = PLANES * own
                ref[at : at + G, :] = jnp.where((s == 0) | (s == G - 1), b, pltpu.roll(total, 4, 0))
                ref[at + G : at + 2 * G, :] = jnp.where((s < 2) | (s >= G - 2), key, pltpu.roll(ey, 4, 0))
        else:
            for f in range(PLANES):
                start = f * own + 8 * k
                near_ref[start : start + 8, :] = jnp.where(even, up[f], down[f])
                far_ref[start : start + 8, :] = jnp.where(even, down[f], up[f])


def late_messages(split_ref, ff, inv, near_ref, far_ref):
    even = lax.rem(lax.axis_index("gx"), 2) == 0
    j = lax.axis_index("gy")
    n, own, wide = ff.shape
    per_tile = 2 * split_ref.shape[0] * split_ref.shape[1]
    near_ref[0:own, :] = jnp.where(even, ff[n - 1], ff[0])
    far_ref[0:own, :] = jnp.where(even, ff[0], ff[n - 1])
    at = own
    unknowns = inv.shape[2]
    top = inv[0, pl.ds(pl.multiple_of(j * per_tile + per_tile - 16, 8), 16), :]
    bottom = inv[0, pl.ds(pl.multiple_of(j * per_tile, 8), 16), :]
    for k in range(0, unknowns, wide):
        w = min(wide, unknowns - k)
        if w < wide:
            near_ref[at : at + 16, :] = jnp.zeros((16, wide), F32)
            far_ref[at : at + 16, :] = jnp.zeros((16, wide), F32)
        near_ref[at : at + 16, :w] = jnp.where(even, top[:, k : k + w], bottom[:, k : k + w])
        far_ref[at : at + 16, :w] = jnp.where(even, bottom[:, k : k + w], top[:, k : k + w])
        at += 16
    lane = lax.broadcasted_iota(jnp.int32, (1, wide), 1)
    zero = jnp.zeros((8, wide), F32)
    near_ref[at : at + 8, :] = zero
    far_ref[at : at + 8, :] = zero
    for q in range(split_ref.shape[1]):
        top = (lane < split_ref[split_ref.shape[0] - 1, q]).astype(F32)
        bottom = (lane < split_ref[0, q]).astype(F32)
        near_ref[at + q : at + q + 1, :] = jnp.where(even, top, bottom)
        far_ref[at + q : at + q + 1, :] = jnp.where(even, bottom, top)


def late_rows(own, unknowns, wide):
    return own + 16 * pl.cdiv(unknowns, wide) + 8


class Planes:
    def __init__(self, near_ref, far_ref, own):
        self.refs, self.own = (near_ref, far_ref), own
        self.even = lax.rem(lax.axis_index("gx"), 2) == 0

    def rows(self, at, n, side):
        near, far = (ref[at : at + n, :] for ref in self.refs)
        return jnp.where(self.even, near, far) if side else jnp.where(self.even, far, near)

    def field(self, f, k, side):
        if 8 * k < self.own:
            return self.rows(f * self.own + 8 * k, 8, side)
        s, _ = places(self.refs[0].shape[1])
        ends = (s == 0) | (s == G - 1)
        if f < 2:
            tile = self.rows(PLANES * self.own, G, side)
            return jnp.where(ends, pltpu.roll(tile, 4, 0) if f else tile, 0.0)
        if f < 4:
            tile = self.rows(PLANES * self.own + G, G, side)
            if f == 2:
                return jnp.where((s < 2) | (s >= G - 2), tile, 0.0)
            return jnp.where(s == G - 1, pltpu.roll(tile, 4, 0), 0.0)
        return jnp.zeros_like(s, F32)


class Inside:
    def __init__(self, groups, ff, rhs, gain, one, fx, fy, fz, gain3, one3, six, end):
        self.groups, self.own_ff, self.own_rhs = groups, ff, rhs
        self.own_gain, self.own_one, self.own_fx, self.own_fy, self.own_fz = gain, one, fx, fy, fz
        self.gain3, self.one3, self.six, self.end = gain3, one3, six, end

    def pick(self, own, which, x, k):
        return self.six[which, x] if k == self.groups else own[x, group(k), :]

    def three(self, own, other, x, k):
        if 0 < k < self.groups - 1:
            return own[x, group(k), :]
        return other[x, group(slot_of(k, self.groups)), :]

    def rhs(self, x, k):
        return self.pick(self.own_rhs, 0, x, k)

    def fx(self, x, k):
        return self.pick(self.own_fx, 1, x, k)

    def fy(self, x, k):
        if k == self.groups - 1:
            return self.end[x]
        return self.pick(self.own_fy, 2, x, k)

    def fz(self, x, k):
        return self.pick(self.own_fz, 3, x, k)

    def ff(self, x, k):
        return self.pick(self.own_ff, 4, x, k)

    def gain(self, x, k):
        return self.three(self.own_gain, self.gain3, x, k)

    def one(self, x, k):
        return self.three(self.own_one, self.one3, x, k)

    def before(self, x, k):
        return self.fx(x - 1, k) * self.one(x - 1, k)

    def after(self, x, k):
        return self.fx(x, k) * self.one(x + 1, k)

    def faces_x(self, x, k):
        ex = self.fx(x, k)
        return ex, ex * (self.ff(x, k) + self.ff(x + 1, k))


def second_row(o, x, s, put):
    total = o.groups + 1
    p = o.one(x, 0)
    p_turned = turn_next(p)
    w_turned = turn_prev(o.fy(x, total - 1) * o.one(x, total - 1))
    for k in range(total):
        p_after = o.one(x, (k + 1) % total)
        after_turned = turn_next(p_after)
        ey, ez = o.fy(x, k), o.fz(x, k)
        mine = turn_prev(ey * p)
        beside = ey * turned_next(p_turned, after_turned, s) + turned_prev(mine, w_turned, s)
        beside = beside + ez * z_next(p) + z_prev(ez * p)
        beside = beside + o.after(x, k) + o.before(x, k)
        put(k, o.gain(x, k) * ((2.0 - relaxation) * o.rhs(x, k) + beside))
        p, p_turned, w_turned = p_after, after_turned, mine


def x_flux(o, x, k, two):
    step = two(x + 1, k) - two(x, k)
    ex, wx = o.faces_x(x, k)
    return ex * step, wx * step


def flux_row(o, x, s, lane, two, res, own_diag, split, carried, put):
    groups = o.groups

    def faces_y(k, p, p_turned, p_after, f, f_turned, f_after):
        ey = o.fy(x, k)
        weighted = ey * (f + turned_next(f_turned, f_after, s))
        return ey, weighted, turned_next(p_turned, p_after, s) - p

    p0, f0 = two(x, 0), o.ff(x, 0)
    p0_turned, f0_turned = turn_next(p0), turn_next(f0)
    p, f = two(x, groups), o.ff(x, groups)
    ghost = faces_y(groups, p, turn_next(p), p0_turned, f, turn_next(f), f0_turned)
    turned = [turn_prev(v) for v in ghost]
    p, f, p_turned, f_turned = p0, f0, p0_turned, f0_turned
    for k in range(groups):
        here = group(k)
        p_after, f_after = two(x, k + 1), o.ff(x, k + 1)
        p_after_turned, f_after_turned = turn_next(p_after), turn_next(f_after)
        mine = faces_y(k, p, p_turned, p_after_turned, f, f_turned, f_after_turned)
        mine_turned = [turn_prev(v) for v in mine]
        ey, wy, dy = mine
        ey_before, wy_before, dy_before = (
            turned_prev(a, b, s) for a, b in zip(mine_turned, turned, strict=True)
        )
        ez = o.fz(x, k)
        wz = ez * (f + z_next(f))
        dz = z_next(p) - p
        ez_before, wz_before, dz_before = z_prev(ez), z_prev(wz), z_prev(dz)
        qx, sx = x_flux(o, x, k, two)
        if carried is None:
            qx_before, sx_before = x_flux(o, x - 1, k, two)
        else:
            qx_before, sx_before = carried[0, here, :], carried[1, here, :]
            carried[0, here, :] = qx
            carried[1, here, :] = sx
        gained = (qx - qx_before) + (ey * dy - ey_before * dy_before)
        gained = gained + (ez * dz - ez_before * dz_before)
        weighed = (sx - sx_before) + (wy * dy - wy_before * dy_before)
        weighed = weighed + (wz * dz - wz_before * dz_before)
        rest = o.rhs(x, k) - own_diag[x, here, :] * p + gained
        below = lane < split(k)
        put(
            k,
            rest,
            res[0, x, here, :] + gained,
            res[1, x, here, :] + 0.5 * weighed,
            jnp.where(s == 0, ey_before, ey),
            jnp.where(s == 0, wy_before, wy),
            jnp.where(below, ez, ez_before),
            jnp.where(below, wz, wz_before),
        )
        turned = mine_turned
        p, f, p_turned, f_turned = p_after, f_after, p_after_turned, f_after_turned


FLUXES = 6


def interior_kernel(split_ref, inv, res, mask, ff, rhs, own_diag, tot, gain, one, fx, fy, fz, ynear, yfar,
                    late_near, late_far, tot3, gain3, one3, six, end, two, acc, *flux_and_carried):
    flux, carried = flux_and_carried[:FLUXES], flux_and_carried[FLUXES]
    late_messages(split_ref, ff, inv, late_near, late_far)
    n, own, wide = mask.shape
    groups = own // 8
    s, lane = places(wide)
    ghosts = Ghosts(ynear, yfar, n)

    def finish(x, carry):
        done = Finished(x, n, ghosts, mask, rhs, tot, fx, fy, s, lane, carry)
        for slot in range(3):
            g = relaxation / done.total[slot]
            tot3[x, group(slot), :] = done.total[slot]
            gain3[x, group(slot), :] = g
            one3[x, group(slot), :] = g * done.all_rhs[slot]
        end[x] = done.end
        for k, v in enumerate((done.rhs, done.fx, done.fy, done.fz, ghosts.frac(x))):
            six[k, x] = v
        return done.ex

    lax.fori_loop(0, n, finish, jnp.zeros((G, wide), F32), unroll=8)
    o = Inside(groups, ff, rhs, gain, one, fx, fy, fz, gain3, one3, six, end)

    def second(x, carry):
        def put(k, v):
            two[x, group(k), :] = v

        second_row(o, x, s, put)
        return carry

    lax.fori_loop(2, n - 2, second, 0, unroll=4)

    def two_of(x, k):
        return two[x, group(k), :]

    for k in range(groups):
        carried[0, group(k), :], carried[1, group(k), :] = x_flux(o, 2, k, two_of)
    acc[...] = jnp.zeros_like(acc)

    def row(x, carry):
        def put(k, rest, *values):
            acc[x // 8, group(k), :] += rest
            for f, v in enumerate(values):
                flux[f][x, group(k), :] = v

        flux_row(o, x, s, lane, two_of, res, own_diag, lambda k: split_ref[x // 8, k], carried, put)
        return carry

    lax.fori_loop(3, n - 3, row, 0, unroll=2)


class Edges(Inside):
    def beyond(self, n, planes, act, tot, tot3, one_edge, gain_edge, edge_fx):
        self.n, self.planes = n, planes
        self.slots = {-1: 0, 0: 1, n - 1: 2, n: 3}
        self.one_edge, self.gain_edge, self.edge_fx = one_edge, gain_edge, edge_fx
        self.far = {-1: 0, n: 1}
        for k in range(self.groups + 1):
            here = group(k)
            low = planes.field(2, k, 0) * act(k)
            high = super().fx(n - 1, k) * planes.field(2, k, 1)
            edge_fx[0, here, :] = low
            edge_fx[1, here, :] = high
            for x, slot in self.slots.items():
                face = low if x <= 0 else high
                if x in self.far:
                    total = jnp.maximum(planes.field(1, k, self.far[x]), 1.0) + face
                else:
                    total = self.three(tot, tot3, x, k) + face
                g = relaxation / total
                gain_edge[slot, here, :] = g
                one_edge[slot, here, :] = g * self.rhs(x, k)

    def rhs(self, x, k):
        return self.planes.field(0, k, self.far[x]) if x in self.far else super().rhs(x, k)

    def fx(self, x, k):
        if x in (-1, self.n - 1):
            return self.edge_fx[0 if x == -1 else 1, group(k), :]
        return super().fx(x, k)

    def fy(self, x, k):
        return self.planes.field(3, k, self.far[x]) if x in self.far else super().fy(x, k)

    def fz(self, x, k):
        return self.planes.field(4, k, self.far[x]) if x in self.far else super().fz(x, k)

    def gain(self, x, k):
        return self.gain_edge[self.slots[x], group(k), :] if x in self.slots else super().gain(x, k)

    def one(self, x, k):
        return self.one_edge[self.slots[x], group(k), :] if x in self.slots else super().one(x, k)

    def before(self, x, k):
        return self.planes.field(5, k, 0) if x == -1 else super().before(x, k)

    def after(self, x, k):
        return self.planes.field(5, k, 1) if x == self.n else super().after(x, k)


def edge_kernel(split_ref, res, mask, ff, rhs, own_diag, tot, gain, one, fx, fy, fz, ynear, yfar, xnear, xfar,
                tot3, gain3, one3, six, end, two, acc, *others):
    flux = others[FLUXES : 2 * FLUXES]
    sent, edge_fx, edge_step, one_edge, gain_edge, two_edge, near_fx, total_acc = others[2 * FLUXES :]
    n, own, wide = mask.shape
    groups = own // 8
    s, lane = places(wide)
    planes = Planes(xnear, xfar, own)
    ghosts = Ghosts(ynear, yfar, n)
    o = Edges(groups, ff, rhs, gain, one, fx, fy, fz, gain3, one3, six, end)

    def act(k):
        return ghosts.first_active() if k == groups else mask[0, group(k), :].astype(F32)

    o.beyond(n, planes, act, tot, tot3, one_edge, gain_edge, edge_fx)
    depth = 5
    bases = (-1, n - depth + 1)
    for side, base in enumerate(bases):
        for r in range(depth):
            x, slot = base + r, depth * side + r
            if x in (-1, 0, 1, n - 2, n - 1, n):

                def put_two(k, v, slot=slot):
                    two_edge[slot, group(k), :] = v

                second_row(o, x, s, put_two)
            else:
                two_edge[slot] = two[x]
            if x == n:
                continue
            for k in range(groups):
                ex = o.fx(x, k)
                near_fx[0, slot, group(k), :] = ex
                if x in (-1, n - 1):
                    near_fx[1, slot, group(k), :] = jnp.zeros_like(ex)
                else:
                    near_fx[1, slot, group(k), :] = ex * (o.ff(x, k) + o.ff(x + 1, k))
    for k in range(groups):
        edge_step[0, group(k), :] = two_edge[1, group(k), :] - two_edge[0, group(k), :]
        edge_step[1, group(k), :] = two_edge[2 * depth - 1, group(k), :] - two_edge[2 * depth - 2, group(k), :]
    total_acc[...] = acc[...]
    plain = Inside(groups, ff, rhs, gain, one, fx, fy, fz, gain3, one3, six, end)

    def row(r, carry):
        high = r >= depth - 2
        x = jnp.where(high, n - 2 * (depth - 2) + r, r)
        shift = jnp.where(high, depth - bases[1], -bases[0])

        def two_of(x, k):
            return two_edge[x + shift, group(k), :]

        def faces_x(x, k):
            return near_fx[0, x + shift, group(k), :], near_fx[1, x + shift, group(k), :]

        plain.faces_x = faces_x

        def put(k, rest, *values):
            total_acc[x // 8, group(k), :] += rest
            for f, v in enumerate(values):
                flux[f][x, group(k), :] = v

        flux_row(plain, x, s, lane, two_of, res, own_diag, lambda k: split_ref[x // 8, k], None, put)
        return carry

    lax.fori_loop(0, 2 * (depth - 2), row, 0, unroll=2)

    rows_b, cols_b = split_ref.shape
    lane = lax.broadcasted_iota(jnp.int32, (1, wide), 1)
    lower, upper = [], []
    for q in range(rows_b):
        for r in range(cols_b):
            column = jnp.sum(total_acc[q, group(r), :], axis=0, keepdims=True)
            below = lane < split_ref[q, r]
            lower.append(jnp.where(below, column, 0.0))
            upper.append(jnp.where(below, 0.0, column))
    count = rows_b * cols_b
    low_sum = jnp.sum(jnp.concatenate(lower, axis=0), axis=1, keepdims=True)
    high_sum = jnp.sum(jnp.concatenate(upper, axis=0), axis=1, keepdims=True)
    span = sent.shape[1]
    place = lax.broadcasted_iota(jnp.int32, (count, span), 1) - 2 * count * lax.axis_index("gy")
    which = 2 * lax.broadcasted_iota(jnp.int32, (count, span), 0)
    laid = jnp.where(place == which, low_sum, jnp.where(place == which + 1, high_sum, 0.0))
    sent[...] = jnp.broadcast_to(jnp.sum(laid, axis=0, keepdims=True), sent.shape)


def final_kernel(tiles_y, split_ref, frac, inv, ynear, yfar, xnear, xfar, fx, edge_fx, edge_step,
                 al0, al1, be0, be1, got, *rest):
    flux = rest[:FLUXES]
    out, coarse, step_y, step_z, across, held, sems = rest[FLUXES:]
    i, j = lax.axis_index("gx"), lax.axis_index("gy")
    n, own, wide = frac.shape
    ext = own + G
    unknowns = inv.shape[2]
    rows_b, cols_b = split_ref.shape
    per_tile = 2 * rows_b * cols_b
    ghosts = Ghosts(ynear, yfar, n)
    planes = Planes(xnear, xfar, own)
    s8, lane8 = places(wide)

    all_got = got[...]
    owner = lax.broadcasted_iota(jnp.int32, all_got.shape, 0)

    def row_of(tile_row):
        mine = (owner >= tile_row * tiles_y) & (owner < (tile_row + 1) * tiles_y)
        return jnp.sum(jnp.where(mine, all_got, 0.0), axis=0, keepdims=True)

    coarse_res = row_of(i)

    def solve(tile):
        start = pl.multiple_of(jnp.clip(tile, 0, tiles_y - 1) * per_tile, 8)
        block = inv[0, pl.ds(start, per_tile), :]
        e = jnp.sum(block * coarse_res[:, :unknowns], axis=1, keepdims=True)
        return jnp.broadcast_to(e, (per_tile, wide))

    mine, before, after = solve(j), solve(j - 1), solve(j + 1)

    def one_of(e, k):
        return jnp.broadcast_to(e[k : k + 1], (8, wide))

    for q in range(rows_b):
        for r in range(cols_b):
            k = 2 * (q * cols_b + r)
            low, high = one_of(mine, k), one_of(mine, k + 1)
            split = split_ref[q, r]
            coarse[q + 1, group(r), :] = jnp.where(lane8 < split, low, high)
            jump = high - low
            step_z[q, group(r), :] = jnp.where(
                lane8 == split - 1, jump, jnp.where(lane8 == split, -jump, 0.0)
            )
        below = ghosts.lower(q) > 0.5
        k_high, k_low = 2 * q * cols_b, 2 * (q * cols_b + cols_b - 1)
        coarse[q + 1, own:ext, :] = jnp.where(
            s8 == 0,
            jnp.where(below, one_of(after, k_high), one_of(after, k_high + 1)),
            jnp.where(below, one_of(before, k_low), one_of(before, k_low + 1)),
        )
        for r in range(cols_b):
            here = coarse[q + 1, group(r), :]
            ahead = turn_next(coarse[q + 1, group(r + 1), :])
            behind = turn_prev(coarse[q + 1, group(r - 1 if r else cols_b), :])
            step_y[q, group(r), :] = jnp.where(
                s8 == G - 1, ahead - here, jnp.where(s8 == 0, behind - here, 0.0)
            )
    blocks = pl.cdiv(unknowns, wide)
    for side, tile_row in ((0, i - 1), (1, i + 1)):
        other = row_of(tile_row)
        e = jnp.zeros((16, 1), F32)
        for k in range(blocks):
            w = min(wide, unknowns - k * wide)
            part = planes.rows(own + 16 * k, 16, side)[:, :w] * other[:, k * wide : k * wide + w]
            e = e + jnp.sum(part, axis=1, keepdims=True)
        e = jnp.broadcast_to(e, (16, wide))
        below = planes.rows(own + 16 * blocks, 8, side)
        skip = 16 - 2 * cols_b if side == 0 else 0
        at = 0 if side == 0 else rows_b + 1
        for r in range(cols_b):
            k = skip + 2 * r
            coarse[at, group(r), :] = jnp.where(one_of(below, r) > 0.5, one_of(e, k), one_of(e, k + 1))

    for q in range(rows_b + 1):
        x = 8 * q - 1
        for r in range(cols_b):
            here = group(r)
            ex = edge_fx[0, here, :] if q == 0 else edge_fx[1, here, :] if q == rows_b else fx[x, here, :]
            f_before = planes.rows(8 * r, 8, 0) if q == 0 else frac[x, here, :]
            f_after = planes.rows(8 * r, 8, 1) if q == rows_b else frac[x + 1, here, :]
            step = coarse[q + 1, here, :] - coarse[q, here, :]
            across[0, q, here, :] = ex * step
            if q in (0, rows_b):
                step = step + edge_step[0 if q == 0 else 1, here, :]
            across[1, q, here, :] = ex * (0.5 * (f_before + f_after)) * step

    def solved(x, q, beside=None, sign=None):
        for r in range(cols_b):
            here = group(r)
            u, v, wy, sy, wz, sz = (ref[x, here, :] for ref in flux)
            along_y, along_z = step_y[q, here, :], step_z[q, here, :]
            u = u + (wy * along_y + wz * along_z)
            v = v + 0.5 * (sy * along_y + sz * along_z)
            if beside is not None:
                u = sign(u, across[0, beside, here, :])
                v = sign(v, across[1, beside, here, :])
            held[0, x, here, :] = al0[x, here, :] * u - al1[x, here, :] * v
            held[1, x, here, :] = be0[x, here, :] * v - be1[x, here, :] * u

    def copies(q):
        return [
            pltpu.make_async_copy(
                held.at[k, pl.ds(4 * q, 4)], out.at[k, pl.ds(4 * q, 4)], sems.at[k, q]
            )
            for k in range(2)
        ]

    def block(q, carry):
        x = 8 * q
        solved(x, q, q, jnp.subtract)
        for k in range(1, 4):
            solved(x + k, q)
        for copy in copies(2 * q):
            copy.start()
        for k in range(4, 7):
            solved(x + k, q)
        solved(x + 7, q, q + 1, jnp.add)
        for copy in copies(2 * q + 1):
            copy.start()
        return carry

    lax.fori_loop(0, rows_b, block, 0)
    for q in range(2 * rows_b):
        for copy in copies(q):
            copy.wait()


def shards(tiles_x, tiles_y, residual, accum_diag, accum_cross, mask, trans_x, trans_y, trans_z,
           frac_flow, split_layer, coarse_inverse):
    n, own, wide = mask.shape
    ext = own + G
    unknowns = coarse_inverse.shape[2]
    columns = (residual, accum_diag, accum_cross, mask, trans_x, trans_y, trans_z, frac_flow)
    hbm = pl.BlockSpec(memory_space=pltpu.HBM)
    far_columns = [pltpu.with_memory_space_constraint(v, pltpu.HBM) for v in columns]

    def array(*shape):
        return jax.ShapeDtypeStruct(shape, F32)

    def group_spec(k, f):
        if f in (3, 4):
            return pl.BlockSpec((n, G, wide), lambda x: (0, k, 0))
        lead = columns[f].shape[:-3]
        return pl.BlockSpec((*lead, STEP, G, wide), lambda x: (*(0,) * len(lead), x, k, 0))

    y_messages = pl.pallas_call(
        y_message_kernel,
        grid=(n // STEP,),
        in_specs=[pl.BlockSpec(split_layer.shape, lambda x: (0, 0))]
        + [group_spec(0, f) for f in range(8)]
        + [group_spec(own // 8 - 1, f) for f in range(8)],
        out_specs=[WHOLE] * 2,
        out_shape=[array(y_message_rows(n), wide)] * 2,
        compiler_params=params(16),
        name="y_messages",
    )(pltpu.with_memory_space_constraint(split_layer, pltpu.HBM), *far_columns, *far_columns)
    ynear, yfar = swap(y_messages, "gy", tiles_y)

    rhs, own_diag, tot, gain, one, fx, fy, fz, al0, al1, be0, be1 = pl.pallas_call(
        prep_kernel,
        in_specs=[hbm] * 2 + [WHOLE] + [hbm] * 4,
        out_specs=[WHOLE] * 12,
        out_shape=[array(n, own, wide)] * 12,
        scratch_shapes=[pltpu.VMEM(v.shape, v.dtype) for v in columns[:2] + columns[3:7]]
        + [pltpu.SemaphoreType.DMA((6, n // 4))],
        compiler_params=params(16),
        cost_estimate=cost(60_000_000, 30_000_000),
        name="prep",
    )(*far_columns[:2], accum_cross, *far_columns[3:7])
    shared = (rhs, tot, gain, one, fx, fy, fz)

    x_messages = pl.pallas_call(
        x_message_kernel,
        in_specs=[WHOLE] * 10,
        out_specs=[WHOLE] * 2,
        out_shape=[array(PLANES * own + 2 * G, wide)] * 2,
        compiler_params=params(8),
        name="x_messages",
    )(mask, *shared, ynear, yfar)
    xnear, xfar = swap(x_messages, "gx", tiles_x)

    shared = (residual, mask, frac_flow, rhs, own_diag, tot, gain, one, fx, fy, fz, ynear, yfar)
    late_near, late_far, tot3, gain3, one3, six, end, two, acc, *flux = pl.pallas_call(
        interior_kernel,
        in_specs=[SCALARS] + [WHOLE] * 14,
        out_specs=[WHOLE] * (9 + FLUXES),
        out_shape=[array(late_rows(own, unknowns, wide), wide)] * 2
        + [array(n, 3 * G, wide)] * 3
        + [
            array(5, n, G, wide),
            array(n, G, wide),
            array(n, ext, wide),
            array(n // 8, own, wide),
        ]
        + [array(n, own, wide)] * FLUXES,
        scratch_shapes=[pltpu.VMEM((2, own, wide), F32)],
        compiler_params=params(8),
        cost_estimate=cost(60_000_000, 30_000_000),
        name="interior",
    )(split_layer, coarse_inverse, *shared)
    late_near, late_far = swap((late_near, late_far), "gx", tiles_x)

    devices = tiles_x * tiles_y
    span = pl.cdiv(unknowns, 128) * 128
    *flux, sent, edge_fx, edge_step = pl.pallas_call(
        edge_kernel,
        in_specs=[SCALARS] + [WHOLE] * (22 + FLUXES),
        out_specs=[WHOLE] * (3 + FLUXES),
        out_shape=[array(n, own, wide)] * FLUXES
        + [
            array(devices, span),
            array(2, ext, wide),
            array(2, own, wide),
        ],
        scratch_shapes=[
            pltpu.VMEM((4, ext, wide), F32),
            pltpu.VMEM((4, ext, wide), F32),
            pltpu.VMEM((10, ext, wide), F32),
            pltpu.VMEM((2, 10, own, wide), F32),
            pltpu.VMEM((n // 8, own, wide), F32),
        ],
        input_output_aliases={23 + f: f for f in range(FLUXES)},
        compiler_params=params(8),
        name="edges",
    )(split_layer, *shared, xnear, xfar, tot3, gain3, one3, six, end, two, acc, *flux)
    got = lax.all_to_all(sent, ("gx", "gy"), 0, 0, tiled=True)

    return pl.pallas_call(
        functools.partial(final_kernel, tiles_y),
        in_specs=[SCALARS] + [WHOLE] * (14 + FLUXES),
        out_specs=pl.BlockSpec(memory_space=pl.ANY),
        out_shape=array(2, n, own, wide),
        scratch_shapes=[
            pltpu.VMEM((n // 8 + 2, ext, wide), F32),
            pltpu.VMEM((n // 8, own, wide), F32),
            pltpu.VMEM((n // 8, own, wide), F32),
            pltpu.VMEM((2, n // 8 + 1, own, wide), F32),
            pltpu.VMEM((2, n, own, wide), F32),
            pltpu.SemaphoreType.DMA((2, n // 4)),
        ],
        compiler_params=params(12),
        name="final",
    )(split_layer, frac_flow, coarse_inverse, ynear, yfar, late_near, late_far, fx, edge_fx,
      edge_step, al0, al1, be0, be1, got, *flux)


def solution(mesh):
    placed = (
        P(None, "gx", "gy", None),
        P(None, "gx", "gy", None),
        P(None, "gx", "gy", None),
        P("gx", "gy", None),
        P("gx", "gy", None),
        P("gx", "gy", None),
        P("gx", "gy", None),
        P("gx", "gy", None),
        P("gx", "gy"),
        P("gx", None, None),
    )
    return jax.shard_map(
        functools.partial(shards, mesh.shape["gx"], mesh.shape["gy"]),
        mesh=mesh,
        in_specs=placed,
        out_specs=P(None, "gx", "gy", None),
        check_vma=False,
    )
```

```python
import functools

import jax
import jax.numpy as jnp
from jax import lax
from jax.experimental import pallas as pl
from jax.experimental.pallas import tpu as pltpu
from jax.sharding import PartitionSpec as P

relaxation = 2.0 / 3.0
F32 = jnp.float32
WHOLE = pl.BlockSpec(memory_space=pltpu.VMEM)
SCALARS = pl.BlockSpec(memory_space=pltpu.SMEM)
G = 8
STEP = 16
PLANES = 6


def params(mib):
    return pltpu.CompilerParams(vmem_limit_bytes=mib << 20)


def cost(flops, size):
    return pl.CostEstimate(flops=flops, bytes_accessed=size, transcendentals=0)


def z_next(v):
    return pltpu.roll(v, v.shape[1] - 1, 1)


def z_prev(v):
    return pltpu.roll(v, 1, 1)


def quasi_impes(active, rp, rs, dpp, dss, dps, dsp):
    weight = dps / dss
    return active * (rp - weight * rs), active * (dpp - weight * dsp) + (1.0 - active)


def swap_pairs(axis, size):
    near = [(i, i ^ 1) for i in range(size) if i ^ 1 < size]
    far = [(i, ((i + 1) ^ 1) - 1) for i in range(size) if 0 <= ((i + 1) ^ 1) - 1 < size]
    return near, far


def swap(message, axis, size):
    near, far = swap_pairs(axis, size)
    return lax.ppermute(message[0], axis, near), lax.ppermute(message[1], axis, far)


def group(k):
    return slice(8 * k, 8 * k + 8)


def turned_next(mine, after, s):
    return jnp.where(s == G - 1, after, mine)


def turned_prev(mine, before, s):
    return jnp.where(s == 0, before, mine)


def turn_next(v):
    return pltpu.roll(v, G - 1, 0)


def turn_prev(v):
    return pltpu.roll(v, 1, 0)


def places(wide):
    shape = (G, wide)
    return lax.broadcasted_iota(jnp.int32, shape, 0), lax.broadcasted_iota(jnp.int32, shape, 1)


def along_z(tz, a, lane):
    return jnp.where(lane < a.shape[1] - 1, tz * a * z_next(a), 0.0)


Y_TURNS = {
    "c": (6, 2),
    "a": (4, 4),
    "tx": (3, 5),
    "e": (3, 6),
    "tz": (1, 7),
}
Y_PLACES = {
    "c": ((4, 5), (2, 3)),
    "a": ((3,), (4,)),
    "tx": ((2,), (5,)),
    "e": ((1,), (6,)),
    "tz": ((0,), (7,)),
}


def y_message_kernel(split_ref, *refs):
    low, high, (near_ref, far_ref) = refs[:8], refs[8:16], refs[16:]
    n, _, wide = low[3].shape
    even = lax.rem(lax.axis_index("gy"), 2) == 0
    step = pl.program_id(0)
    x0 = pl.multiple_of(STEP * step, 8)
    shape = (STEP, G, wide)
    row, s, lane = (lax.broadcasted_iota(jnp.int32, shape, k) for k in range(3))

    def turn(v, k):
        return jnp.stack([pltpu.roll(v[i], k, 0) for i in range(v.shape[0])])

    def fields(group, side):
        res, diag, crs, mask, tx, ty, tz, ff = group
        before, after = jnp.maximum(x0 - 1, 0), jnp.minimum(x0 + STEP, n - 1)
        a, trans = mask[pl.ds(x0, STEP)].astype(F32), tx[pl.ds(x0, STEP)]
        t = trans * a
        a_after = jnp.concatenate([a[1:], mask[pl.ds(after, 1)].astype(F32)], axis=0)
        t_before = jnp.concatenate([tx[pl.ds(before, 1)] * mask[pl.ds(before, 1)].astype(F32), t[:-1]], axis=0)
        b, c = quasi_impes(a, res[0], res[1], diag[0], diag[1], crs[0], crs[1])
        ty_a = ty[...] * a
        ey = ty_a * turn(a, G - 1)
        a_above = jnp.stack([z_next(a[i]) for i in range(STEP)])
        ez = jnp.where(lane < wide - 1, tz[...] * a * a_above, 0.0)
        more = ez + jnp.stack([z_prev(ez[i]) for i in range(STEP)])
        more = more + jnp.where(row + x0 == n - 1, 0.0, t * a_after)
        more = more + jnp.where(row + x0 == 0, 0.0, t_before * a)
        more = more + (ey if side else turn(ey, 1))
        c = jnp.where(s == (1 if side else 6), c + more, c)
        tile = b
        for name, v in (("c", c), ("a", a), ("tx", trans), ("e", ey), ("tz", tz[...])):
            moved = turn(v, Y_TURNS[name][side])
            for place in Y_PLACES[name][side]:
                tile = jnp.where(s == place, moved, tile)
        outer = slice(0, 1) if side else slice(7, 8)
        return tile, ty_a[:, outer], ff[:, outer, :]

    def put(rows, up, down):
        near_ref[rows, :] = jnp.where(even, up, down)
        far_ref[rows, :] = jnp.where(even, down, up)

    up, down = fields(high, 0), fields(low, 1)
    for k in range(STEP):
        put(pl.ds(pl.multiple_of(8 * (x0 + k), 8), 8), up[0][k], down[0][k])
        put(pl.ds(8 * n + x0 + k, 1), up[1][k], down[1][k])
        put(pl.ds(9 * n + x0 + k, 1), up[2][k], down[2][k])

    @pl.when(step == 0)
    def _():
        put(slice(10 * n, y_message_rows(n)), *[jnp.zeros((y_message_rows(n) - 10 * n, wide), F32)] * 2)
        first_lane = lax.broadcasted_iota(jnp.int32, (1, wide), 1)
        for q in range(n // 8):
            splits = split_ref[q : q + 1, :]
            above = (first_lane < splits[:, -1:]).astype(F32)
            below = (first_lane < splits[:, :1]).astype(F32)
            put(slice(10 * n + 2 + q, 10 * n + 3 + q), above, below)
        corners = [
            (tx[n - 1, at, :] * mask[n - 1, at, :].astype(F32), mask[0, at, :].astype(F32))
            for mask, tx, at in ((high[3], high[4], slice(6, 7)), (low[3], low[4], slice(1, 2)))
        ]
        for k in range(2):
            put(slice(10 * n + k, 10 * n + k + 1), corners[0][k], corners[1][k])


def y_message_rows(n):
    return 10 * n + pl.cdiv(2 + n // 8, 8) * 8


class Ghosts:
    def __init__(self, near_ref, far_ref, n):
        self.refs, self.n = (near_ref, far_ref), n
        self.even = lax.rem(lax.axis_index("gy"), 2) == 0
        self.s, _ = places(near_ref.shape[1])

    def both(self, rows):
        near, far = (ref[rows, :] for ref in self.refs)
        return jnp.where(self.even, far, near), jnp.where(self.even, near, far)

    def tiles(self, x):
        return self.both(pl.ds(pl.multiple_of(8 * x, 8), 8))

    def pick(self, tiles, name, low_at=(G - 1,), high_at=(0,)):
        low, high = tiles
        if name != "b":
            up, down = Y_TURNS[name]
            low, high = pltpu.roll(low, 8 - up, 0), pltpu.roll(high, 8 - down, 0)
        picked = jnp.zeros_like(low)
        for place in low_at:
            picked = jnp.where(self.s == place, low, picked)
        for place in high_at:
            picked = jnp.where(self.s == place, high, picked)
        return picked

    def row(self, at, low_at=G - 1, high_at=0):
        low, high = self.both(pl.ds(at, 1))
        return jnp.where(self.s == low_at, low, jnp.where(self.s == high_at, high, 0.0))

    def active(self, x):
        return self.pick(self.tiles(x), "a")

    def first_active(self):
        return self.active(0) + self.row(10 * self.n + 1, G - 2, 1)

    def last_trans(self):
        return self.row(10 * self.n, G - 2, 1)

    def frac(self, x):
        return self.row(9 * self.n + x)

    def lower(self, q):
        return self.row(10 * self.n + 2 + q)


def prep_kernel(res_hbm, diag_hbm, crs, mask_hbm, tx_hbm, ty_hbm, tz_hbm,
                rhs, own_diag, tot, gain, one, fx, fy, fz, al0, al1, be0, be1, fzb,
                res, diag, mask, tx, ty, tz, sems):
    n, own, wide = mask.shape
    groups = own // 8
    chunk = 4
    s, lane = places(wide)

    def copies(q):
        at = pl.ds(chunk * q, chunk)
        pairs = (
            (res_hbm.at[:, at], res.at[:, at]),
            (diag_hbm.at[:, at], diag.at[:, at]),
            (tx_hbm.at[at], tx.at[at]),
            (ty_hbm.at[at], ty.at[at]),
            (tz_hbm.at[at], tz.at[at]),
        )
        return [pltpu.make_async_copy(a, b, sems.at[k + 1, q]) for k, (a, b) in enumerate(pairs)]

    def masks(q):
        at = pl.ds(chunk * q, chunk)
        return pltpu.make_async_copy(mask_hbm.at[at], mask.at[at], sems.at[0, q])

    for q in range(n // chunk):
        for copy in (masks(q), *copies(q)):
            copy.start()
    masks(0).wait()

    def row(x, carry):
        first, last = x == 0, x == n - 1
        after = jnp.minimum(x + 1, n - 1)
        before = jnp.maximum(x - 1, 0)
        a_after = mask[x, group(0), :].astype(F32)
        turned_after = turn_next(a_after)
        ey_before = jnp.zeros((G, wide), F32)
        for k in range(groups):
            here = group(k)
            a, turned = a_after, turned_after
            rp, rs = res[0, x, here, :], res[1, x, here, :]
            dpp, dss = diag[0, x, here, :], diag[1, x, here, :]
            dps, dsp = crs[0, x, here, :], crs[1, x, here, :]
            det = dpp * dss - dps * dsp
            both = 1.0 / (dss * det)
            inverse = both * dss
            weight = dps * (both * det)
            b = a * (rp - weight * rs)
            c = a * (dpp - weight * dsp) + (1.0 - a)
            rhs[x, here, :] = b
            own_diag[x, here, :] = c
            al0[x, here, :] = dss * inverse
            al1[x, here, :] = dps * inverse
            be0[x, here, :] = dpp * inverse
            be1[x, here, :] = dsp * inverse
            t = tx[x, here, :] * a
            ex = t * mask[after, here, :].astype(F32)
            fx[x, here, :] = jnp.where(last, t, ex)
            total = c + jnp.where(last, 0.0, ex)
            total = total + jnp.where(first, 0.0, fx[before, here, :])
            ez = along_z(tz[x, here, :], a, lane)
            fz[x, here, :] = ez
            ez_before = z_prev(ez)
            fzb[x, here, :] = ez_before
            total = total + ez + ez_before
            ey = ty[x, here, :] * a
            if k < groups - 1:
                a_after = mask[x, group(k + 1), :].astype(F32)
                turned_after = turn_next(a_after)
                ey = ey * turned_next(turned, turned_after, s)
                inside = ey
            else:
                ey = jnp.where(s == G - 1, ey, ey * turned)
                inside = jnp.where(s == G - 1, 0.0, ey)
            fy[x, here, :] = ey
            ey_turned = turn_prev(inside)
            total = total + inside + turned_prev(ey_turned, ey_before, s)
            ey_before = ey_turned
            tot[x, here, :] = total
            if 0 < k < groups - 1:
                g = relaxation / total
                gain[x, here, :] = g
                one[x, here, :] = g * b
        return carry

    def part(q, carry):
        @pl.when(q < n // chunk - 1)
        def _():
            masks(q + 1).wait()

        for copy in copies(q):
            copy.wait()
        return lax.fori_loop(0, chunk, lambda k, v: row(chunk * q + k, v), carry, unroll=2)

    lax.fori_loop(0, n // chunk, part, 0)


class Finished:
    def __init__(self, x, n, ghosts, mask, rhs, tot, fx, fy, s, lane, ex_before=None):
        groups = mask.shape[1] // 8
        first, last = x == 0, x == n - 1
        tiles = ghosts.tiles(x)
        ga, gtx, gtz = (ghosts.pick(tiles, name) for name in ("a", "tx", "tz"))
        gb = ghosts.pick(tiles, "b", (G - 1, G - 2), (0, 1))
        gc = jnp.maximum(ghosts.pick(tiles, "c", (G - 1, G - 2), (0, 1)), 1.0)
        before, after = jnp.maximum(x - 1, 0), jnp.minimum(x + 1, n - 1)
        if ex_before is None:
            tiles_before = ghosts.tiles(before)
            ex_before = ghosts.pick(tiles_before, "a") * ghosts.pick(tiles_before, "tx") * ga
            ex_before = jnp.where(first, 0.0, ex_before)
        a_after = ghosts.active(after)
        end = fy[x, group(groups - 1), :]
        end = jnp.where(s == G - 1, end * turn_next(ga), end)
        a_first = turn_next(mask[x, group(0), :].astype(F32))
        ey = ghosts.pick(tiles, "e", (G - 2,), (0,))
        ey = jnp.where(s == G - 1, ghosts.row(8 * n + x) * a_first, ey)
        ey_turned = turn_prev(ey)
        ez = along_z(gtz, ga, lane)
        t = gtx * ga
        ex = t * a_after
        total = gc + ez + z_prev(ez) + ey + turned_prev(ey_turned, turn_prev(end), s)
        total = total + jnp.where(last, 0.0, ex) + ex_before
        self.ex = ex
        self.end = end
        self.fx, self.fy, self.fz = jnp.where(last, t + ghosts.last_trans(), ex), ey, ez
        self.rhs = gb
        self.total = (
            tot[x, group(0), :] + jnp.where(s == 0, ey_turned, 0.0),
            tot[x, group(groups - 1), :] + jnp.where(s == G - 1, end, 0.0),
            total,
        )
        self.all_rhs = (rhs[x, group(0), :], rhs[x, group(groups - 1), :], gb)


def slot_of(k, groups):
    return {0: 0, groups - 1: 1, groups: 2}[k]


def x_message_kernel(mask, rhs, tot, gain, one, fx, fy, fz, ynear, yfar, near_ref, far_ref):
    even = lax.rem(lax.axis_index("gx"), 2) == 0
    n, own, wide = mask.shape
    groups = own // 8
    s, lane = places(wide)
    ghosts = Ghosts(ynear, yfar, n)
    finished = {x: Finished(x, n, ghosts, mask, rhs, tot, fx, fy, s, lane) for x in (0, 1, n - 2, n - 1)}
    for k in range(groups + 1):
        here = group(k)
        touched = k in (0, groups - 1, groups)

        def first_of(x):
            done = finished[x]
            if not touched:
                return one[x, here, :]
            slot = slot_of(k, groups)
            return relaxation * done.all_rhs[slot] / done.total[slot]

        def of(x, key):
            done = finished[x]
            total = done.total[slot_of(k, groups)] if touched else tot[x, here, :]
            if k == groups:
                return done.rhs, total, key, done.fy
            return rhs[x, here, :], total, key, done.end if k == groups - 1 else fy[x, here, :]

        if k == groups:
            up = of(n - 1, finished[n - 1].fx)
            down = of(0, ghosts.first_active())
        else:
            up = of(n - 1, fx[n - 1, here, :])
            down = of(0, mask[0, here, :].astype(F32))
            up += (fz[n - 1, here, :], fx[n - 2, here, :] * first_of(n - 2))
            down += (fz[0, here, :], fx[0, here, :] * first_of(1))
        if k == groups:
            b, total, key, ey = (jnp.where(even, p, q) for p, q in zip(up, down, strict=True))
            ob, ototal, okey, oey = (jnp.where(even, q, p) for p, q in zip(up, down, strict=True))
            for ref, (b, total, key, ey) in (
                (near_ref, (b, total, key, ey)),
                (far_ref, (ob, ototal, okey, oey)),
            ):
                at = PLANES * own
                ref[at : at + G, :] = jnp.where((s == 0) | (s == G - 1), b, pltpu.roll(total, 4, 0))
                ref[at + G : at + 2 * G, :] = jnp.where((s < 2) | (s >= G - 2), key, pltpu.roll(ey, 4, 0))
        else:
            for f in range(PLANES):
                start = f * own + 8 * k
                near_ref[start : start + 8, :] = jnp.where(even, up[f], down[f])
                far_ref[start : start + 8, :] = jnp.where(even, down[f], up[f])


def late_messages(split_ref, ff, inv, near_ref, far_ref):
    even = lax.rem(lax.axis_index("gx"), 2) == 0
    j = lax.axis_index("gy")
    n, own, wide = ff.shape
    per_tile = 2 * split_ref.shape[0] * split_ref.shape[1]
    near_ref[0:own, :] = jnp.where(even, ff[n - 1], ff[0])
    far_ref[0:own, :] = jnp.where(even, ff[0], ff[n - 1])
    at = own
    unknowns = inv.shape[2]
    top = inv[0, pl.ds(pl.multiple_of(j * per_tile + per_tile - 16, 8), 16), :]
    bottom = inv[0, pl.ds(pl.multiple_of(j * per_tile, 8), 16), :]
    for k in range(0, unknowns, wide):
        w = min(wide, unknowns - k)
        if w < wide:
            near_ref[at : at + 16, :] = jnp.zeros((16, wide), F32)
            far_ref[at : at + 16, :] = jnp.zeros((16, wide), F32)
        near_ref[at : at + 16, :w] = jnp.where(even, top[:, k : k + w], bottom[:, k : k + w])
        far_ref[at : at + 16, :w] = jnp.where(even, bottom[:, k : k + w], top[:, k : k + w])
        at += 16
    lane = lax.broadcasted_iota(jnp.int32, (1, wide), 1)
    zero = jnp.zeros((8, wide), F32)
    near_ref[at : at + 8, :] = zero
    far_ref[at : at + 8, :] = zero
    for q in range(split_ref.shape[1]):
        top = (lane < split_ref[split_ref.shape[0] - 1, q]).astype(F32)
        bottom = (lane < split_ref[0, q]).astype(F32)
        near_ref[at + q : at + q + 1, :] = jnp.where(even, top, bottom)
        far_ref[at + q : at + q + 1, :] = jnp.where(even, bottom, top)


def late_rows(own, unknowns, wide):
    return own + 16 * pl.cdiv(unknowns, wide) + 8


class Planes:
    def __init__(self, near_ref, far_ref, own):
        self.refs, self.own = (near_ref, far_ref), own
        self.even = lax.rem(lax.axis_index("gx"), 2) == 0

    def rows(self, at, n, side):
        near, far = (ref[at : at + n, :] for ref in self.refs)
        return jnp.where(self.even, near, far) if side else jnp.where(self.even, far, near)

    def field(self, f, k, side):
        if 8 * k < self.own:
            return self.rows(f * self.own + 8 * k, 8, side)
        s, _ = places(self.refs[0].shape[1])
        ends = (s == 0) | (s == G - 1)
        if f < 2:
            tile = self.rows(PLANES * self.own, G, side)
            return jnp.where(ends, pltpu.roll(tile, 4, 0) if f else tile, 0.0)
        if f < 4:
            tile = self.rows(PLANES * self.own + G, G, side)
            if f == 2:
                return jnp.where((s < 2) | (s >= G - 2), tile, 0.0)
            return jnp.where(s == G - 1, pltpu.roll(tile, 4, 0), 0.0)
        return jnp.zeros_like(s, F32)


class Inside:
    def __init__(self, groups, ff, rhs, gain, one, fx, fy, fz, gain3, one3, six, end):
        self.groups, self.own_ff, self.own_rhs = groups, ff, rhs
        self.own_gain, self.own_one, self.own_fx, self.own_fy, self.own_fz = gain, one, fx, fy, fz
        self.gain3, self.one3, self.six, self.end = gain3, one3, six, end

    def pick(self, own, which, x, k):
        return self.six[which, x] if k == self.groups else own[x, group(k), :]

    def three(self, own, other, x, k):
        if 0 < k < self.groups - 1:
            return own[x, group(k), :]
        return other[x, group(slot_of(k, self.groups)), :]

    def rhs(self, x, k):
        return self.pick(self.own_rhs, 0, x, k)

    def fx(self, x, k):
        return self.pick(self.own_fx, 1, x, k)

    def fy(self, x, k):
        if k == self.groups - 1:
            return self.end[x]
        return self.pick(self.own_fy, 2, x, k)

    def fz(self, x, k):
        return self.pick(self.own_fz, 3, x, k)

    def ff(self, x, k):
        return self.pick(self.own_ff, 4, x, k)

    def gain(self, x, k):
        return self.three(self.own_gain, self.gain3, x, k)

    def one(self, x, k):
        return self.three(self.own_one, self.one3, x, k)

    def before(self, x, k):
        return self.fx(x - 1, k) * self.one(x - 1, k)

    def after(self, x, k):
        return self.fx(x, k) * self.one(x + 1, k)

    def faces_x(self, x, k):
        ex = self.fx(x, k)
        return ex, ex * (self.ff(x, k) + self.ff(x + 1, k))


def second_row(o, x, s, put):
    total = o.groups + 1
    p = o.one(x, 0)
    p_turned = turn_next(p)
    w_turned = turn_prev(o.fy(x, total - 1) * o.one(x, total - 1))
    for k in range(total):
        p_after = o.one(x, (k + 1) % total)
        after_turned = turn_next(p_after)
        ey, ez = o.fy(x, k), o.fz(x, k)
        mine = turn_prev(ey * p)
        beside = ey * turned_next(p_turned, after_turned, s) + turned_prev(mine, w_turned, s)
        beside = beside + ez * z_next(p) + z_prev(ez * p)
        beside = beside + o.after(x, k) + o.before(x, k)
        put(k, o.gain(x, k) * ((2.0 - relaxation) * o.rhs(x, k) + beside))
        p, p_turned, w_turned = p_after, after_turned, mine


def x_flux(o, x, k, two):
    step = two(x + 1, k) - two(x, k)
    ex, wx = o.faces_x(x, k)
    return ex * step, wx * step


def flux_row(o, x, s, lane, two, res, own_diag, fzb, split, carried, put):
    groups = o.groups

    def faces_y(k, p, p_turned, p_after, f, f_turned, f_after):
        ey = o.fy(x, k)
        weighted = ey * (f + turned_next(f_turned, f_after, s))
        return ey, weighted, turned_next(p_turned, p_after, s) - p

    p0, f0 = two(x, 0), o.ff(x, 0)
    p0_turned, f0_turned = turn_next(p0), turn_next(f0)
    p, f = two(x, groups), o.ff(x, groups)
    ghost = faces_y(groups, p, turn_next(p), p0_turned, f, turn_next(f), f0_turned)
    turned = [turn_prev(v) for v in ghost]
    p, f, p_turned, f_turned = p0, f0, p0_turned, f0_turned
    for k in range(groups):
        here = group(k)
        p_after, f_after = two(x, k + 1), o.ff(x, k + 1)
        p_after_turned, f_after_turned = turn_next(p_after), turn_next(f_after)
        mine = faces_y(k, p, p_turned, p_after_turned, f, f_turned, f_after_turned)
        mine_turned = [turn_prev(v) for v in mine]
        ey, wy, dy = mine
        ey_before, wy_before, dy_before = (
            turned_prev(a, b, s) for a, b in zip(mine_turned, turned, strict=True)
        )
        ez = o.fz(x, k)
        wz = ez * (f + z_next(f))
        dz = z_next(p) - p
        wz_before, dz_before = z_prev(wz), z_prev(dz)
        ez_before = fzb[x, here, :]
        qx, sx = x_flux(o, x, k, two)
        if carried is None:
            qx_before, sx_before = x_flux(o, x - 1, k, two)
        else:
            qx_before, sx_before = carried[0, here, :], carried[1, here, :]
            carried[0, here, :] = qx
            carried[1, here, :] = sx
        gained = (qx - qx_before) + (ey * dy - ey_before * dy_before)
        gained = gained + (ez * dz - ez_before * dz_before)
        weighed = (sx - sx_before) + (wy * dy - wy_before * dy_before)
        weighed = weighed + (wz * dz - wz_before * dz_before)
        rest = o.rhs(x, k) - own_diag[x, here, :] * p + gained
        below = lane < split(k)
        put(
            k,
            rest,
            res[0, x, here, :] + gained,
            res[1, x, here, :] + 0.5 * weighed,
            jnp.where(s == 0, ey_before, ey),
            jnp.where(s == 0, wy_before, wy),
            jnp.where(below, ez, ez_before),
            jnp.where(below, wz, wz_before),
        )
        turned = mine_turned
        p, f, p_turned, f_turned = p_after, f_after, p_after_turned, f_after_turned


FLUXES = 6


def interior_kernel(split_ref, inv, fzb, res, mask, ff, rhs, own_diag, tot, gain, one, fx, fy, fz, ynear, yfar,
                    late_near, late_far, tot3, gain3, one3, six, end, two, acc, *flux_and_carried):
    flux, carried = flux_and_carried[:FLUXES], flux_and_carried[FLUXES]
    late_messages(split_ref, ff, inv, late_near, late_far)
    n, own, wide = mask.shape
    groups = own // 8
    s, lane = places(wide)
    ghosts = Ghosts(ynear, yfar, n)

    def finish(x, carry):
        done = Finished(x, n, ghosts, mask, rhs, tot, fx, fy, s, lane, carry)
        for slot in range(3):
            g = relaxation / done.total[slot]
            tot3[x, group(slot), :] = done.total[slot]
            gain3[x, group(slot), :] = g
            one3[x, group(slot), :] = g * done.all_rhs[slot]
        end[x] = done.end
        for k, v in enumerate((done.rhs, done.fx, done.fy, done.fz, ghosts.frac(x))):
            six[k, x] = v
        return done.ex

    lax.fori_loop(0, n, finish, jnp.zeros((G, wide), F32), unroll=8)
    o = Inside(groups, ff, rhs, gain, one, fx, fy, fz, gain3, one3, six, end)

    def second(x, carry):
        def put(k, v):
            two[x, group(k), :] = v

        second_row(o, x, s, put)
        return carry

    lax.fori_loop(2, n - 2, second, 0, unroll=4)

    def two_of(x, k):
        return two[x, group(k), :]

    for k in range(groups):
        carried[0, group(k), :], carried[1, group(k), :] = x_flux(o, 2, k, two_of)
    acc[...] = jnp.zeros_like(acc)

    def row(x, carry):
        def put(k, rest, *values):
            acc[x // 8, group(k), :] += rest
            for f, v in enumerate(values):
                flux[f][x, group(k), :] = v

        flux_row(o, x, s, lane, two_of, res, own_diag, fzb, lambda k: split_ref[x // 8, k], carried, put)
        return carry

    lax.fori_loop(3, n - 3, row, 0, unroll=2)


class Edges(Inside):
    def beyond(self, n, planes, act, tot, tot3, one_edge, gain_edge, edge_fx):
        self.n, self.planes = n, planes
        self.slots = {-1: 0, 0: 1, n - 1: 2, n: 3}
        self.one_edge, self.gain_edge, self.edge_fx = one_edge, gain_edge, edge_fx
        self.far = {-1: 0, n: 1}
        for k in range(self.groups + 1):
            here = group(k)
            low = planes.field(2, k, 0) * act(k)
            high = super().fx(n - 1, k) * planes.field(2, k, 1)
            edge_fx[0, here, :] = low
            edge_fx[1, here, :] = high
            for x, slot in self.slots.items():
                face = low if x <= 0 else high
                if x in self.far:
                    total = jnp.maximum(planes.field(1, k, self.far[x]), 1.0) + face
                else:
                    total = self.three(tot, tot3, x, k) + face
                g = relaxation / total
                gain_edge[slot, here, :] = g
                one_edge[slot, here, :] = g * self.rhs(x, k)

    def rhs(self, x, k):
        return self.planes.field(0, k, self.far[x]) if x in self.far else super().rhs(x, k)

    def fx(self, x, k):
        if x in (-1, self.n - 1):
            return self.edge_fx[0 if x == -1 else 1, group(k), :]
        return super().fx(x, k)

    def fy(self, x, k):
        return self.planes.field(3, k, self.far[x]) if x in self.far else super().fy(x, k)

    def fz(self, x, k):
        return self.planes.field(4, k, self.far[x]) if x in self.far else super().fz(x, k)

    def gain(self, x, k):
        return self.gain_edge[self.slots[x], group(k), :] if x in self.slots else super().gain(x, k)

    def one(self, x, k):
        return self.one_edge[self.slots[x], group(k), :] if x in self.slots else super().one(x, k)

    def before(self, x, k):
        return self.planes.field(5, k, 0) if x == -1 else super().before(x, k)

    def after(self, x, k):
        return self.planes.field(5, k, 1) if x == self.n else super().after(x, k)


def edge_kernel(split_ref, fzb, res, mask, ff, rhs, own_diag, tot, gain, one, fx, fy, fz, ynear, yfar, xnear, xfar,
                tot3, gain3, one3, six, end, two, acc, *others):
    flux = others[FLUXES : 2 * FLUXES]
    sent, edge_fx, edge_step, one_edge, gain_edge, two_edge, near_fx, total_acc = others[2 * FLUXES :]
    n, own, wide = mask.shape
    groups = own // 8
    s, lane = places(wide)
    planes = Planes(xnear, xfar, own)
    ghosts = Ghosts(ynear, yfar, n)
    o = Edges(groups, ff, rhs, gain, one, fx, fy, fz, gain3, one3, six, end)

    def act(k):
        return ghosts.first_active() if k == groups else mask[0, group(k), :].astype(F32)

    o.beyond(n, planes, act, tot, tot3, one_edge, gain_edge, edge_fx)
    depth = 5
    bases = (-1, n - depth + 1)
    for side, base in enumerate(bases):
        for r in range(depth):
            x, slot = base + r, depth * side + r
            if x in (-1, 0, 1, n - 2, n - 1, n):

                def put_two(k, v, slot=slot):
                    two_edge[slot, group(k), :] = v

                second_row(o, x, s, put_two)
            else:
                two_edge[slot] = two[x]
            if x == n:
                continue
            for k in range(groups):
                ex = o.fx(x, k)
                near_fx[0, slot, group(k), :] = ex
                if x in (-1, n - 1):
                    near_fx[1, slot, group(k), :] = jnp.zeros_like(ex)
                else:
                    near_fx[1, slot, group(k), :] = ex * (o.ff(x, k) + o.ff(x + 1, k))
    for k in range(groups):
        edge_step[0, group(k), :] = two_edge[1, group(k), :] - two_edge[0, group(k), :]
        edge_step[1, group(k), :] = two_edge[2 * depth - 1, group(k), :] - two_edge[2 * depth - 2, group(k), :]
    total_acc[...] = acc[...]
    plain = Inside(groups, ff, rhs, gain, one, fx, fy, fz, gain3, one3, six, end)

    def row(r, carry):
        high = r >= depth - 2
        x = jnp.where(high, n - 2 * (depth - 2) + r, r)
        shift = jnp.where(high, depth - bases[1], -bases[0])

        def two_of(x, k):
            return two_edge[x + shift, group(k), :]

        def faces_x(x, k):
            return near_fx[0, x + shift, group(k), :], near_fx[1, x + shift, group(k), :]

        plain.faces_x = faces_x

        def put(k, rest, *values):
            total_acc[x // 8, group(k), :] += rest
            for f, v in enumerate(values):
                flux[f][x, group(k), :] = v

        flux_row(plain, x, s, lane, two_of, res, own_diag, fzb, lambda k: split_ref[x // 8, k], None, put)
        return carry

    lax.fori_loop(0, 2 * (depth - 2), row, 0, unroll=2)

    rows_b, cols_b = split_ref.shape
    lane = lax.broadcasted_iota(jnp.int32, (1, wide), 1)
    lower, upper = [], []
    for q in range(rows_b):
        for r in range(cols_b):
            column = jnp.sum(total_acc[q, group(r), :], axis=0, keepdims=True)
            below = lane < split_ref[q, r]
            lower.append(jnp.where(below, column, 0.0))
            upper.append(jnp.where(below, 0.0, column))
    count = rows_b * cols_b
    low_sum = jnp.sum(jnp.concatenate(lower, axis=0), axis=1, keepdims=True)
    high_sum = jnp.sum(jnp.concatenate(upper, axis=0), axis=1, keepdims=True)
    span = sent.shape[1]
    place = lax.broadcasted_iota(jnp.int32, (count, span), 1) - 2 * count * lax.axis_index("gy")
    which = 2 * lax.broadcasted_iota(jnp.int32, (count, span), 0)
    laid = jnp.where(place == which, low_sum, jnp.where(place == which + 1, high_sum, 0.0))
    sent[...] = jnp.broadcast_to(jnp.sum(laid, axis=0, keepdims=True), sent.shape)


def final_kernel(tiles_y, split_ref, frac, inv, ynear, yfar, xnear, xfar, fx, edge_fx, edge_step,
                 al0, al1, be0, be1, got, *rest):
    flux = rest[:FLUXES]
    out, coarse, step_y, step_z, across, held, sems = rest[FLUXES:]
    i, j = lax.axis_index("gx"), lax.axis_index("gy")
    n, own, wide = frac.shape
    ext = own + G
    unknowns = inv.shape[2]
    rows_b, cols_b = split_ref.shape
    per_tile = 2 * rows_b * cols_b
    ghosts = Ghosts(ynear, yfar, n)
    planes = Planes(xnear, xfar, own)
    s8, lane8 = places(wide)

    all_got = got[...]
    owner = lax.broadcasted_iota(jnp.int32, all_got.shape, 0)

    def row_of(tile_row):
        mine = (owner >= tile_row * tiles_y) & (owner < (tile_row + 1) * tiles_y)
        return jnp.sum(jnp.where(mine, all_got, 0.0), axis=0, keepdims=True)

    coarse_res = row_of(i)

    def solve(tile):
        start = pl.multiple_of(jnp.clip(tile, 0, tiles_y - 1) * per_tile, 8)
        block = inv[0, pl.ds(start, per_tile), :]
        e = jnp.sum(block * coarse_res[:, :unknowns], axis=1, keepdims=True)
        return jnp.broadcast_to(e, (per_tile, wide))

    mine, before, after = solve(j), solve(j - 1), solve(j + 1)

    def one_of(e, k):
        return jnp.broadcast_to(e[k : k + 1], (8, wide))

    for q in range(rows_b):
        for r in range(cols_b):
            k = 2 * (q * cols_b + r)
            low, high = one_of(mine, k), one_of(mine, k + 1)
            split = split_ref[q, r]
            coarse[q + 1, group(r), :] = jnp.where(lane8 < split, low, high)
            jump = high - low
            step_z[q, group(r), :] = jnp.where(
                lane8 == split - 1, jump, jnp.where(lane8 == split, -jump, 0.0)
            )
        below = ghosts.lower(q) > 0.5
        k_high, k_low = 2 * q * cols_b, 2 * (q * cols_b + cols_b - 1)
        coarse[q + 1, own:ext, :] = jnp.where(
            s8 == 0,
            jnp.where(below, one_of(after, k_high), one_of(after, k_high + 1)),
            jnp.where(below, one_of(before, k_low), one_of(before, k_low + 1)),
        )
        for r in range(cols_b):
            here = coarse[q + 1, group(r), :]
            ahead = turn_next(coarse[q + 1, group(r + 1), :])
            behind = turn_prev(coarse[q + 1, group(r - 1 if r else cols_b), :])
            step_y[q, group(r), :] = jnp.where(
                s8 == G - 1, ahead - here, jnp.where(s8 == 0, behind - here, 0.0)
            )
    blocks = pl.cdiv(unknowns, wide)
    for side, tile_row in ((0, i - 1), (1, i + 1)):
        other = row_of(tile_row)
        e = jnp.zeros((16, 1), F32)
        for k in range(blocks):
            w = min(wide, unknowns - k * wide)
            part = planes.rows(own + 16 * k, 16, side)[:, :w] * other[:, k * wide : k * wide + w]
            e = e + jnp.sum(part, axis=1, keepdims=True)
        e = jnp.broadcast_to(e, (16, wide))
        below = planes.rows(own + 16 * blocks, 8, side)
        skip = 16 - 2 * cols_b if side == 0 else 0
        at = 0 if side == 0 else rows_b + 1
        for r in range(cols_b):
            k = skip + 2 * r
            coarse[at, group(r), :] = jnp.where(one_of(below, r) > 0.5, one_of(e, k), one_of(e, k + 1))

    for q in range(rows_b + 1):
        x = 8 * q - 1
        for r in range(cols_b):
            here = group(r)
            ex = edge_fx[0, here, :] if q == 0 else edge_fx[1, here, :] if q == rows_b else fx[x, here, :]
            f_before = planes.rows(8 * r, 8, 0) if q == 0 else frac[x, here, :]
            f_after = planes.rows(8 * r, 8, 1) if q == rows_b else frac[x + 1, here, :]
            step = coarse[q + 1, here, :] - coarse[q, here, :]
            across[0, q, here, :] = ex * step
            if q in (0, rows_b):
                step = step + edge_step[0 if q == 0 else 1, here, :]
            across[1, q, here, :] = ex * (0.5 * (f_before + f_after)) * step

    def solved(x, q, beside=None, sign=None):
        for r in range(cols_b):
            here = group(r)
            u, v, wy, sy, wz, sz = (ref[x, here, :] for ref in flux)
            along_y, along_z = step_y[q, here, :], step_z[q, here, :]
            u = u + (wy * along_y + wz * along_z)
            v = v + 0.5 * (sy * along_y + sz * along_z)
            if beside is not None:
                u = sign(u, across[0, beside, here, :])
                v = sign(v, across[1, beside, here, :])
            held[0, x, here, :] = al0[x, here, :] * u - al1[x, here, :] * v
            held[1, x, here, :] = be0[x, here, :] * v - be1[x, here, :] * u

    def copies(q):
        return [
            pltpu.make_async_copy(
                held.at[k, pl.ds(4 * q, 4)], out.at[k, pl.ds(4 * q, 4)], sems.at[k, q]
            )
            for k in range(2)
        ]

    def block(q, carry):
        x = 8 * q
        solved(x, q, q, jnp.subtract)
        for k in range(1, 4):
            solved(x + k, q)
        for copy in copies(2 * q):
            copy.start()
        for k in range(4, 7):
            solved(x + k, q)
        solved(x + 7, q, q + 1, jnp.add)
        for copy in copies(2 * q + 1):
            copy.start()
        return carry

    lax.fori_loop(0, rows_b, block, 0)
    for q in range(2 * rows_b):
        for copy in copies(q):
            copy.wait()


def shards(tiles_x, tiles_y, residual, accum_diag, accum_cross, mask, trans_x, trans_y, trans_z,
           frac_flow, split_layer, coarse_inverse):
    n, own, wide = mask.shape
    ext = own + G
    unknowns = coarse_inverse.shape[2]
    columns = (residual, accum_diag, accum_cross, mask, trans_x, trans_y, trans_z, frac_flow)
    hbm = pl.BlockSpec(memory_space=pltpu.HBM)
    far_columns = [pltpu.with_memory_space_constraint(v, pltpu.HBM) for v in columns]

    def array(*shape):
        return jax.ShapeDtypeStruct(shape, F32)

    def group_spec(k, f):
        if f in (3, 4):
            return pl.BlockSpec((n, G, wide), lambda x: (0, k, 0))
        lead = columns[f].shape[:-3]
        return pl.BlockSpec((*lead, STEP, G, wide), lambda x: (*(0,) * len(lead), x, k, 0))

    y_messages = pl.pallas_call(
        y_message_kernel,
        grid=(n // STEP,),
        in_specs=[pl.BlockSpec(split_layer.shape, lambda x: (0, 0))]
        + [group_spec(0, f) for f in range(8)]
        + [group_spec(own // 8 - 1, f) for f in range(8)],
        out_specs=[WHOLE] * 2,
        out_shape=[array(y_message_rows(n), wide)] * 2,
        compiler_params=params(16),
        name="y_messages",
    )(pltpu.with_memory_space_constraint(split_layer, pltpu.HBM), *far_columns, *far_columns)
    ynear, yfar = swap(y_messages, "gy", tiles_y)

    rhs, own_diag, tot, gain, one, fx, fy, fz, al0, al1, be0, be1, fzb = pl.pallas_call(
        prep_kernel,
        in_specs=[hbm] * 2 + [WHOLE] + [hbm] * 4,
        out_specs=[WHOLE] * 13,
        out_shape=[array(n, own, wide)] * 13,
        scratch_shapes=[pltpu.VMEM(v.shape, v.dtype) for v in columns[:2] + columns[3:7]]
        + [pltpu.SemaphoreType.DMA((6, n // 4))],
        compiler_params=params(16),
        cost_estimate=cost(60_000_000, 30_000_000),
        name="prep",
    )(*far_columns[:2], accum_cross, *far_columns[3:7])
    shared = (rhs, tot, gain, one, fx, fy, fz)

    x_messages = pl.pallas_call(
        x_message_kernel,
        in_specs=[WHOLE] * 10,
        out_specs=[WHOLE] * 2,
        out_shape=[array(PLANES * own + 2 * G, wide)] * 2,
        compiler_params=params(8),
        name="x_messages",
    )(mask, *shared, ynear, yfar)
    xnear, xfar = swap(x_messages, "gx", tiles_x)

    shared = (residual, mask, frac_flow, rhs, own_diag, tot, gain, one, fx, fy, fz, ynear, yfar)
    late_near, late_far, tot3, gain3, one3, six, end, two, acc, *flux = pl.pallas_call(
        interior_kernel,
        in_specs=[SCALARS] + [WHOLE] * 15,
        out_specs=[WHOLE] * (9 + FLUXES),
        out_shape=[array(late_rows(own, unknowns, wide), wide)] * 2
        + [array(n, 3 * G, wide)] * 3
        + [
            array(5, n, G, wide),
            array(n, G, wide),
            array(n, ext, wide),
            array(n // 8, own, wide),
        ]
        + [array(n, own, wide)] * FLUXES,
        scratch_shapes=[pltpu.VMEM((2, own, wide), F32)],
        compiler_params=params(8),
        cost_estimate=cost(60_000_000, 30_000_000),
        name="interior",
    )(split_layer, coarse_inverse, fzb, *shared)
    late_near, late_far = swap((late_near, late_far), "gx", tiles_x)

    devices = tiles_x * tiles_y
    span = pl.cdiv(unknowns, 128) * 128
    *flux, sent, edge_fx, edge_step = pl.pallas_call(
        edge_kernel,
        in_specs=[SCALARS] + [WHOLE] * (23 + FLUXES),
        out_specs=[WHOLE] * (3 + FLUXES),
        out_shape=[array(n, own, wide)] * FLUXES
        + [
            array(devices, span),
            array(2, ext, wide),
            array(2, own, wide),
        ],
        scratch_shapes=[
            pltpu.VMEM((4, ext, wide), F32),
            pltpu.VMEM((4, ext, wide), F32),
            pltpu.VMEM((10, ext, wide), F32),
            pltpu.VMEM((2, 10, own, wide), F32),
            pltpu.VMEM((n // 8, own, wide), F32),
        ],
        input_output_aliases={24 + f: f for f in range(FLUXES)},
        compiler_params=params(8),
        name="edges",
    )(split_layer, fzb, *shared, xnear, xfar, tot3, gain3, one3, six, end, two, acc, *flux)
    got = lax.all_to_all(sent, ("gx", "gy"), 0, 0, tiled=True)

    return pl.pallas_call(
        functools.partial(final_kernel, tiles_y),
        in_specs=[SCALARS] + [WHOLE] * (14 + FLUXES),
        out_specs=pl.BlockSpec(memory_space=pl.ANY),
        out_shape=array(2, n, own, wide),
        scratch_shapes=[
            pltpu.VMEM((n // 8 + 2, ext, wide), F32),
            pltpu.VMEM((n // 8, own, wide), F32),
            pltpu.VMEM((n // 8, own, wide), F32),
            pltpu.VMEM((2, n // 8 + 1, own, wide), F32),
            pltpu.VMEM((2, n, own, wide), F32),
            pltpu.SemaphoreType.DMA((2, n // 4)),
        ],
        compiler_params=params(12),
        name="final",
    )(split_layer, frac_flow, coarse_inverse, ynear, yfar, late_near, late_far, fx, edge_fx,
      edge_step, al0, al1, be0, be1, got, *flux)


def solution(mesh):
    placed = (
        P(None, "gx", "gy", None),
        P(None, "gx", "gy", None),
        P(None, "gx", "gy", None),
        P("gx", "gy", None),
        P("gx", "gy", None),
        P("gx", "gy", None),
        P("gx", "gy", None),
        P("gx", "gy", None),
        P("gx", "gy"),
        P("gx", None, None),
    )
    return jax.shard_map(
        functools.partial(shards, mesh.shape["gx"], mesh.shape["gy"]),
        mesh=mesh,
        in_specs=placed,
        out_specs=P(None, "gx", "gy", None),
        check_vma=False,
    )
```

```python
import functools

import jax
import jax.numpy as jnp
from jax import lax
from jax.experimental import pallas as pl
from jax.experimental.pallas import tpu as pltpu
from jax.sharding import PartitionSpec as P

relaxation = 2.0 / 3.0
F32 = jnp.float32
WHOLE = pl.BlockSpec(memory_space=pltpu.VMEM)
SCALARS = pl.BlockSpec(memory_space=pltpu.SMEM)
G = 8
STEP = 16
PLANES = 6


def params(mib):
    return pltpu.CompilerParams(vmem_limit_bytes=mib << 20)


def cost(flops, size):
    return pl.CostEstimate(flops=flops, bytes_accessed=size, transcendentals=0)


def z_next(v):
    return pltpu.roll(v, v.shape[1] - 1, 1)


def z_prev(v):
    return pltpu.roll(v, 1, 1)


def quasi_impes(active, rp, rs, dpp, dss, dps, dsp):
    weight = dps / dss
    return active * (rp - weight * rs), active * (dpp - weight * dsp) + (1.0 - active)


def swap_pairs(axis, size):
    near = [(i, i ^ 1) for i in range(size) if i ^ 1 < size]
    far = [(i, ((i + 1) ^ 1) - 1) for i in range(size) if 0 <= ((i + 1) ^ 1) - 1 < size]
    return near, far


def swap(message, axis, size):
    near, far = swap_pairs(axis, size)
    return lax.ppermute(message[0], axis, near), lax.ppermute(message[1], axis, far)


def group(k):
    return slice(8 * k, 8 * k + 8)


def turned_next(mine, after, s):
    return jnp.where(s == G - 1, after, mine)


def turned_prev(mine, before, s):
    return jnp.where(s == 0, before, mine)


def turn_next(v):
    return pltpu.roll(v, G - 1, 0)


def turn_prev(v):
    return pltpu.roll(v, 1, 0)


def places(wide):
    shape = (G, wide)
    return lax.broadcasted_iota(jnp.int32, shape, 0), lax.broadcasted_iota(jnp.int32, shape, 1)


def along_z(tz, a, lane):
    return jnp.where(lane < a.shape[1] - 1, tz * a * z_next(a), 0.0)


Y_TURNS = {
    "c": (6, 2),
    "a": (4, 4),
    "tx": (3, 5),
    "e": (3, 6),
    "tz": (1, 7),
}
Y_PLACES = {
    "c": ((4, 5), (2, 3)),
    "a": ((3,), (4,)),
    "tx": ((2,), (5,)),
    "e": ((1,), (6,)),
    "tz": ((0,), (7,)),
}


def y_message_kernel(split_ref, *refs):
    low, high, (near_ref, far_ref) = refs[:8], refs[8:16], refs[16:]
    n, _, wide = low[3].shape
    even = lax.rem(lax.axis_index("gy"), 2) == 0
    step = pl.program_id(0)
    x0 = pl.multiple_of(STEP * step, 8)
    shape = (STEP, G, wide)
    row, s, lane = (lax.broadcasted_iota(jnp.int32, shape, k) for k in range(3))

    def turn(v, k):
        return jnp.stack([pltpu.roll(v[i], k, 0) for i in range(v.shape[0])])

    def fields(group, side):
        res, diag, crs, mask, tx, ty, tz, ff = group
        before, after = jnp.maximum(x0 - 1, 0), jnp.minimum(x0 + STEP, n - 1)
        a, trans = mask[pl.ds(x0, STEP)].astype(F32), tx[pl.ds(x0, STEP)]
        t = trans * a
        a_after = jnp.concatenate([a[1:], mask[pl.ds(after, 1)].astype(F32)], axis=0)
        t_before = jnp.concatenate([tx[pl.ds(before, 1)] * mask[pl.ds(before, 1)].astype(F32), t[:-1]], axis=0)
        b, c = quasi_impes(a, res[0], res[1], diag[0], diag[1], crs[0], crs[1])
        ty_a = ty[...] * a
        ey = ty_a * turn(a, G - 1)
        a_above = jnp.stack([z_next(a[i]) for i in range(STEP)])
        ez = jnp.where(lane < wide - 1, tz[...] * a * a_above, 0.0)
        more = ez + jnp.stack([z_prev(ez[i]) for i in range(STEP)])
        more = more + jnp.where(row + x0 == n - 1, 0.0, t * a_after)
        more = more + jnp.where(row + x0 == 0, 0.0, t_before * a)
        more = more + (ey if side else turn(ey, 1))
        c = jnp.where(s == (1 if side else 6), c + more, c)
        tile = b
        for name, v in (("c", c), ("a", a), ("tx", trans), ("e", ey), ("tz", tz[...])):
            moved = turn(v, Y_TURNS[name][side])
            for place in Y_PLACES[name][side]:
                tile = jnp.where(s == place, moved, tile)
        outer = slice(0, 1) if side else slice(7, 8)
        return tile, ty_a[:, outer], ff[:, outer, :]

    def put(rows, up, down):
        near_ref[rows, :] = jnp.where(even, up, down)
        far_ref[rows, :] = jnp.where(even, down, up)

    up, down = fields(high, 0), fields(low, 1)
    for k in range(STEP):
        put(pl.ds(pl.multiple_of(8 * (x0 + k), 8), 8), up[0][k], down[0][k])
        put(pl.ds(8 * n + x0 + k, 1), up[1][k], down[1][k])
        put(pl.ds(9 * n + x0 + k, 1), up[2][k], down[2][k])

    @pl.when(step == 0)
    def _():
        put(slice(10 * n, y_message_rows(n)), *[jnp.zeros((y_message_rows(n) - 10 * n, wide), F32)] * 2)
        first_lane = lax.broadcasted_iota(jnp.int32, (1, wide), 1)
        for q in range(n // 8):
            splits = split_ref[q : q + 1, :]
            above = (first_lane < splits[:, -1:]).astype(F32)
            below = (first_lane < splits[:, :1]).astype(F32)
            put(slice(10 * n + 2 + q, 10 * n + 3 + q), above, below)
        corners = [
            (tx[n - 1, at, :] * mask[n - 1, at, :].astype(F32), mask[0, at, :].astype(F32))
            for mask, tx, at in ((high[3], high[4], slice(6, 7)), (low[3], low[4], slice(1, 2)))
        ]
        for k in range(2):
            put(slice(10 * n + k, 10 * n + k + 1), corners[0][k], corners[1][k])


def y_message_rows(n):
    return 10 * n + pl.cdiv(2 + n // 8, 8) * 8


class Ghosts:
    def __init__(self, near_ref, far_ref, n):
        self.refs, self.n = (near_ref, far_ref), n
        self.even = lax.rem(lax.axis_index("gy"), 2) == 0
        self.s, _ = places(near_ref.shape[1])

    def both(self, rows):
        near, far = (ref[rows, :] for ref in self.refs)
        return jnp.where(self.even, far, near), jnp.where(self.even, near, far)

    def tiles(self, x):
        return self.both(pl.ds(pl.multiple_of(8 * x, 8), 8))

    def pick(self, tiles, name, low_at=(G - 1,), high_at=(0,)):
        low, high = tiles
        if name != "b":
            up, down = Y_TURNS[name]
            low, high = pltpu.roll(low, 8 - up, 0), pltpu.roll(high, 8 - down, 0)
        picked = jnp.zeros_like(low)
        for place in low_at:
            picked = jnp.where(self.s == place, low, picked)
        for place in high_at:
            picked = jnp.where(self.s == place, high, picked)
        return picked

    def row(self, at, low_at=G - 1, high_at=0):
        low, high = self.both(pl.ds(at, 1))
        return jnp.where(self.s == low_at, low, jnp.where(self.s == high_at, high, 0.0))

    def active(self, x):
        return self.pick(self.tiles(x), "a")

    def first_active(self):
        return self.active(0) + self.row(10 * self.n + 1, G - 2, 1)

    def last_trans(self):
        return self.row(10 * self.n, G - 2, 1)

    def frac(self, x):
        return self.row(9 * self.n + x)

    def lower(self, q):
        return self.row(10 * self.n + 2 + q)


def prep_kernel(res_hbm, diag_hbm, crs, mask_hbm, tx_hbm, ty_hbm, tz_hbm,
                rhs, own_diag, tot, gain, one, fx, fy, fz, al0, al1, be0, be1, fzb,
                res, diag, mask, tx, ty, tz, sems):
    n, own, wide = mask.shape
    groups = own // 8
    chunk = 4
    s, lane = places(wide)

    def copies(q):
        at = pl.ds(chunk * q, chunk)
        pairs = (
            (res_hbm.at[:, at], res.at[:, at]),
            (diag_hbm.at[:, at], diag.at[:, at]),
            (tx_hbm.at[at], tx.at[at]),
            (ty_hbm.at[at], ty.at[at]),
            (tz_hbm.at[at], tz.at[at]),
        )
        return [pltpu.make_async_copy(a, b, sems.at[k + 1, q]) for k, (a, b) in enumerate(pairs)]

    def masks(q):
        at = pl.ds(chunk * q, chunk)
        return pltpu.make_async_copy(mask_hbm.at[at], mask.at[at], sems.at[0, q])

    for q in range(n // chunk):
        for copy in (masks(q), *copies(q)):
            copy.start()
    masks(0).wait()

    def row(x, carry):
        first, last = x == 0, x == n - 1
        after = jnp.minimum(x + 1, n - 1)
        before = jnp.maximum(x - 1, 0)
        a_after = mask[x, group(0), :].astype(F32)
        turned_after = turn_next(a_after)
        ey_before = jnp.zeros((G, wide), F32)
        for k in range(groups):
            here = group(k)
            a, turned = a_after, turned_after
            rp, rs = res[0, x, here, :], res[1, x, here, :]
            dpp, dss = diag[0, x, here, :], diag[1, x, here, :]
            dps, dsp = crs[0, x, here, :], crs[1, x, here, :]
            det = dpp * dss - dps * dsp
            both = 1.0 / (dss * det)
            inverse = both * dss
            weight = dps * (both * det)
            b = a * (rp - weight * rs)
            c = a * (dpp - weight * dsp) + (1.0 - a)
            rhs[x, here, :] = b
            own_diag[x, here, :] = c
            al0[x, here, :] = dss * inverse
            al1[x, here, :] = dps * inverse
            be0[x, here, :] = dpp * inverse
            be1[x, here, :] = dsp * inverse
            t = tx[x, here, :] * a
            ex = t * mask[after, here, :].astype(F32)
            fx[x, here, :] = jnp.where(last, t, ex)
            total = c + jnp.where(last, 0.0, ex)
            total = total + jnp.where(first, 0.0, fx[before, here, :])
            ez = along_z(tz[x, here, :], a, lane)
            fz[x, here, :] = ez
            ez_before = z_prev(ez)
            fzb[x, here, :] = ez_before
            total = total + ez + ez_before
            ey = ty[x, here, :] * a
            if k < groups - 1:
                a_after = mask[x, group(k + 1), :].astype(F32)
                turned_after = turn_next(a_after)
                ey = ey * turned_next(turned, turned_after, s)
                inside = ey
            else:
                ey = jnp.where(s == G - 1, ey, ey * turned)
                inside = jnp.where(s == G - 1, 0.0, ey)
            fy[x, here, :] = ey
            ey_turned = turn_prev(inside)
            total = total + inside + turned_prev(ey_turned, ey_before, s)
            ey_before = ey_turned
            tot[x, here, :] = total
            if 0 < k < groups - 1:
                g = relaxation / total
                gain[x, here, :] = g
                one[x, here, :] = g * b
        return carry

    def part(q, carry):
        @pl.when(q < n // chunk - 1)
        def _():
            masks(q + 1).wait()

        for copy in copies(q):
            copy.wait()
        return lax.fori_loop(0, chunk, lambda k, v: row(chunk * q + k, v), carry, unroll=2)

    lax.fori_loop(0, n // chunk, part, 0)


class Finished:
    def __init__(self, x, n, ghosts, mask, rhs, tot, fx, fy, s, lane, ex_before=None):
        groups = mask.shape[1] // 8
        first, last = x == 0, x == n - 1
        tiles = ghosts.tiles(x)
        ga, gtx, gtz = (ghosts.pick(tiles, name) for name in ("a", "tx", "tz"))
        gb = ghosts.pick(tiles, "b", (G - 1, G - 2), (0, 1))
        gc = jnp.maximum(ghosts.pick(tiles, "c", (G - 1, G - 2), (0, 1)), 1.0)
        before, after = jnp.maximum(x - 1, 0), jnp.minimum(x + 1, n - 1)
        if ex_before is None:
            tiles_before = ghosts.tiles(before)
            ex_before = ghosts.pick(tiles_before, "a") * ghosts.pick(tiles_before, "tx") * ga
            ex_before = jnp.where(first, 0.0, ex_before)
        a_after = ghosts.active(after)
        end = fy[x, group(groups - 1), :]
        end = jnp.where(s == G - 1, end * turn_next(ga), end)
        a_first = turn_next(mask[x, group(0), :].astype(F32))
        ey = ghosts.pick(tiles, "e", (G - 2,), (0,))
        ey = jnp.where(s == G - 1, ghosts.row(8 * n + x) * a_first, ey)
        ey_turned = turn_prev(ey)
        ez = along_z(gtz, ga, lane)
        t = gtx * ga
        ex = t * a_after
        total = gc + ez + z_prev(ez) + ey + turned_prev(ey_turned, turn_prev(end), s)
        total = total + jnp.where(last, 0.0, ex) + ex_before
        self.ex = ex
        self.end = end
        self.fx, self.fy, self.fz = jnp.where(last, t + ghosts.last_trans(), ex), ey, ez
        self.rhs = gb
        self.total = (
            tot[x, group(0), :] + jnp.where(s == 0, ey_turned, 0.0),
            tot[x, group(groups - 1), :] + jnp.where(s == G - 1, end, 0.0),
            total,
        )
        self.all_rhs = (rhs[x, group(0), :], rhs[x, group(groups - 1), :], gb)


def slot_of(k, groups):
    return {0: 0, groups - 1: 1, groups: 2}[k]


def x_message_kernel(mask, rhs, tot, gain, one, fx, fy, fz, ynear, yfar, near_ref, far_ref):
    even = lax.rem(lax.axis_index("gx"), 2) == 0
    n, own, wide = mask.shape
    groups = own // 8
    s, lane = places(wide)
    ghosts = Ghosts(ynear, yfar, n)
    finished = {x: Finished(x, n, ghosts, mask, rhs, tot, fx, fy, s, lane) for x in (0, 1, n - 2, n - 1)}
    for k in range(groups + 1):
        here = group(k)
        touched = k in (0, groups - 1, groups)

        def first_of(x):
            done = finished[x]
            if not touched:
                return one[x, here, :]
            slot = slot_of(k, groups)
            return relaxation * done.all_rhs[slot] / done.total[slot]

        def of(x, key):
            done = finished[x]
            total = done.total[slot_of(k, groups)] if touched else tot[x, here, :]
            if k == groups:
                return done.rhs, total, key, done.fy
            return rhs[x, here, :], total, key, done.end if k == groups - 1 else fy[x, here, :]

        if k == groups:
            up = of(n - 1, finished[n - 1].fx)
            down = of(0, ghosts.first_active())
        else:
            up = of(n - 1, fx[n - 1, here, :])
            down = of(0, mask[0, here, :].astype(F32))
            up += (fz[n - 1, here, :], fx[n - 2, here, :] * first_of(n - 2))
            down += (fz[0, here, :], fx[0, here, :] * first_of(1))
        if k == groups:
            b, total, key, ey = (jnp.where(even, p, q) for p, q in zip(up, down, strict=True))
            ob, ototal, okey, oey = (jnp.where(even, q, p) for p, q in zip(up, down, strict=True))
            for ref, (b, total, key, ey) in (
                (near_ref, (b, total, key, ey)),
                (far_ref, (ob, ototal, okey, oey)),
            ):
                at = PLANES * own
                ref[at : at + G, :] = jnp.where((s == 0) | (s == G - 1), b, pltpu.roll(total, 4, 0))
                ref[at + G : at + 2 * G, :] = jnp.where((s < 2) | (s >= G - 2), key, pltpu.roll(ey, 4, 0))
        else:
            for f in range(PLANES):
                start = f * own + 8 * k
                near_ref[start : start + 8, :] = jnp.where(even, up[f], down[f])
                far_ref[start : start + 8, :] = jnp.where(even, down[f], up[f])


def late_messages(split_ref, ff, inv, near_ref, far_ref):
    even = lax.rem(lax.axis_index("gx"), 2) == 0
    j = lax.axis_index("gy")
    n, own, wide = ff.shape
    per_tile = 2 * split_ref.shape[0] * split_ref.shape[1]
    near_ref[0:own, :] = jnp.where(even, ff[n - 1], ff[0])
    far_ref[0:own, :] = jnp.where(even, ff[0], ff[n - 1])
    at = own
    unknowns = inv.shape[2]
    top = inv[0, pl.ds(pl.multiple_of(j * per_tile + per_tile - 16, 8), 16), :]
    bottom = inv[0, pl.ds(pl.multiple_of(j * per_tile, 8), 16), :]
    for k in range(0, unknowns, wide):
        w = min(wide, unknowns - k)
        if w < wide:
            near_ref[at : at + 16, :] = jnp.zeros((16, wide), F32)
            far_ref[at : at + 16, :] = jnp.zeros((16, wide), F32)
        near_ref[at : at + 16, :w] = jnp.where(even, top[:, k : k + w], bottom[:, k : k + w])
        far_ref[at : at + 16, :w] = jnp.where(even, bottom[:, k : k + w], top[:, k : k + w])
        at += 16
    lane = lax.broadcasted_iota(jnp.int32, (1, wide), 1)
    zero = jnp.zeros((8, wide), F32)
    near_ref[at : at + 8, :] = zero
    far_ref[at : at + 8, :] = zero
    for q in range(split_ref.shape[1]):
        top = (lane < split_ref[split_ref.shape[0] - 1, q]).astype(F32)
        bottom = (lane < split_ref[0, q]).astype(F32)
        near_ref[at + q : at + q + 1, :] = jnp.where(even, top, bottom)
        far_ref[at + q : at + q + 1, :] = jnp.where(even, bottom, top)


def late_rows(own, unknowns, wide):
    return own + 16 * pl.cdiv(unknowns, wide) + 8


class Planes:
    def __init__(self, near_ref, far_ref, own):
        self.refs, self.own = (near_ref, far_ref), own
        self.even = lax.rem(lax.axis_index("gx"), 2) == 0

    def rows(self, at, n, side):
        near, far = (ref[at : at + n, :] for ref in self.refs)
        return jnp.where(self.even, near, far) if side else jnp.where(self.even, far, near)

    def field(self, f, k, side):
        if 8 * k < self.own:
            return self.rows(f * self.own + 8 * k, 8, side)
        s, _ = places(self.refs[0].shape[1])
        ends = (s == 0) | (s == G - 1)
        if f < 2:
            tile = self.rows(PLANES * self.own, G, side)
            return jnp.where(ends, pltpu.roll(tile, 4, 0) if f else tile, 0.0)
        if f < 4:
            tile = self.rows(PLANES * self.own + G, G, side)
            if f == 2:
                return jnp.where((s < 2) | (s >= G - 2), tile, 0.0)
            return jnp.where(s == G - 1, pltpu.roll(tile, 4, 0), 0.0)
        return jnp.zeros_like(s, F32)


class Inside:
    def __init__(self, groups, ff, rhs, gain, one, fx, fy, fz, gain3, one3, six, end):
        self.groups, self.own_ff, self.own_rhs = groups, ff, rhs
        self.own_gain, self.own_one, self.own_fx, self.own_fy, self.own_fz = gain, one, fx, fy, fz
        self.gain3, self.one3, self.six, self.end = gain3, one3, six, end

    def pick(self, own, which, x, k):
        return self.six[which, x] if k == self.groups else own[x, group(k), :]

    def three(self, own, other, x, k):
        if 0 < k < self.groups - 1:
            return own[x, group(k), :]
        return other[x, group(slot_of(k, self.groups)), :]

    def rhs(self, x, k):
        return self.pick(self.own_rhs, 0, x, k)

    def fx(self, x, k):
        return self.pick(self.own_fx, 1, x, k)

    def fy(self, x, k):
        if k == self.groups - 1:
            return self.end[x]
        return self.pick(self.own_fy, 2, x, k)

    def fz(self, x, k):
        return self.pick(self.own_fz, 3, x, k)

    def ff(self, x, k):
        return self.pick(self.own_ff, 4, x, k)

    def gain(self, x, k):
        return self.three(self.own_gain, self.gain3, x, k)

    def one(self, x, k):
        return self.three(self.own_one, self.one3, x, k)

    def before(self, x, k):
        return self.fx(x - 1, k) * self.one(x - 1, k)

    def after(self, x, k):
        return self.fx(x, k) * self.one(x + 1, k)

    def faces_x(self, x, k):
        ex = self.fx(x, k)
        return ex, ex * (self.ff(x, k) + self.ff(x + 1, k))


def second_row(o, x, s, put):
    total = o.groups + 1
    p = o.one(x, 0)
    p_turned = turn_next(p)
    w_turned = turn_prev(o.fy(x, total - 1) * o.one(x, total - 1))
    for k in range(total):
        p_after = o.one(x, (k + 1) % total)
        after_turned = turn_next(p_after)
        ey, ez = o.fy(x, k), o.fz(x, k)
        mine = turn_prev(ey * p)
        beside = ey * turned_next(p_turned, after_turned, s) + turned_prev(mine, w_turned, s)
        beside = beside + ez * z_next(p) + z_prev(ez * p)
        beside = beside + o.after(x, k) + o.before(x, k)
        put(k, o.gain(x, k) * ((2.0 - relaxation) * o.rhs(x, k) + beside))
        p, p_turned, w_turned = p_after, after_turned, mine


def x_flux(o, x, k, two):
    step = two(x + 1, k) - two(x, k)
    ex, wx = o.faces_x(x, k)
    return ex * step, wx * step


def flux_row(o, x, s, lane, two, res, own_diag, fzb, split, carried, put):
    groups = o.groups

    def faces_y(k, p, p_turned, p_after, f, f_turned, f_after):
        ey = o.fy(x, k)
        weighted = ey * (f + turned_next(f_turned, f_after, s))
        return ey, weighted, turned_next(p_turned, p_after, s) - p

    p0, f0 = two(x, 0), o.ff(x, 0)
    p0_turned, f0_turned = turn_next(p0), turn_next(f0)
    p, f = two(x, groups), o.ff(x, groups)
    ghost = faces_y(groups, p, turn_next(p), p0_turned, f, turn_next(f), f0_turned)
    turned = [turn_prev(v) for v in ghost]
    p, f, p_turned, f_turned = p0, f0, p0_turned, f0_turned
    for k in range(groups):
        here = group(k)
        p_after, f_after = two(x, k + 1), o.ff(x, k + 1)
        p_after_turned, f_after_turned = turn_next(p_after), turn_next(f_after)
        mine = faces_y(k, p, p_turned, p_after_turned, f, f_turned, f_after_turned)
        mine_turned = [turn_prev(v) for v in mine]
        ey, wy, dy = mine
        ey_before, wy_before, dy_before = (
            turned_prev(a, b, s) for a, b in zip(mine_turned, turned, strict=True)
        )
        ez = o.fz(x, k)
        wz = ez * (f + z_next(f))
        dz = z_next(p) - p
        wz_before, dz_before = z_prev(wz), z_prev(dz)
        ez_before = fzb[x, here, :]
        qx, sx = x_flux(o, x, k, two)
        if carried is None:
            qx_before, sx_before = x_flux(o, x - 1, k, two)
        else:
            qx_before, sx_before = carried[0, here, :], carried[1, here, :]
            carried[0, here, :] = qx
            carried[1, here, :] = sx
        gained = (qx - qx_before) + (ey * dy - ey_before * dy_before)
        gained = gained + (ez * dz - ez_before * dz_before)
        weighed = (sx - sx_before) + (wy * dy - wy_before * dy_before)
        weighed = weighed + (wz * dz - wz_before * dz_before)
        rest = o.rhs(x, k) - own_diag[x, here, :] * p + gained
        below = lane < split(k)
        put(
            k,
            rest,
            res[0, x, here, :] + gained,
            res[1, x, here, :] + 0.5 * weighed,
            jnp.where(s == 0, ey_before, ey),
            jnp.where(s == 0, wy_before, wy),
            jnp.where(below, ez, ez_before),
            jnp.where(below, wz, wz_before),
        )
        turned = mine_turned
        p, f, p_turned, f_turned = p_after, f_after, p_after_turned, f_after_turned


FLUXES = 6


def interior_kernel(split_ref, inv, fzb, res, mask, ff, rhs, own_diag, tot, gain, one, fx, fy, fz, ynear, yfar,
                    late_near, late_far, tot3, gain3, one3, six, end, two, acc, *flux_and_carried):
    flux, carried = flux_and_carried[:FLUXES], flux_and_carried[FLUXES]
    late_messages(split_ref, ff, inv, late_near, late_far)
    n, own, wide = mask.shape
    groups = own // 8
    s, lane = places(wide)
    ghosts = Ghosts(ynear, yfar, n)

    def finish(x, carry):
        done = Finished(x, n, ghosts, mask, rhs, tot, fx, fy, s, lane, carry)
        for slot in range(3):
            g = relaxation / done.total[slot]
            tot3[x, group(slot), :] = done.total[slot]
            gain3[x, group(slot), :] = g
            one3[x, group(slot), :] = g * done.all_rhs[slot]
        end[x] = done.end
        for k, v in enumerate((done.rhs, done.fx, done.fy, done.fz, ghosts.frac(x))):
            six[k, x] = v
        return done.ex

    lax.fori_loop(0, n, finish, jnp.zeros((G, wide), F32), unroll=8)
    o = Inside(groups, ff, rhs, gain, one, fx, fy, fz, gain3, one3, six, end)

    def second(x, carry):
        def put(k, v):
            two[x, group(k), :] = v

        second_row(o, x, s, put)
        return carry

    lax.fori_loop(2, n - 2, second, 0, unroll=4)

    def two_of(x, k):
        return two[x, group(k), :]

    for k in range(groups):
        carried[0, group(k), :], carried[1, group(k), :] = x_flux(o, 2, k, two_of)
    acc[...] = jnp.zeros_like(acc)

    def row(x, carry):
        def put(k, rest, *values):
            acc[x // 8, group(k), :] += rest
            for f, v in enumerate(values):
                flux[f][x, group(k), :] = v

        flux_row(o, x, s, lane, two_of, res, own_diag, fzb, lambda k: split_ref[x // 8, k], carried, put)
        return carry

    lax.fori_loop(3, n - 3, row, 0, unroll=2)


class Edges(Inside):
    def beyond(self, n, planes, act, tot, tot3, one_edge, gain_edge, edge_fx):
        self.n, self.planes = n, planes
        self.slots = {-1: 0, 0: 1, n - 1: 2, n: 3}
        self.one_edge, self.gain_edge, self.edge_fx = one_edge, gain_edge, edge_fx
        self.far = {-1: 0, n: 1}
        for k in range(self.groups + 1):
            here = group(k)
            low = planes.field(2, k, 0) * act(k)
            high = super().fx(n - 1, k) * planes.field(2, k, 1)
            edge_fx[0, here, :] = low
            edge_fx[1, here, :] = high
            for x, slot in self.slots.items():
                face = low if x <= 0 else high
                if x in self.far:
                    total = jnp.maximum(planes.field(1, k, self.far[x]), 1.0) + face
                else:
                    total = self.three(tot, tot3, x, k) + face
                g = relaxation / total
                gain_edge[slot, here, :] = g
                one_edge[slot, here, :] = g * self.rhs(x, k)

    def rhs(self, x, k):
        return self.planes.field(0, k, self.far[x]) if x in self.far else super().rhs(x, k)

    def fx(self, x, k):
        if x in (-1, self.n - 1):
            return self.edge_fx[0 if x == -1 else 1, group(k), :]
        return super().fx(x, k)

    def fy(self, x, k):
        return self.planes.field(3, k, self.far[x]) if x in self.far else super().fy(x, k)

    def fz(self, x, k):
        return self.planes.field(4, k, self.far[x]) if x in self.far else super().fz(x, k)

    def gain(self, x, k):
        return self.gain_edge[self.slots[x], group(k), :] if x in self.slots else super().gain(x, k)

    def one(self, x, k):
        return self.one_edge[self.slots[x], group(k), :] if x in self.slots else super().one(x, k)

    def before(self, x, k):
        return self.planes.field(5, k, 0) if x == -1 else super().before(x, k)

    def after(self, x, k):
        return self.planes.field(5, k, 1) if x == self.n else super().after(x, k)


def edge_kernel(split_ref, fzb, res, mask, ff, rhs, own_diag, tot, gain, one, fx, fy, fz, ynear, yfar, xnear, xfar,
                tot3, gain3, one3, six, end, two, acc, *others):
    flux = others[FLUXES : 2 * FLUXES]
    sent, edge_fx, edge_step, one_edge, gain_edge, two_edge, near_fx, total_acc = others[2 * FLUXES :]
    n, own, wide = mask.shape
    groups = own // 8
    s, lane = places(wide)
    planes = Planes(xnear, xfar, own)
    ghosts = Ghosts(ynear, yfar, n)
    o = Edges(groups, ff, rhs, gain, one, fx, fy, fz, gain3, one3, six, end)

    def act(k):
        return ghosts.first_active() if k == groups else mask[0, group(k), :].astype(F32)

    o.beyond(n, planes, act, tot, tot3, one_edge, gain_edge, edge_fx)
    depth = 5
    bases = (-1, n - depth + 1)
    for side, base in enumerate(bases):
        for r in range(depth):
            x, slot = base + r, depth * side + r
            if x in (-1, 0, 1, n - 2, n - 1, n):

                def put_two(k, v, slot=slot):
                    two_edge[slot, group(k), :] = v

                second_row(o, x, s, put_two)
            else:
                two_edge[slot] = two[x]
            if x == n:
                continue
            for k in range(groups):
                ex = o.fx(x, k)
                near_fx[0, slot, group(k), :] = ex
                if x in (-1, n - 1):
                    near_fx[1, slot, group(k), :] = jnp.zeros_like(ex)
                else:
                    near_fx[1, slot, group(k), :] = ex * (o.ff(x, k) + o.ff(x + 1, k))
    for k in range(groups):
        edge_step[0, group(k), :] = two_edge[1, group(k), :] - two_edge[0, group(k), :]
        edge_step[1, group(k), :] = two_edge[2 * depth - 1, group(k), :] - two_edge[2 * depth - 2, group(k), :]
    total_acc[...] = acc[...]
    plain = Inside(groups, ff, rhs, gain, one, fx, fy, fz, gain3, one3, six, end)

    def row(r, carry):
        high = r >= depth - 2
        x = jnp.where(high, n - 2 * (depth - 2) + r, r)
        shift = jnp.where(high, depth - bases[1], -bases[0])

        def two_of(x, k):
            return two_edge[x + shift, group(k), :]

        def faces_x(x, k):
            return near_fx[0, x + shift, group(k), :], near_fx[1, x + shift, group(k), :]

        plain.faces_x = faces_x

        def put(k, rest, *values):
            total_acc[x // 8, group(k), :] += rest
            for f, v in enumerate(values):
                flux[f][x, group(k), :] = v

        flux_row(plain, x, s, lane, two_of, res, own_diag, fzb, lambda k: split_ref[x // 8, k], None, put)
        return carry

    lax.fori_loop(0, 2 * (depth - 2), row, 0, unroll=2)

    rows_b, cols_b = split_ref.shape
    lane = lax.broadcasted_iota(jnp.int32, (1, wide), 1)
    lower, upper = [], []
    for q in range(rows_b):
        for r in range(cols_b):
            column = jnp.sum(total_acc[q, group(r), :], axis=0, keepdims=True)
            below = lane < split_ref[q, r]
            lower.append(jnp.where(below, column, 0.0))
            upper.append(jnp.where(below, 0.0, column))
    count = rows_b * cols_b
    low_sum = jnp.sum(jnp.concatenate(lower, axis=0), axis=1, keepdims=True)
    high_sum = jnp.sum(jnp.concatenate(upper, axis=0), axis=1, keepdims=True)
    span = sent.shape[1]
    place = lax.broadcasted_iota(jnp.int32, (count, span), 1) - 2 * count * lax.axis_index("gy")
    which = 2 * lax.broadcasted_iota(jnp.int32, (count, span), 0)
    laid = jnp.where(place == which, low_sum, jnp.where(place == which + 1, high_sum, 0.0))
    sent[...] = jnp.broadcast_to(jnp.sum(laid, axis=0, keepdims=True), sent.shape)


def final_kernel(tiles_y, split_ref, frac, inv, ynear, yfar, xnear, xfar, fx, edge_fx, edge_step,
                 al0, al1, be0, be1, got, *rest):
    flux = rest[:FLUXES]
    out, coarse, step_y, step_z, across, held, sems = rest[FLUXES:]
    i, j = lax.axis_index("gx"), lax.axis_index("gy")
    n, own, wide = frac.shape
    ext = own + G
    unknowns = inv.shape[2]
    rows_b, cols_b = split_ref.shape
    per_tile = 2 * rows_b * cols_b
    ghosts = Ghosts(ynear, yfar, n)
    planes = Planes(xnear, xfar, own)
    s8, lane8 = places(wide)

    all_got = got[...]
    owner = lax.broadcasted_iota(jnp.int32, all_got.shape, 0)

    def row_of(tile_row):
        mine = (owner >= tile_row * tiles_y) & (owner < (tile_row + 1) * tiles_y)
        return jnp.sum(jnp.where(mine, all_got, 0.0), axis=0, keepdims=True)

    coarse_res = row_of(i)

    def solve(tile):
        start = pl.multiple_of(jnp.clip(tile, 0, tiles_y - 1) * per_tile, 8)
        block = inv[0, pl.ds(start, per_tile), :]
        e = jnp.sum(block * coarse_res[:, :unknowns], axis=1, keepdims=True)
        return jnp.broadcast_to(e, (per_tile, wide))

    mine, before, after = solve(j), solve(j - 1), solve(j + 1)

    def one_of(e, k):
        return jnp.broadcast_to(e[k : k + 1], (8, wide))

    for q in range(rows_b):
        for r in range(cols_b):
            k = 2 * (q * cols_b + r)
            low, high = one_of(mine, k), one_of(mine, k + 1)
            split = split_ref[q, r]
            coarse[q + 1, group(r), :] = jnp.where(lane8 < split, low, high)
            jump = high - low
            step_z[q, group(r), :] = jnp.where(
                lane8 == split - 1, jump, jnp.where(lane8 == split, -jump, 0.0)
            )
        below = ghosts.lower(q) > 0.5
        k_high, k_low = 2 * q * cols_b, 2 * (q * cols_b + cols_b - 1)
        coarse[q + 1, own:ext, :] = jnp.where(
            s8 == 0,
            jnp.where(below, one_of(after, k_high), one_of(after, k_high + 1)),
            jnp.where(below, one_of(before, k_low), one_of(before, k_low + 1)),
        )
        for r in range(cols_b):
            here = coarse[q + 1, group(r), :]
            ahead = turn_next(coarse[q + 1, group(r + 1), :])
            behind = turn_prev(coarse[q + 1, group(r - 1 if r else cols_b), :])
            step_y[q, group(r), :] = jnp.where(
                s8 == G - 1, ahead - here, jnp.where(s8 == 0, behind - here, 0.0)
            )
    blocks = pl.cdiv(unknowns, wide)
    for side, tile_row in ((0, i - 1), (1, i + 1)):
        other = row_of(tile_row)
        e = jnp.zeros((16, 1), F32)
        for k in range(blocks):
            w = min(wide, unknowns - k * wide)
            part = planes.rows(own + 16 * k, 16, side)[:, :w] * other[:, k * wide : k * wide + w]
            e = e + jnp.sum(part, axis=1, keepdims=True)
        e = jnp.broadcast_to(e, (16, wide))
        below = planes.rows(own + 16 * blocks, 8, side)
        skip = 16 - 2 * cols_b if side == 0 else 0
        at = 0 if side == 0 else rows_b + 1
        for r in range(cols_b):
            k = skip + 2 * r
            coarse[at, group(r), :] = jnp.where(one_of(below, r) > 0.5, one_of(e, k), one_of(e, k + 1))

    for q in range(rows_b + 1):
        x = 8 * q - 1
        for r in range(cols_b):
            here = group(r)
            ex = edge_fx[0, here, :] if q == 0 else edge_fx[1, here, :] if q == rows_b else fx[x, here, :]
            f_before = planes.rows(8 * r, 8, 0) if q == 0 else frac[x, here, :]
            f_after = planes.rows(8 * r, 8, 1) if q == rows_b else frac[x + 1, here, :]
            step = coarse[q + 1, here, :] - coarse[q, here, :]
            across[0, q, here, :] = ex * step
            if q in (0, rows_b):
                step = step + edge_step[0 if q == 0 else 1, here, :]
            across[1, q, here, :] = ex * (0.5 * (f_before + f_after)) * step

    def solved(x, q, beside=None, sign=None):
        for r in range(cols_b):
            here = group(r)
            u, v, wy, sy, wz, sz = (ref[x, here, :] for ref in flux)
            along_y, along_z = step_y[q, here, :], step_z[q, here, :]
            u = u + (wy * along_y + wz * along_z)
            v = v + 0.5 * (sy * along_y + sz * along_z)
            if beside is not None:
                u = sign(u, across[0, beside, here, :])
                v = sign(v, across[1, beside, here, :])
            held[0, x, here, :] = al0[x, here, :] * u - al1[x, here, :] * v
            held[1, x, here, :] = be0[x, here, :] * v - be1[x, here, :] * u

    def copies(q):
        return [
            pltpu.make_async_copy(
                held.at[k, pl.ds(4 * q, 4)], out.at[k, pl.ds(4 * q, 4)], sems.at[k, q]
            )
            for k in range(2)
        ]

    def block(q, carry):
        x = 8 * q
        solved(x, q, q, jnp.subtract)
        for k in range(1, 4):
            solved(x + k, q)
        for copy in copies(2 * q):
            copy.start()
        for k in range(4, 7):
            solved(x + k, q)
        solved(x + 7, q, q + 1, jnp.add)
        for copy in copies(2 * q + 1):
            copy.start()
        return carry

    lax.fori_loop(0, rows_b, block, 0, unroll=2)
    for q in range(2 * rows_b):
        for copy in copies(q):
            copy.wait()


def shards(tiles_x, tiles_y, residual, accum_diag, accum_cross, mask, trans_x, trans_y, trans_z,
           frac_flow, split_layer, coarse_inverse):
    n, own, wide = mask.shape
    ext = own + G
    unknowns = coarse_inverse.shape[2]
    columns = (residual, accum_diag, accum_cross, mask, trans_x, trans_y, trans_z, frac_flow)
    hbm = pl.BlockSpec(memory_space=pltpu.HBM)
    far_columns = [pltpu.with_memory_space_constraint(v, pltpu.HBM) for v in columns]

    def array(*shape):
        return jax.ShapeDtypeStruct(shape, F32)

    def group_spec(k, f):
        if f in (3, 4):
            return pl.BlockSpec((n, G, wide), lambda x: (0, k, 0))
        lead = columns[f].shape[:-3]
        return pl.BlockSpec((*lead, STEP, G, wide), lambda x: (*(0,) * len(lead), x, k, 0))

    y_messages = pl.pallas_call(
        y_message_kernel,
        grid=(n // STEP,),
        in_specs=[pl.BlockSpec(split_layer.shape, lambda x: (0, 0))]
        + [group_spec(0, f) for f in range(8)]
        + [group_spec(own // 8 - 1, f) for f in range(8)],
        out_specs=[WHOLE] * 2,
        out_shape=[array(y_message_rows(n), wide)] * 2,
        compiler_params=params(16),
        name="y_messages",
    )(pltpu.with_memory_space_constraint(split_layer, pltpu.HBM), *far_columns, *far_columns)
    ynear, yfar = swap(y_messages, "gy", tiles_y)

    rhs, own_diag, tot, gain, one, fx, fy, fz, al0, al1, be0, be1, fzb = pl.pallas_call(
        prep_kernel,
        in_specs=[hbm] * 2 + [WHOLE] + [hbm] * 4,
        out_specs=[WHOLE] * 13,
        out_shape=[array(n, own, wide)] * 13,
        scratch_shapes=[pltpu.VMEM(v.shape, v.dtype) for v in columns[:2] + columns[3:7]]
        + [pltpu.SemaphoreType.DMA((6, n // 4))],
        compiler_params=params(16),
        cost_estimate=cost(60_000_000, 30_000_000),
        name="prep",
    )(*far_columns[:2], accum_cross, *far_columns[3:7])
    shared = (rhs, tot, gain, one, fx, fy, fz)

    x_messages = pl.pallas_call(
        x_message_kernel,
        in_specs=[WHOLE] * 10,
        out_specs=[WHOLE] * 2,
        out_shape=[array(PLANES * own + 2 * G, wide)] * 2,
        compiler_params=params(8),
        name="x_messages",
    )(mask, *shared, ynear, yfar)
    xnear, xfar = swap(x_messages, "gx", tiles_x)

    shared = (residual, mask, frac_flow, rhs, own_diag, tot, gain, one, fx, fy, fz, ynear, yfar)
    late_near, late_far, tot3, gain3, one3, six, end, two, acc, *flux = pl.pallas_call(
        interior_kernel,
        in_specs=[SCALARS] + [WHOLE] * 15,
        out_specs=[WHOLE] * (9 + FLUXES),
        out_shape=[array(late_rows(own, unknowns, wide), wide)] * 2
        + [array(n, 3 * G, wide)] * 3
        + [
            array(5, n, G, wide),
            array(n, G, wide),
            array(n, ext, wide),
            array(n // 8, own, wide),
        ]
        + [array(n, own, wide)] * FLUXES,
        scratch_shapes=[pltpu.VMEM((2, own, wide), F32)],
        compiler_params=params(8),
        cost_estimate=cost(60_000_000, 30_000_000),
        name="interior",
    )(split_layer, coarse_inverse, fzb, *shared)
    late_near, late_far = swap((late_near, late_far), "gx", tiles_x)

    devices = tiles_x * tiles_y
    span = pl.cdiv(unknowns, 128) * 128
    *flux, sent, edge_fx, edge_step = pl.pallas_call(
        edge_kernel,
        in_specs=[SCALARS] + [WHOLE] * (23 + FLUXES),
        out_specs=[WHOLE] * (3 + FLUXES),
        out_shape=[array(n, own, wide)] * FLUXES
        + [
            array(devices, span),
            array(2, ext, wide),
            array(2, own, wide),
        ],
        scratch_shapes=[
            pltpu.VMEM((4, ext, wide), F32),
            pltpu.VMEM((4, ext, wide), F32),
            pltpu.VMEM((10, ext, wide), F32),
            pltpu.VMEM((2, 10, own, wide), F32),
            pltpu.VMEM((n // 8, own, wide), F32),
        ],
        input_output_aliases={24 + f: f for f in range(FLUXES)},
        compiler_params=params(8),
        name="edges",
    )(split_layer, fzb, *shared, xnear, xfar, tot3, gain3, one3, six, end, two, acc, *flux)
    got = lax.all_to_all(sent, ("gx", "gy"), 0, 0, tiled=True)

    return pl.pallas_call(
        functools.partial(final_kernel, tiles_y),
        in_specs=[SCALARS] + [WHOLE] * (14 + FLUXES),
        out_specs=pl.BlockSpec(memory_space=pl.ANY),
        out_shape=array(2, n, own, wide),
        scratch_shapes=[
            pltpu.VMEM((n // 8 + 2, ext, wide), F32),
            pltpu.VMEM((n // 8, own, wide), F32),
            pltpu.VMEM((n // 8, own, wide), F32),
            pltpu.VMEM((2, n // 8 + 1, own, wide), F32),
            pltpu.VMEM((2, n, own, wide), F32),
            pltpu.SemaphoreType.DMA((2, n // 4)),
        ],
        compiler_params=params(12),
        name="final",
    )(split_layer, frac_flow, coarse_inverse, ynear, yfar, late_near, late_far, fx, edge_fx,
      edge_step, al0, al1, be0, be1, got, *flux)


def solution(mesh):
    placed = (
        P(None, "gx", "gy", None),
        P(None, "gx", "gy", None),
        P(None, "gx", "gy", None),
        P("gx", "gy", None),
        P("gx", "gy", None),
        P("gx", "gy", None),
        P("gx", "gy", None),
        P("gx", "gy", None),
        P("gx", "gy"),
        P("gx", None, None),
    )
    return jax.shard_map(
        functools.partial(shards, mesh.shape["gx"], mesh.shape["gy"]),
        mesh=mesh,
        in_specs=placed,
        out_specs=P(None, "gx", "gy", None),
        check_vma=False,
    )
```
